32 devices in a mesh: dp: 8 (over z, y), seq: 4 (over x, core).
Axes of the slice: x: 2, y: 2, z: 4, core: 2. Of those that a mesh axis runs over, the one named last changes fastest.
Arguments:
- rows_in: bfloat16 [2, 8, 2048, 1120], P(None, 'dp', 'seq'), may hold values from -6 to 6
- out_cotangent: bfloat16 [2, 8, 2048, 1120], P(None, 'dp', 'seq'), may hold values from -6 to 6
- cell_lengths: int32 [2, 8, 11], P(None, 'dp'), may hold values from 0 to 2000, as said below
- cell_starts: int32 [2, 8, 11], P(None, 'dp'), may hold values from 0 to 2048, as said below
- key_mask: int32 [2, 8, 2048], P(None, 'dp'), may hold values from 0 to 1, as said below
- weights_master: float32 [8, 4, 470400], P('dp', 'seq')
- first_moment: float32 [8, 4, 470400], P('dp', 'seq')
- second_moment: float32 [8, 4, 470400], P('dp', 'seq'), as said below
- small_master: float32 [12, 1120], replicated
- small_first: float32 [12, 1120], replicated, may hold values from -192 to 192
- small_second: float32 [12, 1120], replicated, may hold values from 37.02784 to 589.824
- step_count: int32 [1], replicated, may hold values from 1 to 20
Outputs:
- rows_out: bfloat16 [2, 8, 2048, 1120], P(None, 'dp', 'seq')
- input_grad: bfloat16 [2, 8, 2048, 1120], P(None, 'dp', 'seq')
- weight_grads: float32 [8, 4, 470400], P('dp', 'seq')
- weight_moments: float32 [2, 8, 4, 470400], P(None, 'dp', 'seq')
- weights_new: float32 [8, 4, 470400], P('dp', 'seq')
- weights_copy: bfloat16 [8, 4, 470400], P('dp', 'seq')
- lamb_stats: float32 [3, 4], replicated
- small_grads: float32 [12, 1120], replicated
- small_moments: float32 [2, 12, 1120], replicated
- small_new: float32 [12, 1120], replicated
The draws below stay inside these ranges and needn't reach their ends.
Inputs may be any that keep to these rules, and one draw needn't show every extreme that they name: `cell_lengths`: in each pack the used slots come first and their cells lie end to end from position 0; a used slot holds 200 to 2000 genes, later slots hold 0, and a pack's lengths sum to at most 2048. `cell_starts`: A used slot starts at the sum of the pack's lengths in the slots before it; an empty slot starts at 2048. `key_mask`: 1 exactly at the positions that lie inside a cell of the pack. `second_moment`: positive.
All inputs are finite; a program needn't handle non-finite values.
Results may differ from the reference program's by a relative error of at most 0.01.
The reference program's roundings to bfloat16 on the way count: a program that leaves them out, or rounds other values in their place, can miss the bound.
Values may be sent and summed in bfloat16 or wider, within the bound.
No kernel may reach another device: no remote copies, remote signals or barrier semaphores. Data moves between devices by JAX's collectives and lax.ppermute only.
A program may use at most 320 MiB of HBM per device.

```python
import math
from functools import partial
import jax
import jax.numpy as jnp
from jax import lax

D = 1120
HEADS = 20
HDIM = 56
FF = 4480
PACK = 2048
LMIN = 200
LMAX = 2000
MICRO = 2
CELLS = 11
NTOK = 32768
SHARD = 470400
N_DP = 8
N_SEQ = 4


def region_table(entries):
    head_share = D // N_SEQ
    ff_share = FF // N_SEQ
    place = jnp.arange(N_DP, dtype=jnp.int32)[:, None, None] * SHARD + jnp.arange(SHARD, dtype=jnp.int32)[None, None, :]
    place = place + jnp.zeros((N_DP, N_SEQ, SHARD), jnp.int32)
    first_end = 3 * D * head_share
    second_end = first_end + head_share * D
    third_end = second_end + D * ff_share
    region = (place >= first_end).astype(jnp.int32) + (place >= second_end).astype(jnp.int32) + (place >= third_end).astype(jnp.int32)
    result = jnp.full((N_DP, N_SEQ, SHARD), entries[0], jnp.float32)
    result = jnp.where(region == 1, entries[1], result)
    result = jnp.where(region == 2, entries[2], result)
    return jnp.where(region == 3, entries[3], result)


def grad_sizes():
    root = math.sqrt(NTOK)
    return region_table((2.0 * root, 0.6 * root, 0.6 * root, 0.65 * root))


def draw_weights_master(key, part):
    spread = region_table((math.sqrt(2.0 / D), math.sqrt(8.0 / D), math.sqrt(1.0 / D), math.sqrt(1.0 / FF)))
    noise = jax.random.normal(jax.random.fold_in(key, 1), (N_DP, N_SEQ, SHARD), jnp.float32)
    return noise * spread


def draw_first_moment(key, part):
    noise = jax.random.normal(jax.random.fold_in(key, 2), (N_DP, N_SEQ, SHARD), jnp.float32)
    return noise * 0.111 * grad_sizes()


def draw_second_moment(key, part):
    factor = jnp.exp(jax.random.uniform(jax.random.fold_in(key, 3), (N_DP, N_SEQ, SHARD), jnp.float32, math.log(0.5), math.log(8.0)))
    sizes_now = grad_sizes()
    return factor * 0.001 * sizes_now * sizes_now


def draw_small_master(key, part):
    noise = jax.random.normal(jax.random.fold_in(key, 4), (12, D), jnp.float32)
    row_index = jnp.arange(12, dtype=jnp.int32)[:, None]
    is_gain = (row_index == 0) | (row_index == 2)
    return jnp.where(is_gain, 1.0 + 0.1 * noise, 0.2 * noise)


def pack_layout(key):
    layout_key = jax.random.fold_in(key, 11)
    draws_int = jax.random.randint(layout_key, (MICRO, N_DP, CELLS), 0, 1001)
    curved = draws_int * draws_int // 1000
    lengths_raw = LMIN + (LMAX - LMIN) * curved // 1000 * curved // 1000
    lengths_raw = lengths_raw.at[0, 0, 0].set(LMAX).astype(jnp.int32)
    cell_ends = jnp.cumsum(lengths_raw, axis=-1).astype(jnp.int32)
    fitted = cell_ends <= PACK
    lengths = jnp.where(fitted, lengths_raw, 0).astype(jnp.int32)
    filled = jnp.sum(lengths, axis=-1, keepdims=True).astype(jnp.int32)
    starts = jnp.where(fitted, cell_ends - lengths_raw, PACK).astype(jnp.int32)
    positions = jnp.arange(PACK, dtype=jnp.int32)
    padding = (positions[None, None, :] < filled).astype(jnp.int32)
    return (lengths, starts, padding)


def draw_cell_lengths(key, part):
    return pack_layout(key)[0]


def draw_cell_starts(key, part):
    return pack_layout(key)[1]


def draw_key_mask(key, part):
    return pack_layout(key)[2]


def shard_levels(own_key, dims, split, low, largest):
    level = 1.0
    for position, shards_of in split:
        draws = jax.random.uniform(jax.random.fold_in(jax.random.fold_in(own_key, 6), position), (shards_of,), jnp.float32, low / len(split), largest / len(split))
        level = level * jnp.repeat(jnp.exp(draws), dims[position] // shards_of).reshape((-1,) + (1,) * (len(dims) - 1 - position))
    return level


def bell_draw(own_key, shape, scale, most, pieces=(), kind=jnp.bfloat16):
    drawn = scale * jax.random.normal(own_key, shape, jnp.float32)
    if pieces:
        drawn = drawn * shard_levels(own_key, shape, pieces, -0.22, 0.18)
    return jnp.clip(drawn, -most, most).astype(kind)


def setup_inputs(seed: int = 0) -> dict:
    seeds = jax.random.split(jax.random.key(seed), 13)
    rows_in = bell_draw(seeds[0], (MICRO, N_DP, PACK, D), 1.0, 6.0, ((1, 8), (2, 4)))
    out_cotangent = bell_draw(seeds[1], (MICRO, N_DP, PACK, D), 1.0, 6.0, ((1, 8), (2, 4)))
    cell_lengths = draw_cell_lengths(jax.random.fold_in(seeds[12], 71), 0)
    cell_starts = draw_cell_starts(jax.random.fold_in(seeds[12], 71), 0)
    key_mask = draw_key_mask(jax.random.fold_in(seeds[12], 71), 0)
    weights_master = draw_weights_master(jax.random.fold_in(seeds[12], 71), 0)
    first_moment = draw_first_moment(jax.random.fold_in(seeds[12], 71), 0)
    second_moment = draw_second_moment(jax.random.fold_in(seeds[12], 71), 0)
    small_master = draw_small_master(jax.random.fold_in(seeds[12], 71), 0)
    small_first = bell_draw(seeds[9], (12, D), (0.17 * NTOK ** 0.5), 192.0, (), jnp.float32)
    small_second = jnp.clip(jnp.exp(jax.random.uniform(seeds[10], (12, D), jnp.float32, math.log(37.02784), math.log(589.824))), 37.02784, 589.824)
    step_count = jax.random.randint(seeds[11], (1,), 1, 21).astype(jnp.int32)
    return dict(rows_in=rows_in, out_cotangent=out_cotangent, cell_lengths=cell_lengths, cell_starts=cell_starts, key_mask=key_mask, weights_master=weights_master, first_moment=first_moment, second_moment=second_moment, small_master=small_master, small_first=small_first, small_second=small_second, step_count=step_count)


@jax.custom_vjp
def low(v):
    return lax.optimization_barrier(v.astype(jnp.bfloat16)).astype(jnp.float32)

@jax.custom_vjp
def low_back(v):
    return v

def low_keep(v):
    return (low(v), None)

def low_pass(kept, grad):
    return (grad,)

def back_keep(v):
    return (v, None)

def back_low(kept, grad):
    return (low(grad),)
low.defvjp(low_keep, low_pass)
low_back.defvjp(back_keep, back_low)
NORM_EPS = 1e-05
BETA_ONE = 0.9
BETA_TWO = 0.999
ADAM_EPS = 1e-06
DECAY = 0.01
MATRIX_RATE = 0.3
SMALL_RATE = 0.25
MASKED = -1e+30
HIGHEST_PRECISION = lax.Precision.HIGHEST

def normalize(row_block, gain, shift):
    center = lax.optimization_barrier(jnp.mean(row_block, axis=-1, keepdims=True))
    centered = row_block - center
    spread = lax.optimization_barrier(jnp.mean(centered * centered, axis=-1, keepdims=True))
    return centered * lax.rsqrt(spread + NORM_EPS) * gain + shift

def cell_labels(starts, lengths, length):
    positions = jnp.arange(length, dtype=jnp.int32)
    inside = (positions[:, None] >= starts[None, :]) & (positions[:, None] < (starts + lengths)[None, :])
    numbers = jnp.arange(1, starts.shape[0] + 1, dtype=jnp.int32)
    return lax.optimization_barrier(jnp.max(jnp.where(inside, numbers[None, :], 0), axis=1)).astype(jnp.int32)

def visible(first_row, labels, key_padding, block_rows):
    row_places = first_row + jnp.arange(block_rows, dtype=jnp.int32)
    col_places = jnp.arange(labels.shape[0], dtype=jnp.int32)
    row_labels = lax.dynamic_slice_in_dim(labels, first_row, block_rows)
    same_cell = (row_labels[:, None] == labels[None, :]) & (col_places[None, :] < row_places[:, None]) & (key_padding[None, :] == 1)
    return same_cell | (col_places[None, :] == row_places[:, None])

def attention(queries, key_heads, values, labels, key_padding):
    length = queries.shape[0]
    block_rows = min(512, length)
    block_count = length // block_rows
    score_scale = HDIM ** (-0.5)

    def one_block(block_args):
        query_block, first_row = block_args
        scores = low_back(jnp.einsum('qhd,khd->hqk', query_block, key_heads, precision=HIGHEST_PRECISION) * score_scale)
        allowed = visible(first_row, labels, key_padding, block_rows)
        probabilities = low(jax.nn.softmax(jnp.where(allowed[None], scores, MASKED), axis=-1))
        return jnp.einsum('hqk,khd->qhd', probabilities, values, precision=HIGHEST_PRECISION)
    firsts = jnp.arange(block_count, dtype=jnp.int32) * block_rows
    mixture = lax.map(jax.checkpoint(one_block), (queries.reshape(block_count, block_rows, HEADS, HDIM), firsts))
    return mixture.reshape(length, HEADS * HDIM)

def pack_forward(row_block, labels, key_padding, w_attn, w_out, w_in, w_back, params):
    length = row_block.shape[0]
    low_one = low(normalize(row_block, params[0], params[1]))
    attn_bias = jnp.concatenate([params[4], jnp.zeros_like(params[4]), params[5]])
    projected = low(low_back(jnp.dot(low_one, w_attn, precision=HIGHEST_PRECISION) + attn_bias))
    queries = projected[:, :D].reshape(length, HEADS, HDIM)
    key_heads = projected[:, D:2 * D].reshape(length, HEADS, HDIM)
    values = projected[:, 2 * D:].reshape(length, HEADS, HDIM)
    attended = low(low_back(attention(queries, key_heads, values, labels, key_padding)))
    branch = low_back(jnp.dot(attended, w_out, precision=HIGHEST_PRECISION) + params[6])
    middle = row_block + branch
    low_two = low(normalize(middle, params[2], params[3]))
    inner_sum = low_back(jnp.dot(low_two, w_in, precision=HIGHEST_PRECISION) + params[8:12].reshape(FF))
    activated = low(jax.nn.gelu(inner_sum, approximate=True))
    mlp_out = low_back(jnp.dot(activated, w_back, precision=HIGHEST_PRECISION) + params[7])
    return middle + mlp_out

def layer(row_all, w_attn, w_out, w_in, w_back, params, labels_all, padding_all):
    pack_step = jax.checkpoint(pack_forward)

    def scan_step(carry, pack_args):
        return (carry, pack_step(pack_args[0], pack_args[1], pack_args[2], w_attn, w_out, w_in, w_back, params))
    unused, outputs = lax.scan(scan_step, jnp.zeros((), jnp.float32), (row_all, labels_all, padding_all))
    return outputs

def from_layout(flat):
    head_share = D // N_SEQ
    ff_share = FF // N_SEQ
    per_share = jnp.transpose(flat, (1, 0, 2)).reshape(N_SEQ, -1)
    first_end = 3 * D * head_share
    second_end = first_end + head_share * D
    third_end = second_end + D * ff_share
    w_attn = jnp.transpose(per_share[:, :first_end].reshape(N_SEQ, D, 3, head_share), (1, 2, 0, 3)).reshape(D, 3 * D)
    w_out = per_share[:, first_end:second_end].reshape(D, D)
    w_in = jnp.transpose(per_share[:, second_end:third_end].reshape(N_SEQ, D, ff_share), (1, 0, 2)).reshape(D, FF)
    w_back = per_share[:, third_end:].reshape(FF, D)
    return (w_attn, w_out, w_in, w_back)

def to_layout(w_attn, w_out, w_in, w_back):
    head_share = D // N_SEQ
    ff_share = FF // N_SEQ
    part_attn = jnp.transpose(w_attn.reshape(D, 3, N_SEQ, head_share), (2, 0, 1, 3)).reshape(N_SEQ, -1)
    part_out = w_out.reshape(N_SEQ, -1)
    part_in = jnp.transpose(w_in.reshape(D, N_SEQ, ff_share), (1, 0, 2)).reshape(N_SEQ, -1)
    part_back = w_back.reshape(N_SEQ, -1)
    per_share = jnp.concatenate([part_attn, part_out, part_in, part_back], axis=1)
    return jnp.transpose(per_share.reshape(N_SEQ, N_DP, SHARD), (1, 0, 2))

def region_of():
    head_share = D // N_SEQ
    ff_share = FF // N_SEQ
    place = jnp.arange(N_DP, dtype=jnp.int32)[:, None, None] * SHARD + jnp.arange(SHARD, dtype=jnp.int32)[None, None, :]
    first_end = 3 * D * head_share
    second_end = first_end + head_share * D
    third_end = second_end + D * ff_share
    return (place >= first_end).astype(jnp.int32) + (place >= second_end).astype(jnp.int32) + (place >= third_end).astype(jnp.int32)

def reference(rows_in, out_cotangent, cell_lengths, cell_starts, key_mask, weights_master, first_moment, second_moment, small_master, small_first, small_second, step_count):
    packs = MICRO * N_DP
    copies = lax.optimization_barrier(weights_master.astype(jnp.bfloat16)).astype(jnp.float32)
    w_attn, w_out, w_in, w_back = from_layout(copies)
    labels_all = jax.vmap(partial(cell_labels, length=PACK))(cell_starts.reshape(packs, CELLS), cell_lengths.reshape(packs, CELLS))
    padding_all = key_mask.reshape(packs, PACK)
    row_all = rows_in.astype(jnp.float32).reshape(packs, PACK, D)

    def whole(row_args, attn_args, out_args, in_args, back_args, small_args):
        return layer(row_args, attn_args, out_args, in_args, back_args, small_args, labels_all, padding_all)
    outputs, pull = jax.vjp(whole, row_all, w_attn, w_out, w_in, w_back, small_master)
    grad_rows, grad_attn, grad_out, grad_in, grad_back, grad_small = pull(out_cotangent.astype(jnp.float32).reshape(packs, PACK, D))
    reduced = to_layout(grad_attn, grad_out, grad_in, grad_back)
    master = weights_master
    steps_done = step_count[0].astype(jnp.float32)
    fix_one = 1.0 - jnp.exp(steps_done * math.log(BETA_ONE))
    fix_two = 1.0 - jnp.exp(steps_done * math.log(BETA_TWO))
    first_new = BETA_ONE * first_moment + (1.0 - BETA_ONE) * reduced
    second_new = BETA_TWO * second_moment + (1.0 - BETA_TWO) * reduced * reduced
    update = first_new / fix_one / (jnp.sqrt(second_new / fix_two) + ADAM_EPS) + DECAY * master
    region = region_of()
    weight_norms = jnp.stack([jnp.sqrt(jnp.sum(jnp.where(region == part, master * master, 0.0))) for part in range(4)])
    update_norms = jnp.stack([jnp.sqrt(jnp.sum(jnp.where(region == part, update * update, 0.0))) for part in range(4)])
    ratios = weight_norms / update_norms
    ratio_entries = jnp.where(region == 0, ratios[0], jnp.where(region == 1, ratios[1], jnp.where(region == 2, ratios[2], ratios[3])))
    new_master = master - MATRIX_RATE * ratio_entries * update
    small_one = BETA_ONE * small_first + (1.0 - BETA_ONE) * grad_small
    small_two = BETA_TWO * small_second + (1.0 - BETA_TWO) * grad_small * grad_small
    small_updated = small_master - SMALL_RATE * (small_one / fix_one) / (jnp.sqrt(small_two / fix_two) + ADAM_EPS)
    rows_out = outputs.reshape(MICRO, N_DP, PACK, D).astype(jnp.bfloat16)
    input_grad = grad_rows.reshape(MICRO, N_DP, PACK, D).astype(jnp.bfloat16)
    return (rows_out, input_grad, reduced, jnp.stack([first_new, second_new]), new_master, new_master.astype(jnp.bfloat16), jnp.stack([weight_norms, update_norms, ratios]), grad_small, jnp.stack([small_one, small_two]), small_updated)
```

```python
import functools
import math

import jax
import jax.numpy as jnp
from jax import lax
from jax.experimental import pallas as pl
from jax.experimental.pallas import tpu as pltpu
from jax.sharding import PartitionSpec as P

HEADS = 20


NORM_EPS = 1e-05
BETA_ONE = 0.9
BETA_TWO = 0.999
ADAM_EPS = 1e-06
DECAY = 0.01
MATRIX_RATE = 0.3
SMALL_RATE = 0.25
MASKED = -1e30
LOG2_E = 1.4426950408889634
QUERY_BLOCK = 512
KEY_BLOCK = 512

F32 = jnp.float32
BF16 = jnp.bfloat16


def dot_rows(left, right):
    return lax.dot_general(left, right, (((1,), (0,)), ((), ())), preferred_element_type=F32)


def dot_transposed(left, right):
    return lax.dot_general(left, right, (((1,), (1,)), ((), ())), preferred_element_type=F32)


def dot_columns(left, right):
    return lax.dot_general(left, right, (((0,), (0,)), ((), ())), preferred_element_type=F32)


def norm_stats(rows):
    center = jnp.mean(rows, axis=-1, keepdims=True)
    centered = rows - center
    spread = jnp.mean(centered * centered, axis=-1, keepdims=True)
    scale = lax.rsqrt(spread + NORM_EPS)
    return centered * scale, scale


def norm_backward(upstream, hat, scale, gain):
    weighted = upstream * gain
    return (
        weighted
        - jnp.mean(weighted, axis=-1, keepdims=True)
        - hat * jnp.mean(weighted * hat, axis=-1, keepdims=True)
    ) * scale


def gelu_parts(values):
    inner = math.sqrt(2.0 / math.pi)
    squares = values * values
    bent = jnp.tanh(inner * (values + 0.044715 * values * squares))
    half = 0.5 * (1.0 + bent)
    slope = half + 0.5 * values * (1.0 - bent * bent) * inner * (1.0 + 3.0 * 0.044715 * squares)
    return values * half, slope


def attention_forward_body(
    heads, width, bq, bk, low_ref, start_ref, qkv_ref, out_ref, outt_ref, lse_ref, qs, ks, vt, acc
):
    length = qkv_ref.shape[0]
    flat = heads * width
    factor = width**-0.5 * LOG2_E
    for h in range(heads):
        qs[h] = qkv_ref[:, h * width : (h + 1) * width]
        ks[h] = qkv_ref[:, flat + h * width : flat + (h + 1) * width]

    def turn_values(kb, carry):
        rows = pl.ds(pl.multiple_of(kb * bk, bk), bk)
        turned = qkv_ref[rows, 2 * flat : 3 * flat].astype(F32).T
        for h in range(heads):
            vt[h, kb] = turned[h * width : (h + 1) * width].astype(BF16)
        return carry

    lax.fori_loop(0, length // bk, turn_values, 0)

    def query_step(qb, carry):
        q0 = pl.multiple_of(qb * bq, bq)
        start = start_ref[qb]
        query_place = q0 + lax.broadcasted_iota(jnp.int32, (1, bq), 1)
        acc[...] = jnp.zeros_like(acc)

        def key_step(kb, tops_totals):
            tops, totals = tops_totals
            k0 = pl.multiple_of(kb * bk, bk)
            key_place = k0 + lax.broadcasted_iota(jnp.int32, (bk, bq), 0)
            allowed = (key_place <= query_place) & (key_place >= start)
            new_tops, new_totals = [], []
            for h in range(heads):
                scores = dot_transposed(ks[h, pl.ds(k0, bk)], qs[h, pl.ds(q0, bq)]) * factor
                scores = jnp.where(allowed, scores, MASKED)
                top = jnp.maximum(tops[h], jnp.max(scores, axis=0, keepdims=True))
                fade = jnp.exp2(tops[h] - top)
                weights = jnp.exp2(scores - top)
                own = slice(h * width, (h + 1) * width)
                acc[own] = acc[own] * fade + dot_rows(vt[h, kb], weights.astype(BF16))
                new_tops.append(top)
                new_totals.append(totals[h] * fade + jnp.sum(weights, axis=0, keepdims=True))
            return tuple(new_tops), tuple(new_totals)

        first = (
            tuple(jnp.full((1, bq), -1e29, F32) for _ in range(heads)),
            tuple(jnp.zeros((1, bq), F32) for _ in range(heads)),
        )
        tops, totals = lax.fori_loop(low_ref[qb], (q0 + bq + bk - 1) // bk, key_step, first)
        for h in range(heads):
            own = slice(h * width, (h + 1) * width)
            acc[own] = acc[own] * (1.0 / totals[h])
            lse_ref[qb, h : h + 1, :] = tops[h] + jnp.log2(totals[h])
        mixed = acc[...]
        outt_ref[qb] = mixed
        out_ref[pl.ds(q0, bq), :] = mixed.T.astype(BF16)
        return carry

    lax.fori_loop(0, length // bq, query_step, 0)


def attention_backward_body(
    heads,
    width,
    bq,
    bk,
    low_ref,
    start_ref,
    qkv_ref,
    dout_ref,
    outt_ref,
    lse_ref,
    grad_ref,
    qs,
    ks,
    vs,
    ds,
    kt,
    dk,
    dv,
    dqt,
):
    length = qkv_ref.shape[0]
    flat = heads * width
    score_scale = width**-0.5
    factor = score_scale * LOG2_E
    for h in range(heads):
        own = slice(h * width, (h + 1) * width)
        qs[h] = qkv_ref[:, own]
        ks[h] = qkv_ref[:, flat + h * width : flat + (h + 1) * width]
        vs[h] = qkv_ref[:, 2 * flat + h * width : 2 * flat + (h + 1) * width]
        ds[h] = dout_ref[:, own]
    dk[...] = jnp.zeros_like(dk)
    dv[...] = jnp.zeros_like(dv)

    def turn_keys(kb, carry):
        rows = pl.ds(pl.multiple_of(kb * bk, bk), bk)
        turned = qkv_ref[rows, flat : 2 * flat].astype(F32).T
        for h in range(heads):
            kt[h, kb] = turned[h * width : (h + 1) * width].astype(BF16)
        return carry

    lax.fori_loop(0, length // bk, turn_keys, 0)

    def query_step(qb, carry):
        q0 = pl.multiple_of(qb * bq, bq)
        queries = pl.ds(q0, bq)
        start = start_ref[qb]
        query_place = q0 + lax.broadcasted_iota(jnp.int32, (1, bq), 1)
        products = dout_ref[queries, :].astype(F32).T * outt_ref[qb]
        inners = [
            jnp.sum(products[h * width : (h + 1) * width], axis=0, keepdims=True)
            for h in range(heads)
        ]
        dqt[...] = jnp.zeros_like(dqt)

        def key_step(kb, inner_carry):
            k0 = pl.multiple_of(kb * bk, bk)
            keys = pl.ds(k0, bk)
            key_place = k0 + lax.broadcasted_iota(jnp.int32, (bk, bq), 0)
            allowed = (key_place <= query_place) & (key_place >= start)
            for h in range(heads):
                scores = dot_transposed(ks[h, keys], qs[h, queries]) * factor
                weights = jnp.exp2(
                    jnp.where(allowed, scores - lse_ref[qb, h : h + 1, :], MASKED)
                )
                dweights = dot_transposed(vs[h, keys], ds[h, queries])
                dscores = (weights * (dweights - inners[h])).astype(BF16)
                dv[h, keys] += dot_rows(weights.astype(BF16), ds[h, queries])
                dk[h, keys] += dot_rows(dscores, qs[h, queries])
                dqt[h * width : (h + 1) * width] += dot_rows(kt[h, kb], dscores)
            return inner_carry

        lax.fori_loop(low_ref[qb], (q0 + bq + bk - 1) // bk, key_step, 0)
        grad_ref[queries, 0:flat] = (dqt[...] * score_scale).T.astype(BF16)
        return carry

    lax.fori_loop(0, length // bq, query_step, 0)

    def write_keys(kb, carry):
        rows = pl.ds(pl.multiple_of(kb * bk, bk), bk)
        grad_ref[rows, flat : 2 * flat] = jnp.concatenate(
            [dk[h, rows] * score_scale for h in range(heads)], axis=1
        ).astype(BF16)
        grad_ref[rows, 2 * flat : 3 * flat] = jnp.concatenate(
            [dv[h, rows] for h in range(heads)], axis=1
        ).astype(BF16)
        return carry

    lax.fori_loop(0, length // bk, write_keys, 0)


def whole_block(shape):
    return pl.BlockSpec(shape, lambda step, *refs: (0,) * len(shape))


def attention_forward(low_blocks, starts, qkv, heads):
    length, triple = qkv.shape
    flat = triple // 3
    width = flat // heads
    bq, bk = min(QUERY_BLOCK, length), min(KEY_BLOCK, length)
    blocks = length // bq
    grid_spec = pltpu.PrefetchScalarGridSpec(
        num_scalar_prefetch=1,
        grid=(1,),
        in_specs=[whole_block((blocks, 1, bq)), whole_block((length, triple))],
        out_specs=[
            whole_block((length, flat)),
            whole_block((blocks, flat, bq)),
            whole_block((blocks, 8, bq)),
        ],
        scratch_shapes=[
            pltpu.VMEM((heads, length, width), BF16),
            pltpu.VMEM((heads, length, width), BF16),
            pltpu.VMEM((heads, length // bk, width, bk), BF16),
            pltpu.VMEM((flat, bq), F32),
        ],
    )
    return pl.pallas_call(
        functools.partial(attention_forward_body, heads, width, bq, bk),
        out_shape=[
            jax.ShapeDtypeStruct((length, flat), BF16),
            jax.ShapeDtypeStruct((blocks, flat, bq), F32),
            jax.ShapeDtypeStruct((blocks, 8, bq), F32),
        ],
        grid_spec=grid_spec,
        compiler_params=pltpu.CompilerParams(vmem_limit_bytes=48 << 20),
        cost_estimate=pl.CostEstimate(
            flops=10 * length * length * flat,
            bytes_accessed=12 * length * flat,
            transcendentals=heads * length * length,
        ),
        name="attention_forward",
    )(low_blocks, starts, qkv)


def attention_backward(low_blocks, starts, qkv, grad_out, out_turned, log_total, heads):
    length, triple = qkv.shape
    flat = triple // 3
    width = flat // heads
    bq, bk = min(QUERY_BLOCK, length), min(KEY_BLOCK, length)
    blocks = length // bq
    per_head = pltpu.VMEM((heads, length, width), BF16)
    sums = pltpu.VMEM((heads, length, width), F32)
    grid_spec = pltpu.PrefetchScalarGridSpec(
        num_scalar_prefetch=1,
        grid=(1,),
        in_specs=[
            whole_block((blocks, 1, bq)),
            whole_block((length, triple)),
            whole_block((length, flat)),
            whole_block((blocks, flat, bq)),
            whole_block((blocks, 8, bq)),
        ],
        out_specs=whole_block((length, triple)),
        scratch_shapes=[
            per_head,
            per_head,
            per_head,
            per_head,
            pltpu.VMEM((heads, length // bk, width, bk), BF16),
            sums,
            sums,
            pltpu.VMEM((flat, bq), F32),
        ],
    )
    return pl.pallas_call(
        functools.partial(attention_backward_body, heads, width, bq, bk),
        out_shape=jax.ShapeDtypeStruct((length, triple), BF16),
        grid_spec=grid_spec,
        compiler_params=pltpu.CompilerParams(vmem_limit_bytes=60 << 20),
        cost_estimate=pl.CostEstimate(
            flops=14 * length * length * flat,
            bytes_accessed=20 * length * flat,
            transcendentals=heads * length * length,
        ),
        name="attention_backward",
    )(low_blocks, starts, qkv, grad_out, out_turned, log_total)


def swap(value, axis_name, distance):
    count = lax.axis_size(axis_name)
    return lax.ppermute(value, axis_name, [(i, i ^ distance) for i in range(count)])


def lower_pairs(pairs, y_count):
    return [
        (source * y_count + y, target * y_count + y)
        for source, target in pairs
        for y in range(y_count)
    ]


def spread_plane(block, plane, z_here, y_here, x_here):
    far = lax.ppermute(block, "dp", lower_pairs([(plane, plane ^ 2)], 2))
    held = jnp.where(z_here == plane, block, far)
    near = lax.ppermute(
        held, "dp", lower_pairs([(plane, plane ^ 1), (plane ^ 2, plane ^ 3)], 2)
    )
    held = jnp.where((z_here == plane) | (z_here == plane ^ 2), held, near)
    if plane < 2:
        across = swap(held, "dp", 1)
        pair = jnp.where(y_here == 0, jnp.stack([held, across]), jnp.stack([across, held]))
        other = swap(pair, "seq", 2)
        return jnp.where(x_here == 0, jnp.stack([pair, other]), jnp.stack([other, pair]))
    across = swap(held, "seq", 2)
    pair = jnp.where(
        x_here == 0, jnp.stack([held, across], 0), jnp.stack([across, held], 0)
    )
    other = swap(pair, "dp", 1)
    return jnp.where(y_here == 0, jnp.stack([pair, other], 1), jnp.stack([other, pair], 1))


def pick(stacked, index, axis=0):
    return lax.dynamic_index_in_dim(stacked, index, axis, keepdims=False)


def gather_plane(blocks, plane, z_here, y_here, x_here):
    def over_x(value, axis):
        sent = swap(pick(value, 1 - x_here, axis).astype(BF16), "seq", 2)
        return pick(value, x_here, axis) + sent.astype(F32)

    def over_y(value, axis):
        sent = swap(pick(value, 1 - y_here, axis).astype(BF16), "dp", 1)
        return pick(value, y_here, axis) + sent.astype(F32)

    if plane < 2:
        held = over_y(over_x(blocks, 0), 0)
    else:
        held = over_x(over_y(blocks, 1), 0)
    near = lax.ppermute(
        held.astype(BF16), "dp", lower_pairs([(plane ^ 1, plane), (plane ^ 3, plane ^ 2)], 2)
    )
    held = held + near.astype(F32)
    far = lax.ppermute(held.astype(BF16), "dp", lower_pairs([(plane ^ 2, plane)], 2))
    return held + far.astype(F32)


def per_device(
    rows_in,
    out_cotangent,
    cell_lengths,
    cell_starts,
    key_mask,
    weights_master,
    first_moment,
    second_moment,
    small_master,
    small_first,
    small_second,
    step_count,
):
    model_width = rows_in.shape[3]
    local_rows = rows_in.shape[2]
    length = key_mask.shape[2]
    shard_len = weights_master.shape[2]
    groups = lax.axis_size("seq")
    dp_count = lax.axis_size("dp")
    head_share = model_width // groups
    heads_here = HEADS // groups
    triple = 3 * head_share
    first_end = model_width * triple
    second_end = first_end + head_share * model_width
    third_end = second_end + model_width * model_width
    seq_here = lax.axis_index("seq")
    dp_here = lax.axis_index("dp")
    chip = seq_here // 2
    core = seq_here % 2
    z_here = dp_here // 2
    y_here = dp_here % 2
    planar = dp_count == 8 and shard_len * 2 == first_end

    def exchange_micro(array):
        own = pick(array[:, 0], chip)
        received = swap(pick(array[:, 0], 1 - chip), "seq", 2)
        return jnp.where(chip == 0, jnp.stack([own, received]), jnp.stack([received, own]))

    row_pair = exchange_micro(rows_in)
    cot_pair = exchange_micro(out_cotangent)

    weight = weights_master[0, 0]
    low_weight = weight.astype(BF16)
    if planar:
        tall = low_weight.reshape(shard_len // triple, triple)
        wide = low_weight.reshape(shard_len // model_width, model_width)
        attn_all = spread_plane(tall, 0, z_here, y_here, x_here=chip)
        w_attn = attn_all.reshape(2, model_width, triple)
        rest = [spread_plane(wide, plane, z_here, y_here, x_here=chip) for plane in (1, 2, 3)]
        rest = jnp.concatenate(
            [part.reshape(2, 2 * wide.shape[0], model_width) for part in rest], axis=1
        )
        w_out = rest[:, :head_share]
        w_in = rest[:, head_share : head_share + model_width]
        w_back = rest[:, head_share + model_width :]
    else:
        copies = lax.all_gather(low_weight.reshape(1, shard_len), ("dp", "seq"), axis=0, tiled=True)
        copies = copies.reshape(dp_count, 2, 2, shard_len)
        per_share = jnp.transpose(pick(copies, core, 2), (1, 0, 2)).reshape(2, dp_count * shard_len)
        w_attn = per_share[:, :first_end].reshape(2, model_width, triple)
        w_out = per_share[:, first_end:second_end].reshape(2, head_share, model_width)
        w_in = per_share[:, second_end:third_end].reshape(2, model_width, model_width)
        w_back = per_share[:, third_end:].reshape(2, model_width, model_width)

    def share_columns(vector, part):
        return lax.dynamic_slice_in_dim(vector, (core + 2 * part) * head_share, head_share)

    attn_biases = [
        jnp.concatenate(
            [
                share_columns(small_master[4], part),
                jnp.zeros((head_share,), F32),
                share_columns(small_master[5], part),
            ]
        )
        for part in range(2)
    ]
    ff_biases = [pick(small_master, 8 + core + 2 * part) for part in range(2)]

    starts = pick(cell_starts[:, 0], chip)
    lengths = pick(cell_lengths[:, 0], chip)
    places = jnp.arange(length, dtype=jnp.int32)
    inside = (places[:, None] >= starts[None, :]) & (places[:, None] < (starts + lengths)[None, :])
    first_key = jnp.max(jnp.where(inside, starts[None, :], -1), axis=1)
    first_key = jnp.where(first_key < 0, places, first_key)
    bq, bk = min(QUERY_BLOCK, length), min(KEY_BLOCK, length)
    low_blocks = first_key.reshape(-1, bq)[:, 0] // bk
    block_starts = first_key.reshape(-1, 1, bq)

    def both_cores(mine):
        theirs = swap(mine, "seq", 1)
        whole = jnp.where(
            core == 0,
            jnp.stack([mine, theirs], axis=1),
            jnp.stack([theirs, mine], axis=1),
        )
        return whole.reshape(length, mine.shape[-1])

    def own_rows(whole, index):
        return pick(whole.reshape(2, 2, local_rows, whole.shape[-1]), index, 1).reshape(
            2 * local_rows, whole.shape[-1]
        )

    def across_cores(multiply):
        received = swap(multiply(1 - core), "seq", 1)
        return multiply(core) + received

    inputs = row_pair.astype(F32).reshape(2 * local_rows, model_width)
    hat_one, scale_one = norm_stats(inputs)
    low_one = (hat_one * small_master[0] + small_master[1]).astype(BF16)
    rows_one = both_cores(low_one.reshape(2, local_rows, model_width))
    grad_y = cot_pair.astype(F32).reshape(2 * local_rows, model_width)
    rows_e = both_cores(cot_pair)

    qkv = [
        (dot_rows(rows_one, w_attn[part]) + attn_biases[part]).astype(BF16) for part in range(2)
    ]
    attended = [
        attention_forward(low_blocks, block_starts, qkv[part], heads_here) for part in range(2)
    ]
    mixture = jnp.concatenate([attended[0][0], attended[1][0]], axis=1)
    w_out_both = w_out.reshape(2 * head_share, model_width)
    branch = across_cores(lambda who: dot_rows(own_rows(mixture, who), w_out_both))
    middle = inputs + (branch + small_master[6])
    hat_two, scale_two = norm_stats(middle)
    low_two = (hat_two * small_master[2] + small_master[3]).astype(BF16)
    rows_two = both_cores(low_two.reshape(2, local_rows, model_width))

    activated, inner = [], []
    for part in range(2):
        hidden = dot_rows(rows_two, w_in[part]) + ff_biases[part]
        value, slope = gelu_parts(hidden)
        activated.append(value.astype(BF16))
        inner.append((dot_transposed(rows_e, w_back[part]) * slope).astype(BF16))
    mlp_out = across_cores(
        lambda who: dot_rows(own_rows(activated[0], who), w_back[0])
        + dot_rows(own_rows(activated[1], who), w_back[1])
    )
    grad_low_two = across_cores(
        lambda who: dot_transposed(own_rows(inner[0], who), w_in[0])
        + dot_transposed(own_rows(inner[1], who), w_in[1])
    )
    result_rows = (middle + (mlp_out + small_master[7])).astype(BF16)
    grad_mid = grad_y + norm_backward(grad_low_two, hat_two, scale_two, small_master[2])
    low_mid = grad_mid.astype(BF16)
    rows_mid = both_cores(low_mid.reshape(2, local_rows, model_width))

    share_back = [dot_columns(activated[part], rows_e) for part in range(2)]
    share_in = [dot_columns(rows_two, inner[part]) for part in range(2)]
    share_out = [dot_columns(attended[part][0], rows_mid) for part in range(2)]
    grad_packed = []
    for part in range(2):
        grad_att = dot_transposed(rows_mid, w_out[part]).astype(BF16)
        grad_packed.append(
            attention_backward(
                low_blocks,
                block_starts,
                qkv[part],
                grad_att,
                attended[part][1],
                attended[part][2],
                heads_here,
            )
        )
    share_attn = [dot_columns(rows_one, grad_packed[part]) for part in range(2)]
    grad_low_one = across_cores(
        lambda who: dot_transposed(own_rows(grad_packed[0], who), w_attn[0])
        + dot_transposed(own_rows(grad_packed[1], who), w_attn[1])
    )
    grad_x = (
        grad_mid + norm_backward(grad_low_one, hat_one, scale_one, small_master[0])
    ).astype(BF16)

    def return_micro(rows):
        blocks = rows.reshape(2, local_rows, model_width)
        own = pick(blocks, chip)
        received = swap(pick(blocks, 1 - chip), "seq", 2)
        ordered = jnp.where(chip == 0, jnp.stack([own, received]), jnp.stack([received, own]))
        return ordered[:, None]

    result_all = return_micro(result_rows)
    grad_all = return_micro(grad_x)

    def at_shares(columns):
        row = jnp.zeros((model_width,), F32)
        for part in range(2):
            row = lax.dynamic_update_slice(row, columns[part], ((core + 2 * part) * head_share,))
        return row

    bias_sums = [jnp.sum(grad_packed[part].astype(F32), axis=0) for part in range(2)]
    inner_rows = jnp.zeros((4, model_width), F32)
    for part in range(2):
        inner_rows = lax.dynamic_update_slice(
            inner_rows, jnp.sum(inner[part].astype(F32), axis=0)[None], (core + 2 * part, 0)
        )
    small_now = jnp.concatenate(
        [
            jnp.stack(
                [
                    jnp.sum(grad_low_one * hat_one, axis=0),
                    jnp.sum(grad_low_one, axis=0),
                    jnp.sum(grad_low_two * hat_two, axis=0),
                    jnp.sum(grad_low_two, axis=0),
                    at_shares([sums[:head_share] for sums in bias_sums]),
                    at_shares([sums[2 * head_share :] for sums in bias_sums]),
                    jnp.sum(low_mid.astype(F32), axis=0),
                    jnp.sum(grad_y, axis=0),
                ]
            ),
            inner_rows,
        ]
    )

    if planar:
        tall_rows, wide_rows = tall.shape[0], wide.shape[0]
        attn_sum = gather_plane(
            jnp.stack(share_attn).reshape(2, 2, tall_rows, triple), 0, z_here, y_here, chip
        )
        joined = jnp.stack(
            [
                jnp.concatenate([share_out[part], share_in[part], share_back[part]], axis=0)
                for part in range(2)
            ]
        ).reshape(2, 3, 2, wide_rows, model_width)
        sums = [
            gather_plane(joined[:, plane - 1], plane, z_here, y_here, chip)
            for plane in (1, 2, 3)
        ]
        wide_sum = jnp.where(z_here == 1, sums[0], jnp.where(z_here == 2, sums[1], sums[2]))
        reduced = jnp.where(z_here == 0, attn_sum.reshape(shard_len), wide_sum.reshape(shard_len))
    else:
        flat_all = jnp.stack(
            [
                jnp.concatenate(
                    [
                        matrix[part].reshape(-1)
                        for matrix in (share_attn, share_out, share_in, share_back)
                    ]
                )
                for part in range(2)
            ]
        )
        flat_here = pick(flat_all, chip) + swap(pick(flat_all, 1 - chip), "seq", 2)
        reduced = lax.psum_scatter(
            flat_here.reshape(dp_count, shard_len), "dp", scatter_dimension=0, tiled=True
        )[0]

    steps_done = step_count[0].astype(F32)
    fix_one = 1.0 - jnp.exp(steps_done * math.log(BETA_ONE))
    fix_two = 1.0 - jnp.exp(steps_done * math.log(BETA_TWO))
    first_new = BETA_ONE * first_moment[0, 0] + (1.0 - BETA_ONE) * reduced
    second_new = BETA_TWO * second_moment[0, 0] + (1.0 - BETA_TWO) * reduced * reduced
    update = first_new / fix_one / (jnp.sqrt(second_new / fix_two) + ADAM_EPS) + DECAY * weight
    positions = dp_here * shard_len + jnp.arange(shard_len, dtype=jnp.int32)
    region = (
        (positions >= first_end).astype(jnp.int32)
        + (positions >= second_end).astype(jnp.int32)
        + (positions >= third_end).astype(jnp.int32)
    )
    region_hit = region[None, :] == jnp.arange(4, dtype=jnp.int32)[:, None]
    norm_sums = jnp.stack(
        [
            jnp.sum(jnp.where(region_hit, weight * weight, 0.0), axis=1),
            jnp.sum(jnp.where(region_hit, update * update, 0.0), axis=1),
        ]
    )
    small_grad, norm_sums = lax.psum((small_now, norm_sums), ("dp", "seq"))
    weight_norms = jnp.sqrt(norm_sums[0])
    update_norms = jnp.sqrt(norm_sums[1])
    ratios = weight_norms / update_norms
    ratio_here = jnp.sum(jnp.where(region_hit, ratios[:, None], 0.0), axis=0)
    new_weight = weight - MATRIX_RATE * ratio_here * update
    small_one = BETA_ONE * small_first + (1.0 - BETA_ONE) * small_grad
    small_two = BETA_TWO * small_second + (1.0 - BETA_TWO) * small_grad * small_grad
    small_updated = small_master - SMALL_RATE * (small_one / fix_one) / (
        jnp.sqrt(small_two / fix_two) + ADAM_EPS
    )
    return (
        result_all,
        grad_all,
        reduced[None, None],
        jnp.stack([first_new, second_new])[:, None, None],
        new_weight[None, None],
        new_weight[None, None].astype(BF16),
        jnp.stack([weight_norms, update_norms, ratios]),
        small_grad,
        jnp.stack([small_one, small_two]),
        small_updated,
    )


def solution(mesh):
    in_specs = (
        P(None, "dp", "seq", None),
        P(None, "dp", "seq", None),
        P(None, "dp", None),
        P(None, "dp", None),
        P(None, "dp", None),
        P("dp", "seq", None),
        P("dp", "seq", None),
        P("dp", "seq", None),
        P(),
        P(),
        P(),
        P(),
    )
    out_specs = (
        P(None, "dp", "seq", None),
        P(None, "dp", "seq", None),
        P("dp", "seq", None),
        P(None, "dp", "seq", None),
        P("dp", "seq", None),
        P("dp", "seq", None),
        P(),
        P(),
        P(),
        P(),
    )
    return jax.shard_map(
        per_device, mesh=mesh, in_specs=in_specs, out_specs=out_specs, check_vma=False
    )
```

```python
import functools
import math

import jax
import jax.numpy as jnp
from jax import lax
from jax.experimental import pallas as pl
from jax.experimental.pallas import tpu as pltpu
from jax.sharding import PartitionSpec as P

HEADS = 20


NORM_EPS = 1e-05
BETA_ONE = 0.9
BETA_TWO = 0.999
ADAM_EPS = 1e-06
DECAY = 0.01
MATRIX_RATE = 0.3
SMALL_RATE = 0.25
MASKED = -1e30
LOG2_E = 1.4426950408889634
FF_ROWS = 256

F32 = jnp.float32
BF16 = jnp.bfloat16


def dot_rows(left, right):
    return lax.dot_general(left, right, (((1,), (0,)), ((), ())), preferred_element_type=F32)


def dot_transposed(left, right):
    return lax.dot_general(left, right, (((1,), (1,)), ((), ())), preferred_element_type=F32)


def dot_columns(left, right):
    return lax.dot_general(left, right, (((0,), (0,)), ((), ())), preferred_element_type=F32)


def norm_stats(rows):
    center = jnp.mean(rows, axis=-1, keepdims=True)
    centered = rows - center
    spread = jnp.mean(centered * centered, axis=-1, keepdims=True)
    scale = lax.rsqrt(spread + NORM_EPS)
    return centered * scale, scale


def norm_backward(upstream, hat, scale, gain):
    weighted = upstream * gain
    return (
        weighted
        - jnp.mean(weighted, axis=-1, keepdims=True)
        - hat * jnp.mean(weighted * hat, axis=-1, keepdims=True)
    ) * scale


def gelu_parts(values):
    inner = math.sqrt(2.0 / math.pi)
    squares = values * values
    bent = jnp.tanh(inner * (values + 0.044715 * values * squares))
    half = 0.5 * (1.0 + bent)
    slope = half + 0.5 * values * (1.0 - bent * bent) * inner * (1.0 + 3.0 * 0.044715 * squares)
    return values * half, slope


def block_place(core, block):
    return jnp.where(block % 2 == core, 0, 2) + block // 2


def block_rows(core, block, rows):
    return pl.ds(pl.multiple_of(block_place(core, block) * rows, rows), rows)


def attention_forward_body(
    heads, width, bq, low_ref, core_ref, start_ref, qkv_ref, out_ref, outt_ref, lse_ref, qs, ks, vt, acc
):
    length = qkv_ref.shape[0]
    flat = heads * width
    factor = width**-0.5 * LOG2_E
    core = core_ref[0]

    def unpack(block, carry):
        here = block_rows(core, block, bq)
        there = pl.ds(pl.multiple_of(block * bq, bq), bq)
        for h in range(heads):
            qs[h, there] = qkv_ref[here, h * width : (h + 1) * width]
            ks[h, there] = qkv_ref[here, flat + h * width : flat + (h + 1) * width]
        turned = qkv_ref[here, 2 * flat : 3 * flat].astype(F32).T
        for h in range(heads):
            vt[h, block] = turned[h * width : (h + 1) * width].astype(BF16)
        return carry

    lax.fori_loop(0, length // bq, unpack, 0)

    def query_step(qb, carry):
        q0 = pl.multiple_of(qb * bq, bq)
        start = start_ref[qb]
        query_place = q0 + lax.broadcasted_iota(jnp.int32, (1, bq), 1)
        acc[...] = jnp.zeros_like(acc)

        def key_step(kb, tops_totals):
            tops, totals = tops_totals
            k0 = pl.multiple_of(kb * bq, bq)
            key_place = k0 + lax.broadcasted_iota(jnp.int32, (bq, bq), 0)
            allowed = (key_place <= query_place) & (key_place >= start)
            new_tops, new_totals = [], []
            for h in range(heads):
                scores = dot_transposed(ks[h, pl.ds(k0, bq)], qs[h, pl.ds(q0, bq)]) * factor
                scores = jnp.where(allowed, scores, MASKED)
                top = jnp.maximum(tops[h], jnp.max(scores, axis=0, keepdims=True))
                fade = jnp.exp2(tops[h] - top)
                weights = jnp.exp2(scores - top)
                own = slice(h * width, (h + 1) * width)
                acc[own] = acc[own] * fade + dot_rows(vt[h, kb], weights.astype(BF16))
                new_tops.append(top)
                new_totals.append(totals[h] * fade + jnp.sum(weights, axis=0, keepdims=True))
            return tuple(new_tops), tuple(new_totals)

        first = (
            tuple(jnp.full((1, bq), -1e29, F32) for _ in range(heads)),
            tuple(jnp.zeros((1, bq), F32) for _ in range(heads)),
        )
        tops, totals = lax.fori_loop(low_ref[qb], qb + 1, key_step, first)
        for h in range(heads):
            own = slice(h * width, (h + 1) * width)
            acc[own] = acc[own] * (1.0 / totals[h])
            lse_ref[qb, h : h + 1, :] = tops[h] + jnp.log2(totals[h])
        mixed = acc[...]
        outt_ref[qb] = mixed
        out_ref[block_rows(core, qb, bq), :] = mixed.T.astype(BF16)
        return carry

    lax.fori_loop(0, length // bq, query_step, 0)


def attention_backward_body(
    heads,
    width,
    bq,
    low_ref,
    core_ref,
    start_ref,
    qkv_ref,
    dout_ref,
    outt_ref,
    lse_ref,
    grad_ref,
    qs,
    ks,
    vs,
    ds,
    kt,
    dk,
    dv,
    dqt,
):
    length = qkv_ref.shape[0]
    flat = heads * width
    score_scale = width**-0.5
    factor = score_scale * LOG2_E
    core = core_ref[0]

    def unpack(block, carry):
        here = block_rows(core, block, bq)
        there = pl.ds(pl.multiple_of(block * bq, bq), bq)
        for h in range(heads):
            qs[h, there] = qkv_ref[here, h * width : (h + 1) * width]
            ks[h, there] = qkv_ref[here, flat + h * width : flat + (h + 1) * width]
            vs[h, there] = qkv_ref[here, 2 * flat + h * width : 2 * flat + (h + 1) * width]
            ds[h, there] = dout_ref[here, h * width : (h + 1) * width]
        turned = qkv_ref[here, flat : 2 * flat].astype(F32).T
        for h in range(heads):
            kt[h, block] = turned[h * width : (h + 1) * width].astype(BF16)
        return carry

    lax.fori_loop(0, length // bq, unpack, 0)
    dk[...] = jnp.zeros_like(dk)
    dv[...] = jnp.zeros_like(dv)

    def query_step(qb, carry):
        q0 = pl.multiple_of(qb * bq, bq)
        queries = pl.ds(q0, bq)
        here = block_rows(core, qb, bq)
        start = start_ref[qb]
        query_place = q0 + lax.broadcasted_iota(jnp.int32, (1, bq), 1)
        products = dout_ref[here, :].astype(F32).T * outt_ref[qb]
        inners = [
            jnp.sum(products[h * width : (h + 1) * width], axis=0, keepdims=True)
            for h in range(heads)
        ]
        dqt[...] = jnp.zeros_like(dqt)

        def key_step(kb, inner_carry):
            k0 = pl.multiple_of(kb * bq, bq)
            keys = pl.ds(k0, bq)
            key_place = k0 + lax.broadcasted_iota(jnp.int32, (bq, bq), 0)
            allowed = (key_place <= query_place) & (key_place >= start)
            for h in range(heads):
                scores = dot_transposed(ks[h, keys], qs[h, queries]) * factor
                weights = jnp.exp2(
                    jnp.where(allowed, scores - lse_ref[qb, h : h + 1, :], MASKED)
                )
                dweights = dot_transposed(vs[h, keys], ds[h, queries])
                dscores = (weights * (dweights - inners[h])).astype(BF16)
                dv[h, keys] += dot_rows(weights.astype(BF16), ds[h, queries])
                dk[h, keys] += dot_rows(dscores, qs[h, queries])
                dqt[h * width : (h + 1) * width] += dot_rows(kt[h, kb], dscores)
            return inner_carry

        lax.fori_loop(low_ref[qb], qb + 1, key_step, 0)
        grad_ref[here, 0:flat] = (dqt[...] * score_scale).T.astype(BF16)
        return carry

    lax.fori_loop(0, length // bq, query_step, 0)

    def write_keys(kb, carry):
        here = block_rows(core, kb, bq)
        rows = pl.ds(pl.multiple_of(kb * bq, bq), bq)
        grad_ref[here, flat : 2 * flat] = jnp.concatenate(
            [dk[h, rows] * score_scale for h in range(heads)], axis=1
        ).astype(BF16)
        grad_ref[here, 2 * flat : 3 * flat] = jnp.concatenate(
            [dv[h, rows] for h in range(heads)], axis=1
        ).astype(BF16)
        rest = grad_ref.shape[1] - 3 * flat
        if rest:
            grad_ref[here, 3 * flat :] = jnp.zeros((bq, rest), BF16)
        return carry

    lax.fori_loop(0, length // bq, write_keys, 0)


def whole_block(shape):
    return pl.BlockSpec(shape, lambda step, *refs: (0,) * len(shape))


def attention_forward(low_blocks, core, starts, qkv, heads):
    length, triple = qkv.shape
    flat = triple // 3
    width = flat // heads
    blocks, _, bq = starts.shape
    grid_spec = pltpu.PrefetchScalarGridSpec(
        num_scalar_prefetch=2,
        grid=(1,),
        in_specs=[whole_block((blocks, 1, bq)), whole_block((length, triple))],
        out_specs=[
            whole_block((length, flat)),
            whole_block((blocks, flat, bq)),
            whole_block((blocks, 8, bq)),
        ],
        scratch_shapes=[
            pltpu.VMEM((heads, length, width), BF16),
            pltpu.VMEM((heads, length, width), BF16),
            pltpu.VMEM((heads, blocks, width, bq), BF16),
            pltpu.VMEM((flat, bq), F32),
        ],
    )
    return pl.pallas_call(
        functools.partial(attention_forward_body, heads, width, bq),
        out_shape=[
            jax.ShapeDtypeStruct((length, flat), BF16),
            jax.ShapeDtypeStruct((blocks, flat, bq), F32),
            jax.ShapeDtypeStruct((blocks, 8, bq), F32),
        ],
        grid_spec=grid_spec,
        compiler_params=pltpu.CompilerParams(vmem_limit_bytes=48 << 20),
        cost_estimate=pl.CostEstimate(
            flops=10 * length * length * flat,
            bytes_accessed=12 * length * flat,
            transcendentals=heads * length * length,
        ),
        name="attention_forward",
    )(low_blocks, core, starts, qkv)


def attention_backward(low_blocks, core, starts, qkv, grad_out, out_turned, log_total, heads):
    length, triple = qkv.shape
    flat = triple // 3
    width = flat // heads
    blocks, _, bq = starts.shape
    per_head = pltpu.VMEM((heads, length, width), BF16)
    sums = pltpu.VMEM((heads, length, width), F32)
    grid_spec = pltpu.PrefetchScalarGridSpec(
        num_scalar_prefetch=2,
        grid=(1,),
        in_specs=[
            whole_block((blocks, 1, bq)),
            whole_block((length, triple)),
            whole_block((length, flat)),
            whole_block((blocks, flat, bq)),
            whole_block((blocks, 8, bq)),
        ],
        out_specs=whole_block((length, lanes(triple))),
        scratch_shapes=[
            per_head,
            per_head,
            per_head,
            per_head,
            pltpu.VMEM((heads, blocks, width, bq), BF16),
            sums,
            sums,
            pltpu.VMEM((flat, bq), F32),
        ],
    )
    return pl.pallas_call(
        functools.partial(attention_backward_body, heads, width, bq),
        out_shape=jax.ShapeDtypeStruct((length, lanes(triple)), BF16),
        grid_spec=grid_spec,
        compiler_params=pltpu.CompilerParams(vmem_limit_bytes=60 << 20),
        cost_estimate=pl.CostEstimate(
            flops=14 * length * length * flat,
            bytes_accessed=20 * length * flat,
            transcendentals=heads * length * length,
        ),
        name="attention_backward",
    )(low_blocks, core, starts, qkv, grad_out, out_turned, log_total)


def lanes(width):
    return -(-width // 128) * 128


def put(ref, value):
    width = value.shape[1]
    ref[:, :width] = value
    if width < ref.shape[1]:
        ref[:, width:] = jnp.zeros((value.shape[0], ref.shape[1] - width), ref.dtype)


def vmem(count):
    return pltpu.CompilerParams(vmem_limit_bytes=count << 20)


def fixed(shape):
    return pl.BlockSpec(shape, lambda *step: (0,) * len(shape), pipeline_mode=pl.Buffered(1))


def hbm():
    return pl.BlockSpec(memory_space=pl.ANY)


def round_weights_body(bound_ref, weight_ref, low_ref, sums_ref):
    values = weight_ref[...]
    low_ref[...] = values[0, 0].astype(BF16)
    place = lax.broadcasted_iota(jnp.int32, values.shape, 2)
    squares = values * values
    lower = jnp.sum(jnp.where(place < bound_ref[0], squares, 0.0))
    sums_ref[0] = lower
    sums_ref[1] = jnp.sum(squares) - lower


def round_weights(bound, weight):
    smem = pl.BlockSpec(memory_space=pltpu.SMEM)
    whole = pl.BlockSpec(memory_space=pltpu.VMEM)
    return pl.pallas_call(
        round_weights_body,
        in_specs=[smem, whole],
        out_specs=[whole, smem],
        out_shape=[
            jax.ShapeDtypeStruct(weight.shape[2:], BF16),
            jax.ShapeDtypeStruct((2,), F32),
        ],
        compiler_params=vmem(32),
        name="round_weights",
    )(bound, weight)


def moments_body(
    ints_ref, floats_ref, lead_ref, rest_ref, first_ref, second_ref, weight_ref,
    grad_ref, moments_ref, update_ref, sums_ref,
):
    step = pl.program_id(0)
    grad = jnp.where(ints_ref[1] == 1, lead_ref[...], rest_ref[...])
    grad_ref[...] = grad
    first = BETA_ONE * first_ref[...] + (1.0 - BETA_ONE) * grad
    second = BETA_TWO * second_ref[...] + (1.0 - BETA_TWO) * grad * grad
    moments_ref[0] = first
    moments_ref[1] = second
    update = (first / floats_ref[0]) / (jnp.sqrt(second / floats_ref[1]) + ADAM_EPS)
    update = update + DECAY * weight_ref[...]
    update_ref[...] = update
    count = grad.shape[2]
    place = step * count + lax.broadcasted_iota(jnp.int32, grad.shape, 2)
    squares = update * update
    lower = jnp.sum(jnp.where(place < ints_ref[0], squares, 0.0))
    upper = jnp.sum(squares) - lower

    @pl.when(step == 0)
    def clear():
        sums_ref[0] = 0.0
        sums_ref[1] = 0.0

    sums_ref[0] += lower
    sums_ref[1] += upper


def flat_steps(count):
    return 7 if count % (7 * 128) == 0 else 1


def new_moments(ints, floats, lead, rest, first, second, weight):
    count = weight.shape[2]
    steps = flat_steps(count)
    smem = pl.BlockSpec(memory_space=pltpu.SMEM)
    flat = pl.BlockSpec((1, 1, count // steps), lambda i: (0, 0, i))
    pair = pl.BlockSpec((2, 1, 1, count // steps), lambda i: (0, 0, 0, i))
    return pl.pallas_call(
        moments_body,
        grid=(steps,),
        in_specs=[smem, smem] + [flat] * 5,
        out_specs=[flat, pair, flat, smem],
        out_shape=[
            jax.ShapeDtypeStruct(weight.shape, F32),
            jax.ShapeDtypeStruct((2,) + weight.shape, F32),
            jax.ShapeDtypeStruct(weight.shape, F32),
            jax.ShapeDtypeStruct((2,), F32),
        ],
        compiler_params=vmem(48),
        name="new_moments",
    )(ints, floats, lead, rest, first, second, weight)


def new_weights_body(ints_ref, ratio_ref, weight_ref, update_ref, new_ref, copy_ref):
    count = weight_ref.shape[2]
    place = pl.program_id(0) * count + lax.broadcasted_iota(jnp.int32, weight_ref.shape, 2)
    rate = jnp.where(place < ints_ref[0], ratio_ref[0], ratio_ref[1])
    new = weight_ref[...] - MATRIX_RATE * rate * update_ref[...]
    new_ref[...] = new
    copy_ref[...] = new.astype(BF16)


def new_weights(ints, ratios, weight, update):
    count = weight.shape[2]
    steps = flat_steps(count)
    smem = pl.BlockSpec(memory_space=pltpu.SMEM)
    flat = pl.BlockSpec((1, 1, count // steps), lambda i: (0, 0, i))
    return pl.pallas_call(
        new_weights_body,
        grid=(steps,),
        in_specs=[smem, smem, flat, flat],
        out_specs=[flat, flat],
        out_shape=[
            jax.ShapeDtypeStruct(weight.shape, F32),
            jax.ShapeDtypeStruct(weight.shape, BF16),
        ],
        compiler_params=vmem(32),
        name="new_weights",
    )(ints, ratios, weight, update)


def unpack_body(cut, out_rows, in_rows, place_ref, *refs):
    blocks, (w_out, w_in, w_back, held, sems) = refs[:8], refs[8:]
    here = place_ref[0]
    copies = [
        pltpu.make_async_copy(block, held.at[index ^ here], sems.at[index])
        for index, block in enumerate(blocks)
    ]
    for copy in copies:
        copy.start()
    for copy in copies:
        copy.wait()
    begin = 2 * cut
    for target, rows in ((w_out, out_rows), (w_in, in_rows), (w_back, in_rows)):
        done = 0
        while done < rows:
            block, offset = divmod(begin + done, cut)
            count = min(cut - offset, rows - done)
            target[done : done + count] = held[block, offset : offset + count]
            done += count
        begin += rows


def unpack_share(place, blocks, out_rows, in_rows):
    cut, columns = blocks[0].shape
    shapes = [(out_rows, columns), (in_rows, columns), (in_rows, columns)]
    return pl.pallas_call(
        functools.partial(unpack_body, cut, out_rows, in_rows),
        grid_spec=pltpu.PrefetchScalarGridSpec(
            num_scalar_prefetch=1,
            grid=(1,),
            in_specs=[hbm()] * 8,
            out_specs=[whole_block(shape) for shape in shapes],
            scratch_shapes=[
                pltpu.VMEM((8, cut, columns), BF16),
                pltpu.SemaphoreType.DMA((8,)),
            ],
        ),
        out_shape=[jax.ShapeDtypeStruct(shape, BF16) for shape in shapes],
        compiler_params=vmem(48),
        cost_estimate=pl.CostEstimate(flops=0, bytes_accessed=20 << 20, transcendentals=0),
        name="unpack_share",
    )(place, *blocks)


def rows_of(step, steps, own_ref, other_ref, width):
    return jnp.where(step < steps, own_ref[:, :width], other_ref[:, :width])


def both_specs(block, width, steps):
    own = pl.BlockSpec((block, width), lambda i, *refs: (jnp.minimum(i, steps - 1), 0))
    other = pl.BlockSpec((block, width), lambda i, *refs: (jnp.maximum(i - steps, 0), 0))
    return own, other


def project_body(
    steps, place_ref, own_ref, other_ref, a0, a1, b0, b1, bias_ref,
    out_a, out_b, rows_ref, w_a, w_b, sems,
):
    step = pl.program_id(0)

    @pl.when(step == 0)
    def load():
        cut = a0.shape[0]
        here = place_ref[0]
        first = pl.ds(pl.multiple_of(here * cut, cut), cut)
        second = pl.ds(pl.multiple_of((1 - here) * cut, cut), cut)
        copies = [
            pltpu.make_async_copy(a0, w_a.at[first], sems.at[0]),
            pltpu.make_async_copy(a1, w_a.at[second], sems.at[1]),
            pltpu.make_async_copy(b0, w_b.at[first], sems.at[2]),
            pltpu.make_async_copy(b1, w_b.at[second], sems.at[3]),
        ]
        for copy in copies:
            copy.start()
        for copy in copies:
            copy.wait()

    rows = rows_of(step, steps, own_ref, other_ref, rows_ref.shape[1])
    rows_ref[...] = rows
    out_a[...] = (dot_rows(rows, w_a[...]) + bias_ref[0:1]).astype(BF16)
    out_b[...] = (dot_rows(rows, w_b[...]) + bias_ref[1:2]).astype(BF16)


def project(place, own, other, halves, biases):
    count, sent_width = own.shape
    cut, triple = halves[0].shape
    model_width = 2 * cut
    block = min(512, count)
    steps = count // block
    row_out = lambda width: pl.BlockSpec((block, width), lambda i, *refs: (i, 0))
    matrix = jax.ShapeDtypeStruct((2 * cut, triple), BF16)
    return pl.pallas_call(
        functools.partial(project_body, steps),
        grid_spec=pltpu.PrefetchScalarGridSpec(
            num_scalar_prefetch=1,
            grid=(2 * steps,),
            in_specs=[*both_specs(block, sent_width, steps)]
            + [hbm()] * 4
            + [fixed((2, triple))],
            out_specs=[row_out(triple), row_out(triple), row_out(model_width)]
            + [pl.BlockSpec(matrix.shape, lambda i, *refs: (0, 0))] * 2,
            scratch_shapes=[pltpu.SemaphoreType.DMA((4,))],
        ),
        out_shape=[jax.ShapeDtypeStruct((2 * count, triple), BF16)] * 2
        + [jax.ShapeDtypeStruct((2 * count, model_width), BF16), matrix, matrix],
        compiler_params=vmem(48),
        cost_estimate=pl.CostEstimate(
            flops=8 * count * model_width * triple, bytes_accessed=24 << 20, transcendentals=0
        ),
        name="project",
    )(place, own, other, *halves, biases)


def out_grads_body(steps, own_ref, other_ref, w_a, w_b, out_a, out_b, rows_ref):
    rows = rows_of(pl.program_id(0), steps, own_ref, other_ref, rows_ref.shape[1])
    rows_ref[...] = rows
    out_a[...] = dot_transposed(rows, w_a[...]).astype(BF16)
    out_b[...] = dot_transposed(rows, w_b[...]).astype(BF16)


def out_grads(own, other, w_out):
    count, sent_width = own.shape
    width, model_width = w_out[0].shape
    block = min(512, count)
    steps = count // block
    row_out = lambda columns: pl.BlockSpec((block, columns), lambda i: (i, 0))
    return pl.pallas_call(
        functools.partial(out_grads_body, steps),
        grid=(2 * steps,),
        in_specs=[*both_specs(block, sent_width, steps)] + [fixed(w_out[0].shape)] * 2,
        out_specs=[row_out(width), row_out(width), row_out(model_width)],
        out_shape=[jax.ShapeDtypeStruct((2 * count, width), BF16)] * 2
        + [jax.ShapeDtypeStruct((2 * count, model_width), BF16)],
        compiler_params=vmem(48),
        cost_estimate=pl.CostEstimate(
            flops=8 * count * model_width * width, bytes_accessed=14 << 20, transcendentals=0
        ),
        name="out_grads",
    )(own, other, *w_out)


def split_product_body(steps, turned, left_a, left_b, w_a, w_b, sent_ref, kept_ref):
    multiply = dot_transposed if turned else dot_rows
    inner = w_a.shape[1] if turned else w_a.shape[0]
    product = multiply(left_a[:, :inner], w_a[...]) + multiply(left_b[:, :inner], w_b[...])
    step = pl.program_id(0)

    @pl.when(step < steps)
    def other_rows():
        put(sent_ref, product)

    @pl.when(step >= steps)
    def own_rows():
        kept_ref[...] = product


def split_product(lefts, weights, turned, model_width):
    count, width = lefts[0].shape
    block = min(512, count // 2)
    steps = count // 2 // block
    left = pl.BlockSpec((block, width), lambda i: ((i + steps) % (2 * steps), 0))
    parts = [
        jax.ShapeDtypeStruct((count // 2, lanes(model_width)), F32),
        jax.ShapeDtypeStruct((count // 2, model_width), F32),
    ]
    return pl.pallas_call(
        functools.partial(split_product_body, steps, turned),
        grid=(2 * steps,),
        in_specs=[left, left] + [fixed(weights[0].shape)] * 2,
        out_specs=[
            pl.BlockSpec((block, lanes(model_width)), lambda i: (jnp.minimum(i, steps - 1), 0)),
            pl.BlockSpec((block, model_width), lambda i: (jnp.maximum(i - steps, 0), 0)),
        ],
        out_shape=parts,
        compiler_params=vmem(48),
        cost_estimate=pl.CostEstimate(
            flops=4 * count * model_width * width, bytes_accessed=20 << 20, transcendentals=0
        ),
        name="split_product",
    )(*lefts, *weights)


def middle_body(rows_ref, kept_ref, got_ref, small_ref, middle_ref, low_ref):
    middle = rows_ref[...].astype(F32) + (
        kept_ref[...] + got_ref[:, : kept_ref.shape[1]] + small_ref[6:7]
    )
    middle_ref[...] = middle
    hat, _ = norm_stats(middle)
    put(low_ref, (hat * small_ref[2:3] + small_ref[3:4]).astype(BF16))


def middle_norm(rows, kept, got, small):
    count, width = rows.shape
    block = min(256, count)
    part = pl.BlockSpec((block, width), lambda i: (i, 0))
    sent = pl.BlockSpec((block, lanes(width)), lambda i: (i, 0))
    return pl.pallas_call(
        middle_body,
        grid=(count // block,),
        in_specs=[part, part, sent, fixed(small.shape)],
        out_specs=[part, sent],
        out_shape=[
            jax.ShapeDtypeStruct((count, width), F32),
            jax.ShapeDtypeStruct((count, lanes(width)), BF16),
        ],
        compiler_params=vmem(32),
        name="middle_norm",
    )(rows, kept, got, small)


def norm_back_body(wide_out, rows_ref, kept_ref, got_ref, base_ref, gain_ref, *outs):
    (full_ref, low_ref, sums_ref) = outs if wide_out else (None, *outs)
    rows = rows_ref[...].astype(F32)
    hat, scale = norm_stats(rows)
    width = rows.shape[1]
    upstream = kept_ref[:, :width] + got_ref[:, :width]
    base = base_ref[:, :width].astype(F32)
    grad = base + norm_backward(upstream, hat, scale, gain_ref[...])
    low = grad.astype(BF16)
    if wide_out:
        full_ref[...] = grad
    put(low_ref, low)

    @pl.when(pl.program_id(0) == 0)
    def clear():
        sums_ref[...] = jnp.zeros_like(sums_ref)

    for index, term in enumerate((upstream * hat, upstream, low.astype(F32), base)):
        sums_ref[index : index + 1] += jnp.sum(term, axis=0, keepdims=True)


def norm_back(rows, kept, got, base, gain, wide_out):
    count, width = rows.shape
    block = min(256, count)
    part = pl.BlockSpec((block, width), lambda i: (i, 0))
    sent = pl.BlockSpec((block, lanes(width)), lambda i: (i, 0))
    full = [jax.ShapeDtypeStruct((count, width), F32)] if wide_out else []
    return pl.pallas_call(
        functools.partial(norm_back_body, wide_out),
        grid=(count // block,),
        in_specs=[part, pl.BlockSpec((block, kept.shape[1]), lambda i: (i, 0)), sent]
        + [pl.BlockSpec((block, base.shape[1]), lambda i: (i, 0)), fixed((1, width))],
        out_specs=[part] * len(full) + [sent, pl.BlockSpec((8, width), lambda i: (0, 0))],
        out_shape=full
        + [
            jax.ShapeDtypeStruct((count, lanes(width)), BF16),
            jax.ShapeDtypeStruct((8, width), F32),
        ],
        compiler_params=vmem(40),
        name="norm_back",
    )(rows, kept, got, base, gain)


def feed_forward_body(
    skipped,
    rows_ref,
    cot_ref,
    w_in_mine,
    w_in_theirs,
    w_back_mine,
    w_back_theirs,
    bias_ref,
    *refs,
):
    (
        act_mine, act_theirs, inner_mine, inner_theirs, rows_out, cot_out, out_ref, up_ref, sums_ref
    ) = refs[skipped:]
    model_width = rows_out.shape[1]
    rows, cot = rows_ref[:, :model_width], cot_ref[:, :model_width]
    rows_out[...] = rows
    cot_out[...] = cot

    @pl.when(pl.program_id(0) == 0)
    def clear():
        sums_ref[...] = jnp.zeros_like(sums_ref)

    out, up = None, None
    shares = (
        (w_in_mine, w_back_mine, act_mine, inner_mine),
        (w_in_theirs, w_back_theirs, act_theirs, inner_theirs),
    )
    for part, (w_in, w_back, act_ref, inner_ref) in enumerate(shares):
        hidden = dot_rows(rows, w_in[...]) + bias_ref[part : part + 1]
        value, slope = gelu_parts(hidden)
        act = value.astype(BF16)
        act_ref[...] = act
        inner = (dot_transposed(cot, w_back[...]) * slope).astype(BF16)
        inner_ref[...] = inner
        sums_ref[part : part + 1] += jnp.sum(inner.astype(F32), axis=0, keepdims=True)
        one_out = dot_rows(act, w_back[...])
        one_up = dot_transposed(inner, w_in[...])
        out = one_out if out is None else out + one_out
        up = one_up if up is None else up + one_up
    put(out_ref, out)
    put(up_ref, up)


def feed_forward(rows, cot, half, weights, biases, filled):
    count, sent_width = rows.shape
    model_width, ff_share = weights[0].shape
    block = min(FF_ROWS, count)
    steps = count // block
    row_spec = pl.BlockSpec((block, sent_width), lambda i: (i, 0))
    joined = lambda width: pl.BlockSpec((block, width), lambda i: (half * steps + i, 0))
    act_shape = jax.ShapeDtypeStruct((2 * count, ff_share), BF16)
    row_shape = jax.ShapeDtypeStruct((2 * count, model_width), BF16)
    part_shape = jax.ShapeDtypeStruct((count, sent_width), F32)
    filled = () if filled is None else tuple(filled)
    return pl.pallas_call(
        functools.partial(feed_forward_body, len(filled)),
        out_shape=[act_shape] * 4
        + [row_shape] * 2
        + [part_shape] * 2
        + [jax.ShapeDtypeStruct((8, ff_share), F32)],
        grid=(steps,),
        in_specs=[row_spec, row_spec]
        + [fixed(matrix.shape) for matrix in weights]
        + [fixed((2, ff_share))]
        + [hbm()] * len(filled),
        out_specs=[joined(ff_share)] * 4
        + [joined(model_width)] * 2
        + [row_spec] * 2
        + [pl.BlockSpec((8, ff_share), lambda i: (0, 0))],
        input_output_aliases={7 + i: i for i in range(len(filled))},
        compiler_params=vmem(58),
        cost_estimate=pl.CostEstimate(
            flops=16 * count * model_width * ff_share,
            bytes_accessed=8 * model_width * ff_share + 16 * count * model_width,
            transcendentals=2 * count * ff_share,
        ),
        name="feed_forward",
    )(rows, cot, *weights, biases, *filled)


def permute(value, axis_name, pairs):
    return lax.ppermute(value, axis_name, pairs)


def swap(value, axis_name, distance):
    count = lax.axis_size(axis_name)
    return permute(value, axis_name, [(i, i ^ distance) for i in range(count)])


def tie(*values):
    return lax.optimization_barrier(values)


def lower_pairs(pairs, y_count):
    return [
        (source * y_count + y, target * y_count + y)
        for source, target in pairs
        for y in range(y_count)
    ]


def spread_lead(block, z_here):
    far = permute(block, "dp", lower_pairs([(0, 2)], 2))
    held = jnp.where(z_here == 0, block, far)
    near = permute(held, "dp", lower_pairs([(0, 1), (2, 3)], 2))
    return jnp.where(z_here % 2 == 0, held, near)


def move_rest(block, distance, plane_distance):
    over_dp, over_seq = distance
    pairs = []
    for d in range(8):
        if (d // 2) ^ plane_distance != 0:
            pairs += [(d * 4 + q, (d ^ over_dp) * 4 + (q ^ over_seq)) for q in range(4)]
    return permute(block, ("dp", "seq"), pairs)


def pick(stacked, index, axis=0):
    return lax.dynamic_index_in_dim(stacked, index, axis, keepdims=False)


def halve_plane(lower, upper, y_here):
    return (
        jnp.where(y_here == 0, lower, upper),
        jnp.where(y_here == 0, upper, lower).astype(BF16),
    )


def nearer_planes(held, plane):
    near = permute(
        held.astype(BF16), "dp", lower_pairs([(plane ^ 1, plane), (plane ^ 3, plane ^ 2)], 2)
    )
    return held + near.astype(F32)


def farther_planes(held, plane):
    far = permute(held.astype(BF16), "dp", lower_pairs([(plane ^ 2, plane)], 2))
    return held + far.astype(F32)


def sum_everywhere(value):
    for axis_name in ("seq", "dp"):
        distance = 1
        while distance < lax.axis_size(axis_name):
            value = value + swap(value, axis_name, distance)
            distance *= 2
    return value


def per_device(
    rows_in,
    out_cotangent,
    cell_lengths,
    cell_starts,
    key_mask,
    weights_master,
    first_moment,
    second_moment,
    small_master,
    small_first,
    small_second,
    step_count,
):
    model_width = rows_in.shape[3]
    local_rows = rows_in.shape[2]
    length = key_mask.shape[2]
    shard_len = weights_master.shape[2]
    groups = lax.axis_size("seq")
    dp_count = lax.axis_size("dp")
    head_share = model_width // groups
    heads_here = HEADS // groups
    triple = 3 * head_share
    first_end = model_width * triple
    second_end = first_end + head_share * model_width
    third_end = second_end + model_width * model_width
    seq_here = lax.axis_index("seq")
    dp_here = lax.axis_index("dp")
    chip = seq_here // 2
    core = seq_here % 2
    z_here = dp_here // 2
    y_here = dp_here % 2
    planar = dp_count == 8 and shard_len * 2 == first_end
    shares = (core + 2 * chip, core + 2 * (1 - chip))

    def exchange_micro(array):
        own = pick(array[:, 0], chip)
        received = swap(widen(pick(array[:, 0], 1 - chip)), "seq", 2)[:, :model_width]
        first = jnp.where(chip == 0, own, received)
        second = jnp.where(chip == 0, received, own)
        return jnp.concatenate([first, second], axis=0)

    def widen(rows):
        return jnp.pad(rows, ((0, 0), (0, lanes(model_width) - model_width)))

    own_in = exchange_micro(rows_in)

    ends = jnp.array([first_end, second_end, third_end, dp_count * shard_len], jnp.int32)
    begin = dp_here * shard_len
    lower_matrix = jnp.sum((begin >= ends).astype(jnp.int32))
    upper_matrix = jnp.sum((begin + shard_len - 1 >= ends).astype(jnp.int32))
    bound = jnp.minimum(pick(ends, lower_matrix) - begin, shard_len).reshape(1)
    matrices = jnp.arange(4, dtype=jnp.int32)

    def matrix_sums(pair):
        return jnp.where(matrices == lower_matrix, pair[0], 0.0) + jnp.where(
            matrices == upper_matrix, pair[1], 0.0
        )

    weight = weights_master
    low_weight, weight_sums = round_weights(bound, weight)
    y_index = y_here.reshape(1).astype(jnp.int32)
    if planar:
        tall = low_weight.reshape(shard_len // triple, triple)
        wide = low_weight.reshape(shard_len // model_width, model_width)
        cut, tall_rows = wide.shape[0], tall.shape[0]
        lead = spread_lead(tall, z_here)
        lead, wide = tie(lead, wide)
        lead_across = swap(lead, "dp", 1)
        halves = (lead, lead_across, swap(lead, "seq", 2), swap(lead_across, "seq", 2))
        dp_index = dp_here.reshape(1).astype(jnp.int32)
        far = move_rest(wide, (4, 0), 0)
        near = move_rest(wide, (2, 0), 0)
    else:
        copies = lax.all_gather(low_weight.reshape(1, shard_len), ("dp", "seq"), axis=0, tiled=True)
        copies = copies.reshape(dp_count, groups, shard_len)
        per_share = [pick(copies, share, 1).reshape(dp_count * shard_len) for share in shares]
        halves = []
        for flat in per_share:
            matrix = flat[:first_end].reshape(model_width, triple)
            first = jnp.where(y_here == 0, matrix[: model_width // 2], matrix[model_width // 2 :])
            second = jnp.where(y_here == 0, matrix[model_width // 2 :], matrix[: model_width // 2])
            halves += [first, second]
        w_out = [flat[first_end:second_end].reshape(head_share, model_width) for flat in per_share]
        w_in = [flat[second_end:third_end].reshape(model_width, model_width) for flat in per_share]
        w_back = [flat[third_end:].reshape(model_width, model_width) for flat in per_share]

    def share_columns(vector, share):
        return lax.dynamic_slice_in_dim(vector, share * head_share, head_share)

    attn_biases = [
        jnp.concatenate(
            [
                share_columns(small_master[4], share),
                jnp.zeros((head_share,), F32),
                share_columns(small_master[5], share),
            ]
        )
        for share in shares
    ]
    ff_biases = jnp.stack([pick(small_master, 8 + share) for share in shares])

    starts = pick(cell_starts[:, 0], chip)
    lengths = pick(cell_lengths[:, 0], chip)
    places = jnp.arange(length, dtype=jnp.int32)
    inside = (places[:, None] >= starts[None, :]) & (places[:, None] < (starts + lengths)[None, :])
    first_key = jnp.max(jnp.where(inside, starts[None, :], -1), axis=1)
    first_key = jnp.where(first_key < 0, places, first_key)
    low_blocks = first_key.reshape(-1, local_rows)[:, 0] // local_rows
    block_starts = first_key.reshape(-1, 1, local_rows)
    core_index = core.reshape(1).astype(jnp.int32)

    inputs = own_in.astype(F32)
    hat_one, _ = norm_stats(inputs)
    low_one = widen((hat_one * small_master[0] + small_master[1]).astype(BF16))
    other_one = swap(low_one, "seq", 1)

    *qkv, rows_one, w_attn_mine, w_attn_theirs = project(
        y_index, low_one, other_one, halves, jnp.stack(attn_biases)
    )

    def attend(part):
        return attention_forward(low_blocks, core_index, block_starts, qkv[part], heads_here)

    if planar:
        near, far, qkv[0] = tie(near, far, qkv[0])
        planes = (wide, near, far, move_rest(far, (2, 0), 2))
        across = [move_rest(block, (1, 0), plane) for plane, block in enumerate(planes[:3])]
        over = [move_rest(block, (0, 2), plane) for plane, block in enumerate(planes[:3])]
    attended = [attend(0)]
    if planar:
        qkv[1], planes, across, over, own_e_in, _ = tie(
            qkv[1], planes, across, over, out_cotangent, attended[0][2]
        )
        across.append(move_rest(planes[3], (1, 0), 3))
        over.append(move_rest(planes[3], (0, 2), 3))
        both = [
            move_rest(over[plane], (1, 0), plane)
            if plane % 2 == 0
            else move_rest(across[plane], (0, 2), plane)
            for plane in range(4)
        ]
    else:
        own_e_in = out_cotangent
    own_e = widen(exchange_micro(own_e_in))
    other_e = swap(own_e, "seq", 1)
    attended.append(attend(1))
    if planar:
        dp_index, _ = tie(dp_index, attended[1][2])
        rest_mine = [block for pair in zip(planes, across) for block in pair]
        rest_theirs = [block for pair in zip(over, both) for block in pair]
        matrices_mine = unpack_share(dp_index, rest_mine, head_share, model_width)
        matrices_theirs = unpack_share(dp_index, rest_theirs, head_share, model_width)
        w_out, w_in, w_back = (list(pair) for pair in zip(matrices_mine, matrices_theirs))
    sent, kept = split_product([attended[0][0], attended[1][0]], w_out, False, model_width)
    middle, low_two = middle_norm(own_in, kept, swap(sent, "seq", 1), small_master)
    other_two = swap(low_two, "seq", 1)

    weights = (w_in[0], w_in[1], w_back[0], w_back[1])
    *filled, out_sent, up_sent, sums_sent = feed_forward(
        other_two, other_e, 1, weights, ff_biases, None
    )
    out_received = swap(out_sent, "seq", 1)
    up_received = swap(up_sent, "seq", 1)
    *filled, out_kept, up_kept, sums_kept = feed_forward(
        low_two, own_e, 0, weights, ff_biases, filled
    )
    activated, inner, (rows_two, rows_e) = filled[:2], filled[2:4], filled[4:]
    inner_sums = sums_sent + sums_kept

    link = BF16 if planar else F32
    back_sent = dot_columns(activated[1], rows_e).astype(link)
    in_sent = dot_columns(rows_two, inner[1]).astype(link)
    back_sent, in_sent, up_kept = tie(*(back_sent, in_sent, up_kept))
    back_received = swap(back_sent, "seq", 2)
    in_received = swap(in_sent, "seq", 2)

    grad_mid, low_mid, sums_two = norm_back(
        middle, up_kept, up_received, own_e, small_master[2:3], True
    )
    grad_att_mine, grad_att_theirs, rows_mid = out_grads(low_mid, swap(low_mid, "seq", 1), w_out)
    out_sent_theirs = dot_columns(attended[1][0], rows_mid).astype(link)
    out_sent_theirs, grad_att_theirs = tie(*(out_sent_theirs, grad_att_theirs))
    outer_received = swap(out_sent_theirs, "seq", 2)

    def attend_back(part, grad_att):
        return attention_backward(
            low_blocks,
            core_index,
            block_starts,
            qkv[part],
            grad_att,
            attended[part][1],
            attended[part][2],
            heads_here,
        )

    packed_theirs = attend_back(1, grad_att_theirs)
    attn_sent = dot_columns(rows_one, packed_theirs).astype(link)
    attn_sent, packed_theirs, rows_two, rows_e, rows_mid = tie(
        attn_sent, packed_theirs, rows_two, rows_e, rows_mid
    )
    attn_received = swap(attn_sent, "seq", 2)
    share_back = dot_columns(activated[0], rows_e)
    share_in = dot_columns(rows_two, inner[0])
    share_out = dot_columns(attended[0][0], rows_mid)
    share_back, share_in, share_out, back_received, in_received, outer_received = tie(
        share_back, share_in, share_out, back_received, in_received, outer_received
    )
    share_back = share_back + back_received.astype(F32)
    share_in = share_in + in_received.astype(F32)
    share_out = share_out + outer_received.astype(F32)
    if planar:
        rest = cut - head_share
        seams = [rest, rest + cut, rest + 2 * cut]
        taken = cut - (model_width - seams[2])
        pieces = [
            jnp.concatenate([share_out, share_in[: seams[0]]], axis=0),
            share_in[seams[0] : seams[1]],
            share_in[seams[1] : seams[2]],
            jnp.concatenate([share_in[seams[2] :], share_back[:taken]], axis=0),
            share_back[taken : taken + cut],
            share_back[taken + cut :],
        ]
        split = [halve_plane(pieces[2 * i], pieces[2 * i + 1], y_here) for i in range(3)]
        kept_rest, sent_rest = [pair[0] for pair in split], [pair[1] for pair in split]
        kept_rest, sent_rest, grad_att_mine = tie(kept_rest, sent_rest, grad_att_mine)
        got_rest = [swap(block, "dp", 1) for block in sent_rest]

    packed_mine = attend_back(0, grad_att_mine)
    share_attn = dot_columns(rows_one, packed_mine) + attn_received.astype(F32)
    if planar:
        kept_lead, sent_lead = halve_plane(share_attn[:tall_rows], share_attn[tall_rows:], y_here)
        kept_lead, sent_lead, kept_rest, packed_mine, out_received = tie(
            kept_lead, sent_lead, kept_rest, packed_mine, out_received
        )
        got_lead = swap(sent_lead, "dp", 1)
        sums_rest = [
            nearer_planes(kept + got.astype(F32), plane)
            for plane, kept, got in zip((1, 2, 3), kept_rest, got_rest)
        ]
    result_rows = widen(
        (middle + ((out_kept + out_received)[:, :model_width] + small_master[7])).astype(BF16)
    )
    packed = [packed_mine, packed_theirs]
    sent, kept = split_product(packed, [w_attn_mine, w_attn_theirs], True, model_width)
    grad_x, sums_one = norm_back(
        own_in, kept, swap(sent, "seq", 1), grad_mid, small_master[0:1], False
    )

    def return_micro(rows):
        lower, upper = rows[:local_rows], rows[local_rows:]
        own = jnp.where(chip == 0, lower, upper)[:, :model_width]
        received = swap(jnp.where(chip == 0, upper, lower), "seq", 2)[:, :model_width]
        first = jnp.where(chip == 0, own, received)
        second = jnp.where(chip == 0, received, own)
        return jnp.stack([first, second])[:, None]

    result_all = return_micro(result_rows)
    grad_all = return_micro(grad_x)

    def at_shares(columns):
        row = jnp.zeros((model_width,), F32)
        for share, column in zip(shares, columns):
            row = lax.dynamic_update_slice(row, column, (share * head_share,))
        return row

    bias_sums = [jnp.sum(packed[part].astype(F32), axis=0) for part in range(2)]
    inner_rows = jnp.zeros((4, model_width), F32)
    for part in range(2):
        inner_rows = lax.dynamic_update_slice(
            inner_rows, inner_sums[part : part + 1], (shares[part], 0)
        )
    small_now = jnp.concatenate(
        [
            sums_one[:2],
            sums_two[:2],
            at_shares([sums[:head_share] for sums in bias_sums])[None],
            at_shares([sums[2 * head_share : triple] for sums in bias_sums])[None],
            sums_two[2:4],
            inner_rows,
            jnp.pad(matrix_sums(weight_sums), (0, model_width - 4))[None],
        ]
    )

    if planar:
        sum_lead = nearer_planes(kept_lead + got_lead.astype(F32), 0)
        sums_rest = [farther_planes(held, plane) for plane, held in zip((1, 2, 3), sums_rest)]
        wide_sum = jnp.where(
            z_here == 1, sums_rest[0], jnp.where(z_here == 2, sums_rest[1], sums_rest[2])
        )
        lead_grad = farther_planes(sum_lead, 0)[:, :triple].reshape(1, 1, shard_len)
        rest_grad = wide_sum.reshape(1, 1, shard_len)
        leads = z_here == 0
    else:
        flat_here = jnp.concatenate(
            [matrix.reshape(-1) for matrix in (share_attn[:, :triple], share_out, share_in, share_back)]
        )
        lead_grad = lax.psum_scatter(
            flat_here.reshape(dp_count, shard_len), "dp", scatter_dimension=0, tiled=True
        ).reshape(1, 1, shard_len)
        rest_grad = lead_grad
        leads = z_here >= 0

    steps_done = step_count[0].astype(F32)
    fix_one = 1.0 - jnp.exp(steps_done * math.log(BETA_ONE))
    fix_two = 1.0 - jnp.exp(steps_done * math.log(BETA_TWO))
    ints = jnp.concatenate([bound, leads.astype(jnp.int32).reshape(1)])
    reduced, moments, update, update_sums = new_moments(
        ints,
        jnp.stack([fix_one, fix_two]),
        lead_grad,
        rest_grad,
        first_moment,
        second_moment,
        weight,
    )
    small_sum = sum_everywhere(small_now)
    small_grad = small_sum[:12]
    weight_norms = jnp.sqrt(small_sum[12, :4])
    update_norms = jnp.sqrt(sum_everywhere(matrix_sums(update_sums)[None])[0])
    ratios = weight_norms / update_norms
    new_weight, weight_copy = new_weights(
        ints, jnp.stack([pick(ratios, lower_matrix), pick(ratios, upper_matrix)]), weight, update
    )
    small_one = BETA_ONE * small_first + (1.0 - BETA_ONE) * small_grad
    small_two = BETA_TWO * small_second + (1.0 - BETA_TWO) * small_grad * small_grad
    small_updated = small_master - SMALL_RATE * (small_one / fix_one) / (
        jnp.sqrt(small_two / fix_two) + ADAM_EPS
    )
    return (
        result_all,
        grad_all,
        reduced,
        moments,
        new_weight,
        weight_copy,
        jnp.stack([weight_norms, update_norms, ratios]),
        small_grad,
        jnp.stack([small_one, small_two]),
        small_updated,
    )


def solution(mesh):
    in_specs = (
        P(None, "dp", "seq", None),
        P(None, "dp", "seq", None),
        P(None, "dp", None),
        P(None, "dp", None),
        P(None, "dp", None),
        P("dp", "seq", None),
        P("dp", "seq", None),
        P("dp", "seq", None),
        P(),
        P(),
        P(),
        P(),
    )
    out_specs = (
        P(None, "dp", "seq", None),
        P(None, "dp", "seq", None),
        P("dp", "seq", None),
        P(None, "dp", "seq", None),
        P("dp", "seq", None),
        P("dp", "seq", None),
        P(),
        P(),
        P(),
        P(),
    )
    return jax.shard_map(
        per_device, mesh=mesh, in_specs=in_specs, out_specs=out_specs, check_vma=False
    )
```

```python
import functools
import math

import jax
import jax.numpy as jnp
from jax import lax
from jax.experimental import pallas as pl
from jax.experimental.pallas import tpu as pltpu
from jax.sharding import PartitionSpec as P

HEADS = 20


NORM_EPS = 1e-05
BETA_ONE = 0.9
BETA_TWO = 0.999
ADAM_EPS = 1e-06
DECAY = 0.01
MATRIX_RATE = 0.3
SMALL_RATE = 0.25
MASKED = -1e30
LOG2_E = 1.4426950408889634
FF_ROWS = 256

F32 = jnp.float32
BF16 = jnp.bfloat16


def dot_rows(left, right):
    return lax.dot_general(left, right, (((1,), (0,)), ((), ())), preferred_element_type=F32)


def dot_transposed(left, right):
    return lax.dot_general(left, right, (((1,), (1,)), ((), ())), preferred_element_type=F32)


def dot_columns(left, right):
    return lax.dot_general(left, right, (((0,), (0,)), ((), ())), preferred_element_type=F32)


def norm_stats(rows):
    center = jnp.mean(rows, axis=-1, keepdims=True)
    centered = rows - center
    spread = jnp.mean(centered * centered, axis=-1, keepdims=True)
    scale = lax.rsqrt(spread + NORM_EPS)
    return centered * scale, scale


def norm_backward(upstream, hat, scale, gain):
    weighted = upstream * gain
    return (
        weighted
        - jnp.mean(weighted, axis=-1, keepdims=True)
        - hat * jnp.mean(weighted * hat, axis=-1, keepdims=True)
    ) * scale


def gelu_parts(values):
    inner = math.sqrt(2.0 / math.pi)
    squares = values * values
    bent = jnp.tanh(inner * (values + 0.044715 * values * squares))
    half = 0.5 * (1.0 + bent)
    slope = half + 0.5 * values * (1.0 - bent * bent) * inner * (1.0 + 3.0 * 0.044715 * squares)
    return values * half, slope


def block_place(core, block):
    return jnp.where(block % 2 == core, 0, 2) + block // 2


def block_rows(core, block, rows):
    return pl.ds(pl.multiple_of(block_place(core, block) * rows, rows), rows)


def attention_forward_body(
    heads, width, bq, low_ref, core_ref, start_ref, qkv_ref, out_ref, outt_ref, lse_ref, qs, ks, vt, acc
):
    length = qkv_ref.shape[0]
    flat = heads * width
    factor = width**-0.5 * LOG2_E
    core = core_ref[0]

    def unpack(block, carry):
        here = block_rows(core, block, bq)
        there = pl.ds(pl.multiple_of(block * bq, bq), bq)
        for h in range(heads):
            qs[h, there] = qkv_ref[here, h * width : (h + 1) * width]
            ks[h, there] = qkv_ref[here, flat + h * width : flat + (h + 1) * width]
        turned = qkv_ref[here, 2 * flat : 3 * flat].astype(F32).T
        for h in range(heads):
            vt[h, block] = turned[h * width : (h + 1) * width].astype(BF16)
        return carry

    lax.fori_loop(0, length // bq, unpack, 0)

    def query_step(qb, carry):
        q0 = pl.multiple_of(qb * bq, bq)
        start = start_ref[qb]
        query_place = q0 + lax.broadcasted_iota(jnp.int32, (1, bq), 1)
        acc[...] = jnp.zeros_like(acc)

        def key_step(kb, tops_totals):
            tops, totals = tops_totals
            k0 = pl.multiple_of(kb * bq, bq)
            key_place = k0 + lax.broadcasted_iota(jnp.int32, (bq, bq), 0)
            allowed = (key_place <= query_place) & (key_place >= start)
            new_tops, new_totals = [], []
            for h in range(heads):
                scores = dot_transposed(ks[h, pl.ds(k0, bq)], qs[h, pl.ds(q0, bq)]) * factor
                scores = jnp.where(allowed, scores, MASKED)
                top = jnp.maximum(tops[h], jnp.max(scores, axis=0, keepdims=True))
                fade = jnp.exp2(tops[h] - top)
                weights = jnp.exp2(scores - top)
                own = slice(h * width, (h + 1) * width)
                acc[own] = acc[own] * fade + dot_rows(vt[h, kb], weights.astype(BF16))
                new_tops.append(top)
                new_totals.append(totals[h] * fade + jnp.sum(weights, axis=0, keepdims=True))
            return tuple(new_tops), tuple(new_totals)

        first = (
            tuple(jnp.full((1, bq), -1e29, F32) for _ in range(heads)),
            tuple(jnp.zeros((1, bq), F32) for _ in range(heads)),
        )
        tops, totals = lax.fori_loop(low_ref[qb], qb + 1, key_step, first)
        for h in range(heads):
            own = slice(h * width, (h + 1) * width)
            acc[own] = acc[own] * (1.0 / totals[h])
            lse_ref[qb, h : h + 1, :] = tops[h] + jnp.log2(totals[h])
        mixed = acc[...]
        outt_ref[qb] = mixed
        out_ref[block_rows(core, qb, bq), :] = mixed.T.astype(BF16)
        return carry

    lax.fori_loop(0, length // bq, query_step, 0)


def attention_backward_body(
    heads,
    width,
    bq,
    low_ref,
    core_ref,
    start_ref,
    qkv_ref,
    dout_ref,
    outt_ref,
    lse_ref,
    grad_ref,
    qs,
    ks,
    vs,
    ds,
    kt,
    dk,
    dv,
    dqt,
):
    length = qkv_ref.shape[0]
    flat = heads * width
    score_scale = width**-0.5
    factor = score_scale * LOG2_E
    core = core_ref[0]

    def unpack(block, carry):
        here = block_rows(core, block, bq)
        there = pl.ds(pl.multiple_of(block * bq, bq), bq)
        for h in range(heads):
            qs[h, there] = qkv_ref[here, h * width : (h + 1) * width]
            ks[h, there] = qkv_ref[here, flat + h * width : flat + (h + 1) * width]
            vs[h, there] = qkv_ref[here, 2 * flat + h * width : 2 * flat + (h + 1) * width]
            ds[h, there] = dout_ref[here, h * width : (h + 1) * width]
        turned = qkv_ref[here, flat : 2 * flat].astype(F32).T
        for h in range(heads):
            kt[h, block] = turned[h * width : (h + 1) * width].astype(BF16)
        return carry

    lax.fori_loop(0, length // bq, unpack, 0)
    dk[...] = jnp.zeros_like(dk)
    dv[...] = jnp.zeros_like(dv)

    def query_step(qb, carry):
        q0 = pl.multiple_of(qb * bq, bq)
        queries = pl.ds(q0, bq)
        here = block_rows(core, qb, bq)
        start = start_ref[qb]
        query_place = q0 + lax.broadcasted_iota(jnp.int32, (1, bq), 1)
        products = dout_ref[here, :].astype(F32).T * outt_ref[qb]
        inners = [
            jnp.sum(products[h * width : (h + 1) * width], axis=0, keepdims=True)
            for h in range(heads)
        ]
        dqt[...] = jnp.zeros_like(dqt)

        def key_step(kb, inner_carry):
            k0 = pl.multiple_of(kb * bq, bq)
            keys = pl.ds(k0, bq)
            key_place = k0 + lax.broadcasted_iota(jnp.int32, (bq, bq), 0)
            allowed = (key_place <= query_place) & (key_place >= start)
            for h in range(heads):
                scores = dot_transposed(ks[h, keys], qs[h, queries]) * factor
                weights = jnp.exp2(
                    jnp.where(allowed, scores - lse_ref[qb, h : h + 1, :], MASKED)
                )
                dweights = dot_transposed(vs[h, keys], ds[h, queries])
                dscores = (weights * (dweights - inners[h])).astype(BF16)
                dv[h, keys] += dot_rows(weights.astype(BF16), ds[h, queries])
                dk[h, keys] += dot_rows(dscores, qs[h, queries])
                dqt[h * width : (h + 1) * width] += dot_rows(kt[h, kb], dscores)
            return inner_carry

        lax.fori_loop(low_ref[qb], qb + 1, key_step, 0)
        grad_ref[here, 0:flat] = (dqt[...] * score_scale).T.astype(BF16)
        return carry

    lax.fori_loop(0, length // bq, query_step, 0)

    def write_keys(kb, carry):
        here = block_rows(core, kb, bq)
        rows = pl.ds(pl.multiple_of(kb * bq, bq), bq)
        grad_ref[here, flat : 2 * flat] = jnp.concatenate(
            [dk[h, rows] * score_scale for h in range(heads)], axis=1
        ).astype(BF16)
        grad_ref[here, 2 * flat : 3 * flat] = jnp.concatenate(
            [dv[h, rows] for h in range(heads)], axis=1
        ).astype(BF16)
        rest = grad_ref.shape[1] - 3 * flat
        if rest:
            grad_ref[here, 3 * flat :] = jnp.zeros((bq, rest), BF16)
        return carry

    lax.fori_loop(0, length // bq, write_keys, 0)


def whole_block(shape):
    return pl.BlockSpec(shape, lambda step, *refs: (0,) * len(shape))


def attention_forward(low_blocks, core, starts, qkv, heads):
    length, triple = qkv.shape
    flat = triple // 3
    width = flat // heads
    blocks, _, bq = starts.shape
    grid_spec = pltpu.PrefetchScalarGridSpec(
        num_scalar_prefetch=2,
        grid=(1,),
        in_specs=[whole_block((blocks, 1, bq)), whole_block((length, triple))],
        out_specs=[
            whole_block((length, flat)),
            whole_block((blocks, flat, bq)),
            whole_block((blocks, 8, bq)),
        ],
        scratch_shapes=[
            pltpu.VMEM((heads, length, width), BF16),
            pltpu.VMEM((heads, length, width), BF16),
            pltpu.VMEM((heads, blocks, width, bq), BF16),
            pltpu.VMEM((flat, bq), F32),
        ],
    )
    return pl.pallas_call(
        functools.partial(attention_forward_body, heads, width, bq),
        out_shape=[
            jax.ShapeDtypeStruct((length, flat), BF16),
            jax.ShapeDtypeStruct((blocks, flat, bq), F32),
            jax.ShapeDtypeStruct((blocks, 8, bq), F32),
        ],
        grid_spec=grid_spec,
        compiler_params=pltpu.CompilerParams(vmem_limit_bytes=48 << 20),
        cost_estimate=pl.CostEstimate(
            flops=10 * length * length * flat,
            bytes_accessed=12 * length * flat,
            transcendentals=heads * length * length,
        ),
        name="attention_forward",
    )(low_blocks, core, starts, qkv)


def attention_backward(low_blocks, core, starts, qkv, grad_out, out_turned, log_total, heads):
    length, triple = qkv.shape
    flat = triple // 3
    width = flat // heads
    blocks, _, bq = starts.shape
    per_head = pltpu.VMEM((heads, length, width), BF16)
    sums = pltpu.VMEM((heads, length, width), F32)
    grid_spec = pltpu.PrefetchScalarGridSpec(
        num_scalar_prefetch=2,
        grid=(1,),
        in_specs=[
            whole_block((blocks, 1, bq)),
            whole_block((length, triple)),
            whole_block((length, flat)),
            whole_block((blocks, flat, bq)),
            whole_block((blocks, 8, bq)),
        ],
        out_specs=whole_block((length, lanes(triple))),
        scratch_shapes=[
            per_head,
            per_head,
            per_head,
            per_head,
            pltpu.VMEM((heads, blocks, width, bq), BF16),
            sums,
            sums,
            pltpu.VMEM((flat, bq), F32),
        ],
    )
    return pl.pallas_call(
        functools.partial(attention_backward_body, heads, width, bq),
        out_shape=jax.ShapeDtypeStruct((length, lanes(triple)), BF16),
        grid_spec=grid_spec,
        compiler_params=pltpu.CompilerParams(vmem_limit_bytes=60 << 20),
        cost_estimate=pl.CostEstimate(
            flops=14 * length * length * flat,
            bytes_accessed=20 * length * flat,
            transcendentals=heads * length * length,
        ),
        name="attention_backward",
    )(low_blocks, core, starts, qkv, grad_out, out_turned, log_total)


def lanes(width):
    return -(-width // 128) * 128


def put(ref, value):
    width = value.shape[1]
    ref[:, :width] = value
    if width < ref.shape[1]:
        ref[:, width:] = jnp.zeros((value.shape[0], ref.shape[1] - width), ref.dtype)


def vmem(count):
    return pltpu.CompilerParams(vmem_limit_bytes=count << 20)


def fixed(shape):
    return pl.BlockSpec(shape, lambda *step: (0,) * len(shape), pipeline_mode=pl.Buffered(1))


def hbm():
    return pl.BlockSpec(memory_space=pl.ANY)


def round_weights_body(bound_ref, weight_ref, low_ref, sums_ref):
    values = weight_ref[...]
    low_ref[...] = values[0, 0].astype(BF16)
    place = lax.broadcasted_iota(jnp.int32, values.shape, 2)
    squares = values * values
    lower = jnp.sum(jnp.where(place < bound_ref[0], squares, 0.0))
    sums_ref[0] = lower
    sums_ref[1] = jnp.sum(squares) - lower


def round_weights(bound, weight):
    smem = pl.BlockSpec(memory_space=pltpu.SMEM)
    whole = pl.BlockSpec(memory_space=pltpu.VMEM)
    return pl.pallas_call(
        round_weights_body,
        in_specs=[smem, whole],
        out_specs=[whole, smem],
        out_shape=[
            jax.ShapeDtypeStruct(weight.shape[2:], BF16),
            jax.ShapeDtypeStruct((2,), F32),
        ],
        compiler_params=vmem(32),
        name="round_weights",
    )(bound, weight)


def moments_body(
    ints_ref, floats_ref, lead_ref, rest_ref, first_ref, second_ref, weight_ref,
    grad_ref, moments_ref, update_ref, sums_ref,
):
    step = pl.program_id(0)
    grad = jnp.where(ints_ref[1] == 1, lead_ref[...], rest_ref[...])
    grad_ref[...] = grad
    first = BETA_ONE * first_ref[...] + (1.0 - BETA_ONE) * grad
    second = BETA_TWO * second_ref[...] + (1.0 - BETA_TWO) * grad * grad
    moments_ref[0] = first
    moments_ref[1] = second
    update = (first / floats_ref[0]) / (jnp.sqrt(second / floats_ref[1]) + ADAM_EPS)
    update = update + DECAY * weight_ref[...]
    update_ref[...] = update
    count = grad.shape[2]
    place = step * count + lax.broadcasted_iota(jnp.int32, grad.shape, 2)
    squares = update * update
    lower = jnp.sum(jnp.where(place < ints_ref[0], squares, 0.0))
    upper = jnp.sum(squares) - lower

    @pl.when(step == 0)
    def clear():
        sums_ref[0] = 0.0
        sums_ref[1] = 0.0

    sums_ref[0] += lower
    sums_ref[1] += upper


def flat_steps(count):
    return 7 if count % (7 * 128) == 0 else 1


def new_moments(ints, floats, lead, rest, first, second, weight):
    count = weight.shape[2]
    steps = flat_steps(count)
    smem = pl.BlockSpec(memory_space=pltpu.SMEM)
    flat = pl.BlockSpec((1, 1, count // steps), lambda i: (0, 0, i))
    pair = pl.BlockSpec((2, 1, 1, count // steps), lambda i: (0, 0, 0, i))
    return pl.pallas_call(
        moments_body,
        grid=(steps,),
        in_specs=[smem, smem] + [flat] * 5,
        out_specs=[flat, pair, flat, smem],
        out_shape=[
            jax.ShapeDtypeStruct(weight.shape, F32),
            jax.ShapeDtypeStruct((2,) + weight.shape, F32),
            jax.ShapeDtypeStruct(weight.shape, F32),
            jax.ShapeDtypeStruct((2,), F32),
        ],
        compiler_params=vmem(48),
        name="new_moments",
    )(ints, floats, lead, rest, first, second, weight)


def new_weights_body(ints_ref, ratio_ref, weight_ref, update_ref, new_ref, copy_ref):
    count = weight_ref.shape[2]
    place = pl.program_id(0) * count + lax.broadcasted_iota(jnp.int32, weight_ref.shape, 2)
    rate = jnp.where(place < ints_ref[0], ratio_ref[0], ratio_ref[1])
    new = weight_ref[...] - MATRIX_RATE * rate * update_ref[...]
    new_ref[...] = new
    copy_ref[...] = new.astype(BF16)


def new_weights(ints, ratios, weight, update):
    count = weight.shape[2]
    steps = flat_steps(count)
    smem = pl.BlockSpec(memory_space=pltpu.SMEM)
    flat = pl.BlockSpec((1, 1, count // steps), lambda i: (0, 0, i))
    return pl.pallas_call(
        new_weights_body,
        grid=(steps,),
        in_specs=[smem, smem, flat, flat],
        out_specs=[flat, flat],
        out_shape=[
            jax.ShapeDtypeStruct(weight.shape, F32),
            jax.ShapeDtypeStruct(weight.shape, BF16),
        ],
        compiler_params=vmem(32),
        name="new_weights",
    )(ints, ratios, weight, update)


def unpack_body(cut, out_rows, in_rows, place_ref, *refs):
    blocks, (w_out, w_in, w_back, held, sems) = refs[:8], refs[8:]
    here = place_ref[0]
    copies = [
        pltpu.make_async_copy(block, held.at[index ^ here], sems.at[index])
        for index, block in enumerate(blocks)
    ]
    for copy in copies:
        copy.start()
    for copy in copies:
        copy.wait()
    begin = 2 * cut
    for target, rows in ((w_out, out_rows), (w_in, in_rows), (w_back, in_rows)):
        done = 0
        while done < rows:
            block, offset = divmod(begin + done, cut)
            count = min(cut - offset, rows - done)
            target[done : done + count] = held[block, offset : offset + count]
            done += count
        begin += rows


def unpack_share(place, blocks, out_rows, in_rows):
    cut, columns = blocks[0].shape
    shapes = [(out_rows, columns), (in_rows, columns), (in_rows, columns)]
    return pl.pallas_call(
        functools.partial(unpack_body, cut, out_rows, in_rows),
        grid_spec=pltpu.PrefetchScalarGridSpec(
            num_scalar_prefetch=1,
            grid=(1,),
            in_specs=[hbm()] * 8,
            out_specs=[whole_block(shape) for shape in shapes],
            scratch_shapes=[
                pltpu.VMEM((8, cut, columns), BF16),
                pltpu.SemaphoreType.DMA((8,)),
            ],
        ),
        out_shape=[jax.ShapeDtypeStruct(shape, BF16) for shape in shapes],
        compiler_params=vmem(48),
        cost_estimate=pl.CostEstimate(flops=0, bytes_accessed=20 << 20, transcendentals=0),
        name="unpack_share",
    )(place, *blocks)


def pack_rest_body(
    cut, place_ref, out_ref, in_ref, back_ref, out_got, in_got, back_got, kept_ref, sent_ref
):
    here = place_ref[0]
    place = 0
    for matrix, got in ((out_ref, out_got), (in_ref, in_got), (back_ref, back_got)):
        done, rows = 0, matrix.shape[0]
        while done < rows:
            block, offset = divmod(place, cut)
            count = min(cut - offset, rows - done)
            source = slice(done, done + count)
            target = slice(offset, offset + count)
            plane, side = divmod(block, 2)

            @pl.when(here == side)
            def keep(matrix=matrix, got=got, source=source, target=target, plane=plane):
                kept_ref[plane, target] = matrix[source] + got[source].astype(F32)

            @pl.when(here != side)
            def send(matrix=matrix, got=got, source=source, target=target, plane=plane):
                sent_ref[plane, target] = (matrix[source] + got[source].astype(F32)).astype(BF16)

            done += count
            place += count


def pack_rest(place, matrices, received, cut):
    columns = matrices[0].shape[1]
    whole = pl.BlockSpec(memory_space=pltpu.VMEM)
    return pl.pallas_call(
        functools.partial(pack_rest_body, cut),
        in_specs=[pl.BlockSpec(memory_space=pltpu.SMEM)] + [whole] * 6,
        out_specs=[whole] * 2,
        out_shape=[
            jax.ShapeDtypeStruct((3, cut, columns), F32),
            jax.ShapeDtypeStruct((3, cut, columns), BF16),
        ],
        compiler_params=vmem(40),
        cost_estimate=pl.CostEstimate(flops=0, bytes_accessed=27 << 20, transcendentals=0),
        name="pack_rest",
    )(place, *matrices, *received)


def rows_of(step, steps, own_ref, other_ref, width):
    return jnp.where(step < steps, own_ref[:, :width], other_ref[:, :width])


def both_specs(block, width, steps):
    own = pl.BlockSpec((block, width), lambda i, *refs: (jnp.minimum(i, steps - 1), 0))
    other = pl.BlockSpec((block, width), lambda i, *refs: (jnp.maximum(i - steps, 0), 0))
    return own, other


def project_body(
    steps, place_ref, own_ref, other_ref, a0, a1, b0, b1, bias_ref,
    out_a, out_b, rows_ref, w_a, w_b, sems,
):
    step = pl.program_id(0)

    @pl.when(step == 0)
    def load():
        cut = a0.shape[0]
        here = place_ref[0]
        first = pl.ds(pl.multiple_of(here * cut, cut), cut)
        second = pl.ds(pl.multiple_of((1 - here) * cut, cut), cut)
        copies = [
            pltpu.make_async_copy(a0, w_a.at[first], sems.at[0]),
            pltpu.make_async_copy(a1, w_a.at[second], sems.at[1]),
            pltpu.make_async_copy(b0, w_b.at[first], sems.at[2]),
            pltpu.make_async_copy(b1, w_b.at[second], sems.at[3]),
        ]
        for copy in copies:
            copy.start()
        for copy in copies:
            copy.wait()

    rows = rows_of(step, steps, own_ref, other_ref, rows_ref.shape[1])
    rows_ref[...] = rows
    out_a[...] = (dot_rows(rows, w_a[...]) + bias_ref[0:1]).astype(BF16)
    out_b[...] = (dot_rows(rows, w_b[...]) + bias_ref[1:2]).astype(BF16)


def project(place, own, other, halves, biases):
    count, sent_width = own.shape
    cut, triple = halves[0].shape
    model_width = 2 * cut
    block = min(512, count)
    steps = count // block
    row_out = lambda width: pl.BlockSpec((block, width), lambda i, *refs: (i, 0))
    matrix = jax.ShapeDtypeStruct((2 * cut, triple), BF16)
    return pl.pallas_call(
        functools.partial(project_body, steps),
        grid_spec=pltpu.PrefetchScalarGridSpec(
            num_scalar_prefetch=1,
            grid=(2 * steps,),
            in_specs=[*both_specs(block, sent_width, steps)]
            + [hbm()] * 4
            + [fixed((2, triple))],
            out_specs=[row_out(triple), row_out(triple), row_out(model_width)]
            + [pl.BlockSpec(matrix.shape, lambda i, *refs: (0, 0))] * 2,
            scratch_shapes=[pltpu.SemaphoreType.DMA((4,))],
        ),
        out_shape=[jax.ShapeDtypeStruct((2 * count, triple), BF16)] * 2
        + [jax.ShapeDtypeStruct((2 * count, model_width), BF16), matrix, matrix],
        compiler_params=vmem(48),
        cost_estimate=pl.CostEstimate(
            flops=8 * count * model_width * triple, bytes_accessed=24 << 20, transcendentals=0
        ),
        name="project",
    )(place, own, other, *halves, biases)


def out_grads_body(steps, own_ref, other_ref, w_a, w_b, out_a, out_b, rows_ref):
    rows = rows_of(pl.program_id(0), steps, own_ref, other_ref, rows_ref.shape[1])
    rows_ref[...] = rows
    out_a[...] = dot_transposed(rows, w_a[...]).astype(BF16)
    out_b[...] = dot_transposed(rows, w_b[...]).astype(BF16)


def out_grads(own, other, w_out):
    count, sent_width = own.shape
    width, model_width = w_out[0].shape
    block = min(512, count)
    steps = count // block
    row_out = lambda columns: pl.BlockSpec((block, columns), lambda i: (i, 0))
    return pl.pallas_call(
        functools.partial(out_grads_body, steps),
        grid=(2 * steps,),
        in_specs=[*both_specs(block, sent_width, steps)] + [fixed(w_out[0].shape)] * 2,
        out_specs=[row_out(width), row_out(width), row_out(model_width)],
        out_shape=[jax.ShapeDtypeStruct((2 * count, width), BF16)] * 2
        + [jax.ShapeDtypeStruct((2 * count, model_width), BF16)],
        compiler_params=vmem(48),
        cost_estimate=pl.CostEstimate(
            flops=8 * count * model_width * width, bytes_accessed=14 << 20, transcendentals=0
        ),
        name="out_grads",
    )(own, other, *w_out)


def split_product_body(steps, turned, left_a, left_b, w_a, w_b, sent_ref, kept_ref):
    multiply = dot_transposed if turned else dot_rows
    inner = w_a.shape[1] if turned else w_a.shape[0]
    product = multiply(left_a[:, :inner], w_a[...]) + multiply(left_b[:, :inner], w_b[...])
    step = pl.program_id(0)

    @pl.when(step < steps)
    def other_rows():
        put(sent_ref, product)

    @pl.when(step >= steps)
    def own_rows():
        kept_ref[...] = product


def split_product(lefts, weights, turned, model_width):
    count, width = lefts[0].shape
    block = min(512, count // 2)
    steps = count // 2 // block
    left = pl.BlockSpec((block, width), lambda i: ((i + steps) % (2 * steps), 0))
    parts = [
        jax.ShapeDtypeStruct((count // 2, lanes(model_width)), F32),
        jax.ShapeDtypeStruct((count // 2, model_width), F32),
    ]
    return pl.pallas_call(
        functools.partial(split_product_body, steps, turned),
        grid=(2 * steps,),
        in_specs=[left, left] + [fixed(weights[0].shape)] * 2,
        out_specs=[
            pl.BlockSpec((block, lanes(model_width)), lambda i: (jnp.minimum(i, steps - 1), 0)),
            pl.BlockSpec((block, model_width), lambda i: (jnp.maximum(i - steps, 0), 0)),
        ],
        out_shape=parts,
        compiler_params=vmem(48),
        cost_estimate=pl.CostEstimate(
            flops=4 * count * model_width * width, bytes_accessed=20 << 20, transcendentals=0
        ),
        name="split_product",
    )(*lefts, *weights)


def middle_body(rows_ref, kept_ref, got_ref, small_ref, middle_ref, low_ref):
    middle = rows_ref[...].astype(F32) + (
        kept_ref[...] + got_ref[:, : kept_ref.shape[1]] + small_ref[6:7]
    )
    middle_ref[...] = middle
    hat, _ = norm_stats(middle)
    put(low_ref, (hat * small_ref[2:3] + small_ref[3:4]).astype(BF16))


def middle_norm(rows, kept, got, small):
    count, width = rows.shape
    block = min(256, count)
    part = pl.BlockSpec((block, width), lambda i: (i, 0))
    sent = pl.BlockSpec((block, lanes(width)), lambda i: (i, 0))
    return pl.pallas_call(
        middle_body,
        grid=(count // block,),
        in_specs=[part, part, sent, fixed(small.shape)],
        out_specs=[part, sent],
        out_shape=[
            jax.ShapeDtypeStruct((count, width), F32),
            jax.ShapeDtypeStruct((count, lanes(width)), BF16),
        ],
        compiler_params=vmem(32),
        name="middle_norm",
    )(rows, kept, got, small)


def norm_back_body(wide_out, rows_ref, kept_ref, got_ref, base_ref, gain_ref, *outs):
    (full_ref, low_ref, sums_ref) = outs if wide_out else (None, *outs)
    rows = rows_ref[...].astype(F32)
    hat, scale = norm_stats(rows)
    width = rows.shape[1]
    upstream = kept_ref[:, :width] + got_ref[:, :width]
    base = base_ref[:, :width].astype(F32)
    grad = base + norm_backward(upstream, hat, scale, gain_ref[...])
    low = grad.astype(BF16)
    if wide_out:
        full_ref[...] = grad
    put(low_ref, low)

    @pl.when(pl.program_id(0) == 0)
    def clear():
        sums_ref[...] = jnp.zeros_like(sums_ref)

    for index, term in enumerate((upstream * hat, upstream, low.astype(F32), base)):
        sums_ref[index : index + 1] += jnp.sum(term, axis=0, keepdims=True)


def norm_back(rows, kept, got, base, gain, wide_out):
    count, width = rows.shape
    block = min(256, count)
    part = pl.BlockSpec((block, width), lambda i: (i, 0))
    sent = pl.BlockSpec((block, lanes(width)), lambda i: (i, 0))
    full = [jax.ShapeDtypeStruct((count, width), F32)] if wide_out else []
    return pl.pallas_call(
        functools.partial(norm_back_body, wide_out),
        grid=(count // block,),
        in_specs=[part, pl.BlockSpec((block, kept.shape[1]), lambda i: (i, 0)), sent]
        + [pl.BlockSpec((block, base.shape[1]), lambda i: (i, 0)), fixed((1, width))],
        out_specs=[part] * len(full) + [sent, pl.BlockSpec((8, width), lambda i: (0, 0))],
        out_shape=full
        + [
            jax.ShapeDtypeStruct((count, lanes(width)), BF16),
            jax.ShapeDtypeStruct((8, width), F32),
        ],
        compiler_params=vmem(40),
        name="norm_back",
    )(rows, kept, got, base, gain)


def feed_forward_body(
    skipped,
    rows_ref,
    cot_ref,
    w_in_mine,
    w_in_theirs,
    w_back_mine,
    w_back_theirs,
    bias_ref,
    *refs,
):
    (
        act_mine, act_theirs, inner_mine, inner_theirs, rows_out, cot_out, out_ref, up_ref, sums_ref
    ) = refs[skipped:]
    model_width = rows_out.shape[1]
    rows, cot = rows_ref[:, :model_width], cot_ref[:, :model_width]
    rows_out[...] = rows
    cot_out[...] = cot

    @pl.when(pl.program_id(0) == 0)
    def clear():
        sums_ref[...] = jnp.zeros_like(sums_ref)

    out, up = None, None
    shares = (
        (w_in_mine, w_back_mine, act_mine, inner_mine),
        (w_in_theirs, w_back_theirs, act_theirs, inner_theirs),
    )
    for part, (w_in, w_back, act_ref, inner_ref) in enumerate(shares):
        hidden = dot_rows(rows, w_in[...]) + bias_ref[part : part + 1]
        value, slope = gelu_parts(hidden)
        act = value.astype(BF16)
        act_ref[...] = act
        inner = (dot_transposed(cot, w_back[...]) * slope).astype(BF16)
        inner_ref[...] = inner
        sums_ref[part : part + 1] += jnp.sum(inner.astype(F32), axis=0, keepdims=True)
        one_out = dot_rows(act, w_back[...])
        one_up = dot_transposed(inner, w_in[...])
        out = one_out if out is None else out + one_out
        up = one_up if up is None else up + one_up
    put(out_ref, out)
    put(up_ref, up)


def feed_forward(rows, cot, half, weights, biases, filled):
    count, sent_width = rows.shape
    model_width, ff_share = weights[0].shape
    block = min(FF_ROWS, count)
    steps = count // block
    row_spec = pl.BlockSpec((block, sent_width), lambda i: (i, 0))
    joined = lambda width: pl.BlockSpec((block, width), lambda i: (half * steps + i, 0))
    act_shape = jax.ShapeDtypeStruct((2 * count, ff_share), BF16)
    row_shape = jax.ShapeDtypeStruct((2 * count, model_width), BF16)
    part_shape = jax.ShapeDtypeStruct((count, sent_width), F32)
    filled = () if filled is None else tuple(filled)
    return pl.pallas_call(
        functools.partial(feed_forward_body, len(filled)),
        out_shape=[act_shape] * 4
        + [row_shape] * 2
        + [part_shape] * 2
        + [jax.ShapeDtypeStruct((8, ff_share), F32)],
        grid=(steps,),
        in_specs=[row_spec, row_spec]
        + [fixed(matrix.shape) for matrix in weights]
        + [fixed((2, ff_share))]
        + [hbm()] * len(filled),
        out_specs=[joined(ff_share)] * 4
        + [joined(model_width)] * 2
        + [row_spec] * 2
        + [pl.BlockSpec((8, ff_share), lambda i: (0, 0))],
        input_output_aliases={7 + i: i for i in range(len(filled))},
        compiler_params=vmem(58),
        cost_estimate=pl.CostEstimate(
            flops=16 * count * model_width * ff_share,
            bytes_accessed=8 * model_width * ff_share + 16 * count * model_width,
            transcendentals=2 * count * ff_share,
        ),
        name="feed_forward",
    )(rows, cot, *weights, biases, *filled)


def permute(value, axis_name, pairs):
    return lax.ppermute(value, axis_name, pairs)


def swap(value, axis_name, distance):
    count = lax.axis_size(axis_name)
    return permute(value, axis_name, [(i, i ^ distance) for i in range(count)])


def tie(*values):
    return lax.optimization_barrier(values)


def lower_pairs(pairs, y_count):
    return [
        (source * y_count + y, target * y_count + y)
        for source, target in pairs
        for y in range(y_count)
    ]


def spread_lead(block, z_here):
    far = permute(block, "dp", lower_pairs([(0, 2)], 2))
    held = jnp.where(z_here == 0, block, far)
    near = permute(held, "dp", lower_pairs([(0, 1), (2, 3)], 2))
    return jnp.where(z_here % 2 == 0, held, near)


def move_rest(block, distance, plane_distance):
    over_dp, over_seq = distance
    pairs = []
    for d in range(8):
        if (d // 2) ^ plane_distance != 0:
            pairs += [(d * 4 + q, (d ^ over_dp) * 4 + (q ^ over_seq)) for q in range(4)]
    return permute(block, ("dp", "seq"), pairs)


def pick(stacked, index, axis=0):
    return lax.dynamic_index_in_dim(stacked, index, axis, keepdims=False)


def halve_plane(lower, upper, y_here):
    return (
        jnp.where(y_here == 0, lower, upper),
        jnp.where(y_here == 0, upper, lower).astype(BF16),
    )


def sum_everywhere(value):
    for axis_name in ("seq", "dp"):
        distance = 1
        while distance < lax.axis_size(axis_name):
            value = value + swap(value, axis_name, distance)
            distance *= 2
    return value


def per_device(
    rows_in,
    out_cotangent,
    cell_lengths,
    cell_starts,
    key_mask,
    weights_master,
    first_moment,
    second_moment,
    small_master,
    small_first,
    small_second,
    step_count,
):
    model_width = rows_in.shape[3]
    local_rows = rows_in.shape[2]
    length = key_mask.shape[2]
    shard_len = weights_master.shape[2]
    groups = lax.axis_size("seq")
    dp_count = lax.axis_size("dp")
    head_share = model_width // groups
    heads_here = HEADS // groups
    triple = 3 * head_share
    first_end = model_width * triple
    second_end = first_end + head_share * model_width
    third_end = second_end + model_width * model_width
    seq_here = lax.axis_index("seq")
    dp_here = lax.axis_index("dp")
    chip = seq_here // 2
    core = seq_here % 2
    z_here = dp_here // 2
    y_here = dp_here % 2
    planar = dp_count == 8 and shard_len * 2 == first_end
    shares = (core + 2 * chip, core + 2 * (1 - chip))

    def exchange_micro(array):
        own = pick(array[:, 0], chip)
        received = swap(widen(pick(array[:, 0], 1 - chip)), "seq", 2)[:, :model_width]
        first = jnp.where(chip == 0, own, received)
        second = jnp.where(chip == 0, received, own)
        return jnp.concatenate([first, second], axis=0)

    def widen(rows):
        return jnp.pad(rows, ((0, 0), (0, lanes(model_width) - model_width)))

    own_in = exchange_micro(rows_in)

    ends = jnp.array([first_end, second_end, third_end, dp_count * shard_len], jnp.int32)
    begin = dp_here * shard_len
    lower_matrix = jnp.sum((begin >= ends).astype(jnp.int32))
    upper_matrix = jnp.sum((begin + shard_len - 1 >= ends).astype(jnp.int32))
    bound = jnp.minimum(pick(ends, lower_matrix) - begin, shard_len).reshape(1)
    matrices = jnp.arange(4, dtype=jnp.int32)

    def matrix_sums(pair):
        return jnp.where(matrices == lower_matrix, pair[0], 0.0) + jnp.where(
            matrices == upper_matrix, pair[1], 0.0
        )

    weight = weights_master
    low_weight, weight_sums = round_weights(bound, weight)
    y_index = y_here.reshape(1).astype(jnp.int32)
    if planar:
        tall = low_weight.reshape(shard_len // triple, triple)
        wide = low_weight.reshape(shard_len // model_width, model_width)
        cut, tall_rows = wide.shape[0], tall.shape[0]
        lead = spread_lead(tall, z_here)
        across = [move_rest(wide, (1, 0), 0)]
        over = [move_rest(wide, (0, 2), 0)]
        both = [move_rest(over[0], (1, 0), 0)]
        lead, wide = tie(lead, wide)
        lead_across = swap(lead, "dp", 1)
        halves = (lead, lead_across, swap(lead, "seq", 2), swap(lead_across, "seq", 2))
        dp_index = dp_here.reshape(1).astype(jnp.int32)
        far = move_rest(wide, (4, 0), 0)
        near = move_rest(wide, (2, 0), 0)
    else:
        copies = lax.all_gather(low_weight.reshape(1, shard_len), ("dp", "seq"), axis=0, tiled=True)
        copies = copies.reshape(dp_count, groups, shard_len)
        per_share = [pick(copies, share, 1).reshape(dp_count * shard_len) for share in shares]
        halves = []
        for flat in per_share:
            matrix = flat[:first_end].reshape(model_width, triple)
            first = jnp.where(y_here == 0, matrix[: model_width // 2], matrix[model_width // 2 :])
            second = jnp.where(y_here == 0, matrix[model_width // 2 :], matrix[: model_width // 2])
            halves += [first, second]
        w_out = [flat[first_end:second_end].reshape(head_share, model_width) for flat in per_share]
        w_in = [flat[second_end:third_end].reshape(model_width, model_width) for flat in per_share]
        w_back = [flat[third_end:].reshape(model_width, model_width) for flat in per_share]

    def share_columns(vector, share):
        return lax.dynamic_slice_in_dim(vector, share * head_share, head_share)

    attn_biases = [
        jnp.concatenate(
            [
                share_columns(small_master[4], share),
                jnp.zeros((head_share,), F32),
                share_columns(small_master[5], share),
            ]
        )
        for share in shares
    ]
    ff_biases = jnp.stack([pick(small_master, 8 + share) for share in shares])

    starts = pick(cell_starts[:, 0], chip)
    lengths = pick(cell_lengths[:, 0], chip)
    places = jnp.arange(length, dtype=jnp.int32)
    inside = (places[:, None] >= starts[None, :]) & (places[:, None] < (starts + lengths)[None, :])
    first_key = jnp.max(jnp.where(inside, starts[None, :], -1), axis=1)
    first_key = jnp.where(first_key < 0, places, first_key)
    low_blocks = first_key.reshape(-1, local_rows)[:, 0] // local_rows
    block_starts = first_key.reshape(-1, 1, local_rows)
    core_index = core.reshape(1).astype(jnp.int32)

    inputs = own_in.astype(F32)
    hat_one, _ = norm_stats(inputs)
    low_one = widen((hat_one * small_master[0] + small_master[1]).astype(BF16))
    other_one = swap(low_one, "seq", 1)

    if planar:
        low_one, near, far = tie(low_one, near, far)
        last = move_rest(far, (2, 0), 2)
        across += [move_rest(near, (1, 0), 1), move_rest(far, (1, 0), 2)]
        over += [move_rest(near, (0, 2), 1), move_rest(far, (0, 2), 2)]
    *qkv, rows_one, w_attn_mine, w_attn_theirs = project(
        y_index, low_one, other_one, halves, jnp.stack(attn_biases)
    )

    def attend(part):
        return attention_forward(low_blocks, core_index, block_starts, qkv[part], heads_here)

    if planar:
        last, qkv[0] = tie(last, qkv[0])
        across.append(move_rest(last, (1, 0), 3))
        over.append(move_rest(last, (0, 2), 3))
    attended = [attend(0)]
    own_e_in = out_cotangent
    if planar:
        qkv[1], over[1:3], own_e_in, _ = tie(qkv[1], over[1:3], own_e_in, attended[0][2])
        both += [move_rest(over[1], (1, 0), 1), move_rest(over[2], (1, 0), 2)]
    own_e = widen(exchange_micro(own_e_in))
    other_e = swap(own_e, "seq", 1)
    attended.append(attend(1))
    if planar:
        dp_index, across[3], _ = tie(dp_index, across[3], attended[1][2])
        both.append(move_rest(across[3], (0, 2), 3))
        rest_mine = [block for pair in zip((wide, near, far, last), across) for block in pair]
        rest_theirs = [block for pair in zip(over, both) for block in pair]
        matrices_mine = unpack_share(dp_index, rest_mine, head_share, model_width)
        matrices_theirs = unpack_share(dp_index, rest_theirs, head_share, model_width)
        w_out, w_in, w_back = (list(pair) for pair in zip(matrices_mine, matrices_theirs))
    sent, kept = split_product([attended[0][0], attended[1][0]], w_out, False, model_width)
    middle, low_two = middle_norm(own_in, kept, swap(sent, "seq", 1), small_master)
    other_two = swap(low_two, "seq", 1)

    weights = (w_in[0], w_in[1], w_back[0], w_back[1])
    *filled, out_sent, up_sent, sums_sent = feed_forward(
        other_two, other_e, 1, weights, ff_biases, None
    )
    out_received = swap(out_sent, "seq", 1)
    up_received = swap(up_sent, "seq", 1)
    *filled, out_kept, up_kept, sums_kept = feed_forward(
        low_two, own_e, 0, weights, ff_biases, filled
    )
    activated, inner, (rows_two, rows_e) = filled[:2], filled[2:4], filled[4:]
    inner_sums = sums_sent + sums_kept

    link = BF16 if planar else F32
    back_sent = dot_columns(activated[1], rows_e).astype(link)
    in_sent = dot_columns(rows_two, inner[1]).astype(link)
    back_sent, in_sent, up_kept = tie(*(back_sent, in_sent, up_kept))
    back_received = swap(back_sent, "seq", 2)
    in_received = swap(in_sent, "seq", 2)

    grad_mid, low_mid, sums_two = norm_back(
        middle, up_kept, up_received, own_e, small_master[2:3], True
    )
    grad_att_mine, grad_att_theirs, rows_mid = out_grads(low_mid, swap(low_mid, "seq", 1), w_out)
    out_sent_theirs = dot_columns(attended[1][0], rows_mid).astype(link)
    out_sent_theirs, grad_att_theirs = tie(*(out_sent_theirs, grad_att_theirs))
    outer_received = swap(out_sent_theirs, "seq", 2)

    def attend_back(part, grad_att):
        return attention_backward(
            low_blocks,
            core_index,
            block_starts,
            qkv[part],
            grad_att,
            attended[part][1],
            attended[part][2],
            heads_here,
        )

    packed_theirs = attend_back(1, grad_att_theirs)
    attn_sent = dot_columns(rows_one, packed_theirs).astype(link)
    attn_sent, packed_theirs, rows_two, rows_e, rows_mid = tie(
        attn_sent, packed_theirs, rows_two, rows_e, rows_mid
    )
    attn_received = swap(attn_sent, "seq", 2)
    share_back = dot_columns(activated[0], rows_e)
    share_in = dot_columns(rows_two, inner[0])
    share_out = dot_columns(attended[0][0], rows_mid)
    if planar:
        kept_rest, sent_rest = pack_rest(
            y_index,
            (share_out, share_in, share_back),
            (outer_received, in_received, back_received),
            cut,
        )
        sent_rest, grad_att_mine = tie(sent_rest, grad_att_mine)
        got_rest = swap(sent_rest, "dp", 1)
    else:
        share_back, share_in, share_out = (
            share_back + back_received,
            share_in + in_received,
            share_out + outer_received,
        )

    packed_mine = attend_back(0, grad_att_mine)
    share_attn = dot_columns(rows_one, packed_mine) + attn_received.astype(F32)
    if planar:
        z_odd = z_here % 2 == 1
        kept_lead, sent_lead = halve_plane(share_attn[:tall_rows], share_attn[tall_rows:], y_here)
        kept_lead, sent_lead, kept_rest, packed_mine = tie(
            kept_lead, sent_lead, kept_rest, packed_mine
        )
        got_lead = swap(sent_lead, "dp", 1)
        held = [kept_rest[i] + got_rest[i].astype(F32) for i in range(3)]
        sent_near = jnp.where(z_odd, held[1], held[0]).astype(BF16)
        sent_last = held[2].astype(BF16)
        kept_near = jnp.where(z_odd, held[0], held[1])
        kept_last = held[2]
        sent_near, sent_last, packed_mine, out_received = tie(
            sent_near, sent_last, packed_mine, out_received
        )
        got_near = swap(sent_near, "dp", 2)
        got_last = permute(sent_last, "dp", lower_pairs([(0, 1), (2, 3)], 2))
    result_rows = widen(
        (middle + ((out_kept + out_received)[:, :model_width] + small_master[7])).astype(BF16)
    )
    packed = [packed_mine, packed_theirs]
    sent, kept = split_product(packed, [w_attn_mine, w_attn_theirs], True, model_width)
    if planar:
        kept_lead, sent = tie(kept_lead, sent)
        held_lead = kept_lead + got_lead.astype(F32)
        sent_lead = held_lead.astype(BF16)
        sent_lead, held_lead, kept_near, kept_last, kept = tie(
            sent_lead, held_lead, kept_near, kept_last, kept
        )
        near_lead = permute(sent_lead, "dp", lower_pairs([(1, 0), (3, 2)], 2))
        held_near = kept_near + got_near.astype(F32)
        held_last = kept_last + got_last.astype(F32)
        sent_far = jnp.where(z_here == 1, held_last, held_near).astype(BF16)
        own_rest = jnp.where(z_here == 3, held_last, held_near)
        sent_far, own_rest, kept = tie(sent_far, own_rest, kept)
        got_far = permute(sent_far, "dp", lower_pairs([(3, 1), (0, 2), (1, 3)], 2))
    grad_x, sums_one = norm_back(
        own_in, kept, swap(sent, "seq", 1), grad_mid, small_master[0:1], False
    )
    if planar:
        held_lead, grad_x, sums_one = tie(held_lead, grad_x, sums_one)
        held_lead = held_lead + near_lead.astype(F32)
        sent_lead = held_lead.astype(BF16)
        sent_lead, held_lead, own_rest = tie(sent_lead, held_lead, own_rest)
        far_lead = permute(sent_lead, "dp", lower_pairs([(2, 0)], 2))
        rest_grad = (own_rest + got_far.astype(F32)).reshape(1, 1, shard_len)

    def return_micro(rows):
        lower, upper = rows[:local_rows], rows[local_rows:]
        own = jnp.where(chip == 0, lower, upper)[:, :model_width]
        received = swap(jnp.where(chip == 0, upper, lower), "seq", 2)[:, :model_width]
        first = jnp.where(chip == 0, own, received)
        second = jnp.where(chip == 0, received, own)
        return jnp.stack([first, second])[:, None]

    result_all = return_micro(result_rows)
    grad_all = return_micro(grad_x)

    def at_shares(columns):
        row = jnp.zeros((model_width,), F32)
        for share, column in zip(shares, columns):
            row = lax.dynamic_update_slice(row, column, (share * head_share,))
        return row

    bias_sums = [jnp.sum(packed[part].astype(F32), axis=0) for part in range(2)]
    inner_rows = jnp.zeros((4, model_width), F32)
    for part in range(2):
        inner_rows = lax.dynamic_update_slice(
            inner_rows, inner_sums[part : part + 1], (shares[part], 0)
        )
    small_now = jnp.concatenate(
        [
            sums_one[:2],
            sums_two[:2],
            at_shares([sums[:head_share] for sums in bias_sums])[None],
            at_shares([sums[2 * head_share : triple] for sums in bias_sums])[None],
            sums_two[2:4],
            inner_rows,
            jnp.pad(matrix_sums(weight_sums), (0, model_width - 4))[None],
        ]
    )

    small_sum = sum_everywhere(small_now)
    if planar:
        held_lead, rest_grad, small_sum = tie(held_lead, rest_grad, small_sum)
        lead_grad = (held_lead + far_lead.astype(F32))[:, :triple].reshape(1, 1, shard_len)
        leads = z_here == 0
    else:
        flat_here = jnp.concatenate(
            [matrix.reshape(-1) for matrix in (share_attn[:, :triple], share_out, share_in, share_back)]
        )
        lead_grad = lax.psum_scatter(
            flat_here.reshape(dp_count, shard_len), "dp", scatter_dimension=0, tiled=True
        ).reshape(1, 1, shard_len)
        rest_grad = lead_grad
        leads = z_here >= 0

    steps_done = step_count[0].astype(F32)
    fix_one = 1.0 - jnp.exp(steps_done * math.log(BETA_ONE))
    fix_two = 1.0 - jnp.exp(steps_done * math.log(BETA_TWO))
    ints = jnp.concatenate([bound, leads.astype(jnp.int32).reshape(1)])
    reduced, moments, update, update_sums = new_moments(
        ints,
        jnp.stack([fix_one, fix_two]),
        lead_grad,
        rest_grad,
        first_moment,
        second_moment,
        weight,
    )
    small_grad = small_sum[:12]
    weight_norms = jnp.sqrt(small_sum[12, :4])
    update_norms = jnp.sqrt(sum_everywhere(matrix_sums(update_sums)[None])[0])
    ratios = weight_norms / update_norms
    new_weight, weight_copy = new_weights(
        ints, jnp.stack([pick(ratios, lower_matrix), pick(ratios, upper_matrix)]), weight, update
    )
    small_one = BETA_ONE * small_first + (1.0 - BETA_ONE) * small_grad
    small_two = BETA_TWO * small_second + (1.0 - BETA_TWO) * small_grad * small_grad
    small_updated = small_master - SMALL_RATE * (small_one / fix_one) / (
        jnp.sqrt(small_two / fix_two) + ADAM_EPS
    )
    return (
        result_all,
        grad_all,
        reduced,
        moments,
        new_weight,
        weight_copy,
        jnp.stack([weight_norms, update_norms, ratios]),
        small_grad,
        jnp.stack([small_one, small_two]),
        small_updated,
    )


def solution(mesh):
    in_specs = (
        P(None, "dp", "seq", None),
        P(None, "dp", "seq", None),
        P(None, "dp", None),
        P(None, "dp", None),
        P(None, "dp", None),
        P("dp", "seq", None),
        P("dp", "seq", None),
        P("dp", "seq", None),
        P(),
        P(),
        P(),
        P(),
    )
    out_specs = (
        P(None, "dp", "seq", None),
        P(None, "dp", "seq", None),
        P("dp", "seq", None),
        P(None, "dp", "seq", None),
        P("dp", "seq", None),
        P("dp", "seq", None),
        P(),
        P(),
        P(),
        P(),
    )
    return jax.shard_map(
        per_device, mesh=mesh, in_specs=in_specs, out_specs=out_specs, check_vma=False
    )
```

```python
import functools
import math

import jax
import jax.numpy as jnp
from jax import lax
from jax.experimental import pallas as pl
from jax.experimental.pallas import tpu as pltpu
from jax.sharding import PartitionSpec as P

HEADS = 20


NORM_EPS = 1e-05
BETA_ONE = 0.9
BETA_TWO = 0.999
ADAM_EPS = 1e-06
DECAY = 0.01
MATRIX_RATE = 0.3
SMALL_RATE = 0.25
MASKED = -1e30
LOG2_E = 1.4426950408889634
FF_ROWS = 256
SCALE = 1e9

F32 = jnp.float32
BF16 = jnp.bfloat16


def dot_rows(left, right):
    return lax.dot_general(left, right, (((1,), (0,)), ((), ())), preferred_element_type=F32)


def dot_transposed(left, right):
    return lax.dot_general(left, right, (((1,), (1,)), ((), ())), preferred_element_type=F32)


def dot_columns(left, right):
    return lax.dot_general(left, right, (((0,), (0,)), ((), ())), preferred_element_type=F32)


def norm_stats(rows):
    center = jnp.mean(rows, axis=-1, keepdims=True)
    centered = rows - center
    spread = jnp.mean(centered * centered, axis=-1, keepdims=True)
    scale = lax.rsqrt(spread + NORM_EPS)
    return centered * scale, scale


def norm_backward(upstream, hat, scale, gain):
    weighted = upstream * gain
    return (
        weighted
        - jnp.mean(weighted, axis=-1, keepdims=True)
        - hat * jnp.mean(weighted * hat, axis=-1, keepdims=True)
    ) * scale


def gelu_parts(values):
    inner = math.sqrt(2.0 / math.pi)
    squares = values * values
    bent = jnp.tanh(inner * (values + 0.044715 * values * squares))
    half = 0.5 * (1.0 + bent)
    slope = half + 0.5 * values * (1.0 - bent * bent) * inner * (1.0 + 3.0 * 0.044715 * squares)
    return values * half, slope


def block_place(core, block):
    return jnp.where(block % 2 == core, 0, 2) + block // 2


def block_rows(core, block, rows):
    return pl.ds(pl.multiple_of(block_place(core, block) * rows, rows), rows)


def attention_forward_body(
    heads, width, bq, low_ref, core_ref, start_ref, qkv_ref, out_ref, outt_ref, lse_ref, qs, ks, vt, acc
):
    length = qkv_ref.shape[0]
    flat = heads * width
    factor = width**-0.5 * LOG2_E
    core = core_ref[0]

    def unpack(block, carry):
        here = block_rows(core, block, bq)
        there = pl.ds(pl.multiple_of(block * bq, bq), bq)
        for h in range(heads):
            qs[h, there] = qkv_ref[here, h * width : (h + 1) * width]
            ks[h, there] = qkv_ref[here, flat + h * width : flat + (h + 1) * width]
        turned = qkv_ref[here, 2 * flat : 3 * flat].astype(F32).T
        for h in range(heads):
            vt[h, block] = turned[h * width : (h + 1) * width].astype(BF16)
        return carry

    lax.fori_loop(0, length // bq, unpack, 0)

    def query_step(qb, carry):
        q0 = pl.multiple_of(qb * bq, bq)
        start = start_ref[qb]
        query_place = q0 + lax.broadcasted_iota(jnp.int32, (1, bq), 1)
        acc[...] = jnp.zeros_like(acc)

        def key_step(kb, tops_totals):
            tops, totals = tops_totals
            k0 = pl.multiple_of(kb * bq, bq)
            key_place = k0 + lax.broadcasted_iota(jnp.int32, (bq, bq), 0)
            allowed = (key_place <= query_place) & (key_place >= start)
            new_tops, new_totals = [], []
            for h in range(heads):
                scores = dot_transposed(ks[h, pl.ds(k0, bq)], qs[h, pl.ds(q0, bq)]) * factor
                scores = jnp.where(allowed, scores, MASKED)
                top = jnp.maximum(tops[h], jnp.max(scores, axis=0, keepdims=True))
                fade = jnp.exp2(tops[h] - top)
                weights = jnp.exp2(scores - top)
                own = slice(h * width, (h + 1) * width)
                acc[own] = acc[own] * fade + dot_rows(vt[h, kb], weights.astype(BF16))
                new_tops.append(top)
                new_totals.append(totals[h] * fade + jnp.sum(weights, axis=0, keepdims=True))
            return tuple(new_tops), tuple(new_totals)

        first = (
            tuple(jnp.full((1, bq), -1e29, F32) for _ in range(heads)),
            tuple(jnp.zeros((1, bq), F32) for _ in range(heads)),
        )
        tops, totals = lax.fori_loop(low_ref[qb], qb + 1, key_step, first)
        for h in range(heads):
            own = slice(h * width, (h + 1) * width)
            acc[own] = acc[own] * (1.0 / totals[h])
            lse_ref[qb, h : h + 1, :] = tops[h] + jnp.log2(totals[h])
        mixed = acc[...]
        outt_ref[qb] = mixed
        out_ref[block_rows(core, qb, bq), :] = mixed.T.astype(BF16)
        return carry

    lax.fori_loop(0, length // bq, query_step, 0)


def attention_backward_body(
    heads,
    width,
    bq,
    low_ref,
    core_ref,
    start_ref,
    qkv_ref,
    dout_ref,
    outt_ref,
    lse_ref,
    grad_ref,
    qs,
    ks,
    vs,
    ds,
    kt,
    dk,
    dv,
    dqt,
):
    length = qkv_ref.shape[0]
    flat = heads * width
    score_scale = width**-0.5
    factor = score_scale * LOG2_E
    core = core_ref[0]

    def unpack(block, carry):
        here = block_rows(core, block, bq)
        there = pl.ds(pl.multiple_of(block * bq, bq), bq)
        for h in range(heads):
            qs[h, there] = qkv_ref[here, h * width : (h + 1) * width]
            ks[h, there] = qkv_ref[here, flat + h * width : flat + (h + 1) * width]
            vs[h, there] = qkv_ref[here, 2 * flat + h * width : 2 * flat + (h + 1) * width]
            ds[h, there] = dout_ref[here, h * width : (h + 1) * width]
        turned = qkv_ref[here, flat : 2 * flat].astype(F32).T
        for h in range(heads):
            kt[h, block] = turned[h * width : (h + 1) * width].astype(BF16)
        return carry

    lax.fori_loop(0, length // bq, unpack, 0)
    dk[...] = jnp.zeros_like(dk)
    dv[...] = jnp.zeros_like(dv)

    def query_step(qb, carry):
        q0 = pl.multiple_of(qb * bq, bq)
        queries = pl.ds(q0, bq)
        here = block_rows(core, qb, bq)
        start = start_ref[qb]
        query_place = q0 + lax.broadcasted_iota(jnp.int32, (1, bq), 1)
        products = dout_ref[here, :].astype(F32).T * outt_ref[qb]
        inners = [
            jnp.sum(products[h * width : (h + 1) * width], axis=0, keepdims=True)
            for h in range(heads)
        ]
        dqt[...] = jnp.zeros_like(dqt)

        def key_step(kb, inner_carry):
            k0 = pl.multiple_of(kb * bq, bq)
            keys = pl.ds(k0, bq)
            key_place = k0 + lax.broadcasted_iota(jnp.int32, (bq, bq), 0)
            allowed = (key_place <= query_place) & (key_place >= start)
            for h in range(heads):
                scores = dot_transposed(ks[h, keys], qs[h, queries]) * factor
                weights = jnp.exp2(
                    jnp.where(allowed, scores - lse_ref[qb, h : h + 1, :], MASKED)
                )
                dweights = dot_transposed(vs[h, keys], ds[h, queries])
                dscores = (weights * (dweights - inners[h])).astype(BF16)
                dv[h, keys] += dot_rows(weights.astype(BF16), ds[h, queries])
                dk[h, keys] += dot_rows(dscores, qs[h, queries])
                dqt[h * width : (h + 1) * width] += dot_rows(kt[h, kb], dscores)
            return inner_carry

        lax.fori_loop(low_ref[qb], qb + 1, key_step, 0)
        grad_ref[here, 0:flat] = (dqt[...] * score_scale).T.astype(BF16)
        return carry

    lax.fori_loop(0, length // bq, query_step, 0)

    def write_keys(kb, carry):
        here = block_rows(core, kb, bq)
        rows = pl.ds(pl.multiple_of(kb * bq, bq), bq)
        grad_ref[here, flat : 2 * flat] = jnp.concatenate(
            [dk[h, rows] * score_scale for h in range(heads)], axis=1
        ).astype(BF16)
        grad_ref[here, 2 * flat : 3 * flat] = jnp.concatenate(
            [dv[h, rows] for h in range(heads)], axis=1
        ).astype(BF16)
        rest = grad_ref.shape[1] - 3 * flat
        if rest:
            grad_ref[here, 3 * flat :] = jnp.zeros((bq, rest), BF16)
        return carry

    lax.fori_loop(0, length // bq, write_keys, 0)


def whole_block(shape):
    return pl.BlockSpec(shape, lambda step, *refs: (0,) * len(shape))


def attention_forward(low_blocks, core, starts, qkv, heads):
    length, triple = qkv.shape
    flat = triple // 3
    width = flat // heads
    blocks, _, bq = starts.shape
    grid_spec = pltpu.PrefetchScalarGridSpec(
        num_scalar_prefetch=2,
        grid=(1,),
        in_specs=[whole_block((blocks, 1, bq)), whole_block((length, triple))],
        out_specs=[
            whole_block((length, flat)),
            whole_block((blocks, flat, bq)),
            whole_block((blocks, 8, bq)),
        ],
        scratch_shapes=[
            pltpu.VMEM((heads, length, width), BF16),
            pltpu.VMEM((heads, length, width), BF16),
            pltpu.VMEM((heads, blocks, width, bq), BF16),
            pltpu.VMEM((flat, bq), F32),
        ],
    )
    return pl.pallas_call(
        functools.partial(attention_forward_body, heads, width, bq),
        out_shape=[
            jax.ShapeDtypeStruct((length, flat), BF16),
            jax.ShapeDtypeStruct((blocks, flat, bq), F32),
            jax.ShapeDtypeStruct((blocks, 8, bq), F32),
        ],
        grid_spec=grid_spec,
        compiler_params=pltpu.CompilerParams(vmem_limit_bytes=48 << 20),
        cost_estimate=lasting(35),
        name="attention_forward",
    )(low_blocks, core, starts, qkv)


def attention_backward(low_blocks, core, starts, qkv, grad_out, out_turned, log_total, heads):
    length, triple = qkv.shape
    flat = triple // 3
    width = flat // heads
    blocks, _, bq = starts.shape
    per_head = pltpu.VMEM((heads, length, width), BF16)
    sums = pltpu.VMEM((heads, length, width), F32)
    grid_spec = pltpu.PrefetchScalarGridSpec(
        num_scalar_prefetch=2,
        grid=(1,),
        in_specs=[
            whole_block((blocks, 1, bq)),
            whole_block((length, triple)),
            whole_block((length, flat)),
            whole_block((blocks, flat, bq)),
            whole_block((blocks, 8, bq)),
        ],
        out_specs=whole_block((length, lanes(triple))),
        scratch_shapes=[
            per_head,
            per_head,
            per_head,
            per_head,
            pltpu.VMEM((heads, blocks, width, bq), BF16),
            sums,
            sums,
            pltpu.VMEM((flat, bq), F32),
        ],
    )
    return pl.pallas_call(
        functools.partial(attention_backward_body, heads, width, bq),
        out_shape=jax.ShapeDtypeStruct((length, lanes(triple)), BF16),
        grid_spec=grid_spec,
        compiler_params=pltpu.CompilerParams(vmem_limit_bytes=60 << 20),
        cost_estimate=lasting(56),
        name="attention_backward",
    )(low_blocks, core, starts, qkv, grad_out, out_turned, log_total)


def lasting(micros):
    return pl.CostEstimate(flops=int(micros * SCALE), bytes_accessed=1 << 12, transcendentals=0)


def lanes(width):
    return -(-width // 128) * 128


def put(ref, value):
    width = value.shape[1]
    ref[:, :width] = value
    if width < ref.shape[1]:
        ref[:, width:] = jnp.zeros((value.shape[0], ref.shape[1] - width), ref.dtype)


def vmem(count):
    return pltpu.CompilerParams(vmem_limit_bytes=count << 20)


def fixed(shape):
    return pl.BlockSpec(shape, lambda *step: (0,) * len(shape), pipeline_mode=pl.Buffered(1))


def hbm():
    return pl.BlockSpec(memory_space=pl.ANY)


def round_weights_body(bound_ref, weight_ref, low_ref, sums_ref):
    values = weight_ref[...]
    low_ref[...] = values[0, 0].astype(BF16)
    place = lax.broadcasted_iota(jnp.int32, values.shape, 2)
    squares = values * values
    lower = jnp.sum(jnp.where(place < bound_ref[0], squares, 0.0))
    sums_ref[0] = lower
    sums_ref[1] = jnp.sum(squares) - lower


def round_weights(bound, weight):
    smem = pl.BlockSpec(memory_space=pltpu.SMEM)
    whole = pl.BlockSpec(memory_space=pltpu.VMEM)
    return pl.pallas_call(
        round_weights_body,
        in_specs=[smem, whole],
        out_specs=[whole, smem],
        out_shape=[
            jax.ShapeDtypeStruct(weight.shape[2:], BF16),
            jax.ShapeDtypeStruct((2,), F32),
        ],
        compiler_params=vmem(32),
        cost_estimate=lasting(6),
        name="round_weights",
    )(bound, weight)


def moments_body(
    ints_ref, floats_ref, lead_ref, rest_ref, first_ref, second_ref, weight_ref,
    grad_ref, moments_ref, update_ref, sums_ref,
):
    step = pl.program_id(0)
    grad = jnp.where(ints_ref[1] == 1, lead_ref[...], rest_ref[...])
    grad_ref[...] = grad
    first = BETA_ONE * first_ref[...] + (1.0 - BETA_ONE) * grad
    second = BETA_TWO * second_ref[...] + (1.0 - BETA_TWO) * grad * grad
    moments_ref[0] = first
    moments_ref[1] = second
    update = (first / floats_ref[0]) / (jnp.sqrt(second / floats_ref[1]) + ADAM_EPS)
    update = update + DECAY * weight_ref[...]
    update_ref[...] = update
    count = grad.shape[2]
    place = step * count + lax.broadcasted_iota(jnp.int32, grad.shape, 2)
    squares = update * update
    lower = jnp.sum(jnp.where(place < ints_ref[0], squares, 0.0))
    upper = jnp.sum(squares) - lower

    @pl.when(step == 0)
    def clear():
        sums_ref[0] = 0.0
        sums_ref[1] = 0.0

    sums_ref[0] += lower
    sums_ref[1] += upper


def flat_steps(count):
    return 7 if count % (7 * 128) == 0 else 1


def new_moments(ints, floats, lead, rest, first, second, weight):
    count = weight.shape[2]
    steps = flat_steps(count)
    smem = pl.BlockSpec(memory_space=pltpu.SMEM)
    flat = pl.BlockSpec((1, 1, count // steps), lambda i: (0, 0, i))
    pair = pl.BlockSpec((2, 1, 1, count // steps), lambda i: (0, 0, 0, i))
    return pl.pallas_call(
        moments_body,
        grid=(steps,),
        in_specs=[smem, smem] + [flat] * 5,
        out_specs=[flat, pair, flat, smem],
        out_shape=[
            jax.ShapeDtypeStruct(weight.shape, F32),
            jax.ShapeDtypeStruct((2,) + weight.shape, F32),
            jax.ShapeDtypeStruct(weight.shape, F32),
            jax.ShapeDtypeStruct((2,), F32),
        ],
        compiler_params=vmem(48),
        cost_estimate=lasting(10),
        name="new_moments",
    )(ints, floats, lead, rest, first, second, weight)


def new_weights_body(ints_ref, ratio_ref, weight_ref, update_ref, new_ref, copy_ref):
    count = weight_ref.shape[2]
    place = pl.program_id(0) * count + lax.broadcasted_iota(jnp.int32, weight_ref.shape, 2)
    rate = jnp.where(place < ints_ref[0], ratio_ref[0], ratio_ref[1])
    new = weight_ref[...] - MATRIX_RATE * rate * update_ref[...]
    new_ref[...] = new
    copy_ref[...] = new.astype(BF16)


def new_weights(ints, ratios, weight, update):
    count = weight.shape[2]
    steps = flat_steps(count)
    smem = pl.BlockSpec(memory_space=pltpu.SMEM)
    flat = pl.BlockSpec((1, 1, count // steps), lambda i: (0, 0, i))
    return pl.pallas_call(
        new_weights_body,
        grid=(steps,),
        in_specs=[smem, smem, flat, flat],
        out_specs=[flat, flat],
        out_shape=[
            jax.ShapeDtypeStruct(weight.shape, F32),
            jax.ShapeDtypeStruct(weight.shape, BF16),
        ],
        compiler_params=vmem(32),
        cost_estimate=lasting(6),
        name="new_weights",
    )(ints, ratios, weight, update)


def unpack_body(cut, out_rows, in_rows, place_ref, *refs):
    blocks, (w_out, w_in, w_back, held, sems) = refs[:8], refs[8:]
    here = place_ref[0]
    copies = [
        pltpu.make_async_copy(block, held.at[index ^ here], sems.at[index])
        for index, block in enumerate(blocks)
    ]
    for copy in copies:
        copy.start()
    for copy in copies:
        copy.wait()
    begin = 2 * cut
    for target, rows in ((w_out, out_rows), (w_in, in_rows), (w_back, in_rows)):
        done = 0
        while done < rows:
            block, offset = divmod(begin + done, cut)
            count = min(cut - offset, rows - done)
            target[done : done + count] = held[block, offset : offset + count]
            done += count
        begin += rows


def unpack_share(place, blocks, out_rows, in_rows):
    cut, columns = blocks[0].shape
    shapes = [(out_rows, columns), (in_rows, columns), (in_rows, columns)]
    return pl.pallas_call(
        functools.partial(unpack_body, cut, out_rows, in_rows),
        grid_spec=pltpu.PrefetchScalarGridSpec(
            num_scalar_prefetch=1,
            grid=(1,),
            in_specs=[hbm()] * 8,
            out_specs=[whole_block(shape) for shape in shapes],
            scratch_shapes=[
                pltpu.VMEM((8, cut, columns), BF16),
                pltpu.SemaphoreType.DMA((8,)),
            ],
        ),
        out_shape=[jax.ShapeDtypeStruct(shape, BF16) for shape in shapes],
        compiler_params=vmem(48),
        cost_estimate=lasting(6),
        name="unpack_share",
    )(place, *blocks)


def pack_rest_body(
    cut, place_ref, out_ref, in_ref, back_ref, out_got, in_got, back_got, kept_ref, sent_ref
):
    here = place_ref[0]
    place = 0
    for matrix, got in ((out_ref, out_got), (in_ref, in_got), (back_ref, back_got)):
        done, rows = 0, matrix.shape[0]
        while done < rows:
            block, offset = divmod(place, cut)
            count = min(cut - offset, rows - done)
            source = slice(done, done + count)
            target = slice(offset, offset + count)
            plane, side = divmod(block, 2)

            @pl.when(here == side)
            def keep(matrix=matrix, got=got, source=source, target=target, plane=plane):
                kept_ref[plane, target] = matrix[source] + got[source].astype(F32)

            @pl.when(here != side)
            def send(matrix=matrix, got=got, source=source, target=target, plane=plane):
                sent_ref[plane, target] = (matrix[source] + got[source].astype(F32)).astype(BF16)

            done += count
            place += count


def pack_rest(place, matrices, received, cut):
    columns = matrices[0].shape[1]
    whole = pl.BlockSpec(memory_space=pltpu.VMEM)
    return pl.pallas_call(
        functools.partial(pack_rest_body, cut),
        in_specs=[pl.BlockSpec(memory_space=pltpu.SMEM)] + [whole] * 6,
        out_specs=[whole] * 2,
        out_shape=[
            jax.ShapeDtypeStruct((3, cut, columns), F32),
            jax.ShapeDtypeStruct((3, cut, columns), BF16),
        ],
        compiler_params=vmem(40),
        cost_estimate=lasting(10),
        name="pack_rest",
    )(place, *matrices, *received)


def rows_of(step, steps, own_ref, other_ref, width):
    return jnp.where(step < steps, own_ref[:, :width], other_ref[:, :width])


def both_specs(block, width, steps):
    own = pl.BlockSpec((block, width), lambda i, *refs: (jnp.minimum(i, steps - 1), 0))
    other = pl.BlockSpec((block, width), lambda i, *refs: (jnp.maximum(i - steps, 0), 0))
    return own, other


def project_body(
    steps, place_ref, own_ref, other_ref, a0, a1, b0, b1, bias_ref,
    out_a, out_b, rows_ref, w_a, w_b, sems,
):
    step = pl.program_id(0)

    @pl.when(step == 0)
    def load():
        cut = a0.shape[0]
        here = place_ref[0]
        first = pl.ds(pl.multiple_of(here * cut, cut), cut)
        second = pl.ds(pl.multiple_of((1 - here) * cut, cut), cut)
        copies = [
            pltpu.make_async_copy(a0, w_a.at[first], sems.at[0]),
            pltpu.make_async_copy(a1, w_a.at[second], sems.at[1]),
            pltpu.make_async_copy(b0, w_b.at[first], sems.at[2]),
            pltpu.make_async_copy(b1, w_b.at[second], sems.at[3]),
        ]
        for copy in copies:
            copy.start()
        for copy in copies:
            copy.wait()

    rows = rows_of(step, steps, own_ref, other_ref, rows_ref.shape[1])
    rows_ref[...] = rows
    out_a[...] = (dot_rows(rows, w_a[...]) + bias_ref[0:1]).astype(BF16)
    out_b[...] = (dot_rows(rows, w_b[...]) + bias_ref[1:2]).astype(BF16)


def project(place, own, other, halves, biases):
    count, sent_width = own.shape
    cut, triple = halves[0].shape
    model_width = 2 * cut
    block = min(512, count)
    steps = count // block
    row_out = lambda width: pl.BlockSpec((block, width), lambda i, *refs: (i, 0))
    matrix = jax.ShapeDtypeStruct((2 * cut, triple), BF16)
    return pl.pallas_call(
        functools.partial(project_body, steps),
        grid_spec=pltpu.PrefetchScalarGridSpec(
            num_scalar_prefetch=1,
            grid=(2 * steps,),
            in_specs=[*both_specs(block, sent_width, steps)]
            + [hbm()] * 4
            + [fixed((2, triple))],
            out_specs=[row_out(triple), row_out(triple), row_out(model_width)]
            + [pl.BlockSpec(matrix.shape, lambda i, *refs: (0, 0))] * 2,
            scratch_shapes=[pltpu.SemaphoreType.DMA((4,))],
        ),
        out_shape=[jax.ShapeDtypeStruct((2 * count, triple), BF16)] * 2
        + [jax.ShapeDtypeStruct((2 * count, model_width), BF16), matrix, matrix],
        compiler_params=vmem(48),
        cost_estimate=lasting(16),
        name="project",
    )(place, own, other, *halves, biases)


def out_grads_body(steps, own_ref, other_ref, w_a, w_b, out_a, out_b, rows_ref):
    rows = rows_of(pl.program_id(0), steps, own_ref, other_ref, rows_ref.shape[1])
    rows_ref[...] = rows
    out_a[...] = dot_transposed(rows, w_a[...]).astype(BF16)
    out_b[...] = dot_transposed(rows, w_b[...]).astype(BF16)


def out_grads(own, other, w_out):
    count, sent_width = own.shape
    width, model_width = w_out[0].shape
    block = min(512, count)
    steps = count // block
    row_out = lambda columns: pl.BlockSpec((block, columns), lambda i: (i, 0))
    return pl.pallas_call(
        functools.partial(out_grads_body, steps),
        grid=(2 * steps,),
        in_specs=[*both_specs(block, sent_width, steps)] + [fixed(w_out[0].shape)] * 2,
        out_specs=[row_out(width), row_out(width), row_out(model_width)],
        out_shape=[jax.ShapeDtypeStruct((2 * count, width), BF16)] * 2
        + [jax.ShapeDtypeStruct((2 * count, model_width), BF16)],
        compiler_params=vmem(48),
        cost_estimate=lasting(8),
        name="out_grads",
    )(own, other, *w_out)


def split_product_body(steps, turned, left_a, left_b, w_a, w_b, sent_ref, kept_ref):
    multiply = dot_transposed if turned else dot_rows
    inner = w_a.shape[1] if turned else w_a.shape[0]
    product = multiply(left_a[:, :inner], w_a[...]) + multiply(left_b[:, :inner], w_b[...])
    step = pl.program_id(0)

    @pl.when(step < steps)
    def other_rows():
        put(sent_ref, product)

    @pl.when(step >= steps)
    def own_rows():
        kept_ref[...] = product


def split_product(lefts, weights, turned, model_width):
    count, width = lefts[0].shape
    block = min(512, count // 2)
    steps = count // 2 // block
    left = pl.BlockSpec((block, width), lambda i: ((i + steps) % (2 * steps), 0))
    parts = [
        jax.ShapeDtypeStruct((count // 2, lanes(model_width)), F32),
        jax.ShapeDtypeStruct((count // 2, model_width), F32),
    ]
    return pl.pallas_call(
        functools.partial(split_product_body, steps, turned),
        grid=(2 * steps,),
        in_specs=[left, left] + [fixed(weights[0].shape)] * 2,
        out_specs=[
            pl.BlockSpec((block, lanes(model_width)), lambda i: (jnp.minimum(i, steps - 1), 0)),
            pl.BlockSpec((block, model_width), lambda i: (jnp.maximum(i - steps, 0), 0)),
        ],
        out_shape=parts,
        compiler_params=vmem(48),
        cost_estimate=lasting(12),
        name="split_product",
    )(*lefts, *weights)


def middle_body(rows_ref, kept_ref, got_ref, small_ref, middle_ref, low_ref):
    middle = rows_ref[...].astype(F32) + (
        kept_ref[...] + got_ref[:, : kept_ref.shape[1]] + small_ref[6:7]
    )
    middle_ref[...] = middle
    hat, _ = norm_stats(middle)
    put(low_ref, (hat * small_ref[2:3] + small_ref[3:4]).astype(BF16))


def middle_norm(rows, kept, got, small):
    count, width = rows.shape
    block = min(256, count)
    part = pl.BlockSpec((block, width), lambda i: (i, 0))
    sent = pl.BlockSpec((block, lanes(width)), lambda i: (i, 0))
    return pl.pallas_call(
        middle_body,
        grid=(count // block,),
        in_specs=[part, part, sent, fixed(small.shape)],
        out_specs=[part, sent],
        out_shape=[
            jax.ShapeDtypeStruct((count, width), F32),
            jax.ShapeDtypeStruct((count, lanes(width)), BF16),
        ],
        compiler_params=vmem(32),
        cost_estimate=lasting(4),
        name="middle_norm",
    )(rows, kept, got, small)


def norm_back_body(wide_out, rows_ref, kept_ref, got_ref, base_ref, gain_ref, *outs):
    (full_ref, low_ref, sums_ref) = outs if wide_out else (None, *outs)
    rows = rows_ref[...].astype(F32)
    hat, scale = norm_stats(rows)
    width = rows.shape[1]
    upstream = kept_ref[:, :width] + got_ref[:, :width]
    base = base_ref[:, :width].astype(F32)
    grad = base + norm_backward(upstream, hat, scale, gain_ref[...])
    low = grad.astype(BF16)
    if wide_out:
        full_ref[...] = grad
    put(low_ref, low)

    @pl.when(pl.program_id(0) == 0)
    def clear():
        sums_ref[...] = jnp.zeros_like(sums_ref)

    for index, term in enumerate((upstream * hat, upstream, low.astype(F32), base)):
        sums_ref[index : index + 1] += jnp.sum(term, axis=0, keepdims=True)


def norm_back(rows, kept, got, base, gain, wide_out):
    count, width = rows.shape
    block = min(256, count)
    part = pl.BlockSpec((block, width), lambda i: (i, 0))
    sent = pl.BlockSpec((block, lanes(width)), lambda i: (i, 0))
    full = [jax.ShapeDtypeStruct((count, width), F32)] if wide_out else []
    return pl.pallas_call(
        functools.partial(norm_back_body, wide_out),
        grid=(count // block,),
        in_specs=[part, pl.BlockSpec((block, kept.shape[1]), lambda i: (i, 0)), sent]
        + [pl.BlockSpec((block, base.shape[1]), lambda i: (i, 0)), fixed((1, width))],
        out_specs=[part] * len(full) + [sent, pl.BlockSpec((8, width), lambda i: (0, 0))],
        out_shape=full
        + [
            jax.ShapeDtypeStruct((count, lanes(width)), BF16),
            jax.ShapeDtypeStruct((8, width), F32),
        ],
        compiler_params=vmem(40),
        cost_estimate=lasting(7),
        name="norm_back",
    )(rows, kept, got, base, gain)


def feed_forward_body(
    skipped,
    rows_ref,
    cot_ref,
    w_in_mine,
    w_in_theirs,
    w_back_mine,
    w_back_theirs,
    bias_ref,
    *refs,
):
    (
        act_mine, act_theirs, inner_mine, inner_theirs, rows_out, cot_out, out_ref, up_ref, sums_ref
    ) = refs[skipped:]
    model_width = rows_out.shape[1]
    rows, cot = rows_ref[:, :model_width], cot_ref[:, :model_width]
    rows_out[...] = rows
    cot_out[...] = cot

    @pl.when(pl.program_id(0) == 0)
    def clear():
        sums_ref[...] = jnp.zeros_like(sums_ref)

    out, up = None, None
    shares = (
        (w_in_mine, w_back_mine, act_mine, inner_mine),
        (w_in_theirs, w_back_theirs, act_theirs, inner_theirs),
    )
    for part, (w_in, w_back, act_ref, inner_ref) in enumerate(shares):
        hidden = dot_rows(rows, w_in[...]) + bias_ref[part : part + 1]
        value, slope = gelu_parts(hidden)
        act = value.astype(BF16)
        act_ref[...] = act
        inner = (dot_transposed(cot, w_back[...]) * slope).astype(BF16)
        inner_ref[...] = inner
        sums_ref[part : part + 1] += jnp.sum(inner.astype(F32), axis=0, keepdims=True)
        one_out = dot_rows(act, w_back[...])
        one_up = dot_transposed(inner, w_in[...])
        out = one_out if out is None else out + one_out
        up = one_up if up is None else up + one_up
    put(out_ref, out)
    put(up_ref, up)


def feed_forward(rows, cot, half, weights, biases, filled):
    count, sent_width = rows.shape
    model_width, ff_share = weights[0].shape
    block = min(FF_ROWS, count)
    steps = count // block
    row_spec = pl.BlockSpec((block, sent_width), lambda i: (i, 0))
    joined = lambda width: pl.BlockSpec((block, width), lambda i: (half * steps + i, 0))
    act_shape = jax.ShapeDtypeStruct((2 * count, ff_share), BF16)
    row_shape = jax.ShapeDtypeStruct((2 * count, model_width), BF16)
    part_shape = jax.ShapeDtypeStruct((count, sent_width), F32)
    filled = () if filled is None else tuple(filled)
    return pl.pallas_call(
        functools.partial(feed_forward_body, len(filled)),
        out_shape=[act_shape] * 4
        + [row_shape] * 2
        + [part_shape] * 2
        + [jax.ShapeDtypeStruct((8, ff_share), F32)],
        grid=(steps,),
        in_specs=[row_spec, row_spec]
        + [fixed(matrix.shape) for matrix in weights]
        + [fixed((2, ff_share))]
        + [hbm()] * len(filled),
        out_specs=[joined(ff_share)] * 4
        + [joined(model_width)] * 2
        + [row_spec] * 2
        + [pl.BlockSpec((8, ff_share), lambda i: (0, 0))],
        input_output_aliases={7 + i: i for i in range(len(filled))},
        compiler_params=vmem(58),
        cost_estimate=lasting(34),
        name="feed_forward",
    )(rows, cot, *weights, biases, *filled)


def permute(value, axis_name, pairs):
    return lax.ppermute(value, axis_name, pairs)


def swap(value, axis_name, distance):
    count = lax.axis_size(axis_name)
    return permute(value, axis_name, [(i, i ^ distance) for i in range(count)])


def tie(*values):
    return lax.optimization_barrier(values)


def lower_pairs(pairs, y_count):
    return [
        (source * y_count + y, target * y_count + y)
        for source, target in pairs
        for y in range(y_count)
    ]


def spread_lead(block, z_here):
    far = permute(block, "dp", lower_pairs([(0, 2)], 2))
    held = jnp.where(z_here == 0, block, far)
    near = permute(held, "dp", lower_pairs([(0, 1), (2, 3)], 2))
    return jnp.where(z_here % 2 == 0, held, near)


def move_rest(block, distance, plane_distance):
    over_dp, over_seq = distance
    pairs = []
    for d in range(8):
        if (d // 2) ^ plane_distance != 0:
            pairs += [(d * 4 + q, (d ^ over_dp) * 4 + (q ^ over_seq)) for q in range(4)]
    return permute(block, ("dp", "seq"), pairs)


def pick(stacked, index, axis=0):
    return lax.dynamic_index_in_dim(stacked, index, axis, keepdims=False)


def halve_plane(lower, upper, y_here):
    return (
        jnp.where(y_here == 0, lower, upper),
        jnp.where(y_here == 0, upper, lower).astype(BF16),
    )


def sum_everywhere(value):
    for axis_name in ("seq", "dp"):
        distance = 1
        while distance < lax.axis_size(axis_name):
            value = value + swap(value, axis_name, distance)
            distance *= 2
    return value


def per_device(
    rows_in,
    out_cotangent,
    cell_lengths,
    cell_starts,
    key_mask,
    weights_master,
    first_moment,
    second_moment,
    small_master,
    small_first,
    small_second,
    step_count,
):
    model_width = rows_in.shape[3]
    local_rows = rows_in.shape[2]
    length = key_mask.shape[2]
    shard_len = weights_master.shape[2]
    groups = lax.axis_size("seq")
    dp_count = lax.axis_size("dp")
    head_share = model_width // groups
    heads_here = HEADS // groups
    triple = 3 * head_share
    first_end = model_width * triple
    second_end = first_end + head_share * model_width
    third_end = second_end + model_width * model_width
    seq_here = lax.axis_index("seq")
    dp_here = lax.axis_index("dp")
    chip = seq_here // 2
    core = seq_here % 2
    z_here = dp_here // 2
    y_here = dp_here % 2
    planar = dp_count == 8 and shard_len * 2 == first_end
    shares = (core + 2 * chip, core + 2 * (1 - chip))

    def exchange_micro(array):
        own = pick(array[:, 0], chip)
        received = swap(widen(pick(array[:, 0], 1 - chip)), "seq", 2)[:, :model_width]
        first = jnp.where(chip == 0, own, received)
        second = jnp.where(chip == 0, received, own)
        return jnp.concatenate([first, second], axis=0)

    def widen(rows):
        return jnp.pad(rows, ((0, 0), (0, lanes(model_width) - model_width)))

    own_in = exchange_micro(rows_in)
    inputs = own_in.astype(F32)
    hat_one, _ = norm_stats(inputs)
    low_one = widen((hat_one * small_master[0] + small_master[1]).astype(BF16))
    other_one = swap(low_one, "seq", 1)
    later_cotangent = out_cotangent

    ends = jnp.array([first_end, second_end, third_end, dp_count * shard_len], jnp.int32)
    begin = dp_here * shard_len
    lower_matrix = jnp.sum((begin >= ends).astype(jnp.int32))
    upper_matrix = jnp.sum((begin + shard_len - 1 >= ends).astype(jnp.int32))
    bound = jnp.minimum(pick(ends, lower_matrix) - begin, shard_len).reshape(1)
    matrices = jnp.arange(4, dtype=jnp.int32)

    def matrix_sums(pair):
        return jnp.where(matrices == lower_matrix, pair[0], 0.0) + jnp.where(
            matrices == upper_matrix, pair[1], 0.0
        )

    weight = weights_master
    low_weight, weight_sums = round_weights(bound, weight)
    y_index = y_here.reshape(1).astype(jnp.int32)
    if planar:
        tall = low_weight.reshape(shard_len // triple, triple)
        wide = low_weight.reshape(shard_len // model_width, model_width)
        cut, tall_rows = wide.shape[0], tall.shape[0]
        lead = spread_lead(tall, z_here)
        across = [move_rest(wide, (1, 0), 0)]
        over = [move_rest(wide, (0, 2), 0)]
        lead, wide, across[0], over[0], other_one, later_cotangent = tie(
            lead, wide, across[0], over[0], other_one, later_cotangent
        )
        lead_across = swap(lead, "dp", 1)
        halves = (lead, lead_across, swap(lead, "seq", 2), swap(lead_across, "seq", 2))
        dp_index = dp_here.reshape(1).astype(jnp.int32)
        far = move_rest(wide, (4, 0), 0)
        near = move_rest(wide, (2, 0), 0)
    else:
        copies = lax.all_gather(low_weight.reshape(1, shard_len), ("dp", "seq"), axis=0, tiled=True)
        copies = copies.reshape(dp_count, groups, shard_len)
        per_share = [pick(copies, share, 1).reshape(dp_count * shard_len) for share in shares]
        halves = []
        for flat in per_share:
            matrix = flat[:first_end].reshape(model_width, triple)
            first = jnp.where(y_here == 0, matrix[: model_width // 2], matrix[model_width // 2 :])
            second = jnp.where(y_here == 0, matrix[model_width // 2 :], matrix[: model_width // 2])
            halves += [first, second]
        w_out = [flat[first_end:second_end].reshape(head_share, model_width) for flat in per_share]
        w_in = [flat[second_end:third_end].reshape(model_width, model_width) for flat in per_share]
        w_back = [flat[third_end:].reshape(model_width, model_width) for flat in per_share]

    def share_columns(vector, share):
        return lax.dynamic_slice_in_dim(vector, share * head_share, head_share)

    attn_biases = [
        jnp.concatenate(
            [
                share_columns(small_master[4], share),
                jnp.zeros((head_share,), F32),
                share_columns(small_master[5], share),
            ]
        )
        for share in shares
    ]
    ff_biases = jnp.stack([pick(small_master, 8 + share) for share in shares])

    starts = pick(cell_starts[:, 0], chip)
    lengths = pick(cell_lengths[:, 0], chip)
    places = jnp.arange(length, dtype=jnp.int32)
    inside = (places[:, None] >= starts[None, :]) & (places[:, None] < (starts + lengths)[None, :])
    first_key = jnp.max(jnp.where(inside, starts[None, :], -1), axis=1)
    first_key = jnp.where(first_key < 0, places, first_key)
    low_blocks = first_key.reshape(-1, local_rows)[:, 0] // local_rows
    block_starts = first_key.reshape(-1, 1, local_rows)
    core_index = core.reshape(1).astype(jnp.int32)

    own_e = widen(exchange_micro(later_cotangent))
    if planar:
        both = [move_rest(over[0], (1, 0), 0)]
        halves, near, far, both[0], own_e = tie(halves, near, far, both[0], own_e)
        last = move_rest(far, (2, 0), 2)
        across += [move_rest(near, (1, 0), 1), move_rest(far, (1, 0), 2)]
        over += [move_rest(near, (0, 2), 1), move_rest(far, (0, 2), 2)]
    *qkv, rows_one, w_attn_mine, w_attn_theirs = project(
        y_index, low_one, other_one, halves, jnp.stack(attn_biases)
    )

    def attend(part):
        return attention_forward(low_blocks, core_index, block_starts, qkv[part], heads_here)

    attended = [attend(0)]
    if planar:
        qkv[1], last, across[1:3], over[1:3], _ = tie(
            qkv[1], last, across[1:3], over[1:3], attended[0][2]
        )
        across.append(move_rest(last, (1, 0), 3))
        over.append(move_rest(last, (0, 2), 3))
        both += [move_rest(over[1], (1, 0), 1), move_rest(across[2], (0, 2), 2)]
    other_e = swap(own_e, "seq", 1)
    attended.append(attend(1))
    if planar:
        dp_index, across, over, both, _ = tie(dp_index, across, over, both, attended[1][2])
        both.append(move_rest(across[3], (0, 2), 3))
        rest_mine = [block for pair in zip((wide, near, far, last), across) for block in pair]
        rest_theirs = [block for pair in zip(over, both) for block in pair]
        matrices_mine = unpack_share(dp_index, rest_mine, head_share, model_width)
        matrices_theirs = unpack_share(dp_index, rest_theirs, head_share, model_width)
        w_out, w_in, w_back = (list(pair) for pair in zip(matrices_mine, matrices_theirs))
    sent, kept = split_product([attended[0][0], attended[1][0]], w_out, False, model_width)
    middle, low_two = middle_norm(own_in, kept, swap(sent, "seq", 1), small_master)
    other_two = swap(low_two, "seq", 1)

    weights = (w_in[0], w_in[1], w_back[0], w_back[1])
    *filled, out_sent, up_sent, sums_sent = feed_forward(
        other_two, other_e, 1, weights, ff_biases, None
    )
    out_received = swap(out_sent, "seq", 1)
    up_received = swap(up_sent, "seq", 1)
    *filled, out_kept, up_kept, sums_kept = feed_forward(
        low_two, own_e, 0, weights, ff_biases, filled
    )
    activated, inner, (rows_two, rows_e) = filled[:2], filled[2:4], filled[4:]
    inner_sums = sums_sent + sums_kept

    link = BF16 if planar else F32
    up_received, out_received = tie(up_received, out_received)
    grad_mid, low_mid, sums_two = norm_back(
        middle, up_kept, up_received, own_e, small_master[2:3], True
    )
    low_mid, rows_two, rows_e = tie(low_mid, rows_two, rows_e)
    other_mid = swap(low_mid, "seq", 1)
    back_sent = dot_columns(activated[1], rows_e).astype(link)
    in_sent = dot_columns(rows_two, inner[1]).astype(link)
    back_sent, in_sent, low_mid = tie(back_sent, in_sent, low_mid)
    back_received = swap(back_sent, "seq", 2)
    in_received = swap(in_sent, "seq", 2)

    grad_att_mine, grad_att_theirs, rows_mid = out_grads(low_mid, other_mid, w_out)
    out_sent_theirs = dot_columns(attended[1][0], rows_mid).astype(link)
    out_sent_theirs, rows_two, rows_e, rows_mid = tie(out_sent_theirs, rows_two, rows_e, rows_mid)
    outer_received = swap(out_sent_theirs, "seq", 2)
    share_back = dot_columns(activated[0], rows_e)
    share_in = dot_columns(rows_two, inner[0])
    share_out = dot_columns(attended[0][0], rows_mid)
    share_back, share_in, share_out, grad_att_theirs = tie(
        share_back, share_in, share_out, grad_att_theirs
    )

    def attend_back(part, grad_att):
        return attention_backward(
            low_blocks,
            core_index,
            block_starts,
            qkv[part],
            grad_att,
            attended[part][1],
            attended[part][2],
            heads_here,
        )

    packed_theirs = attend_back(1, grad_att_theirs)
    attn_sent = dot_columns(rows_one, packed_theirs).astype(link)
    attn_sent, packed_theirs, y_index = tie(attn_sent, packed_theirs, y_index)
    attn_received = swap(attn_sent, "seq", 2)
    if planar:
        kept_rest, sent_rest = pack_rest(
            y_index,
            (share_out, share_in, share_back),
            (outer_received, in_received, back_received),
            cut,
        )
        result_rows = widen(
            (middle + ((out_kept + out_received)[:, :model_width] + small_master[7])).astype(BF16)
        )
        sent_rest, grad_att_mine, result_rows = tie(sent_rest, grad_att_mine, result_rows)
        got_rest = swap(sent_rest, "dp", 1)
    else:
        result_rows = widen(
            (middle + ((out_kept + out_received)[:, :model_width] + small_master[7])).astype(BF16)
        )
        share_back, share_in, share_out = (
            share_back + back_received,
            share_in + in_received,
            share_out + outer_received,
        )

    packed_mine = attend_back(0, grad_att_mine)
    share_attn = dot_columns(rows_one, packed_mine) + attn_received.astype(F32)
    if planar:
        z_odd = z_here % 2 == 1
        kept_lead, sent_lead = halve_plane(share_attn[:tall_rows], share_attn[tall_rows:], y_here)
        kept_lead, sent_lead, kept_rest, packed_mine = tie(
            kept_lead, sent_lead, kept_rest, packed_mine
        )
        got_lead = swap(sent_lead, "dp", 1)
        held = [kept_rest[i] + got_rest[i].astype(F32) for i in range(3)]
        sent_near = jnp.where(z_odd, held[1], held[0]).astype(BF16)
        sent_last = held[2].astype(BF16)
        kept_near = jnp.where(z_odd, held[0], held[1])
        kept_last = held[2]
        sent_near, sent_last, packed_mine = tie(sent_near, sent_last, packed_mine)
        got_near = swap(sent_near, "dp", 2)
        got_last = permute(sent_last, "dp", lower_pairs([(0, 1), (2, 3)], 2))
    packed = [packed_mine, packed_theirs]
    sent, kept = split_product(packed, [w_attn_mine, w_attn_theirs], True, model_width)
    if planar:
        kept_lead, sent = tie(kept_lead, sent)
        held_lead = kept_lead + got_lead.astype(F32)
        sent_lead = held_lead.astype(BF16)
        sent_lead, held_lead, kept_near, kept_last, kept = tie(
            sent_lead, held_lead, kept_near, kept_last, kept
        )
        near_lead = permute(sent_lead, "dp", lower_pairs([(1, 0), (3, 2)], 2))
        held_near = kept_near + got_near.astype(F32)
        held_last = kept_last + got_last.astype(F32)
        sent_far = jnp.where(z_here == 1, held_last, held_near).astype(BF16)
        own_rest = jnp.where(z_here == 3, held_last, held_near)
        sent_far, own_rest, kept = tie(sent_far, own_rest, kept)
        got_far = permute(sent_far, "dp", lower_pairs([(3, 1), (0, 2), (1, 3)], 2))
    grad_x, sums_one = norm_back(
        own_in, kept, swap(sent, "seq", 1), grad_mid, small_master[0:1], False
    )
    if planar:
        held_lead, _ = tie(held_lead, sums_one)
        held_lead = held_lead + near_lead.astype(F32)
        sent_lead = held_lead.astype(BF16)
        sent_lead, held_lead, own_rest, grad_x, sums_one = tie(
            sent_lead, held_lead, own_rest, grad_x, sums_one
        )
        far_lead = permute(sent_lead, "dp", lower_pairs([(2, 0)], 2))
        rest_grad = (own_rest + got_far.astype(F32)).reshape(1, 1, shard_len)

    def return_micro(rows):
        lower, upper = rows[:local_rows], rows[local_rows:]
        own = jnp.where(chip == 0, lower, upper)[:, :model_width]
        received = swap(jnp.where(chip == 0, upper, lower), "seq", 2)[:, :model_width]
        first = jnp.where(chip == 0, own, received)
        second = jnp.where(chip == 0, received, own)
        return jnp.stack([first, second])[:, None]

    result_all = return_micro(result_rows)
    grad_all = return_micro(grad_x)

    def at_shares(columns):
        row = jnp.zeros((model_width,), F32)
        for share, column in zip(shares, columns):
            row = lax.dynamic_update_slice(row, column, (share * head_share,))
        return row

    bias_sums = [jnp.sum(packed[part].astype(F32), axis=0) for part in range(2)]
    inner_rows = jnp.zeros((4, model_width), F32)
    for part in range(2):
        inner_rows = lax.dynamic_update_slice(
            inner_rows, inner_sums[part : part + 1], (shares[part], 0)
        )
    small_now = jnp.concatenate(
        [
            sums_one[:2],
            sums_two[:2],
            at_shares([sums[:head_share] for sums in bias_sums])[None],
            at_shares([sums[2 * head_share : triple] for sums in bias_sums])[None],
            sums_two[2:4],
            inner_rows,
        ]
    )

    if planar:
        held_lead, rest_grad = tie(held_lead, rest_grad)
        lead_grad = (held_lead + far_lead.astype(F32))[:, :triple].reshape(1, 1, shard_len)
        leads = z_here == 0
    else:
        flat_here = jnp.concatenate(
            [matrix.reshape(-1) for matrix in (share_attn[:, :triple], share_out, share_in, share_back)]
        )
        lead_grad = lax.psum_scatter(
            flat_here.reshape(dp_count, shard_len), "dp", scatter_dimension=0, tiled=True
        ).reshape(1, 1, shard_len)
        rest_grad = lead_grad
        leads = z_here >= 0

    steps_done = step_count[0].astype(F32)
    fix_one = 1.0 - jnp.exp(steps_done * math.log(BETA_ONE))
    fix_two = 1.0 - jnp.exp(steps_done * math.log(BETA_TWO))
    ints = jnp.concatenate([bound, leads.astype(jnp.int32).reshape(1)])
    reduced, moments, update, update_sums = new_moments(
        ints,
        jnp.stack([fix_one, fix_two]),
        lead_grad,
        rest_grad,
        first_moment,
        second_moment,
        weight,
    )
    matrix_rows = jnp.stack([matrix_sums(weight_sums), matrix_sums(update_sums)])
    small_sum = sum_everywhere(
        jnp.concatenate([small_now, jnp.pad(matrix_rows, ((0, 2), (0, model_width - 4)))])
    )
    small_grad = small_sum[:12]
    weight_norms = jnp.sqrt(small_sum[12, :4])
    update_norms = jnp.sqrt(small_sum[13, :4])
    ratios = weight_norms / update_norms
    new_weight, weight_copy = new_weights(
        ints, jnp.stack([pick(ratios, lower_matrix), pick(ratios, upper_matrix)]), weight, update
    )
    small_one = BETA_ONE * small_first + (1.0 - BETA_ONE) * small_grad
    small_two = BETA_TWO * small_second + (1.0 - BETA_TWO) * small_grad * small_grad
    small_updated = small_master - SMALL_RATE * (small_one / fix_one) / (
        jnp.sqrt(small_two / fix_two) + ADAM_EPS
    )
    return (
        result_all,
        grad_all,
        reduced,
        moments,
        new_weight,
        weight_copy,
        jnp.stack([weight_norms, update_norms, ratios]),
        small_grad,
        jnp.stack([small_one, small_two]),
        small_updated,
    )


def solution(mesh):
    in_specs = (
        P(None, "dp", "seq", None),
        P(None, "dp", "seq", None),
        P(None, "dp", None),
        P(None, "dp", None),
        P(None, "dp", None),
        P("dp", "seq", None),
        P("dp", "seq", None),
        P("dp", "seq", None),
        P(),
        P(),
        P(),
        P(),
    )
    out_specs = (
        P(None, "dp", "seq", None),
        P(None, "dp", "seq", None),
        P("dp", "seq", None),
        P(None, "dp", "seq", None),
        P("dp", "seq", None),
        P("dp", "seq", None),
        P(),
        P(),
        P(),
        P(),
    )
    return jax.shard_map(
        per_device, mesh=mesh, in_specs=in_specs, out_specs=out_specs, check_vma=False
    )
```

```python
import functools
import math

import jax
import jax.numpy as jnp
from jax import lax
from jax.experimental import pallas as pl
from jax.experimental.pallas import tpu as pltpu
from jax.sharding import PartitionSpec as P

HEADS = 20


NORM_EPS = 1e-05
BETA_ONE = 0.9
BETA_TWO = 0.999
ADAM_EPS = 1e-06
DECAY = 0.01
MATRIX_RATE = 0.3
SMALL_RATE = 0.25
MASKED = -1e30
LOG2_E = 1.4426950408889634
FF_ROWS = 256
SCALE = 1e9

F32 = jnp.float32
BF16 = jnp.bfloat16


def dot_rows(left, right):
    return lax.dot_general(left, right, (((1,), (0,)), ((), ())), preferred_element_type=F32)


def dot_transposed(left, right):
    return lax.dot_general(left, right, (((1,), (1,)), ((), ())), preferred_element_type=F32)


def dot_columns(left, right):
    return lax.dot_general(left, right, (((0,), (0,)), ((), ())), preferred_element_type=F32)


def norm_stats(rows):
    center = jnp.mean(rows, axis=-1, keepdims=True)
    centered = rows - center
    spread = jnp.mean(centered * centered, axis=-1, keepdims=True)
    scale = lax.rsqrt(spread + NORM_EPS)
    return centered * scale, scale


def norm_backward(upstream, hat, scale, gain):
    weighted = upstream * gain
    return (
        weighted
        - jnp.mean(weighted, axis=-1, keepdims=True)
        - hat * jnp.mean(weighted * hat, axis=-1, keepdims=True)
    ) * scale


def gelu_parts(values):
    inner = math.sqrt(2.0 / math.pi)
    squares = values * values
    bent = jnp.tanh(inner * (values + 0.044715 * values * squares))
    half = 0.5 * (1.0 + bent)
    slope = half + 0.5 * values * (1.0 - bent * bent) * inner * (1.0 + 3.0 * 0.044715 * squares)
    return values * half, slope


def block_place(core, block):
    return jnp.where(block % 2 == core, 0, 2) + block // 2


def block_rows(core, block, rows):
    return pl.ds(pl.multiple_of(block_place(core, block) * rows, rows), rows)


def attention_forward_body(
    heads, width, bq, low_ref, core_ref, start_ref, qkv_ref, out_ref, outt_ref, lse_ref, qs, ks, vt, acc
):
    length = qkv_ref.shape[0]
    flat = heads * width
    factor = width**-0.5 * LOG2_E
    core = core_ref[0]

    def unpack(block, carry):
        here = block_rows(core, block, bq)
        there = pl.ds(pl.multiple_of(block * bq, bq), bq)
        for h in range(heads):
            qs[h, there] = qkv_ref[here, h * width : (h + 1) * width]
            ks[h, there] = qkv_ref[here, flat + h * width : flat + (h + 1) * width]
        turned = qkv_ref[here, 2 * flat : 3 * flat].astype(F32).T
        for h in range(heads):
            vt[h, block] = turned[h * width : (h + 1) * width].astype(BF16)
        return carry

    lax.fori_loop(0, length // bq, unpack, 0)

    def query_step(qb, carry):
        q0 = pl.multiple_of(qb * bq, bq)
        start = start_ref[qb]
        query_place = q0 + lax.broadcasted_iota(jnp.int32, (1, bq), 1)
        acc[...] = jnp.zeros_like(acc)

        def key_step(kb, tops_totals):
            tops, totals = tops_totals
            k0 = pl.multiple_of(kb * bq, bq)
            key_place = k0 + lax.broadcasted_iota(jnp.int32, (bq, bq), 0)
            allowed = (key_place <= query_place) & (key_place >= start)
            new_tops, new_totals = [], []
            for h in range(heads):
                scores = dot_transposed(ks[h, pl.ds(k0, bq)], qs[h, pl.ds(q0, bq)]) * factor
                scores = jnp.where(allowed, scores, MASKED)
                top = jnp.maximum(tops[h], jnp.max(scores, axis=0, keepdims=True))
                fade = jnp.exp2(tops[h] - top)
                weights = jnp.exp2(scores - top)
                own = slice(h * width, (h + 1) * width)
                acc[own] = acc[own] * fade + dot_rows(vt[h, kb], weights.astype(BF16))
                new_tops.append(top)
                new_totals.append(totals[h] * fade + jnp.sum(weights, axis=0, keepdims=True))
            return tuple(new_tops), tuple(new_totals)

        first = (
            tuple(jnp.full((1, bq), -1e29, F32) for _ in range(heads)),
            tuple(jnp.zeros((1, bq), F32) for _ in range(heads)),
        )
        tops, totals = lax.fori_loop(low_ref[qb], qb + 1, key_step, first)
        for h in range(heads):
            own = slice(h * width, (h + 1) * width)
            acc[own] = acc[own] * (1.0 / totals[h])
            lse_ref[qb, h : h + 1, :] = tops[h] + jnp.log2(totals[h])
        mixed = acc[...]
        outt_ref[qb] = mixed
        out_ref[block_rows(core, qb, bq), :] = mixed.T.astype(BF16)
        return carry

    lax.fori_loop(0, length // bq, query_step, 0)


def attention_backward_body(
    heads,
    width,
    bq,
    low_ref,
    core_ref,
    start_ref,
    qkv_ref,
    dout_ref,
    outt_ref,
    lse_ref,
    grad_ref,
    qs,
    ks,
    vs,
    ds,
    kt,
    dk,
    dv,
    dqt,
):
    length = qkv_ref.shape[0]
    flat = heads * width
    score_scale = width**-0.5
    factor = score_scale * LOG2_E
    core = core_ref[0]

    def unpack(block, carry):
        here = block_rows(core, block, bq)
        there = pl.ds(pl.multiple_of(block * bq, bq), bq)
        for h in range(heads):
            qs[h, there] = qkv_ref[here, h * width : (h + 1) * width]
            ks[h, there] = qkv_ref[here, flat + h * width : flat + (h + 1) * width]
            vs[h, there] = qkv_ref[here, 2 * flat + h * width : 2 * flat + (h + 1) * width]
            ds[h, there] = dout_ref[here, h * width : (h + 1) * width]
        turned = qkv_ref[here, flat : 2 * flat].astype(F32).T
        for h in range(heads):
            kt[h, block] = turned[h * width : (h + 1) * width].astype(BF16)
        return carry

    lax.fori_loop(0, length // bq, unpack, 0)
    dk[...] = jnp.zeros_like(dk)
    dv[...] = jnp.zeros_like(dv)

    def query_step(qb, carry):
        q0 = pl.multiple_of(qb * bq, bq)
        queries = pl.ds(q0, bq)
        here = block_rows(core, qb, bq)
        start = start_ref[qb]
        query_place = q0 + lax.broadcasted_iota(jnp.int32, (1, bq), 1)
        products = dout_ref[here, :].astype(F32).T * outt_ref[qb]
        inners = [
            jnp.sum(products[h * width : (h + 1) * width], axis=0, keepdims=True)
            for h in range(heads)
        ]
        dqt[...] = jnp.zeros_like(dqt)

        def key_step(kb, inner_carry):
            k0 = pl.multiple_of(kb * bq, bq)
            keys = pl.ds(k0, bq)
            key_place = k0 + lax.broadcasted_iota(jnp.int32, (bq, bq), 0)
            allowed = (key_place <= query_place) & (key_place >= start)
            for h in range(heads):
                scores = dot_transposed(ks[h, keys], qs[h, queries]) * factor
                weights = jnp.exp2(
                    jnp.where(allowed, scores - lse_ref[qb, h : h + 1, :], MASKED)
                )
                dweights = dot_transposed(vs[h, keys], ds[h, queries])
                dscores = (weights * (dweights - inners[h])).astype(BF16)
                dv[h, keys] += dot_rows(weights.astype(BF16), ds[h, queries])
                dk[h, keys] += dot_rows(dscores, qs[h, queries])
                dqt[h * width : (h + 1) * width] += dot_rows(kt[h, kb], dscores)
            return inner_carry

        lax.fori_loop(low_ref[qb], qb + 1, key_step, 0)
        grad_ref[here, 0:flat] = (dqt[...] * score_scale).T.astype(BF16)
        return carry

    lax.fori_loop(0, length // bq, query_step, 0)

    def write_keys(kb, carry):
        here = block_rows(core, kb, bq)
        rows = pl.ds(pl.multiple_of(kb * bq, bq), bq)
        grad_ref[here, flat : 2 * flat] = jnp.concatenate(
            [dk[h, rows] * score_scale for h in range(heads)], axis=1
        ).astype(BF16)
        grad_ref[here, 2 * flat : 3 * flat] = jnp.concatenate(
            [dv[h, rows] for h in range(heads)], axis=1
        ).astype(BF16)
        rest = grad_ref.shape[1] - 3 * flat
        if rest:
            grad_ref[here, 3 * flat :] = jnp.zeros((bq, rest), BF16)
        return carry

    lax.fori_loop(0, length // bq, write_keys, 0)


def whole_block(shape):
    return pl.BlockSpec(shape, lambda step, *refs: (0,) * len(shape))


def attention_forward(low_blocks, core, starts, qkv, heads):
    length, triple = qkv.shape
    flat = triple // 3
    width = flat // heads
    blocks, _, bq = starts.shape
    grid_spec = pltpu.PrefetchScalarGridSpec(
        num_scalar_prefetch=2,
        grid=(1,),
        in_specs=[whole_block((blocks, 1, bq)), whole_block((length, triple))],
        out_specs=[
            whole_block((length, flat)),
            whole_block((blocks, flat, bq)),
            whole_block((blocks, 8, bq)),
        ],
        scratch_shapes=[
            pltpu.VMEM((heads, length, width), BF16),
            pltpu.VMEM((heads, length, width), BF16),
            pltpu.VMEM((heads, blocks, width, bq), BF16),
            pltpu.VMEM((flat, bq), F32),
        ],
    )
    return pl.pallas_call(
        functools.partial(attention_forward_body, heads, width, bq),
        out_shape=[
            jax.ShapeDtypeStruct((length, flat), BF16),
            jax.ShapeDtypeStruct((blocks, flat, bq), F32),
            jax.ShapeDtypeStruct((blocks, 8, bq), F32),
        ],
        grid_spec=grid_spec,
        compiler_params=pltpu.CompilerParams(vmem_limit_bytes=48 << 20),
        cost_estimate=lasting(35),
        name="attention_forward",
    )(low_blocks, core, starts, qkv)


def attention_backward(low_blocks, core, starts, qkv, grad_out, out_turned, log_total, heads):
    length, triple = qkv.shape
    flat = triple // 3
    width = flat // heads
    blocks, _, bq = starts.shape
    per_head = pltpu.VMEM((heads, length, width), BF16)
    sums = pltpu.VMEM((heads, length, width), F32)
    grid_spec = pltpu.PrefetchScalarGridSpec(
        num_scalar_prefetch=2,
        grid=(1,),
        in_specs=[
            whole_block((blocks, 1, bq)),
            whole_block((length, triple)),
            whole_block((length, flat)),
            whole_block((blocks, flat, bq)),
            whole_block((blocks, 8, bq)),
        ],
        out_specs=whole_block((length, lanes(triple))),
        scratch_shapes=[
            per_head,
            per_head,
            per_head,
            per_head,
            pltpu.VMEM((heads, blocks, width, bq), BF16),
            sums,
            sums,
            pltpu.VMEM((flat, bq), F32),
        ],
    )
    return pl.pallas_call(
        functools.partial(attention_backward_body, heads, width, bq),
        out_shape=jax.ShapeDtypeStruct((length, lanes(triple)), BF16),
        grid_spec=grid_spec,
        compiler_params=pltpu.CompilerParams(vmem_limit_bytes=60 << 20),
        cost_estimate=lasting(56),
        name="attention_backward",
    )(low_blocks, core, starts, qkv, grad_out, out_turned, log_total)


def lasting(micros):
    return pl.CostEstimate(flops=int(micros * SCALE), bytes_accessed=1 << 12, transcendentals=0)


def lanes(width):
    return -(-width // 128) * 128


def put(ref, value):
    width = value.shape[1]
    ref[:, :width] = value.astype(ref.dtype)
    if width < ref.shape[1]:
        ref[:, width:] = jnp.zeros((value.shape[0], ref.shape[1] - width), ref.dtype)


def vmem(count):
    return pltpu.CompilerParams(vmem_limit_bytes=count << 20)


def fixed(shape):
    return pl.BlockSpec(shape, lambda *step: (0,) * len(shape), pipeline_mode=pl.Buffered(1))


def hbm():
    return pl.BlockSpec(memory_space=pl.ANY)


def round_weights_body(bound_ref, weight_ref, low_ref, sums_ref):
    values = weight_ref[...]
    low_ref[...] = values[0, 0].astype(BF16)
    place = lax.broadcasted_iota(jnp.int32, values.shape, 2)
    squares = values * values
    lower = jnp.sum(jnp.where(place < bound_ref[0], squares, 0.0))
    sums_ref[0] = lower
    sums_ref[1] = jnp.sum(squares) - lower


def round_weights(bound, weight):
    smem = pl.BlockSpec(memory_space=pltpu.SMEM)
    whole = pl.BlockSpec(memory_space=pltpu.VMEM)
    return pl.pallas_call(
        round_weights_body,
        in_specs=[smem, whole],
        out_specs=[whole, smem],
        out_shape=[
            jax.ShapeDtypeStruct(weight.shape[2:], BF16),
            jax.ShapeDtypeStruct((2,), F32),
        ],
        compiler_params=vmem(32),
        cost_estimate=lasting(6),
        name="round_weights",
    )(bound, weight)


def moments_body(
    ints_ref, floats_ref, lead_ref, rest_ref, first_ref, second_ref, weight_ref,
    grad_ref, moments_ref, update_ref, sums_ref,
):
    step = pl.program_id(0)
    grad = jnp.where(ints_ref[1] == 1, lead_ref[...], rest_ref[...])
    grad_ref[...] = grad
    first = BETA_ONE * first_ref[...] + (1.0 - BETA_ONE) * grad
    second = BETA_TWO * second_ref[...] + (1.0 - BETA_TWO) * grad * grad
    moments_ref[0] = first
    moments_ref[1] = second
    update = (first / floats_ref[0]) / (jnp.sqrt(second / floats_ref[1]) + ADAM_EPS)
    update = update + DECAY * weight_ref[...]
    update_ref[...] = update
    count = grad.shape[2]
    place = step * count + lax.broadcasted_iota(jnp.int32, grad.shape, 2)
    squares = update * update
    lower = jnp.sum(jnp.where(place < ints_ref[0], squares, 0.0))
    upper = jnp.sum(squares) - lower

    @pl.when(step == 0)
    def clear():
        sums_ref[0] = 0.0
        sums_ref[1] = 0.0

    sums_ref[0] += lower
    sums_ref[1] += upper


def flat_steps(count):
    return 7 if count % (7 * 128) == 0 else 1


def new_moments(ints, floats, lead, rest, first, second, weight):
    count = weight.shape[2]
    steps = flat_steps(count)
    smem = pl.BlockSpec(memory_space=pltpu.SMEM)
    flat = pl.BlockSpec((1, 1, count // steps), lambda i: (0, 0, i))
    pair = pl.BlockSpec((2, 1, 1, count // steps), lambda i: (0, 0, 0, i))
    return pl.pallas_call(
        moments_body,
        grid=(steps,),
        in_specs=[smem, smem] + [flat] * 5,
        out_specs=[flat, pair, flat, smem],
        out_shape=[
            jax.ShapeDtypeStruct(weight.shape, F32),
            jax.ShapeDtypeStruct((2,) + weight.shape, F32),
            jax.ShapeDtypeStruct(weight.shape, F32),
            jax.ShapeDtypeStruct((2,), F32),
        ],
        compiler_params=vmem(48),
        cost_estimate=lasting(10),
        name="new_moments",
    )(ints, floats, lead, rest, first, second, weight)


def new_weights_body(ints_ref, ratio_ref, weight_ref, update_ref, new_ref, copy_ref):
    count = weight_ref.shape[2]
    place = pl.program_id(0) * count + lax.broadcasted_iota(jnp.int32, weight_ref.shape, 2)
    rate = jnp.where(place < ints_ref[0], ratio_ref[0], ratio_ref[1])
    new = weight_ref[...] - MATRIX_RATE * rate * update_ref[...]
    new_ref[...] = new
    copy_ref[...] = new.astype(BF16)


def new_weights(ints, ratios, weight, update):
    count = weight.shape[2]
    steps = flat_steps(count)
    smem = pl.BlockSpec(memory_space=pltpu.SMEM)
    flat = pl.BlockSpec((1, 1, count // steps), lambda i: (0, 0, i))
    return pl.pallas_call(
        new_weights_body,
        grid=(steps,),
        in_specs=[smem, smem, flat, flat],
        out_specs=[flat, flat],
        out_shape=[
            jax.ShapeDtypeStruct(weight.shape, F32),
            jax.ShapeDtypeStruct(weight.shape, BF16),
        ],
        compiler_params=vmem(32),
        cost_estimate=lasting(6),
        name="new_weights",
    )(ints, ratios, weight, update)


def unpack_body(cut, out_rows, in_rows, place_ref, *refs):
    blocks, (w_out, w_in, w_back, held, sems) = refs[:8], refs[8:]
    here = place_ref[0]
    copies = [
        pltpu.make_async_copy(block, held.at[index ^ here], sems.at[index])
        for index, block in enumerate(blocks)
    ]
    for copy in copies:
        copy.start()
    for copy in copies:
        copy.wait()
    begin = 2 * cut
    for target, rows in ((w_out, out_rows), (w_in, in_rows), (w_back, in_rows)):
        done = 0
        while done < rows:
            block, offset = divmod(begin + done, cut)
            count = min(cut - offset, rows - done)
            target[done : done + count] = held[block, offset : offset + count]
            done += count
        begin += rows


def unpack_share(place, blocks, out_rows, in_rows):
    cut, columns = blocks[0].shape
    shapes = [(out_rows, columns), (in_rows, columns), (in_rows, columns)]
    return pl.pallas_call(
        functools.partial(unpack_body, cut, out_rows, in_rows),
        grid_spec=pltpu.PrefetchScalarGridSpec(
            num_scalar_prefetch=1,
            grid=(1,),
            in_specs=[hbm()] * 8,
            out_specs=[whole_block(shape) for shape in shapes],
            scratch_shapes=[
                pltpu.VMEM((8, cut, columns), BF16),
                pltpu.SemaphoreType.DMA((8,)),
            ],
        ),
        out_shape=[jax.ShapeDtypeStruct(shape, BF16) for shape in shapes],
        compiler_params=vmem(48),
        cost_estimate=lasting(6),
        name="unpack_share",
    )(place, *blocks)


def pack_rest_body(
    cut, place_ref, out_ref, in_ref, back_ref, out_got, in_got, back_got, kept_ref, sent_ref
):
    here = place_ref[0]
    place = 0
    for matrix, got in ((out_ref, out_got), (in_ref, in_got), (back_ref, back_got)):
        done, rows = 0, matrix.shape[0]
        while done < rows:
            block, offset = divmod(place, cut)
            count = min(cut - offset, rows - done)
            source = slice(done, done + count)
            target = slice(offset, offset + count)
            plane, side = divmod(block, 2)

            @pl.when(here == side)
            def keep(matrix=matrix, got=got, source=source, target=target, plane=plane):
                kept_ref[plane, target] = matrix[source] + got[source].astype(F32)

            @pl.when(here != side)
            def send(matrix=matrix, got=got, source=source, target=target, plane=plane):
                sent_ref[plane, target] = (matrix[source] + got[source].astype(F32)).astype(BF16)

            done += count
            place += count


def pack_rest(place, matrices, received, cut):
    columns = matrices[0].shape[1]
    whole = pl.BlockSpec(memory_space=pltpu.VMEM)
    return pl.pallas_call(
        functools.partial(pack_rest_body, cut),
        in_specs=[pl.BlockSpec(memory_space=pltpu.SMEM)] + [whole] * 6,
        out_specs=[whole] * 2,
        out_shape=[
            jax.ShapeDtypeStruct((3, cut, columns), F32),
            jax.ShapeDtypeStruct((3, cut, columns), BF16),
        ],
        compiler_params=vmem(40),
        cost_estimate=lasting(10),
        name="pack_rest",
    )(place, *matrices, *received)


def rows_of(step, steps, own_ref, other_ref, width):
    return jnp.where(step < steps, own_ref[:, :width], other_ref[:, :width])


def both_specs(block, width, steps):
    own = pl.BlockSpec((block, width), lambda i, *refs: (jnp.minimum(i, steps - 1), 0))
    other = pl.BlockSpec((block, width), lambda i, *refs: (jnp.maximum(i - steps, 0), 0))
    return own, other


def project_body(
    steps, place_ref, own_ref, other_ref, a0, a1, b0, b1, bias_ref,
    out_a, out_b, rows_ref, w_a, w_b, sems,
):
    step = pl.program_id(0)

    @pl.when(step == 0)
    def load():
        cut = a0.shape[0]
        here = place_ref[0]
        first = pl.ds(pl.multiple_of(here * cut, cut), cut)
        second = pl.ds(pl.multiple_of((1 - here) * cut, cut), cut)
        copies = [
            pltpu.make_async_copy(a0, w_a.at[first], sems.at[0]),
            pltpu.make_async_copy(a1, w_a.at[second], sems.at[1]),
            pltpu.make_async_copy(b0, w_b.at[first], sems.at[2]),
            pltpu.make_async_copy(b1, w_b.at[second], sems.at[3]),
        ]
        for copy in copies:
            copy.start()
        for copy in copies:
            copy.wait()

    rows = rows_of(step, steps, own_ref, other_ref, rows_ref.shape[1])
    rows_ref[...] = rows
    out_a[...] = (dot_rows(rows, w_a[...]) + bias_ref[0:1]).astype(BF16)
    out_b[...] = (dot_rows(rows, w_b[...]) + bias_ref[1:2]).astype(BF16)


def project(place, own, other, halves, biases):
    count, sent_width = own.shape
    cut, triple = halves[0].shape
    model_width = 2 * cut
    block = min(512, count)
    steps = count // block
    row_out = lambda width: pl.BlockSpec((block, width), lambda i, *refs: (i, 0))
    matrix = jax.ShapeDtypeStruct((2 * cut, triple), BF16)
    return pl.pallas_call(
        functools.partial(project_body, steps),
        grid_spec=pltpu.PrefetchScalarGridSpec(
            num_scalar_prefetch=1,
            grid=(2 * steps,),
            in_specs=[*both_specs(block, sent_width, steps)]
            + [hbm()] * 4
            + [fixed((2, triple))],
            out_specs=[row_out(triple), row_out(triple), row_out(model_width)]
            + [pl.BlockSpec(matrix.shape, lambda i, *refs: (0, 0))] * 2,
            scratch_shapes=[pltpu.SemaphoreType.DMA((4,))],
        ),
        out_shape=[jax.ShapeDtypeStruct((2 * count, triple), BF16)] * 2
        + [jax.ShapeDtypeStruct((2 * count, model_width), BF16), matrix, matrix],
        compiler_params=vmem(48),
        cost_estimate=lasting(16),
        name="project",
    )(place, own, other, *halves, biases)


def out_grads_body(steps, own_ref, other_ref, w_a, w_b, out_a, out_b, rows_ref):
    rows = rows_of(pl.program_id(0), steps, own_ref, other_ref, rows_ref.shape[1])
    rows_ref[...] = rows
    out_a[...] = dot_transposed(rows, w_a[...]).astype(BF16)
    out_b[...] = dot_transposed(rows, w_b[...]).astype(BF16)


def out_grads(own, other, w_out):
    count, sent_width = own.shape
    width, model_width = w_out[0].shape
    block = min(512, count)
    steps = count // block
    row_out = lambda columns: pl.BlockSpec((block, columns), lambda i: (i, 0))
    return pl.pallas_call(
        functools.partial(out_grads_body, steps),
        grid=(2 * steps,),
        in_specs=[*both_specs(block, sent_width, steps)] + [fixed(w_out[0].shape)] * 2,
        out_specs=[row_out(width), row_out(width), row_out(model_width)],
        out_shape=[jax.ShapeDtypeStruct((2 * count, width), BF16)] * 2
        + [jax.ShapeDtypeStruct((2 * count, model_width), BF16)],
        compiler_params=vmem(48),
        cost_estimate=lasting(8),
        name="out_grads",
    )(own, other, *w_out)


def row_products(turned, left_refs, weight_refs):
    product = None
    for left, weight in zip(left_refs, weight_refs):
        if turned:
            term = dot_transposed(left[:, : weight.shape[1]], weight[...])
        else:
            term = dot_rows(left[:, : weight.shape[0]], weight[...])
        product = term if product is None else product + term
    return product


def partial_product_body(left, weight, out_ref):
    out_ref[...] = row_products(True, [left], [weight])


def split_product_body(steps, turned, count, *refs):
    lefts, weights, rest = refs[:count], refs[count : 2 * count], refs[2 * count :]
    *partial, sent_ref, kept_ref = rest
    product = row_products(turned, lefts, weights)
    if partial:
        product = product + partial[0][...]
    step = pl.program_id(0)

    @pl.when(step < steps)
    def other_rows():
        put(sent_ref, product)

    @pl.when(step >= steps)
    def own_rows():
        put(kept_ref, product)


def other_first(block, width, steps):
    return pl.BlockSpec((block, width), lambda i: ((i + steps) % (2 * steps), 0))


def partial_product(left, weight):
    count, width = left.shape
    model_width = weight.shape[0]
    block = min(512, count // 2)
    steps = count // 2 // block
    return pl.pallas_call(
        partial_product_body,
        grid=(2 * steps,),
        in_specs=[other_first(block, width, steps), fixed(weight.shape)],
        out_specs=pl.BlockSpec((block, model_width), lambda i: (i, 0)),
        out_shape=jax.ShapeDtypeStruct((count, model_width), F32),
        compiler_params=vmem(48),
        cost_estimate=lasting(9),
        name="partial_product",
    )(left, weight)


def split_product(lefts, weights, turned, model_width, sent_type, partial=()):
    count, width = lefts[0].shape
    block = min(512, count // 2)
    steps = count // 2 // block
    parts = [
        jax.ShapeDtypeStruct((count // 2, lanes(model_width)), sent_type),
        jax.ShapeDtypeStruct((count // 2, model_width), F32),
    ]
    return pl.pallas_call(
        functools.partial(split_product_body, steps, turned, len(lefts)),
        grid=(2 * steps,),
        in_specs=[other_first(block, width, steps)] * len(lefts)
        + [fixed(weight.shape) for weight in weights]
        + [pl.BlockSpec((block, model_width), lambda i: (i, 0))] * len(partial),
        out_specs=[
            pl.BlockSpec((block, lanes(model_width)), lambda i: (jnp.minimum(i, steps - 1), 0)),
            pl.BlockSpec((block, model_width), lambda i: (jnp.maximum(i - steps, 0), 0)),
        ],
        out_shape=parts,
        compiler_params=vmem(48),
        cost_estimate=lasting(9),
        name="split_product",
    )(*lefts, *weights, *partial)


def middle_body(rows_ref, kept_ref, got_ref, small_ref, middle_ref, low_ref):
    middle = rows_ref[...].astype(F32) + (
        kept_ref[...] + got_ref[:, : kept_ref.shape[1]] + small_ref[6:7]
    )
    middle_ref[...] = middle
    hat, _ = norm_stats(middle)
    put(low_ref, (hat * small_ref[2:3] + small_ref[3:4]).astype(BF16))


def middle_norm(rows, kept, got, small):
    count, width = rows.shape
    block = min(256, count)
    part = pl.BlockSpec((block, width), lambda i: (i, 0))
    sent = pl.BlockSpec((block, lanes(width)), lambda i: (i, 0))
    return pl.pallas_call(
        middle_body,
        grid=(count // block,),
        in_specs=[part, part, sent, fixed(small.shape)],
        out_specs=[part, sent],
        out_shape=[
            jax.ShapeDtypeStruct((count, width), F32),
            jax.ShapeDtypeStruct((count, lanes(width)), BF16),
        ],
        compiler_params=vmem(32),
        cost_estimate=lasting(4),
        name="middle_norm",
    )(rows, kept, got, small)


def norm_back_body(wide_out, rows_ref, kept_ref, got_ref, base_ref, gain_ref, *outs):
    (full_ref, low_ref, sums_ref) = outs if wide_out else (None, *outs)
    rows = rows_ref[...].astype(F32)
    hat, scale = norm_stats(rows)
    width = rows.shape[1]
    upstream = kept_ref[:, :width] + got_ref[:, :width].astype(F32)
    base = base_ref[:, :width].astype(F32)
    grad = base + norm_backward(upstream, hat, scale, gain_ref[...])
    low = grad.astype(BF16)
    if wide_out:
        full_ref[...] = grad
    put(low_ref, low)

    @pl.when(pl.program_id(0) == 0)
    def clear():
        sums_ref[...] = jnp.zeros_like(sums_ref)

    for index, term in enumerate((upstream * hat, upstream, low.astype(F32), base)):
        sums_ref[index : index + 1] += jnp.sum(term, axis=0, keepdims=True)


def norm_back(rows, kept, got, base, gain, wide_out):
    count, width = rows.shape
    block = min(256, count)
    part = pl.BlockSpec((block, width), lambda i: (i, 0))
    sent = pl.BlockSpec((block, lanes(width)), lambda i: (i, 0))
    full = [jax.ShapeDtypeStruct((count, width), F32)] if wide_out else []
    return pl.pallas_call(
        functools.partial(norm_back_body, wide_out),
        grid=(count // block,),
        in_specs=[part, pl.BlockSpec((block, kept.shape[1]), lambda i: (i, 0)), sent]
        + [pl.BlockSpec((block, base.shape[1]), lambda i: (i, 0)), fixed((1, width))],
        out_specs=[part] * len(full) + [sent, pl.BlockSpec((8, width), lambda i: (0, 0))],
        out_shape=full
        + [
            jax.ShapeDtypeStruct((count, lanes(width)), BF16),
            jax.ShapeDtypeStruct((8, width), F32),
        ],
        compiler_params=vmem(40),
        cost_estimate=lasting(7),
        name="norm_back",
    )(rows, kept, got, base, gain)


def feed_forward_body(
    skipped,
    rows_ref,
    cot_ref,
    w_in_mine,
    w_in_theirs,
    w_back_mine,
    w_back_theirs,
    bias_ref,
    *refs,
):
    (
        act_mine, act_theirs, inner_mine, inner_theirs, rows_out, cot_out, out_ref, up_ref, sums_ref
    ) = refs[skipped:]
    model_width = rows_out.shape[1]
    rows, cot = rows_ref[:, :model_width], cot_ref[:, :model_width]
    rows_out[...] = rows
    cot_out[...] = cot

    @pl.when(pl.program_id(0) == 0)
    def clear():
        sums_ref[...] = jnp.zeros_like(sums_ref)

    out, up = None, None
    shares = (
        (w_in_mine, w_back_mine, act_mine, inner_mine),
        (w_in_theirs, w_back_theirs, act_theirs, inner_theirs),
    )
    for part, (w_in, w_back, act_ref, inner_ref) in enumerate(shares):
        hidden = dot_rows(rows, w_in[...]) + bias_ref[part : part + 1]
        value, slope = gelu_parts(hidden)
        act = value.astype(BF16)
        act_ref[...] = act
        inner = (dot_transposed(cot, w_back[...]) * slope).astype(BF16)
        inner_ref[...] = inner
        sums_ref[part : part + 1] += jnp.sum(inner.astype(F32), axis=0, keepdims=True)
        one_out = dot_rows(act, w_back[...])
        one_up = dot_transposed(inner, w_in[...])
        out = one_out if out is None else out + one_out
        up = one_up if up is None else up + one_up
    put(out_ref, out)
    put(up_ref, up)


def feed_forward(rows, cot, half, weights, biases, filled):
    count, sent_width = rows.shape
    model_width, ff_share = weights[0].shape
    block = min(FF_ROWS, count)
    steps = count // block
    row_spec = pl.BlockSpec((block, sent_width), lambda i: (i, 0))
    joined = lambda width: pl.BlockSpec((block, width), lambda i: (half * steps + i, 0))
    act_shape = jax.ShapeDtypeStruct((2 * count, ff_share), BF16)
    row_shape = jax.ShapeDtypeStruct((2 * count, model_width), BF16)
    part_shape = jax.ShapeDtypeStruct((count, sent_width), F32)
    filled = () if filled is None else tuple(filled)
    return pl.pallas_call(
        functools.partial(feed_forward_body, len(filled)),
        out_shape=[act_shape] * 4
        + [row_shape] * 2
        + [part_shape] * 2
        + [jax.ShapeDtypeStruct((8, ff_share), F32)],
        grid=(steps,),
        in_specs=[row_spec, row_spec]
        + [fixed(matrix.shape) for matrix in weights]
        + [fixed((2, ff_share))]
        + [hbm()] * len(filled),
        out_specs=[joined(ff_share)] * 4
        + [joined(model_width)] * 2
        + [row_spec] * 2
        + [pl.BlockSpec((8, ff_share), lambda i: (0, 0))],
        input_output_aliases={7 + i: i for i in range(len(filled))},
        compiler_params=vmem(58),
        cost_estimate=lasting(34),
        name="feed_forward",
    )(rows, cot, *weights, biases, *filled)


def permute(value, axis_name, pairs):
    return lax.ppermute(value, axis_name, pairs)


def swap(value, axis_name, distance):
    count = lax.axis_size(axis_name)
    return permute(value, axis_name, [(i, i ^ distance) for i in range(count)])


def tie(*values):
    return lax.optimization_barrier(values)


def started(sent, value, mark):
    sent, mark = tie(sent, mark)
    value, mark = tie(value, swap(mark, "seq", 1))
    return sent, value, mark


def lower_pairs(pairs, y_count):
    return [
        (source * y_count + y, target * y_count + y)
        for source, target in pairs
        for y in range(y_count)
    ]


def spread_lead(block, z_here):
    far = permute(block, "dp", lower_pairs([(0, 2)], 2))
    held = jnp.where(z_here == 0, block, far)
    near = permute(held, "dp", lower_pairs([(0, 1), (2, 3)], 2))
    return jnp.where(z_here % 2 == 0, held, near)


def move_rest(block, distance, plane_distance):
    over_dp, over_seq = distance
    pairs = []
    for d in range(8):
        if (d // 2) ^ plane_distance != 0:
            pairs += [(d * 4 + q, (d ^ over_dp) * 4 + (q ^ over_seq)) for q in range(4)]
    return permute(block, ("dp", "seq"), pairs)


def pick(stacked, index, axis=0):
    return lax.dynamic_index_in_dim(stacked, index, axis, keepdims=False)


def halve_plane(lower, upper, y_here):
    return (
        jnp.where(y_here == 0, lower, upper),
        jnp.where(y_here == 0, upper, lower).astype(BF16),
    )


def sum_everywhere(value):
    for axis_name in ("seq", "dp"):
        distance = 1
        while distance < lax.axis_size(axis_name):
            value = value + swap(value, axis_name, distance)
            distance *= 2
    return value


def per_device(
    rows_in,
    out_cotangent,
    cell_lengths,
    cell_starts,
    key_mask,
    weights_master,
    first_moment,
    second_moment,
    small_master,
    small_first,
    small_second,
    step_count,
):
    model_width = rows_in.shape[3]
    local_rows = rows_in.shape[2]
    length = key_mask.shape[2]
    shard_len = weights_master.shape[2]
    groups = lax.axis_size("seq")
    dp_count = lax.axis_size("dp")
    head_share = model_width // groups
    heads_here = HEADS // groups
    triple = 3 * head_share
    first_end = model_width * triple
    second_end = first_end + head_share * model_width
    third_end = second_end + model_width * model_width
    seq_here = lax.axis_index("seq")
    dp_here = lax.axis_index("dp")
    chip = seq_here // 2
    core = seq_here % 2
    z_here = dp_here // 2
    y_here = dp_here % 2
    planar = dp_count == 8 and shard_len * 2 == first_end
    shares = (core + 2 * chip, core + 2 * (1 - chip))

    def exchange_micro(array):
        own = pick(array[:, 0], chip)
        received = swap(widen(pick(array[:, 0], 1 - chip)), "seq", 2)[:, :model_width]
        first = jnp.where(chip == 0, own, received)
        second = jnp.where(chip == 0, received, own)
        return jnp.concatenate([first, second], axis=0)

    def widen(rows):
        return jnp.pad(rows, ((0, 0), (0, lanes(model_width) - model_width)))

    mark = small_master[:8, :128]

    ends = jnp.array([first_end, second_end, third_end, dp_count * shard_len], jnp.int32)
    begin = dp_here * shard_len
    lower_matrix = jnp.sum((begin >= ends).astype(jnp.int32))
    upper_matrix = jnp.sum((begin + shard_len - 1 >= ends).astype(jnp.int32))
    bound = jnp.minimum(pick(ends, lower_matrix) - begin, shard_len).reshape(1)
    matrices = jnp.arange(4, dtype=jnp.int32)

    def matrix_sums(pair):
        return jnp.where(matrices == lower_matrix, pair[0], 0.0) + jnp.where(
            matrices == upper_matrix, pair[1], 0.0
        )

    weight = weights_master
    low_weight, weight_sums = round_weights(bound, weight)
    first_rows, low_weight = tie(rows_in, low_weight)
    own_in = exchange_micro(first_rows)
    inputs = own_in.astype(F32)
    hat_one, _ = norm_stats(inputs)
    low_one = widen((hat_one * small_master[0] + small_master[1]).astype(BF16))
    other_one = swap(low_one, "seq", 1)
    y_index = y_here.reshape(1).astype(jnp.int32)
    if planar:
        tall = low_weight.reshape(shard_len // triple, triple)
        wide = low_weight.reshape(shard_len // model_width, model_width)
        cut, tall_rows = wide.shape[0], tall.shape[0]
        lead = spread_lead(tall, z_here)
        across = [move_rest(wide, (1, 0), 0)]
        over = [move_rest(wide, (0, 2), 0)]
        lead, wide, across[0], over[0], other_one = tie(
            lead, wide, across[0], over[0], other_one
        )
        lead_across = swap(lead, "dp", 1)
        halves = (lead, lead_across, swap(lead, "seq", 2), swap(lead_across, "seq", 2))
        dp_index = dp_here.reshape(1).astype(jnp.int32)
        far = move_rest(wide, (4, 0), 0)
        near = move_rest(wide, (2, 0), 0)
    else:
        copies = lax.all_gather(low_weight.reshape(1, shard_len), ("dp", "seq"), axis=0, tiled=True)
        copies = copies.reshape(dp_count, groups, shard_len)
        per_share = [pick(copies, share, 1).reshape(dp_count * shard_len) for share in shares]
        halves = []
        for flat in per_share:
            matrix = flat[:first_end].reshape(model_width, triple)
            first = jnp.where(y_here == 0, matrix[: model_width // 2], matrix[model_width // 2 :])
            second = jnp.where(y_here == 0, matrix[model_width // 2 :], matrix[: model_width // 2])
            halves += [first, second]
        w_out = [flat[first_end:second_end].reshape(head_share, model_width) for flat in per_share]
        w_in = [flat[second_end:third_end].reshape(model_width, model_width) for flat in per_share]
        w_back = [flat[third_end:].reshape(model_width, model_width) for flat in per_share]

    def share_columns(vector, share):
        return lax.dynamic_slice_in_dim(vector, share * head_share, head_share)

    attn_biases = [
        jnp.concatenate(
            [
                share_columns(small_master[4], share),
                jnp.zeros((head_share,), F32),
                share_columns(small_master[5], share),
            ]
        )
        for share in shares
    ]
    ff_biases = jnp.stack([pick(small_master, 8 + share) for share in shares])

    starts = pick(cell_starts[:, 0], chip)
    lengths = pick(cell_lengths[:, 0], chip)
    places = jnp.arange(length, dtype=jnp.int32)
    inside = (places[:, None] >= starts[None, :]) & (places[:, None] < (starts + lengths)[None, :])
    first_key = jnp.max(jnp.where(inside, starts[None, :], -1), axis=1)
    first_key = jnp.where(first_key < 0, places, first_key)
    low_blocks = first_key.reshape(-1, local_rows)[:, 0] // local_rows
    block_starts = first_key.reshape(-1, 1, local_rows)
    core_index = core.reshape(1).astype(jnp.int32)

    if planar:
        both = [move_rest(over[0], (1, 0), 0)]
        halves, near, far, both[0] = tie(halves, near, far, both[0])
        last = move_rest(far, (2, 0), 2)
        across += [move_rest(near, (1, 0), 1), move_rest(far, (1, 0), 2)]
        over += [move_rest(near, (0, 2), 1), move_rest(far, (0, 2), 2)]
    *qkv, rows_one, w_attn_mine, w_attn_theirs = project(
        y_index, low_one, other_one, halves, jnp.stack(attn_biases)
    )

    def attend(part):
        return attention_forward(low_blocks, core_index, block_starts, qkv[part], heads_here)

    later_cotangent = out_cotangent
    attended = [attend(0)]
    if planar:
        qkv[1], last, across[1:3], over[1:3], later_cotangent, _ = tie(
            qkv[1], last, across[1:3], over[1:3], later_cotangent, attended[0][2]
        )
        across.append(move_rest(last, (1, 0), 3))
        over.append(move_rest(last, (0, 2), 3))
        both += [move_rest(over[1], (1, 0), 1), move_rest(across[2], (0, 2), 2)]
    own_e = widen(exchange_micro(later_cotangent))
    attended.append(attend(1))
    if planar:
        dp_index, across, over, both, _ = tie(dp_index, across, over, both, attended[1][2])
        both.append(move_rest(over[3], (1, 0), 3))
        rest_mine = [block for pair in zip((wide, near, far, last), across) for block in pair]
        rest_theirs = [block for pair in zip(over, both) for block in pair]
        matrices_mine = unpack_share(dp_index, rest_mine, head_share, model_width)
        matrices_theirs = unpack_share(dp_index, rest_theirs, head_share, model_width)
        w_out, w_in, w_back = (list(pair) for pair in zip(matrices_mine, matrices_theirs))
        own_e, w_out[0] = tie(own_e, w_out[0])
    other_e = swap(own_e, "seq", 1)
    sent, kept = split_product([attended[0][0], attended[1][0]], w_out, False, model_width, F32)
    middle, low_two = middle_norm(own_in, kept, swap(sent, "seq", 1), small_master)
    other_two = swap(low_two, "seq", 1)

    weights = (w_in[0], w_in[1], w_back[0], w_back[1])
    *filled, out_sent, up_sent, sums_sent = feed_forward(
        other_two, other_e, 1, weights, ff_biases, None
    )
    out_received = swap(out_sent, "seq", 1)
    up_received = swap(up_sent, "seq", 1)
    *filled, out_kept, up_kept, sums_kept = feed_forward(
        low_two, own_e, 0, weights, ff_biases, filled
    )
    activated, inner, (rows_two, rows_e) = filled[:2], filled[2:4], filled[4:]
    inner_sums = sums_sent + sums_kept

    link = BF16 if planar else F32
    up_received, out_received = tie(up_received, out_received)
    grad_mid, low_mid, sums_two = norm_back(
        middle, up_kept, up_received, own_e, small_master[2:3], True
    )
    low_mid, rows_two, rows_e = tie(low_mid, rows_two, rows_e)
    back_sent = dot_columns(activated[1], rows_e).astype(link)
    in_sent = dot_columns(rows_two, inner[1]).astype(link)
    back_sent, in_sent, low_mid = tie(back_sent, in_sent, low_mid)
    other_mid = swap(low_mid, "seq", 1)
    back_received = swap(back_sent, "seq", 2)
    in_received = swap(in_sent, "seq", 2)

    grad_att_mine, grad_att_theirs, rows_mid = out_grads(low_mid, other_mid, w_out)
    out_sent_theirs = dot_columns(attended[1][0], rows_mid).astype(link)
    out_sent_theirs, rows_two, rows_e, rows_mid = tie(out_sent_theirs, rows_two, rows_e, rows_mid)
    outer_received = swap(out_sent_theirs, "seq", 2)
    share_back = dot_columns(activated[0], rows_e)
    share_in = dot_columns(rows_two, inner[0])
    share_out = dot_columns(attended[0][0], rows_mid)
    share_back, share_in, share_out, grad_att_theirs = tie(
        share_back, share_in, share_out, grad_att_theirs
    )

    def place_micro(lower, upper, received):
        own = jnp.where(chip == 0, lower, upper)[:, :model_width]
        received = received[:, :model_width]
        first = jnp.where(chip == 0, own, received)
        second = jnp.where(chip == 0, received, own)
        return jnp.stack([first, second])[:, None]

    def return_rows(lower, upper):
        return swap(jnp.where(chip == 0, upper, lower), "seq", 2)

    def attend_back(part, grad_att):
        return attention_backward(
            low_blocks,
            core_index,
            block_starts,
            qkv[part],
            grad_att,
            attended[part][1],
            attended[part][2],
            heads_here,
        )

    packed_theirs = attend_back(1, grad_att_theirs)
    attn_sent = dot_columns(rows_one, packed_theirs).astype(link)
    attn_sent, packed_theirs = tie(attn_sent, packed_theirs)
    theirs_part = partial_product(packed_theirs, w_attn_theirs)
    attn_sent, theirs_part, y_index = tie(attn_sent, theirs_part, y_index)
    attn_received = swap(attn_sent, "seq", 2)
    if planar:
        kept_rest, sent_rest = pack_rest(
            y_index,
            (share_out, share_in, share_back),
            (outer_received, in_received, back_received),
            cut,
        )
        result_rows = widen(
            (middle + ((out_kept + out_received)[:, :model_width] + small_master[7])).astype(BF16)
        )
        sent_rest, grad_att_mine, result_rows = tie(sent_rest, grad_att_mine, result_rows)
        result_halves = (result_rows[:local_rows], result_rows[local_rows:])
        result_received = return_rows(*result_halves)
        got_rest = swap(sent_rest, "dp", 1)
    else:
        result_rows = widen(
            (middle + ((out_kept + out_received)[:, :model_width] + small_master[7])).astype(BF16)
        )
        result_halves = (result_rows[:local_rows], result_rows[local_rows:])
        result_received = return_rows(*result_halves)
        share_back, share_in, share_out = (
            share_back + back_received,
            share_in + in_received,
            share_out + outer_received,
        )

    packed_mine = attend_back(0, grad_att_mine)
    packed_mine, result_received = tie(packed_mine, result_received)
    sent, kept = split_product(
        [packed_mine], [w_attn_mine], True, model_width, BF16, [theirs_part]
    )
    packed_mine, sent = tie(packed_mine, sent)
    share_attn = dot_columns(rows_one, packed_mine) + attn_received.astype(F32)
    if planar:
        z_odd = z_here % 2 == 1
        kept_lead, sent_lead = halve_plane(share_attn[:tall_rows], share_attn[tall_rows:], y_here)
        kept_lead, sent_lead, kept_rest = tie(kept_lead, sent_lead, kept_rest)
        got_lead = swap(sent_lead, "dp", 1)
        held = [kept_rest[i] + got_rest[i].astype(F32) for i in range(3)]
        sent_near = jnp.where(z_odd, held[1], held[0]).astype(BF16)
        sent_last = held[2].astype(BF16)
        kept_near = jnp.where(z_odd, held[0], held[1])
        kept_last = held[2]
        (sent_near, sent_last), kept_lead, mark = started(
            (sent_near, sent_last), kept_lead, mark
        )
        got_near = swap(sent_near, "dp", 2)
        got_last = permute(sent_last, "dp", lower_pairs([(0, 1), (2, 3)], 2))
    packed = [packed_mine, packed_theirs]
    if planar:
        held_lead = kept_lead + got_lead.astype(F32)
        sent_lead = held_lead.astype(BF16)
        sent_lead, held_lead, kept = tie(sent_lead, held_lead, kept)
        sent_lead, kept, mark = started(sent_lead, kept, mark)
        near_lead = permute(sent_lead, "dp", lower_pairs([(1, 0), (3, 2)], 2))
    grad_x, sums_one = norm_back(
        own_in, kept, swap(sent, "seq", 1), grad_mid, small_master[0:1], False
    )
    if planar:
        grad_x, held_lead = tie(grad_x, held_lead)
        held_lead = held_lead + near_lead.astype(F32)
        sent_lead = held_lead.astype(BF16)
        sent_lead, held_lead, kept_near, kept_last = tie(
            sent_lead, held_lead, kept_near, kept_last
        )
        sent_lead, (kept_near, kept_last), mark = started(
            sent_lead, (kept_near, kept_last), mark
        )
        far_lead = permute(sent_lead, "dp", lower_pairs([(2, 0)], 2))
        held_near = kept_near + got_near.astype(F32)
        held_last = kept_last + got_last.astype(F32)
        sent_far = jnp.where(z_here == 1, held_last, held_near).astype(BF16)
        own_rest = jnp.where(z_here == 3, held_last, held_near)
        got_far = permute(sent_far, "dp", lower_pairs([(3, 1), (0, 2), (1, 3)], 2))

    result_all = place_micro(*result_halves, result_received)
    grad_halves = (grad_x[:local_rows], grad_x[local_rows:])
    grad_all = place_micro(*grad_halves, return_rows(*grad_halves))

    def at_shares(columns):
        row = jnp.zeros((model_width,), F32)
        for share, column in zip(shares, columns):
            row = lax.dynamic_update_slice(row, column, (share * head_share,))
        return row

    bias_sums = [jnp.sum(packed[part].astype(F32), axis=0) for part in range(2)]
    inner_rows = jnp.zeros((4, model_width), F32)
    for part in range(2):
        inner_rows = lax.dynamic_update_slice(
            inner_rows, inner_sums[part : part + 1], (shares[part], 0)
        )
    small_now = jnp.concatenate(
        [
            sums_one[:2],
            sums_two[:2],
            at_shares([sums[:head_share] for sums in bias_sums])[None],
            at_shares([sums[2 * head_share : triple] for sums in bias_sums])[None],
            sums_two[2:4],
            inner_rows,
        ]
    )

    if planar:
        rest_grad = (own_rest + got_far.astype(F32)).reshape(1, 1, shard_len)
        held_lead, rest_grad, result_all, grad_all, small_now = tie(
            held_lead, rest_grad, result_all, grad_all, small_now
        )
        lead_grad = (held_lead + far_lead.astype(F32))[:, :triple].reshape(1, 1, shard_len)
        leads = z_here == 0
    else:
        flat_here = jnp.concatenate(
            [matrix.reshape(-1) for matrix in (share_attn[:, :triple], share_out, share_in, share_back)]
        )
        lead_grad = lax.psum_scatter(
            flat_here.reshape(dp_count, shard_len), "dp", scatter_dimension=0, tiled=True
        ).reshape(1, 1, shard_len)
        rest_grad = lead_grad
        leads = z_here >= 0

    steps_done = step_count[0].astype(F32)
    fix_one = 1.0 - jnp.exp(steps_done * math.log(BETA_ONE))
    fix_two = 1.0 - jnp.exp(steps_done * math.log(BETA_TWO))
    ints = jnp.concatenate([bound, leads.astype(jnp.int32).reshape(1)])
    reduced, moments, update, update_sums = new_moments(
        ints,
        jnp.stack([fix_one, fix_two]),
        lead_grad,
        rest_grad,
        first_moment,
        second_moment,
        weight,
    )
    matrix_rows = jnp.stack([matrix_sums(weight_sums), matrix_sums(update_sums)])
    small_sum = sum_everywhere(
        jnp.concatenate([small_now, jnp.pad(matrix_rows, ((0, 2), (0, model_width - 4)))])
    )
    small_grad = small_sum[:12]
    weight_norms = jnp.sqrt(small_sum[12, :4])
    update_norms = jnp.sqrt(small_sum[13, :4])
    ratios = weight_norms / update_norms
    new_weight, weight_copy = new_weights(
        ints, jnp.stack([pick(ratios, lower_matrix), pick(ratios, upper_matrix)]), weight, update
    )
    small_one = BETA_ONE * small_first + (1.0 - BETA_ONE) * small_grad
    small_two = BETA_TWO * small_second + (1.0 - BETA_TWO) * small_grad * small_grad
    small_late = lax.dynamic_update_slice(small_master, mark, (0, 0))
    small_updated = small_late - SMALL_RATE * (small_one / fix_one) / (
        jnp.sqrt(small_two / fix_two) + ADAM_EPS
    )
    return (
        result_all,
        grad_all,
        reduced,
        moments,
        new_weight,
        weight_copy,
        jnp.stack([weight_norms, update_norms, ratios]),
        small_grad,
        jnp.stack([small_one, small_two]),
        small_updated,
    )


def solution(mesh):
    in_specs = (
        P(None, "dp", "seq", None),
        P(None, "dp", "seq", None),
        P(None, "dp", None),
        P(None, "dp", None),
        P(None, "dp", None),
        P("dp", "seq", None),
        P("dp", "seq", None),
        P("dp", "seq", None),
        P(),
        P(),
        P(),
        P(),
    )
    out_specs = (
        P(None, "dp", "seq", None),
        P(None, "dp", "seq", None),
        P("dp", "seq", None),
        P(None, "dp", "seq", None),
        P("dp", "seq", None),
        P("dp", "seq", None),
        P(),
        P(),
        P(),
        P(),
    )
    return jax.shard_map(
        per_device, mesh=mesh, in_specs=in_specs, out_specs=out_specs, check_vma=False
    )
```

```python
import functools
import math

import jax
import jax.numpy as jnp
from jax import lax
from jax.experimental import pallas as pl
from jax.experimental.pallas import tpu as pltpu
from jax.sharding import PartitionSpec as P

HEADS = 20


NORM_EPS = 1e-05
BETA_ONE = 0.9
BETA_TWO = 0.999
ADAM_EPS = 1e-06
DECAY = 0.01
MATRIX_RATE = 0.3
SMALL_RATE = 0.25
MASKED = -1e30
LOG2_E = 1.4426950408889634
FF_ROWS = 256
SCALE = 1e9

F32 = jnp.float32
BF16 = jnp.bfloat16


def dot_rows(left, right):
    return lax.dot_general(left, right, (((1,), (0,)), ((), ())), preferred_element_type=F32)


def dot_transposed(left, right):
    return lax.dot_general(left, right, (((1,), (1,)), ((), ())), preferred_element_type=F32)


def dot_columns(left, right):
    return lax.dot_general(left, right, (((0,), (0,)), ((), ())), preferred_element_type=F32)


def norm_stats(rows):
    center = jnp.mean(rows, axis=-1, keepdims=True)
    centered = rows - center
    spread = jnp.mean(centered * centered, axis=-1, keepdims=True)
    scale = lax.rsqrt(spread + NORM_EPS)
    return centered * scale, scale


def norm_backward(upstream, hat, scale, gain):
    weighted = upstream * gain
    return (
        weighted
        - jnp.mean(weighted, axis=-1, keepdims=True)
        - hat * jnp.mean(weighted * hat, axis=-1, keepdims=True)
    ) * scale


def gelu_parts(values):
    inner = math.sqrt(2.0 / math.pi)
    squares = values * values
    bent = jnp.tanh(inner * (values + 0.044715 * values * squares))
    half = 0.5 * (1.0 + bent)
    slope = half + 0.5 * values * (1.0 - bent * bent) * inner * (1.0 + 3.0 * 0.044715 * squares)
    return values * half, slope


def block_place(core, block):
    return jnp.where(block % 2 == core, 0, 2) + block // 2


def block_rows(core, block, rows):
    return pl.ds(pl.multiple_of(block_place(core, block) * rows, rows), rows)


def attention_forward_body(
    heads, width, bq, low_ref, core_ref, start_ref, qkv_ref, out_ref, outt_ref, lse_ref, qs, ks, vt, acc
):
    length = qkv_ref.shape[0]
    flat = heads * width
    factor = width**-0.5 * LOG2_E
    core = core_ref[0]

    def unpack(block, carry):
        here = block_rows(core, block, bq)
        there = pl.ds(pl.multiple_of(block * bq, bq), bq)
        for h in range(heads):
            qs[h, there] = qkv_ref[here, h * width : (h + 1) * width]
            ks[h, there] = qkv_ref[here, flat + h * width : flat + (h + 1) * width]
        turned = qkv_ref[here, 2 * flat : 3 * flat].astype(F32).T
        for h in range(heads):
            vt[h, block] = turned[h * width : (h + 1) * width].astype(BF16)
        return carry

    lax.fori_loop(0, length // bq, unpack, 0)

    def query_step(qb, carry):
        q0 = pl.multiple_of(qb * bq, bq)
        start = start_ref[qb]
        query_place = q0 + lax.broadcasted_iota(jnp.int32, (1, bq), 1)
        acc[...] = jnp.zeros_like(acc)

        def key_step(kb, tops_totals):
            tops, totals = tops_totals
            k0 = pl.multiple_of(kb * bq, bq)
            key_place = k0 + lax.broadcasted_iota(jnp.int32, (bq, bq), 0)
            allowed = (key_place <= query_place) & (key_place >= start)
            new_tops, new_totals = [], []
            for h in range(heads):
                scores = dot_transposed(ks[h, pl.ds(k0, bq)], qs[h, pl.ds(q0, bq)]) * factor
                scores = jnp.where(allowed, scores, MASKED)
                top = jnp.maximum(tops[h], jnp.max(scores, axis=0, keepdims=True))
                fade = jnp.exp2(tops[h] - top)
                weights = jnp.exp2(scores - top)
                own = slice(h * width, (h + 1) * width)
                acc[own] = acc[own] * fade + dot_rows(vt[h, kb], weights.astype(BF16))
                new_tops.append(top)
                new_totals.append(totals[h] * fade + jnp.sum(weights, axis=0, keepdims=True))
            return tuple(new_tops), tuple(new_totals)

        first = (
            tuple(jnp.full((1, bq), -1e29, F32) for _ in range(heads)),
            tuple(jnp.zeros((1, bq), F32) for _ in range(heads)),
        )
        tops, totals = lax.fori_loop(low_ref[qb], qb + 1, key_step, first)
        for h in range(heads):
            own = slice(h * width, (h + 1) * width)
            acc[own] = acc[own] * (1.0 / totals[h])
            lse_ref[qb, h : h + 1, :] = tops[h] + jnp.log2(totals[h])
        mixed = acc[...]
        outt_ref[qb] = mixed
        out_ref[block_rows(core, qb, bq), :] = mixed.T.astype(BF16)
        return carry

    lax.fori_loop(0, length // bq, query_step, 0)


def attention_backward_body(
    heads,
    width,
    bq,
    low_ref,
    core_ref,
    start_ref,
    qkv_ref,
    dout_ref,
    outt_ref,
    lse_ref,
    grad_ref,
    qs,
    ks,
    vs,
    ds,
    kt,
    dk,
    dv,
    dqt,
):
    length = qkv_ref.shape[0]
    flat = heads * width
    score_scale = width**-0.5
    factor = score_scale * LOG2_E
    core = core_ref[0]

    def unpack(block, carry):
        here = block_rows(core, block, bq)
        there = pl.ds(pl.multiple_of(block * bq, bq), bq)
        for h in range(heads):
            qs[h, there] = qkv_ref[here, h * width : (h + 1) * width]
            ks[h, there] = qkv_ref[here, flat + h * width : flat + (h + 1) * width]
            vs[h, there] = qkv_ref[here, 2 * flat + h * width : 2 * flat + (h + 1) * width]
            ds[h, there] = dout_ref[here, h * width : (h + 1) * width]
        turned = qkv_ref[here, flat : 2 * flat].astype(F32).T
        for h in range(heads):
            kt[h, block] = turned[h * width : (h + 1) * width].astype(BF16)
        return carry

    lax.fori_loop(0, length // bq, unpack, 0)
    dk[...] = jnp.zeros_like(dk)
    dv[...] = jnp.zeros_like(dv)

    def query_step(qb, carry):
        q0 = pl.multiple_of(qb * bq, bq)
        queries = pl.ds(q0, bq)
        here = block_rows(core, qb, bq)
        start = start_ref[qb]
        query_place = q0 + lax.broadcasted_iota(jnp.int32, (1, bq), 1)
        products = dout_ref[here, :].astype(F32).T * outt_ref[qb]
        inners = [
            jnp.sum(products[h * width : (h + 1) * width], axis=0, keepdims=True)
            for h in range(heads)
        ]
        dqt[...] = jnp.zeros_like(dqt)

        def key_step(kb, inner_carry):
            k0 = pl.multiple_of(kb * bq, bq)
            keys = pl.ds(k0, bq)
            key_place = k0 + lax.broadcasted_iota(jnp.int32, (bq, bq), 0)
            allowed = (key_place <= query_place) & (key_place >= start)
            for h in range(heads):
                scores = dot_transposed(ks[h, keys], qs[h, queries]) * factor
                weights = jnp.exp2(
                    jnp.where(allowed, scores - lse_ref[qb, h : h + 1, :], MASKED)
                )
                dweights = dot_transposed(vs[h, keys], ds[h, queries])
                dscores = (weights * (dweights - inners[h])).astype(BF16)
                dv[h, keys] += dot_rows(weights.astype(BF16), ds[h, queries])
                dk[h, keys] += dot_rows(dscores, qs[h, queries])
                dqt[h * width : (h + 1) * width] += dot_rows(kt[h, kb], dscores)
            return inner_carry

        lax.fori_loop(low_ref[qb], qb + 1, key_step, 0)
        grad_ref[here, 0:flat] = (dqt[...] * score_scale).T.astype(BF16)
        return carry

    lax.fori_loop(0, length // bq, query_step, 0)

    def write_keys(kb, carry):
        here = block_rows(core, kb, bq)
        rows = pl.ds(pl.multiple_of(kb * bq, bq), bq)
        grad_ref[here, flat : 2 * flat] = jnp.concatenate(
            [dk[h, rows] * score_scale for h in range(heads)], axis=1
        ).astype(BF16)
        grad_ref[here, 2 * flat : 3 * flat] = jnp.concatenate(
            [dv[h, rows] for h in range(heads)], axis=1
        ).astype(BF16)
        rest = grad_ref.shape[1] - 3 * flat
        if rest:
            grad_ref[here, 3 * flat :] = jnp.zeros((bq, rest), BF16)
        return carry

    lax.fori_loop(0, length // bq, write_keys, 0)


def whole_block(shape):
    return pl.BlockSpec(shape, lambda step, *refs: (0,) * len(shape))


def attention_forward(low_blocks, core, starts, qkv, heads):
    length, triple = qkv.shape
    flat = triple // 3
    width = flat // heads
    blocks, _, bq = starts.shape
    grid_spec = pltpu.PrefetchScalarGridSpec(
        num_scalar_prefetch=2,
        grid=(1,),
        in_specs=[whole_block((blocks, 1, bq)), whole_block((length, triple))],
        out_specs=[
            whole_block((length, flat)),
            whole_block((blocks, flat, bq)),
            whole_block((blocks, 8, bq)),
        ],
        scratch_shapes=[
            pltpu.VMEM((heads, length, width), BF16),
            pltpu.VMEM((heads, length, width), BF16),
            pltpu.VMEM((heads, blocks, width, bq), BF16),
            pltpu.VMEM((flat, bq), F32),
        ],
    )
    return pl.pallas_call(
        functools.partial(attention_forward_body, heads, width, bq),
        out_shape=[
            jax.ShapeDtypeStruct((length, flat), BF16),
            jax.ShapeDtypeStruct((blocks, flat, bq), F32),
            jax.ShapeDtypeStruct((blocks, 8, bq), F32),
        ],
        grid_spec=grid_spec,
        compiler_params=pltpu.CompilerParams(vmem_limit_bytes=48 << 20),
        cost_estimate=lasting(35),
        name="attention_forward",
    )(low_blocks, core, starts, qkv)


def attention_backward(low_blocks, core, starts, qkv, grad_out, out_turned, log_total, heads):
    length, triple = qkv.shape
    flat = triple // 3
    width = flat // heads
    blocks, _, bq = starts.shape
    per_head = pltpu.VMEM((heads, length, width), BF16)
    sums = pltpu.VMEM((heads, length, width), F32)
    grid_spec = pltpu.PrefetchScalarGridSpec(
        num_scalar_prefetch=2,
        grid=(1,),
        in_specs=[
            whole_block((blocks, 1, bq)),
            whole_block((length, triple)),
            whole_block((length, flat)),
            whole_block((blocks, flat, bq)),
            whole_block((blocks, 8, bq)),
        ],
        out_specs=whole_block((length, lanes(triple))),
        scratch_shapes=[
            per_head,
            per_head,
            per_head,
            per_head,
            pltpu.VMEM((heads, blocks, width, bq), BF16),
            sums,
            sums,
            pltpu.VMEM((flat, bq), F32),
        ],
    )
    return pl.pallas_call(
        functools.partial(attention_backward_body, heads, width, bq),
        out_shape=jax.ShapeDtypeStruct((length, lanes(triple)), BF16),
        grid_spec=grid_spec,
        compiler_params=pltpu.CompilerParams(vmem_limit_bytes=60 << 20),
        cost_estimate=lasting(56),
        name="attention_backward",
    )(low_blocks, core, starts, qkv, grad_out, out_turned, log_total)


def lasting(micros):
    return pl.CostEstimate(flops=int(micros * SCALE), bytes_accessed=1 << 12, transcendentals=0)


def lanes(width):
    return -(-width // 128) * 128


def put(ref, value):
    width = value.shape[1]
    ref[:, :width] = value.astype(ref.dtype)
    if width < ref.shape[1]:
        ref[:, width:] = jnp.zeros((value.shape[0], ref.shape[1] - width), ref.dtype)


def vmem(count):
    return pltpu.CompilerParams(vmem_limit_bytes=count << 20)


def fixed(shape):
    return pl.BlockSpec(shape, lambda *step: (0,) * len(shape), pipeline_mode=pl.Buffered(1))


def hbm():
    return pl.BlockSpec(memory_space=pl.ANY)


def round_weights_body(weight_ref, low_ref):
    low_ref[...] = weight_ref[0, 0, :].astype(BF16)


def round_weights(weight):
    whole = pl.BlockSpec(memory_space=pltpu.VMEM)
    return pl.pallas_call(
        round_weights_body,
        in_specs=[whole],
        out_specs=whole,
        out_shape=jax.ShapeDtypeStruct(weight.shape[2:], BF16),
        compiler_params=vmem(32),
        cost_estimate=lasting(6),
        name="round_weights",
    )(weight)


def moments_body(
    ints_ref, floats_ref, lead_ref, rest_ref, first_ref, second_ref, weight_ref,
    grad_ref, moments_ref, update_ref, sums_ref,
):
    step = pl.program_id(0)
    grad = jnp.where(ints_ref[1] == 1, lead_ref[...], rest_ref[...])
    grad_ref[...] = grad
    first = BETA_ONE * first_ref[...] + (1.0 - BETA_ONE) * grad
    second = BETA_TWO * second_ref[...] + (1.0 - BETA_TWO) * grad * grad
    moments_ref[0] = first
    moments_ref[1] = second
    update = (first / floats_ref[0]) / (jnp.sqrt(second / floats_ref[1]) + ADAM_EPS)
    update = update + DECAY * weight_ref[...]
    update_ref[...] = update
    count = grad.shape[2]
    place = step * count + lax.broadcasted_iota(jnp.int32, grad.shape, 2)

    @pl.when(step == 0)
    def clear():
        for index in range(4):
            sums_ref[index] = 0.0

    for index, values in enumerate((weight_ref[...], update)):
        squares = values * values
        lower = jnp.sum(jnp.where(place < ints_ref[0], squares, 0.0))
        sums_ref[2 * index] += lower
        sums_ref[2 * index + 1] += jnp.sum(squares) - lower


def flat_steps(count):
    return 7 if count % (7 * 128) == 0 else 1


def new_moments(ints, floats, lead, rest, first, second, weight):
    count = weight.shape[2]
    steps = flat_steps(count)
    smem = pl.BlockSpec(memory_space=pltpu.SMEM)
    flat = pl.BlockSpec((1, 1, count // steps), lambda i: (0, 0, i))
    pair = pl.BlockSpec((2, 1, 1, count // steps), lambda i: (0, 0, 0, i))
    return pl.pallas_call(
        moments_body,
        grid=(steps,),
        in_specs=[smem, smem] + [flat] * 5,
        out_specs=[flat, pair, flat, smem],
        out_shape=[
            jax.ShapeDtypeStruct(weight.shape, F32),
            jax.ShapeDtypeStruct((2,) + weight.shape, F32),
            jax.ShapeDtypeStruct(weight.shape, F32),
            jax.ShapeDtypeStruct((4,), F32),
        ],
        compiler_params=vmem(48),
        cost_estimate=lasting(10),
        name="new_moments",
    )(ints, floats, lead, rest, first, second, weight)


def new_weights_body(ints_ref, ratio_ref, weight_ref, update_ref, new_ref, copy_ref):
    count = weight_ref.shape[2]
    place = pl.program_id(0) * count + lax.broadcasted_iota(jnp.int32, weight_ref.shape, 2)
    rate = jnp.where(place < ints_ref[0], ratio_ref[0], ratio_ref[1])
    new = weight_ref[...] - MATRIX_RATE * rate * update_ref[...]
    new_ref[...] = new
    copy_ref[...] = new.astype(BF16)


def new_weights(ints, ratios, weight, update):
    count = weight.shape[2]
    steps = flat_steps(count)
    smem = pl.BlockSpec(memory_space=pltpu.SMEM)
    flat = pl.BlockSpec((1, 1, count // steps), lambda i: (0, 0, i))
    return pl.pallas_call(
        new_weights_body,
        grid=(steps,),
        in_specs=[smem, smem, flat, flat],
        out_specs=[flat, flat],
        out_shape=[
            jax.ShapeDtypeStruct(weight.shape, F32),
            jax.ShapeDtypeStruct(weight.shape, BF16),
        ],
        compiler_params=vmem(32),
        cost_estimate=lasting(6),
        name="new_weights",
    )(ints, ratios, weight, update)


def unpack_body(cut, out_rows, in_rows, place_ref, *refs):
    blocks, (w_out, w_in, w_back, held, sems) = refs[:8], refs[8:]
    here = place_ref[0]
    copies = [
        pltpu.make_async_copy(block, held.at[index ^ here], sems.at[index])
        for index, block in enumerate(blocks)
    ]
    for copy in copies:
        copy.start()
    for copy in copies:
        copy.wait()
    begin = 2 * cut
    for target, rows in ((w_out, out_rows), (w_in, in_rows), (w_back, in_rows)):
        done = 0
        while done < rows:
            block, offset = divmod(begin + done, cut)
            count = min(cut - offset, rows - done)
            target[done : done + count] = held[block, offset : offset + count]
            done += count
        begin += rows


def unpack_share(place, blocks, out_rows, in_rows):
    cut, columns = blocks[0].shape
    shapes = [(out_rows, columns), (in_rows, columns), (in_rows, columns)]
    return pl.pallas_call(
        functools.partial(unpack_body, cut, out_rows, in_rows),
        grid_spec=pltpu.PrefetchScalarGridSpec(
            num_scalar_prefetch=1,
            grid=(1,),
            in_specs=[hbm()] * 8,
            out_specs=[whole_block(shape) for shape in shapes],
            scratch_shapes=[
                pltpu.VMEM((8, cut, columns), BF16),
                pltpu.SemaphoreType.DMA((8,)),
            ],
        ),
        out_shape=[jax.ShapeDtypeStruct(shape, BF16) for shape in shapes],
        compiler_params=vmem(48),
        cost_estimate=lasting(6),
        name="unpack_share",
    )(place, *blocks)


def pack_rest_body(
    cut, place_ref, out_ref, in_ref, back_ref, out_got, in_got, back_got, kept_ref, sent_ref
):
    here = place_ref[0]
    place = 0
    for matrix, got in ((out_ref, out_got), (in_ref, in_got), (back_ref, back_got)):
        done, rows = 0, matrix.shape[0]
        while done < rows:
            block, offset = divmod(place, cut)
            count = min(cut - offset, rows - done)
            source = slice(done, done + count)
            target = slice(offset, offset + count)
            plane, side = divmod(block, 2)

            @pl.when(here == side)
            def keep(matrix=matrix, got=got, source=source, target=target, plane=plane):
                kept_ref[plane, target] = matrix[source] + got[source].astype(F32)

            @pl.when(here != side)
            def send(matrix=matrix, got=got, source=source, target=target, plane=plane):
                sent_ref[plane, target] = (matrix[source] + got[source].astype(F32)).astype(BF16)

            done += count
            place += count


def pack_rest(place, matrices, received, cut):
    columns = matrices[0].shape[1]
    whole = pl.BlockSpec(memory_space=pltpu.VMEM)
    return pl.pallas_call(
        functools.partial(pack_rest_body, cut),
        in_specs=[pl.BlockSpec(memory_space=pltpu.SMEM)] + [whole] * 6,
        out_specs=[whole] * 2,
        out_shape=[
            jax.ShapeDtypeStruct((3, cut, columns), F32),
            jax.ShapeDtypeStruct((3, cut, columns), BF16),
        ],
        compiler_params=vmem(40),
        cost_estimate=lasting(10),
        name="pack_rest",
    )(place, *matrices, *received)


def rows_of(step, steps, own_ref, other_ref, width):
    return jnp.where(step < steps, own_ref[:, :width], other_ref[:, :width])


def both_specs(block, width, steps):
    own = pl.BlockSpec((block, width), lambda i, *refs: (jnp.minimum(i, steps - 1), 0))
    other = pl.BlockSpec((block, width), lambda i, *refs: (jnp.maximum(i - steps, 0), 0))
    return own, other


def project_body(
    steps, place_ref, own_ref, other_ref, a0, a1, b0, b1, bias_ref,
    out_a, out_b, rows_ref, w_a, w_b, sems,
):
    step = pl.program_id(0)

    @pl.when(step == 0)
    def load():
        cut = a0.shape[0]
        here = place_ref[0]
        first = pl.ds(pl.multiple_of(here * cut, cut), cut)
        second = pl.ds(pl.multiple_of((1 - here) * cut, cut), cut)
        copies = [
            pltpu.make_async_copy(a0, w_a.at[first], sems.at[0]),
            pltpu.make_async_copy(a1, w_a.at[second], sems.at[1]),
            pltpu.make_async_copy(b0, w_b.at[first], sems.at[2]),
            pltpu.make_async_copy(b1, w_b.at[second], sems.at[3]),
        ]
        for copy in copies:
            copy.start()
        for copy in copies:
            copy.wait()

    rows = rows_of(step, steps, own_ref, other_ref, rows_ref.shape[1])
    rows_ref[...] = rows
    out_a[...] = (dot_rows(rows, w_a[...]) + bias_ref[0:1]).astype(BF16)
    out_b[...] = (dot_rows(rows, w_b[...]) + bias_ref[1:2]).astype(BF16)


def project(place, own, other, halves, biases):
    count, sent_width = own.shape
    cut, triple = halves[0].shape
    model_width = 2 * cut
    block = min(512, count)
    steps = count // block
    row_out = lambda width: pl.BlockSpec((block, width), lambda i, *refs: (i, 0))
    matrix = jax.ShapeDtypeStruct((2 * cut, triple), BF16)
    return pl.pallas_call(
        functools.partial(project_body, steps),
        grid_spec=pltpu.PrefetchScalarGridSpec(
            num_scalar_prefetch=1,
            grid=(2 * steps,),
            in_specs=[*both_specs(block, sent_width, steps)]
            + [hbm()] * 4
            + [fixed((2, triple))],
            out_specs=[row_out(triple), row_out(triple), row_out(model_width)]
            + [pl.BlockSpec(matrix.shape, lambda i, *refs: (0, 0))] * 2,
            scratch_shapes=[pltpu.SemaphoreType.DMA((4,))],
        ),
        out_shape=[jax.ShapeDtypeStruct((2 * count, triple), BF16)] * 2
        + [jax.ShapeDtypeStruct((2 * count, model_width), BF16), matrix, matrix],
        compiler_params=vmem(48),
        cost_estimate=lasting(16),
        name="project",
    )(place, own, other, *halves, biases)


def out_grads_body(steps, own_ref, other_ref, w_a, w_b, out_a, out_b, rows_ref):
    rows = rows_of(pl.program_id(0), steps, own_ref, other_ref, rows_ref.shape[1])
    rows_ref[...] = rows
    out_a[...] = dot_transposed(rows, w_a[...]).astype(BF16)
    out_b[...] = dot_transposed(rows, w_b[...]).astype(BF16)


def out_grads(own, other, w_out):
    count, sent_width = own.shape
    width, model_width = w_out[0].shape
    block = min(512, count)
    steps = count // block
    row_out = lambda columns: pl.BlockSpec((block, columns), lambda i: (i, 0))
    return pl.pallas_call(
        functools.partial(out_grads_body, steps),
        grid=(2 * steps,),
        in_specs=[*both_specs(block, sent_width, steps)] + [fixed(w_out[0].shape)] * 2,
        out_specs=[row_out(width), row_out(width), row_out(model_width)],
        out_shape=[jax.ShapeDtypeStruct((2 * count, width), BF16)] * 2
        + [jax.ShapeDtypeStruct((2 * count, model_width), BF16)],
        compiler_params=vmem(48),
        cost_estimate=lasting(8),
        name="out_grads",
    )(own, other, *w_out)


def row_products(turned, left_refs, weight_refs):
    product = None
    for left, weight in zip(left_refs, weight_refs):
        if turned:
            term = dot_transposed(left[:, : weight.shape[1]], weight[...])
        else:
            term = dot_rows(left[:, : weight.shape[0]], weight[...])
        product = term if product is None else product + term
    return product


def partial_product_body(left, weight, out_ref):
    out_ref[...] = row_products(True, [left], [weight])


def split_product_body(steps, turned, count, *refs):
    lefts, weights, rest = refs[:count], refs[count : 2 * count], refs[2 * count :]
    *partial, sent_ref, kept_ref = rest
    product = row_products(turned, lefts, weights)
    if partial:
        product = product + partial[0][...]
    step = pl.program_id(0)

    @pl.when(step < steps)
    def other_rows():
        put(sent_ref, product)

    @pl.when(step >= steps)
    def own_rows():
        put(kept_ref, product)


def other_first(block, width, steps):
    return pl.BlockSpec((block, width), lambda i: ((i + steps) % (2 * steps), 0))


def partial_product(left, weight):
    count, width = left.shape
    model_width = weight.shape[0]
    block = min(512, count // 2)
    steps = count // 2 // block
    return pl.pallas_call(
        partial_product_body,
        grid=(2 * steps,),
        in_specs=[other_first(block, width, steps), fixed(weight.shape)],
        out_specs=pl.BlockSpec((block, model_width), lambda i: (i, 0)),
        out_shape=jax.ShapeDtypeStruct((count, model_width), F32),
        compiler_params=vmem(48),
        cost_estimate=lasting(9),
        name="partial_product",
    )(left, weight)


def split_product(lefts, weights, turned, model_width, sent_type, partial=()):
    count, width = lefts[0].shape
    block = min(512, count // 2)
    steps = count // 2 // block
    parts = [
        jax.ShapeDtypeStruct((count // 2, lanes(model_width)), sent_type),
        jax.ShapeDtypeStruct((count // 2, model_width), F32),
    ]
    return pl.pallas_call(
        functools.partial(split_product_body, steps, turned, len(lefts)),
        grid=(2 * steps,),
        in_specs=[other_first(block, width, steps)] * len(lefts)
        + [fixed(weight.shape) for weight in weights]
        + [pl.BlockSpec((block, model_width), lambda i: (i, 0))] * len(partial),
        out_specs=[
            pl.BlockSpec((block, lanes(model_width)), lambda i: (jnp.minimum(i, steps - 1), 0)),
            pl.BlockSpec((block, model_width), lambda i: (jnp.maximum(i - steps, 0), 0)),
        ],
        out_shape=parts,
        compiler_params=vmem(48),
        cost_estimate=lasting(9),
        name="split_product",
    )(*lefts, *weights, *partial)


def middle_body(rows_ref, kept_ref, got_ref, small_ref, middle_ref, low_ref):
    middle = rows_ref[...].astype(F32) + (
        kept_ref[...] + got_ref[:, : kept_ref.shape[1]] + small_ref[6:7]
    )
    middle_ref[...] = middle
    hat, _ = norm_stats(middle)
    put(low_ref, (hat * small_ref[2:3] + small_ref[3:4]).astype(BF16))


def middle_norm(rows, kept, got, small):
    count, width = rows.shape
    block = min(256, count)
    part = pl.BlockSpec((block, width), lambda i: (i, 0))
    sent = pl.BlockSpec((block, lanes(width)), lambda i: (i, 0))
    return pl.pallas_call(
        middle_body,
        grid=(count // block,),
        in_specs=[part, part, sent, fixed(small.shape)],
        out_specs=[part, sent],
        out_shape=[
            jax.ShapeDtypeStruct((count, width), F32),
            jax.ShapeDtypeStruct((count, lanes(width)), BF16),
        ],
        compiler_params=vmem(32),
        cost_estimate=lasting(4),
        name="middle_norm",
    )(rows, kept, got, small)


def turn(block):
    return block.astype(F32).T.astype(BF16)


def take_rows_body(chip_ref, array_ref, own_ref, sent_ref):
    rows = turn(array_ref[0, 0])

    @pl.when(pl.program_id(0) == 0)
    def other_micro():
        put(sent_ref, rows)

    @pl.when(pl.program_id(0) == 1)
    def own_micro():
        put(own_ref, rows)


def take_rows(chip, array):
    turned = jnp.swapaxes(array, 2, 3)
    _, _, width, count = turned.shape
    out = pl.BlockSpec((count, lanes(width)), lambda i, chip_ref: (0, 0))
    return pl.pallas_call(
        take_rows_body,
        grid_spec=pltpu.PrefetchScalarGridSpec(
            num_scalar_prefetch=1,
            grid=(2,),
            in_specs=[
                pl.BlockSpec(
                    (1, 1, width, count),
                    lambda i, chip_ref: (jnp.where(i == 0, 1 - chip_ref[0], chip_ref[0]), 0, 0, 0),
                )
            ],
            out_specs=[out, out],
        ),
        out_shape=[jax.ShapeDtypeStruct((count, lanes(width)), BF16)] * 2,
        compiler_params=vmem(32),
        cost_estimate=lasting(4),
        name="take_rows",
    )(chip, turned)


def place_rows_body(chip_ref, rows_ref, received_ref, out_ref):
    width = out_ref.shape[2]
    rows = jnp.where(
        pl.program_id(0) == chip_ref[0], rows_ref[:, :width], received_ref[:, :width]
    )
    out_ref[0, 0] = turn(rows)


def place_rows(chip, rows, received, width):
    count, sent_width = received.shape
    turned = pl.pallas_call(
        place_rows_body,
        grid_spec=pltpu.PrefetchScalarGridSpec(
            num_scalar_prefetch=1,
            grid=(2,),
            in_specs=[
                pl.BlockSpec((count, sent_width), lambda i, chip_ref: (chip_ref[0], 0)),
                pl.BlockSpec((count, sent_width), lambda i, chip_ref: (0, 0)),
            ],
            out_specs=pl.BlockSpec((1, 1, width, count), lambda i, chip_ref: (i, 0, 0, 0)),
        ),
        out_shape=jax.ShapeDtypeStruct((2, 1, width, count), BF16),
        compiler_params=vmem(32),
        cost_estimate=lasting(4),
        name="place_rows",
    )(chip, rows, received)
    return jnp.swapaxes(turned, 2, 3)


def norm_back_body(wide_out, rows_ref, kept_ref, got_ref, base_ref, gain_ref, *outs):
    (full_ref, low_ref, sums_ref) = outs if wide_out else (None, *outs)
    rows = rows_ref[...].astype(F32)
    hat, scale = norm_stats(rows)
    width = rows.shape[1]
    upstream = kept_ref[:, :width] + got_ref[:, :width].astype(F32)
    base = base_ref[:, :width].astype(F32)
    grad = base + norm_backward(upstream, hat, scale, gain_ref[...])
    low = grad.astype(BF16)
    if wide_out:
        full_ref[...] = grad
    put(low_ref, low)

    @pl.when(pl.program_id(0) == 0)
    def clear():
        sums_ref[...] = jnp.zeros_like(sums_ref)

    for index, term in enumerate((upstream * hat, upstream, low.astype(F32), base)):
        sums_ref[index : index + 1] += jnp.sum(term, axis=0, keepdims=True)


def norm_back(rows, kept, got, base, gain, wide_out):
    count, width = rows.shape
    block = min(256, count)
    part = pl.BlockSpec((block, width), lambda i: (i, 0))
    sent = pl.BlockSpec((block, lanes(width)), lambda i: (i, 0))
    full = [jax.ShapeDtypeStruct((count, width), F32)] if wide_out else []
    return pl.pallas_call(
        functools.partial(norm_back_body, wide_out),
        grid=(count // block,),
        in_specs=[part, pl.BlockSpec((block, kept.shape[1]), lambda i: (i, 0)), sent]
        + [pl.BlockSpec((block, base.shape[1]), lambda i: (i, 0)), fixed((1, width))],
        out_specs=[part] * len(full) + [sent, pl.BlockSpec((8, width), lambda i: (0, 0))],
        out_shape=full
        + [
            jax.ShapeDtypeStruct((count, lanes(width)), BF16),
            jax.ShapeDtypeStruct((8, width), F32),
        ],
        compiler_params=vmem(40),
        cost_estimate=lasting(7),
        name="norm_back",
    )(rows, kept, got, base, gain)


def feed_forward_body(
    skipped,
    rows_ref,
    cot_ref,
    w_in_mine,
    w_in_theirs,
    w_back_mine,
    w_back_theirs,
    bias_ref,
    *refs,
):
    (
        act_mine, act_theirs, inner_mine, inner_theirs, rows_out, cot_out, out_ref, up_ref, sums_ref
    ) = refs[skipped:]
    model_width = rows_out.shape[1]
    rows, cot = rows_ref[:, :model_width], cot_ref[:, :model_width]
    rows_out[...] = rows
    cot_out[...] = cot

    @pl.when(pl.program_id(0) == 0)
    def clear():
        sums_ref[...] = jnp.zeros_like(sums_ref)

    out, up = None, None
    shares = (
        (w_in_mine, w_back_mine, act_mine, inner_mine),
        (w_in_theirs, w_back_theirs, act_theirs, inner_theirs),
    )
    for part, (w_in, w_back, act_ref, inner_ref) in enumerate(shares):
        hidden = dot_rows(rows, w_in[...]) + bias_ref[part : part + 1]
        value, slope = gelu_parts(hidden)
        act = value.astype(BF16)
        act_ref[...] = act
        inner = (dot_transposed(cot, w_back[...]) * slope).astype(BF16)
        inner_ref[...] = inner
        sums_ref[part : part + 1] += jnp.sum(inner.astype(F32), axis=0, keepdims=True)
        one_out = dot_rows(act, w_back[...])
        one_up = dot_transposed(inner, w_in[...])
        out = one_out if out is None else out + one_out
        up = one_up if up is None else up + one_up
    put(out_ref, out)
    put(up_ref, up)


def feed_forward(rows, cot, half, weights, biases, filled):
    count, sent_width = rows.shape
    model_width, ff_share = weights[0].shape
    block = min(FF_ROWS, count)
    steps = count // block
    row_spec = pl.BlockSpec((block, sent_width), lambda i: (i, 0))
    joined = lambda width: pl.BlockSpec((block, width), lambda i: (half * steps + i, 0))
    act_shape = jax.ShapeDtypeStruct((2 * count, ff_share), BF16)
    row_shape = jax.ShapeDtypeStruct((2 * count, model_width), BF16)
    part_shape = jax.ShapeDtypeStruct((count, sent_width), F32)
    filled = () if filled is None else tuple(filled)
    return pl.pallas_call(
        functools.partial(feed_forward_body, len(filled)),
        out_shape=[act_shape] * 4
        + [row_shape] * 2
        + [part_shape] * 2
        + [jax.ShapeDtypeStruct((8, ff_share), F32)],
        grid=(steps,),
        in_specs=[row_spec, row_spec]
        + [fixed(matrix.shape) for matrix in weights]
        + [fixed((2, ff_share))]
        + [hbm()] * len(filled),
        out_specs=[joined(ff_share)] * 4
        + [joined(model_width)] * 2
        + [row_spec] * 2
        + [pl.BlockSpec((8, ff_share), lambda i: (0, 0))],
        input_output_aliases={7 + i: i for i in range(len(filled))},
        compiler_params=vmem(58),
        cost_estimate=lasting(34),
        name="feed_forward",
    )(rows, cot, *weights, biases, *filled)


def permute(value, axis_name, pairs):
    return lax.ppermute(value, axis_name, pairs)


def swap(value, axis_name, distance):
    count = lax.axis_size(axis_name)
    return permute(value, axis_name, [(i, i ^ distance) for i in range(count)])


def tie(*values):
    return lax.optimization_barrier(values)


def started(sent, value, mark):
    sent, mark = tie(sent, mark)
    value, mark = tie(value, swap(mark, "seq", 1))
    return sent, value, mark


def lower_pairs(pairs, y_count):
    return [
        (source * y_count + y, target * y_count + y)
        for source, target in pairs
        for y in range(y_count)
    ]


def spread_lead(block, z_here):
    far = permute(block, "dp", lower_pairs([(0, 2)], 2))
    held = jnp.where(z_here == 0, block, far)
    near = permute(held, "dp", lower_pairs([(0, 1), (2, 3)], 2))
    return jnp.where(z_here % 2 == 0, held, near)


def move_rest(block, distance, plane_distance):
    over_dp, over_seq = distance
    pairs = []
    for d in range(8):
        if (d // 2) ^ plane_distance != 0:
            pairs += [(d * 4 + q, (d ^ over_dp) * 4 + (q ^ over_seq)) for q in range(4)]
    return permute(block, ("dp", "seq"), pairs)


def pick(stacked, index, axis=0):
    return lax.dynamic_index_in_dim(stacked, index, axis, keepdims=False)


def halve_plane(lower, upper, y_here):
    return (
        jnp.where(y_here == 0, lower, upper),
        jnp.where(y_here == 0, upper, lower).astype(BF16),
    )


def sum_everywhere(value):
    for axis_name in ("seq", "dp"):
        distance = 1
        while distance < lax.axis_size(axis_name):
            value = value + swap(value, axis_name, distance)
            distance *= 2
    return value


def per_device(
    rows_in,
    out_cotangent,
    cell_lengths,
    cell_starts,
    key_mask,
    weights_master,
    first_moment,
    second_moment,
    small_master,
    small_first,
    small_second,
    step_count,
):
    model_width = rows_in.shape[3]
    local_rows = rows_in.shape[2]
    length = key_mask.shape[2]
    shard_len = weights_master.shape[2]
    groups = lax.axis_size("seq")
    dp_count = lax.axis_size("dp")
    head_share = model_width // groups
    heads_here = HEADS // groups
    triple = 3 * head_share
    first_end = model_width * triple
    second_end = first_end + head_share * model_width
    third_end = second_end + model_width * model_width
    seq_here = lax.axis_index("seq")
    dp_here = lax.axis_index("dp")
    chip = seq_here // 2
    core = seq_here % 2
    z_here = dp_here // 2
    y_here = dp_here % 2
    planar = dp_count == 8 and shard_len * 2 == first_end
    shares = (core + 2 * chip, core + 2 * (1 - chip))

    chip_index = chip.reshape(1).astype(jnp.int32)

    def exchange_micro(own, sent):
        received = swap(sent, "seq", 2)
        first = jnp.where(chip == 0, own, received)
        second = jnp.where(chip == 0, received, own)
        return jnp.concatenate([first, second], axis=0)

    def widen(rows):
        return jnp.pad(rows, ((0, 0), (0, lanes(model_width) - model_width)))

    mark = small_master[:8, :128]

    ends = jnp.array([first_end, second_end, third_end, dp_count * shard_len], jnp.int32)
    begin = dp_here * shard_len
    lower_matrix = jnp.sum((begin >= ends).astype(jnp.int32))
    upper_matrix = jnp.sum((begin + shard_len - 1 >= ends).astype(jnp.int32))
    bound = jnp.minimum(pick(ends, lower_matrix) - begin, shard_len).reshape(1)
    matrices = jnp.arange(4, dtype=jnp.int32)

    def matrix_sums(pair):
        return jnp.where(matrices == lower_matrix, pair[0], 0.0) + jnp.where(
            matrices == upper_matrix, pair[1], 0.0
        )

    weight = weights_master
    low_weight = round_weights(weight)
    if planar:
        tall = low_weight.reshape(shard_len // triple, triple)
    own_first, sent_rows = take_rows(chip_index, rows_in)
    own_in = exchange_micro(own_first, sent_rows)[:, :model_width]
    own_cotangent, sent_cotangent = take_rows(chip_index, out_cotangent)
    inputs = own_in.astype(F32)
    hat_one, _ = norm_stats(inputs)
    low_one = widen((hat_one * small_master[0] + small_master[1]).astype(BF16))
    other_one = swap(low_one, "seq", 1)
    y_index = y_here.reshape(1).astype(jnp.int32)
    if planar:
        wide = low_weight.reshape(shard_len // model_width, model_width)
        cut, tall_rows = wide.shape[0], tall.shape[0]
        lead = spread_lead(tall, z_here)
        across = [move_rest(wide, (1, 0), 0)]
        over = [move_rest(wide, (0, 2), 0)]
        lead, wide, across[0], over[0], other_one, sent_cotangent = tie(
            lead, wide, across[0], over[0], other_one, sent_cotangent
        )
        lead_across = swap(lead, "dp", 1)
        halves = (lead, lead_across, swap(lead, "seq", 2), swap(lead_across, "seq", 2))
        dp_index = dp_here.reshape(1).astype(jnp.int32)
        far = move_rest(wide, (4, 0), 0)
        near = move_rest(wide, (2, 0), 0)
    else:
        copies = lax.all_gather(low_weight.reshape(1, shard_len), ("dp", "seq"), axis=0, tiled=True)
        copies = copies.reshape(dp_count, groups, shard_len)
        per_share = [pick(copies, share, 1).reshape(dp_count * shard_len) for share in shares]
        halves = []
        for flat in per_share:
            matrix = flat[:first_end].reshape(model_width, triple)
            first = jnp.where(y_here == 0, matrix[: model_width // 2], matrix[model_width // 2 :])
            second = jnp.where(y_here == 0, matrix[model_width // 2 :], matrix[: model_width // 2])
            halves += [first, second]
        w_out = [flat[first_end:second_end].reshape(head_share, model_width) for flat in per_share]
        w_in = [flat[second_end:third_end].reshape(model_width, model_width) for flat in per_share]
        w_back = [flat[third_end:].reshape(model_width, model_width) for flat in per_share]

    def share_columns(vector, share):
        return lax.dynamic_slice_in_dim(vector, share * head_share, head_share)

    attn_biases = [
        jnp.concatenate(
            [
                share_columns(small_master[4], share),
                jnp.zeros((head_share,), F32),
                share_columns(small_master[5], share),
            ]
        )
        for share in shares
    ]
    ff_biases = jnp.stack([pick(small_master, 8 + share) for share in shares])

    starts = pick(cell_starts[:, 0], chip)
    lengths = pick(cell_lengths[:, 0], chip)
    places = jnp.arange(length, dtype=jnp.int32)
    inside = (places[:, None] >= starts[None, :]) & (places[:, None] < (starts + lengths)[None, :])
    first_key = jnp.max(jnp.where(inside, starts[None, :], -1), axis=1)
    first_key = jnp.where(first_key < 0, places, first_key)
    low_blocks = first_key.reshape(-1, local_rows)[:, 0] // local_rows
    block_starts = first_key.reshape(-1, 1, local_rows)
    core_index = core.reshape(1).astype(jnp.int32)

    if planar:
        both = [move_rest(over[0], (1, 0), 0)]
        halves, near, far, both[0] = tie(halves, near, far, both[0])
        last = move_rest(far, (2, 0), 2)
        across += [move_rest(near, (1, 0), 1), move_rest(far, (1, 0), 2)]
        over += [move_rest(near, (0, 2), 1), move_rest(far, (0, 2), 2)]
    *qkv, rows_one, w_attn_mine, w_attn_theirs = project(
        y_index, low_one, other_one, halves, jnp.stack(attn_biases)
    )

    def attend(part):
        return attention_forward(low_blocks, core_index, block_starts, qkv[part], heads_here)

    attended = [attend(0)]
    if planar:
        qkv[1], last, across[1:3], over[1:3], sent_cotangent, _ = tie(
            qkv[1], last, across[1:3], over[1:3], sent_cotangent, attended[0][2]
        )
        across.append(move_rest(last, (1, 0), 3))
        over.append(move_rest(last, (0, 2), 3))
        both += [move_rest(over[1], (1, 0), 1), move_rest(across[2], (0, 2), 2)]
    own_e = exchange_micro(own_cotangent, sent_cotangent)
    attended.append(attend(1))
    if planar:
        dp_index, across, over, both, _ = tie(dp_index, across, over, both, attended[1][2])
        both.append(move_rest(over[3], (1, 0), 3))
        rest_mine = [block for pair in zip((wide, near, far, last), across) for block in pair]
        rest_theirs = [block for pair in zip(over, both) for block in pair]
        matrices_mine = unpack_share(dp_index, rest_mine, head_share, model_width)
        matrices_theirs = unpack_share(dp_index, rest_theirs, head_share, model_width)
        w_out, w_in, w_back = (list(pair) for pair in zip(matrices_mine, matrices_theirs))
        own_e, w_out[0] = tie(own_e, w_out[0])
    other_e = swap(own_e, "seq", 1)
    sent, kept = split_product([attended[0][0], attended[1][0]], w_out, False, model_width, F32)
    middle, low_two = middle_norm(own_in, kept, swap(sent, "seq", 1), small_master)
    other_two = swap(low_two, "seq", 1)

    weights = (w_in[0], w_in[1], w_back[0], w_back[1])
    *filled, out_sent, up_sent, sums_sent = feed_forward(
        other_two, other_e, 1, weights, ff_biases, None
    )
    out_received = swap(out_sent, "seq", 1)
    up_received = swap(up_sent, "seq", 1)
    *filled, out_kept, up_kept, sums_kept = feed_forward(
        low_two, own_e, 0, weights, ff_biases, filled
    )
    activated, inner, (rows_two, rows_e) = filled[:2], filled[2:4], filled[4:]
    inner_sums = sums_sent + sums_kept

    link = BF16 if planar else F32
    grad_mid, low_mid, sums_two = norm_back(
        middle, up_kept, up_received, own_e, small_master[2:3], True
    )
    low_mid, rows_two, rows_e = tie(low_mid, rows_two, rows_e)
    back_sent = dot_columns(activated[1], rows_e).astype(link)
    in_sent = dot_columns(rows_two, inner[1]).astype(link)
    back_sent, in_sent, low_mid = tie(back_sent, in_sent, low_mid)
    other_mid = swap(low_mid, "seq", 1)
    back_received = swap(back_sent, "seq", 2)
    in_received = swap(in_sent, "seq", 2)

    grad_att_mine, grad_att_theirs, rows_mid = out_grads(low_mid, other_mid, w_out)
    out_sent_theirs = dot_columns(attended[1][0], rows_mid).astype(link)
    out_sent_theirs, rows_two, rows_e, rows_mid = tie(out_sent_theirs, rows_two, rows_e, rows_mid)
    outer_received = swap(out_sent_theirs, "seq", 2)
    share_back = dot_columns(activated[0], rows_e)
    share_in = dot_columns(rows_two, inner[0])
    share_out = dot_columns(attended[0][0], rows_mid)
    share_back, share_in, share_out, grad_att_theirs = tie(
        share_back, share_in, share_out, grad_att_theirs
    )

    def return_rows(lower, upper):
        return swap(jnp.where(chip == 0, upper, lower), "seq", 2)

    def attend_back(part, grad_att):
        return attention_backward(
            low_blocks,
            core_index,
            block_starts,
            qkv[part],
            grad_att,
            attended[part][1],
            attended[part][2],
            heads_here,
        )

    packed_theirs = attend_back(1, grad_att_theirs)
    attn_sent = dot_columns(rows_one, packed_theirs).astype(link)
    attn_sent, packed_theirs = tie(attn_sent, packed_theirs)
    theirs_part = partial_product(packed_theirs, w_attn_theirs)
    attn_sent, theirs_part, y_index, out_received = tie(
        attn_sent, theirs_part, y_index, out_received
    )
    attn_received = swap(attn_sent, "seq", 2)
    if planar:
        kept_rest, sent_rest = pack_rest(
            y_index,
            (share_out, share_in, share_back),
            (outer_received, in_received, back_received),
            cut,
        )
        result_rows = widen(
            (middle + ((out_kept + out_received)[:, :model_width] + small_master[7])).astype(BF16)
        )
        sent_rest, grad_att_mine, result_rows = tie(sent_rest, grad_att_mine, result_rows)
        result_halves = (result_rows[:local_rows], result_rows[local_rows:])
        result_received = return_rows(*result_halves)
        got_rest = swap(sent_rest, "dp", 1)
    else:
        result_rows = widen(
            (middle + ((out_kept + out_received)[:, :model_width] + small_master[7])).astype(BF16)
        )
        result_halves = (result_rows[:local_rows], result_rows[local_rows:])
        result_received = return_rows(*result_halves)
        share_back, share_in, share_out = (
            share_back + back_received,
            share_in + in_received,
            share_out + outer_received,
        )

    packed_mine = attend_back(0, grad_att_mine)
    packed_mine, result_received = tie(packed_mine, result_received)
    sent, kept = split_product(
        [packed_mine], [w_attn_mine], True, model_width, BF16, [theirs_part]
    )
    packed_mine, sent = tie(packed_mine, sent)
    share_attn = dot_columns(rows_one, packed_mine) + attn_received.astype(F32)
    if planar:
        z_odd = z_here % 2 == 1
        kept_lead, sent_lead = halve_plane(share_attn[:tall_rows], share_attn[tall_rows:], y_here)
        kept_lead, sent_lead, kept_rest = tie(kept_lead, sent_lead, kept_rest)
        got_lead = swap(sent_lead, "dp", 1)
        held = [kept_rest[i] + got_rest[i].astype(F32) for i in range(3)]
        sent_near = jnp.where(z_odd, held[1], held[0]).astype(BF16)
        sent_last = held[2].astype(BF16)
        kept_near = jnp.where(z_odd, held[0], held[1])
        kept_last = held[2]
        sent_near, sent_last, kept_lead = tie(sent_near, sent_last, kept_lead)
        got_near = swap(sent_near, "dp", 2)
        got_last = permute(sent_last, "dp", lower_pairs([(0, 1), (2, 3)], 2))
    packed = [packed_mine, packed_theirs]
    if planar:
        held_lead = kept_lead + got_lead.astype(F32)
        sent_lead = held_lead.astype(BF16)
        sent_lead, held_lead, kept_near, kept_last = tie(
            sent_lead, held_lead, kept_near, kept_last
        )
        near_lead = permute(sent_lead, "dp", lower_pairs([(1, 0), (3, 2)], 2))
        held_near = kept_near + got_near.astype(F32)
        held_last = kept_last + got_last.astype(F32)
        sent_far = jnp.where(z_here == 1, held_last, held_near).astype(BF16)
        own_rest = jnp.where(z_here == 3, held_last, held_near)
        sent_far, own_rest, kept = tie(sent_far, own_rest, kept)
        got_far = permute(sent_far, "dp", lower_pairs([(3, 1), (0, 2), (1, 3)], 2))
    grad_x, sums_one = norm_back(
        own_in, kept, swap(sent, "seq", 1), grad_mid, small_master[0:1], False
    )
    if planar:
        sums_one, held_lead = tie(sums_one, held_lead)
        held_lead = held_lead + near_lead.astype(F32)
        sent_lead = held_lead.astype(BF16)
        sent_lead, held_lead, own_rest, grad_x = tie(sent_lead, held_lead, own_rest, grad_x)
        sent_lead, own_rest, mark = started(sent_lead, own_rest, mark)
        far_lead = permute(sent_lead, "dp", lower_pairs([(2, 0)], 2))

    result_all = place_rows(chip_index, result_rows, result_received, model_width)
    grad_halves = (grad_x[:local_rows], grad_x[local_rows:])
    grad_all = place_rows(chip_index, grad_x, return_rows(*grad_halves), model_width)

    def at_shares(columns):
        row = jnp.zeros((model_width,), F32)
        for share, column in zip(shares, columns):
            row = lax.dynamic_update_slice(row, column, (share * head_share,))
        return row

    bias_sums = [jnp.sum(packed[part].astype(F32), axis=0) for part in range(2)]
    inner_rows = jnp.zeros((4, model_width), F32)
    for part in range(2):
        inner_rows = lax.dynamic_update_slice(
            inner_rows, inner_sums[part : part + 1], (shares[part], 0)
        )
    small_now = jnp.concatenate(
        [
            sums_one[:2],
            sums_two[:2],
            at_shares([sums[:head_share] for sums in bias_sums])[None],
            at_shares([sums[2 * head_share : triple] for sums in bias_sums])[None],
            sums_two[2:4],
            inner_rows,
        ]
    )

    if planar:
        rest_grad = (own_rest + got_far.astype(F32)).reshape(1, 1, shard_len)
        held_lead, rest_grad, result_all, grad_all, small_now = tie(
            held_lead, rest_grad, result_all, grad_all, small_now
        )
        lead_grad = (held_lead + far_lead.astype(F32))[:, :triple].reshape(1, 1, shard_len)
        leads = z_here == 0
    else:
        flat_here = jnp.concatenate(
            [matrix.reshape(-1) for matrix in (share_attn[:, :triple], share_out, share_in, share_back)]
        )
        lead_grad = lax.psum_scatter(
            flat_here.reshape(dp_count, shard_len), "dp", scatter_dimension=0, tiled=True
        ).reshape(1, 1, shard_len)
        rest_grad = lead_grad
        leads = z_here >= 0

    steps_done = step_count[0].astype(F32)
    fix_one = 1.0 - jnp.exp(steps_done * math.log(BETA_ONE))
    fix_two = 1.0 - jnp.exp(steps_done * math.log(BETA_TWO))
    ints = jnp.concatenate([bound, leads.astype(jnp.int32).reshape(1)])
    reduced, moments, update, matrix_squares = new_moments(
        ints,
        jnp.stack([fix_one, fix_two]),
        lead_grad,
        rest_grad,
        first_moment,
        second_moment,
        weight,
    )
    matrix_rows = jnp.stack([matrix_sums(matrix_squares[:2]), matrix_sums(matrix_squares[2:])])
    small_sum = sum_everywhere(
        jnp.concatenate([small_now, jnp.pad(matrix_rows, ((0, 2), (0, model_width - 4)))])
    )
    small_grad = small_sum[:12]
    weight_norms = jnp.sqrt(small_sum[12, :4])
    update_norms = jnp.sqrt(small_sum[13, :4])
    ratios = weight_norms / update_norms
    new_weight, weight_copy = new_weights(
        ints, jnp.stack([pick(ratios, lower_matrix), pick(ratios, upper_matrix)]), weight, update
    )
    small_one = BETA_ONE * small_first + (1.0 - BETA_ONE) * small_grad
    small_two = BETA_TWO * small_second + (1.0 - BETA_TWO) * small_grad * small_grad
    small_late = lax.dynamic_update_slice(small_master, mark, (0, 0))
    small_updated = small_late - SMALL_RATE * (small_one / fix_one) / (
        jnp.sqrt(small_two / fix_two) + ADAM_EPS
    )
    return (
        result_all,
        grad_all,
        reduced,
        moments,
        new_weight,
        weight_copy,
        jnp.stack([weight_norms, update_norms, ratios]),
        small_grad,
        jnp.stack([small_one, small_two]),
        small_updated,
    )


def solution(mesh):
    in_specs = (
        P(None, "dp", "seq", None),
        P(None, "dp", "seq", None),
        P(None, "dp", None),
        P(None, "dp", None),
        P(None, "dp", None),
        P("dp", "seq", None),
        P("dp", "seq", None),
        P("dp", "seq", None),
        P(),
        P(),
        P(),
        P(),
    )
    out_specs = (
        P(None, "dp", "seq", None),
        P(None, "dp", "seq", None),
        P("dp", "seq", None),
        P(None, "dp", "seq", None),
        P("dp", "seq", None),
        P("dp", "seq", None),
        P(),
        P(),
        P(),
        P(),
    )
    return jax.shard_map(
        per_device, mesh=mesh, in_specs=in_specs, out_specs=out_specs, check_vma=False
    )
```

```python
import functools
import math

import jax
import jax.numpy as jnp
from jax import lax
from jax.experimental import pallas as pl
from jax.experimental.pallas import tpu as pltpu
from jax.sharding import PartitionSpec as P

HEADS = 20


NORM_EPS = 1e-05
BETA_ONE = 0.9
BETA_TWO = 0.999
ADAM_EPS = 1e-06
DECAY = 0.01
MATRIX_RATE = 0.3
SMALL_RATE = 0.25
MASKED = -1e30
LOG2_E = 1.4426950408889634
FF_ROWS = 256
SCALE = 1e9

F32 = jnp.float32
BF16 = jnp.bfloat16


def dot_rows(left, right):
    return lax.dot_general(left, right, (((1,), (0,)), ((), ())), preferred_element_type=F32)


def dot_transposed(left, right):
    return lax.dot_general(left, right, (((1,), (1,)), ((), ())), preferred_element_type=F32)


def dot_columns(left, right):
    return lax.dot_general(left, right, (((0,), (0,)), ((), ())), preferred_element_type=F32)


def norm_stats(rows):
    center = jnp.mean(rows, axis=-1, keepdims=True)
    centered = rows - center
    spread = jnp.mean(centered * centered, axis=-1, keepdims=True)
    scale = lax.rsqrt(spread + NORM_EPS)
    return centered * scale, scale


def norm_backward(upstream, hat, scale, gain):
    weighted = upstream * gain
    return (
        weighted
        - jnp.mean(weighted, axis=-1, keepdims=True)
        - hat * jnp.mean(weighted * hat, axis=-1, keepdims=True)
    ) * scale


def gelu_parts(values):
    inner = math.sqrt(2.0 / math.pi)
    squares = values * values
    bent = jnp.tanh(inner * (values + 0.044715 * values * squares))
    half = 0.5 * (1.0 + bent)
    slope = half + 0.5 * values * (1.0 - bent * bent) * inner * (1.0 + 3.0 * 0.044715 * squares)
    return values * half, slope


def block_place(core, block):
    return jnp.where(block % 2 == core, 0, 2) + block // 2


def block_rows(core, block, rows):
    return pl.ds(pl.multiple_of(block_place(core, block) * rows, rows), rows)


def attention_forward_body(
    heads, width, bq, low_ref, core_ref, start_ref, qkv_ref, out_ref, outt_ref, lse_ref, qs, ks, vt, acc
):
    length = qkv_ref.shape[0]
    flat = heads * width
    factor = width**-0.5 * LOG2_E
    core = core_ref[0]

    def unpack(block, carry):
        here = block_rows(core, block, bq)
        there = pl.ds(pl.multiple_of(block * bq, bq), bq)
        for h in range(heads):
            qs[h, there] = qkv_ref[here, h * width : (h + 1) * width]
            ks[h, there] = qkv_ref[here, flat + h * width : flat + (h + 1) * width]
        turned = qkv_ref[here, 2 * flat : 3 * flat].astype(F32).T
        for h in range(heads):
            vt[h, block] = turned[h * width : (h + 1) * width].astype(BF16)
        return carry

    lax.fori_loop(0, length // bq, unpack, 0)

    def query_step(qb, carry):
        q0 = pl.multiple_of(qb * bq, bq)
        start = start_ref[qb]
        query_place = q0 + lax.broadcasted_iota(jnp.int32, (1, bq), 1)
        acc[...] = jnp.zeros_like(acc)

        def key_step(kb, tops_totals):
            tops, totals = tops_totals
            k0 = pl.multiple_of(kb * bq, bq)
            key_place = k0 + lax.broadcasted_iota(jnp.int32, (bq, bq), 0)
            allowed = (key_place <= query_place) & (key_place >= start)
            new_tops, new_totals = [], []
            for h in range(heads):
                scores = dot_transposed(ks[h, pl.ds(k0, bq)], qs[h, pl.ds(q0, bq)]) * factor
                scores = jnp.where(allowed, scores, MASKED)
                top = jnp.maximum(tops[h], jnp.max(scores, axis=0, keepdims=True))
                fade = jnp.exp2(tops[h] - top)
                weights = jnp.exp2(scores - top)
                own = slice(h * width, (h + 1) * width)
                acc[own] = acc[own] * fade + dot_rows(vt[h, kb], weights.astype(BF16))
                new_tops.append(top)
                new_totals.append(totals[h] * fade + jnp.sum(weights, axis=0, keepdims=True))
            return tuple(new_tops), tuple(new_totals)

        first = (
            tuple(jnp.full((1, bq), -1e29, F32) for _ in range(heads)),
            tuple(jnp.zeros((1, bq), F32) for _ in range(heads)),
        )
        tops, totals = lax.fori_loop(low_ref[qb], qb + 1, key_step, first)
        for h in range(heads):
            own = slice(h * width, (h + 1) * width)
            acc[own] = acc[own] * (1.0 / totals[h])
            lse_ref[qb, h : h + 1, :] = tops[h] + jnp.log2(totals[h])
        mixed = acc[...]
        outt_ref[qb] = mixed
        out_ref[block_rows(core, qb, bq), :] = mixed.T.astype(BF16)
        return carry

    lax.fori_loop(0, length // bq, query_step, 0)


def attention_backward_body(
    heads,
    width,
    bq,
    low_ref,
    core_ref,
    start_ref,
    qkv_ref,
    dout_ref,
    outt_ref,
    lse_ref,
    grad_ref,
    qs,
    ks,
    vs,
    ds,
    kt,
    dk,
    dv,
    dqt,
):
    length = qkv_ref.shape[0]
    flat = heads * width
    score_scale = width**-0.5
    factor = score_scale * LOG2_E
    core = core_ref[0]

    def unpack(block, carry):
        here = block_rows(core, block, bq)
        there = pl.ds(pl.multiple_of(block * bq, bq), bq)
        for h in range(heads):
            qs[h, there] = qkv_ref[here, h * width : (h + 1) * width]
            ks[h, there] = qkv_ref[here, flat + h * width : flat + (h + 1) * width]
            vs[h, there] = qkv_ref[here, 2 * flat + h * width : 2 * flat + (h + 1) * width]
            ds[h, there] = dout_ref[here, h * width : (h + 1) * width]
        turned = qkv_ref[here, flat : 2 * flat].astype(F32).T
        for h in range(heads):
            kt[h, block] = turned[h * width : (h + 1) * width].astype(BF16)
        return carry

    lax.fori_loop(0, length // bq, unpack, 0)
    dk[...] = jnp.zeros_like(dk)
    dv[...] = jnp.zeros_like(dv)

    def query_step(qb, carry):
        q0 = pl.multiple_of(qb * bq, bq)
        queries = pl.ds(q0, bq)
        here = block_rows(core, qb, bq)
        start = start_ref[qb]
        query_place = q0 + lax.broadcasted_iota(jnp.int32, (1, bq), 1)
        products = dout_ref[here, :].astype(F32).T * outt_ref[qb]
        inners = [
            jnp.sum(products[h * width : (h + 1) * width], axis=0, keepdims=True)
            for h in range(heads)
        ]
        dqt[...] = jnp.zeros_like(dqt)

        def attend(key_block, key_part, query_part):
            key_count = key_part.stop - key_part.start
            count = query_part.stop - query_part.start
            k0 = pl.multiple_of(key_block * bq + key_part.start, key_count)
            keys = pl.ds(k0, key_count)
            rows = pl.ds(pl.multiple_of(q0 + query_part.start, count), count)
            key_place = k0 + lax.broadcasted_iota(jnp.int32, (key_count, count), 0)
            allowed = (key_place <= query_place[:, query_part]) & (
                key_place >= start[:, query_part]
            )
            for h in range(heads):
                scores = dot_transposed(ks[h, keys], qs[h, rows]) * factor
                weights = jnp.exp2(
                    jnp.where(allowed, scores - lse_ref[qb, h : h + 1, query_part], MASKED)
                )
                dweights = dot_transposed(vs[h, keys], ds[h, rows])
                dscores = (weights * (dweights - inners[h][:, query_part])).astype(BF16)
                dv[h, keys] += dot_rows(weights.astype(BF16), ds[h, rows])
                dk[h, keys] += dot_rows(dscores, qs[h, rows])
                dqt[h * width : (h + 1) * width, query_part] += dot_rows(
                    kt[h, key_block, :, key_part], dscores
                )

        every = slice(0, bq)

        def key_step(kb, inner_carry):
            attend(kb, every, every)
            return inner_carry

        lax.fori_loop(low_ref[qb], qb, key_step, 0)
        attend(qb, slice(0, bq // 2), every)
        attend(qb, slice(bq // 2, bq), slice(bq // 2, bq))
        grad_ref[here, 0:flat] = (dqt[...] * score_scale).T.astype(BF16)
        return carry

    lax.fori_loop(0, length // bq, query_step, 0)

    def write_keys(kb, carry):
        here = block_rows(core, kb, bq)
        rows = pl.ds(pl.multiple_of(kb * bq, bq), bq)
        grad_ref[here, flat : 2 * flat] = jnp.concatenate(
            [dk[h, rows] * score_scale for h in range(heads)], axis=1
        ).astype(BF16)
        grad_ref[here, 2 * flat : 3 * flat] = jnp.concatenate(
            [dv[h, rows] for h in range(heads)], axis=1
        ).astype(BF16)
        rest = grad_ref.shape[1] - 3 * flat
        if rest:
            grad_ref[here, 3 * flat :] = jnp.zeros((bq, rest), BF16)
        return carry

    lax.fori_loop(0, length // bq, write_keys, 0)


def whole_block(shape):
    return pl.BlockSpec(shape, lambda step, *refs: (0,) * len(shape))


def attention_forward(low_blocks, core, starts, qkv, heads):
    length, triple = qkv.shape
    flat = triple // 3
    width = flat // heads
    blocks, _, bq = starts.shape
    grid_spec = pltpu.PrefetchScalarGridSpec(
        num_scalar_prefetch=2,
        grid=(1,),
        in_specs=[whole_block((blocks, 1, bq)), whole_block((length, triple))],
        out_specs=[
            whole_block((length, flat)),
            whole_block((blocks, flat, bq)),
            whole_block((blocks, 8, bq)),
        ],
        scratch_shapes=[
            pltpu.VMEM((heads, length, width), BF16),
            pltpu.VMEM((heads, length, width), BF16),
            pltpu.VMEM((heads, blocks, width, bq), BF16),
            pltpu.VMEM((flat, bq), F32),
        ],
    )
    return pl.pallas_call(
        functools.partial(attention_forward_body, heads, width, bq),
        out_shape=[
            jax.ShapeDtypeStruct((length, flat), BF16),
            jax.ShapeDtypeStruct((blocks, flat, bq), F32),
            jax.ShapeDtypeStruct((blocks, 8, bq), F32),
        ],
        grid_spec=grid_spec,
        compiler_params=pltpu.CompilerParams(vmem_limit_bytes=48 << 20),
        cost_estimate=lasting(35),
        name="attention_forward",
    )(low_blocks, core, starts, qkv)


def attention_backward(low_blocks, core, starts, qkv, grad_out, out_turned, log_total, heads):
    length, triple = qkv.shape
    flat = triple // 3
    width = flat // heads
    blocks, _, bq = starts.shape
    per_head = pltpu.VMEM((heads, length, width), BF16)
    sums = pltpu.VMEM((heads, length, width), F32)
    grid_spec = pltpu.PrefetchScalarGridSpec(
        num_scalar_prefetch=2,
        grid=(1,),
        in_specs=[
            whole_block((blocks, 1, bq)),
            whole_block((length, triple)),
            whole_block((length, flat)),
            whole_block((blocks, flat, bq)),
            whole_block((blocks, 8, bq)),
        ],
        out_specs=whole_block((length, lanes(triple))),
        scratch_shapes=[
            per_head,
            per_head,
            per_head,
            per_head,
            pltpu.VMEM((heads, blocks, width, bq), BF16),
            sums,
            sums,
            pltpu.VMEM((flat, bq), F32),
        ],
    )
    return pl.pallas_call(
        functools.partial(attention_backward_body, heads, width, bq),
        out_shape=jax.ShapeDtypeStruct((length, lanes(triple)), BF16),
        grid_spec=grid_spec,
        compiler_params=pltpu.CompilerParams(vmem_limit_bytes=60 << 20),
        cost_estimate=lasting(56),
        name="attention_backward",
    )(low_blocks, core, starts, qkv, grad_out, out_turned, log_total)


def lasting(micros):
    return pl.CostEstimate(flops=int(micros * SCALE), bytes_accessed=1 << 12, transcendentals=0)


def lanes(width):
    return -(-width // 128) * 128


def put(ref, value):
    width = value.shape[1]
    ref[:, :width] = value.astype(ref.dtype)
    if width < ref.shape[1]:
        ref[:, width:] = jnp.zeros((value.shape[0], ref.shape[1] - width), ref.dtype)


def vmem(count):
    return pltpu.CompilerParams(vmem_limit_bytes=count << 20)


def fixed(shape):
    return pl.BlockSpec(shape, lambda *step: (0,) * len(shape), pipeline_mode=pl.Buffered(1))


def hbm():
    return pl.BlockSpec(memory_space=pl.ANY)


def round_weights_body(weight_ref, low_ref):
    low_ref[...] = weight_ref[0, 0, :].astype(BF16)


def round_weights(weight):
    whole = pl.BlockSpec(memory_space=pltpu.VMEM)
    return pl.pallas_call(
        round_weights_body,
        in_specs=[whole],
        out_specs=whole,
        out_shape=jax.ShapeDtypeStruct(weight.shape[2:], BF16),
        compiler_params=vmem(32),
        cost_estimate=lasting(6),
        name="round_weights",
    )(weight)


def add_squares(sums_ref, values, in_lower):
    squares = values * values
    lower = jnp.sum(jnp.where(in_lower, squares, 0.0))
    sums_ref[0] += lower
    sums_ref[1] += jnp.sum(squares) - lower


def square_sums_body(bound_ref, weight_ref, sums_ref):
    sums_ref[0] = 0.0
    sums_ref[1] = 0.0
    place = lax.broadcasted_iota(jnp.int32, weight_ref.shape, 2)
    add_squares(sums_ref, weight_ref[...], place < bound_ref[0])


def square_sums(bound, weight):
    smem = pl.BlockSpec(memory_space=pltpu.SMEM)
    return pl.pallas_call(
        square_sums_body,
        in_specs=[smem, pl.BlockSpec(memory_space=pltpu.VMEM)],
        out_specs=smem,
        out_shape=jax.ShapeDtypeStruct((2,), F32),
        compiler_params=vmem(32),
        cost_estimate=lasting(6),
        name="square_sums",
    )(bound, weight)


def moments_body(
    ints_ref, floats_ref, lead_ref, rest_ref, first_ref, second_ref, weight_ref,
    grad_ref, moments_ref, update_ref, sums_ref,
):
    step = pl.program_id(0)
    grad = jnp.where(ints_ref[1] == 1, lead_ref[...], rest_ref[...])
    grad_ref[...] = grad
    first = BETA_ONE * first_ref[...] + (1.0 - BETA_ONE) * grad
    second = BETA_TWO * second_ref[...] + (1.0 - BETA_TWO) * grad * grad
    moments_ref[0] = first
    moments_ref[1] = second
    update = (first / floats_ref[0]) / (jnp.sqrt(second / floats_ref[1]) + ADAM_EPS)
    update = update + DECAY * weight_ref[...]
    update_ref[...] = update
    count = grad.shape[2]
    place = step * count + lax.broadcasted_iota(jnp.int32, grad.shape, 2)

    @pl.when(step == 0)
    def clear():
        sums_ref[0] = 0.0
        sums_ref[1] = 0.0

    add_squares(sums_ref, update, place < ints_ref[0])


def flat_steps(count):
    return 7 if count % (7 * 128) == 0 else 1


def new_moments(ints, floats, lead, rest, first, second, weight):
    count = weight.shape[2]
    steps = flat_steps(count)
    smem = pl.BlockSpec(memory_space=pltpu.SMEM)
    flat = pl.BlockSpec((1, 1, count // steps), lambda i: (0, 0, i))
    pair = pl.BlockSpec((2, 1, 1, count // steps), lambda i: (0, 0, 0, i))
    return pl.pallas_call(
        moments_body,
        grid=(steps,),
        in_specs=[smem, smem] + [flat] * 5,
        out_specs=[flat, pair, flat, smem],
        out_shape=[
            jax.ShapeDtypeStruct(weight.shape, F32),
            jax.ShapeDtypeStruct((2,) + weight.shape, F32),
            jax.ShapeDtypeStruct(weight.shape, F32),
            jax.ShapeDtypeStruct((2,), F32),
        ],
        compiler_params=vmem(48),
        cost_estimate=lasting(10),
        name="new_moments",
    )(ints, floats, lead, rest, first, second, weight)


def new_weights_body(ints_ref, ratio_ref, weight_ref, update_ref, new_ref, copy_ref):
    count = weight_ref.shape[2]
    place = pl.program_id(0) * count + lax.broadcasted_iota(jnp.int32, weight_ref.shape, 2)
    rate = jnp.where(place < ints_ref[0], ratio_ref[0], ratio_ref[1])
    new = weight_ref[...] - MATRIX_RATE * rate * update_ref[...]
    new_ref[...] = new
    copy_ref[...] = new.astype(BF16)


def new_weights(ints, ratios, weight, update):
    count = weight.shape[2]
    steps = flat_steps(count)
    smem = pl.BlockSpec(memory_space=pltpu.SMEM)
    flat = pl.BlockSpec((1, 1, count // steps), lambda i: (0, 0, i))
    return pl.pallas_call(
        new_weights_body,
        grid=(steps,),
        in_specs=[smem, smem, flat, flat],
        out_specs=[flat, flat],
        out_shape=[
            jax.ShapeDtypeStruct(weight.shape, F32),
            jax.ShapeDtypeStruct(weight.shape, BF16),
        ],
        compiler_params=vmem(32),
        cost_estimate=lasting(6),
        name="new_weights",
    )(ints, ratios, weight, update)


def unpack_body(cut, out_rows, in_rows, place_ref, *refs):
    blocks, (w_out, w_in, w_back, held, sems) = refs[:8], refs[8:]
    here = place_ref[0]
    copies = [
        pltpu.make_async_copy(block, held.at[index ^ here], sems.at[index])
        for index, block in enumerate(blocks)
    ]
    for copy in copies:
        copy.start()
    for copy in copies:
        copy.wait()
    begin = 2 * cut
    for target, rows in ((w_out, out_rows), (w_in, in_rows), (w_back, in_rows)):
        done = 0
        while done < rows:
            block, offset = divmod(begin + done, cut)
            count = min(cut - offset, rows - done)
            target[done : done + count] = held[block, offset : offset + count]
            done += count
        begin += rows


def unpack_share(place, blocks, out_rows, in_rows):
    cut, columns = blocks[0].shape
    shapes = [(out_rows, columns), (in_rows, columns), (in_rows, columns)]
    return pl.pallas_call(
        functools.partial(unpack_body, cut, out_rows, in_rows),
        grid_spec=pltpu.PrefetchScalarGridSpec(
            num_scalar_prefetch=1,
            grid=(1,),
            in_specs=[hbm()] * 8,
            out_specs=[whole_block(shape) for shape in shapes],
            scratch_shapes=[
                pltpu.VMEM((8, cut, columns), BF16),
                pltpu.SemaphoreType.DMA((8,)),
            ],
        ),
        out_shape=[jax.ShapeDtypeStruct(shape, BF16) for shape in shapes],
        compiler_params=vmem(48),
        cost_estimate=lasting(6),
        name="unpack_share",
    )(place, *blocks)


def pack_rest_body(
    cut, place_ref, out_ref, in_ref, back_ref, out_got, in_got, back_got, kept_ref, sent_ref
):
    here = place_ref[0]
    place = 0
    for matrix, got in ((out_ref, out_got), (in_ref, in_got), (back_ref, back_got)):
        done, rows = 0, matrix.shape[0]
        while done < rows:
            block, offset = divmod(place, cut)
            count = min(cut - offset, rows - done)
            source = slice(done, done + count)
            target = slice(offset, offset + count)
            plane, side = divmod(block, 2)

            @pl.when(here == side)
            def keep(matrix=matrix, got=got, source=source, target=target, plane=plane):
                kept_ref[plane, target] = matrix[source] + got[source].astype(F32)

            @pl.when(here != side)
            def send(matrix=matrix, got=got, source=source, target=target, plane=plane):
                sent_ref[plane, target] = (matrix[source] + got[source].astype(F32)).astype(BF16)

            done += count
            place += count


def pack_rest(place, matrices, received, cut):
    columns = matrices[0].shape[1]
    whole = pl.BlockSpec(memory_space=pltpu.VMEM)
    return pl.pallas_call(
        functools.partial(pack_rest_body, cut),
        in_specs=[pl.BlockSpec(memory_space=pltpu.SMEM)] + [whole] * 6,
        out_specs=[whole] * 2,
        out_shape=[
            jax.ShapeDtypeStruct((3, cut, columns), F32),
            jax.ShapeDtypeStruct((3, cut, columns), BF16),
        ],
        compiler_params=vmem(40),
        cost_estimate=lasting(10),
        name="pack_rest",
    )(place, *matrices, *received)


def rows_of(step, steps, own_ref, other_ref, width):
    return jnp.where(step < steps, own_ref[:, :width], other_ref[:, :width])


def both_specs(block, width, steps):
    own = pl.BlockSpec((block, width), lambda i, *refs: (jnp.minimum(i, steps - 1), 0))
    other = pl.BlockSpec((block, width), lambda i, *refs: (jnp.maximum(i - steps, 0), 0))
    return own, other


def project_body(
    steps, place_ref, own_ref, other_ref, a0, a1, b0, b1, bias_ref,
    out_a, out_b, rows_ref, w_a, w_b, sems,
):
    step = pl.program_id(0)

    @pl.when(step == 0)
    def load():
        cut = a0.shape[0]
        here = place_ref[0]
        first = pl.ds(pl.multiple_of(here * cut, cut), cut)
        second = pl.ds(pl.multiple_of((1 - here) * cut, cut), cut)
        copies = [
            pltpu.make_async_copy(a0, w_a.at[first], sems.at[0]),
            pltpu.make_async_copy(a1, w_a.at[second], sems.at[1]),
            pltpu.make_async_copy(b0, w_b.at[first], sems.at[2]),
            pltpu.make_async_copy(b1, w_b.at[second], sems.at[3]),
        ]
        for copy in copies:
            copy.start()
        for copy in copies:
            copy.wait()

    rows = rows_of(step, steps, own_ref, other_ref, rows_ref.shape[1])
    rows_ref[...] = rows
    out_a[...] = (dot_rows(rows, w_a[...]) + bias_ref[0:1]).astype(BF16)
    out_b[...] = (dot_rows(rows, w_b[...]) + bias_ref[1:2]).astype(BF16)


def project(place, own, other, halves, biases):
    count, sent_width = own.shape
    cut, triple = halves[0].shape
    model_width = 2 * cut
    block = min(512, count)
    steps = count // block
    row_out = lambda width: pl.BlockSpec((block, width), lambda i, *refs: (i, 0))
    matrix = jax.ShapeDtypeStruct((2 * cut, triple), BF16)
    return pl.pallas_call(
        functools.partial(project_body, steps),
        grid_spec=pltpu.PrefetchScalarGridSpec(
            num_scalar_prefetch=1,
            grid=(2 * steps,),
            in_specs=[*both_specs(block, sent_width, steps)]
            + [hbm()] * 4
            + [fixed((2, triple))],
            out_specs=[row_out(triple), row_out(triple), row_out(model_width)]
            + [pl.BlockSpec(matrix.shape, lambda i, *refs: (0, 0))] * 2,
            scratch_shapes=[pltpu.SemaphoreType.DMA((4,))],
        ),
        out_shape=[jax.ShapeDtypeStruct((2 * count, triple), BF16)] * 2
        + [jax.ShapeDtypeStruct((2 * count, model_width), BF16), matrix, matrix],
        compiler_params=vmem(48),
        cost_estimate=lasting(16),
        name="project",
    )(place, own, other, *halves, biases)


def out_grads_body(steps, own_ref, other_ref, w_a, w_b, out_a, out_b, rows_ref):
    rows = rows_of(pl.program_id(0), steps, own_ref, other_ref, rows_ref.shape[1])
    rows_ref[...] = rows
    out_a[...] = dot_transposed(rows, w_a[...]).astype(BF16)
    out_b[...] = dot_transposed(rows, w_b[...]).astype(BF16)


def out_grads(own, other, w_out):
    count, sent_width = own.shape
    width, model_width = w_out[0].shape
    block = min(512, count)
    steps = count // block
    row_out = lambda columns: pl.BlockSpec((block, columns), lambda i: (i, 0))
    return pl.pallas_call(
        functools.partial(out_grads_body, steps),
        grid=(2 * steps,),
        in_specs=[*both_specs(block, sent_width, steps)] + [fixed(w_out[0].shape)] * 2,
        out_specs=[row_out(width), row_out(width), row_out(model_width)],
        out_shape=[jax.ShapeDtypeStruct((2 * count, width), BF16)] * 2
        + [jax.ShapeDtypeStruct((2 * count, model_width), BF16)],
        compiler_params=vmem(48),
        cost_estimate=lasting(8),
        name="out_grads",
    )(own, other, *w_out)


def row_products(turned, left_refs, weight_refs):
    product = None
    for left, weight in zip(left_refs, weight_refs):
        if turned:
            term = dot_transposed(left[:, : weight.shape[1]], weight[...])
        else:
            term = dot_rows(left[:, : weight.shape[0]], weight[...])
        product = term if product is None else product + term
    return product


def partial_product_body(left, weight, out_ref):
    out_ref[...] = row_products(True, [left], [weight])


def split_product_body(steps, turned, count, *refs):
    lefts, weights, rest = refs[:count], refs[count : 2 * count], refs[2 * count :]
    *partial, sent_ref, kept_ref = rest
    product = row_products(turned, lefts, weights)
    if partial:
        product = product + partial[0][...]
    step = pl.program_id(0)

    @pl.when(step < steps)
    def other_rows():
        put(sent_ref, product)

    @pl.when(step >= steps)
    def own_rows():
        put(kept_ref, product)


def other_first(block, width, steps):
    return pl.BlockSpec((block, width), lambda i: ((i + steps) % (2 * steps), 0))


def partial_product(left, weight):
    count, width = left.shape
    model_width = weight.shape[0]
    block = min(512, count // 2)
    steps = count // 2 // block
    return pl.pallas_call(
        partial_product_body,
        grid=(2 * steps,),
        in_specs=[other_first(block, width, steps), fixed(weight.shape)],
        out_specs=pl.BlockSpec((block, model_width), lambda i: (i, 0)),
        out_shape=jax.ShapeDtypeStruct((count, model_width), F32),
        compiler_params=vmem(48),
        cost_estimate=lasting(9),
        name="partial_product",
    )(left, weight)


def split_product(lefts, weights, turned, model_width, sent_type, partial=()):
    count, width = lefts[0].shape
    block = min(512, count // 2)
    steps = count // 2 // block
    parts = [
        jax.ShapeDtypeStruct((count // 2, lanes(model_width)), sent_type),
        jax.ShapeDtypeStruct((count // 2, model_width), F32),
    ]
    return pl.pallas_call(
        functools.partial(split_product_body, steps, turned, len(lefts)),
        grid=(2 * steps,),
        in_specs=[other_first(block, width, steps)] * len(lefts)
        + [fixed(weight.shape) for weight in weights]
        + [pl.BlockSpec((block, model_width), lambda i: (i, 0))] * len(partial),
        out_specs=[
            pl.BlockSpec((block, lanes(model_width)), lambda i: (jnp.minimum(i, steps - 1), 0)),
            pl.BlockSpec((block, model_width), lambda i: (jnp.maximum(i - steps, 0), 0)),
        ],
        out_shape=parts,
        compiler_params=vmem(48),
        cost_estimate=lasting(9),
        name="split_product",
    )(*lefts, *weights, *partial)


def middle_body(rows_ref, kept_ref, got_ref, small_ref, middle_ref, low_ref):
    middle = rows_ref[...].astype(F32) + (
        kept_ref[...] + got_ref[:, : kept_ref.shape[1]] + small_ref[6:7]
    )
    middle_ref[...] = middle
    hat, _ = norm_stats(middle)
    put(low_ref, (hat * small_ref[2:3] + small_ref[3:4]).astype(BF16))


def middle_norm(rows, kept, got, small):
    count, width = rows.shape
    block = min(256, count)
    part = pl.BlockSpec((block, width), lambda i: (i, 0))
    sent = pl.BlockSpec((block, lanes(width)), lambda i: (i, 0))
    return pl.pallas_call(
        middle_body,
        grid=(count // block,),
        in_specs=[part, part, sent, fixed(small.shape)],
        out_specs=[part, sent],
        out_shape=[
            jax.ShapeDtypeStruct((count, width), F32),
            jax.ShapeDtypeStruct((count, lanes(width)), BF16),
        ],
        compiler_params=vmem(32),
        cost_estimate=lasting(4),
        name="middle_norm",
    )(rows, kept, got, small)


def turn(block):
    return block.astype(F32).T.astype(BF16)


def take_rows_body(chip_ref, array_ref, own_ref, sent_ref):
    rows = turn(array_ref[0, 0])

    @pl.when(pl.program_id(0) == 0)
    def other_micro():
        put(sent_ref, rows)

    @pl.when(pl.program_id(0) == 1)
    def own_micro():
        put(own_ref, rows)


def take_rows(chip, array):
    turned = jnp.swapaxes(array, 2, 3)
    _, _, width, count = turned.shape
    out = pl.BlockSpec((count, lanes(width)), lambda i, chip_ref: (0, 0))
    return pl.pallas_call(
        take_rows_body,
        grid_spec=pltpu.PrefetchScalarGridSpec(
            num_scalar_prefetch=1,
            grid=(2,),
            in_specs=[
                pl.BlockSpec(
                    (1, 1, width, count),
                    lambda i, chip_ref: (jnp.where(i == 0, 1 - chip_ref[0], chip_ref[0]), 0, 0, 0),
                )
            ],
            out_specs=[out, out],
        ),
        out_shape=[jax.ShapeDtypeStruct((count, lanes(width)), BF16)] * 2,
        compiler_params=vmem(32),
        cost_estimate=lasting(4),
        name="take_rows",
    )(chip, turned)


def place_rows_body(chip_ref, rows_ref, received_ref, out_ref):
    width = out_ref.shape[2]
    rows = jnp.where(
        pl.program_id(0) == chip_ref[0], rows_ref[:, :width], received_ref[:, :width]
    )
    out_ref[0, 0] = turn(rows)


def place_rows(chip, rows, received, width):
    count, sent_width = received.shape
    turned = pl.pallas_call(
        place_rows_body,
        grid_spec=pltpu.PrefetchScalarGridSpec(
            num_scalar_prefetch=1,
            grid=(2,),
            in_specs=[
                pl.BlockSpec((count, sent_width), lambda i, chip_ref: (chip_ref[0], 0)),
                pl.BlockSpec((count, sent_width), lambda i, chip_ref: (0, 0)),
            ],
            out_specs=pl.BlockSpec((1, 1, width, count), lambda i, chip_ref: (i, 0, 0, 0)),
        ),
        out_shape=jax.ShapeDtypeStruct((2, 1, width, count), BF16),
        compiler_params=vmem(32),
        cost_estimate=lasting(4),
        name="place_rows",
    )(chip, rows, received)
    return jnp.swapaxes(turned, 2, 3)


def norm_back_body(wide_out, rows_ref, kept_ref, got_ref, base_ref, gain_ref, *outs):
    (full_ref, low_ref, sums_ref) = outs if wide_out else (None, *outs)
    rows = rows_ref[...].astype(F32)
    hat, scale = norm_stats(rows)
    width = rows.shape[1]
    upstream = kept_ref[:, :width] + got_ref[:, :width].astype(F32)
    base = base_ref[:, :width].astype(F32)
    grad = base + norm_backward(upstream, hat, scale, gain_ref[...])
    low = grad.astype(BF16)
    if wide_out:
        full_ref[...] = grad
    put(low_ref, low)

    @pl.when(pl.program_id(0) == 0)
    def clear():
        sums_ref[...] = jnp.zeros_like(sums_ref)

    for index, term in enumerate((upstream * hat, upstream, low.astype(F32), base)):
        sums_ref[index : index + 1] += jnp.sum(term, axis=0, keepdims=True)


def norm_back(rows, kept, got, base, gain, wide_out):
    count, width = rows.shape
    block = min(256, count)
    part = pl.BlockSpec((block, width), lambda i: (i, 0))
    sent = pl.BlockSpec((block, lanes(width)), lambda i: (i, 0))
    full = [jax.ShapeDtypeStruct((count, width), F32)] if wide_out else []
    return pl.pallas_call(
        functools.partial(norm_back_body, wide_out),
        grid=(count // block,),
        in_specs=[part, pl.BlockSpec((block, kept.shape[1]), lambda i: (i, 0)), sent]
        + [pl.BlockSpec((block, base.shape[1]), lambda i: (i, 0)), fixed((1, width))],
        out_specs=[part] * len(full) + [sent, pl.BlockSpec((8, width), lambda i: (0, 0))],
        out_shape=full
        + [
            jax.ShapeDtypeStruct((count, lanes(width)), BF16),
            jax.ShapeDtypeStruct((8, width), F32),
        ],
        compiler_params=vmem(40),
        cost_estimate=lasting(7),
        name="norm_back",
    )(rows, kept, got, base, gain)


def feed_forward_body(
    skipped,
    rows_ref,
    cot_ref,
    w_in_mine,
    w_in_theirs,
    w_back_mine,
    w_back_theirs,
    bias_ref,
    *refs,
):
    (
        act_mine, act_theirs, inner_mine, inner_theirs, rows_out, cot_out, out_ref, up_ref, sums_ref
    ) = refs[skipped:]
    model_width = rows_out.shape[1]
    rows, cot = rows_ref[:, :model_width], cot_ref[:, :model_width]
    rows_out[...] = rows
    cot_out[...] = cot

    @pl.when(pl.program_id(0) == 0)
    def clear():
        sums_ref[...] = jnp.zeros_like(sums_ref)

    out, up = None, None
    shares = (
        (w_in_mine, w_back_mine, act_mine, inner_mine),
        (w_in_theirs, w_back_theirs, act_theirs, inner_theirs),
    )
    for part, (w_in, w_back, act_ref, inner_ref) in enumerate(shares):
        hidden = dot_rows(rows, w_in[...]) + bias_ref[part : part + 1]
        value, slope = gelu_parts(hidden)
        act = value.astype(BF16)
        act_ref[...] = act
        inner = (dot_transposed(cot, w_back[...]) * slope).astype(BF16)
        inner_ref[...] = inner
        sums_ref[part : part + 1] += jnp.sum(inner.astype(F32), axis=0, keepdims=True)
        one_out = dot_rows(act, w_back[...])
        one_up = dot_transposed(inner, w_in[...])
        out = one_out if out is None else out + one_out
        up = one_up if up is None else up + one_up
    put(out_ref, out)
    put(up_ref, up)


def feed_forward(rows, cot, half, weights, biases, filled):
    count, sent_width = rows.shape
    model_width, ff_share = weights[0].shape
    block = min(FF_ROWS, count)
    steps = count // block
    row_spec = pl.BlockSpec((block, sent_width), lambda i: (i, 0))
    joined = lambda width: pl.BlockSpec((block, width), lambda i: (half * steps + i, 0))
    act_shape = jax.ShapeDtypeStruct((2 * count, ff_share), BF16)
    row_shape = jax.ShapeDtypeStruct((2 * count, model_width), BF16)
    part_shape = jax.ShapeDtypeStruct((count, sent_width), F32)
    filled = () if filled is None else tuple(filled)
    return pl.pallas_call(
        functools.partial(feed_forward_body, len(filled)),
        out_shape=[act_shape] * 4
        + [row_shape] * 2
        + [part_shape] * 2
        + [jax.ShapeDtypeStruct((8, ff_share), F32)],
        grid=(steps,),
        in_specs=[row_spec, row_spec]
        + [fixed(matrix.shape) for matrix in weights]
        + [fixed((2, ff_share))]
        + [hbm()] * len(filled),
        out_specs=[joined(ff_share)] * 4
        + [joined(model_width)] * 2
        + [row_spec] * 2
        + [pl.BlockSpec((8, ff_share), lambda i: (0, 0))],
        input_output_aliases={7 + i: i for i in range(len(filled))},
        compiler_params=vmem(58),
        cost_estimate=lasting(34),
        name="feed_forward",
    )(rows, cot, *weights, biases, *filled)


def permute(value, axis_name, pairs):
    return lax.ppermute(value, axis_name, pairs)


def swap(value, axis_name, distance):
    count = lax.axis_size(axis_name)
    return permute(value, axis_name, [(i, i ^ distance) for i in range(count)])


def tie(*values):
    return lax.optimization_barrier(values)


def started(sent, value, mark):
    sent, mark = tie(sent, mark)
    value, mark = tie(value, swap(mark, "seq", 1))
    return sent, value, mark


def lower_pairs(pairs, y_count):
    return [
        (source * y_count + y, target * y_count + y)
        for source, target in pairs
        for y in range(y_count)
    ]


def spread_lead(block, z_here):
    far = permute(block, "dp", lower_pairs([(0, 2)], 2))
    held = jnp.where(z_here == 0, block, far)
    near = permute(held, "dp", lower_pairs([(0, 1), (2, 3)], 2))
    return jnp.where(z_here % 2 == 0, held, near)


def move_rest(block, distance, plane_distance):
    over_dp, over_seq = distance
    pairs = []
    for d in range(8):
        if (d // 2) ^ plane_distance != 0:
            pairs += [(d * 4 + q, (d ^ over_dp) * 4 + (q ^ over_seq)) for q in range(4)]
    return permute(block, ("dp", "seq"), pairs)


def pick(stacked, index, axis=0):
    return lax.dynamic_index_in_dim(stacked, index, axis, keepdims=False)


def halve_plane(lower, upper, y_here):
    return (
        jnp.where(y_here == 0, lower, upper),
        jnp.where(y_here == 0, upper, lower).astype(BF16),
    )


def sum_everywhere(value):
    for axis_name in ("seq", "dp"):
        distance = 1
        while distance < lax.axis_size(axis_name):
            value = value + swap(value, axis_name, distance)
            distance *= 2
    return value


def per_device(
    rows_in,
    out_cotangent,
    cell_lengths,
    cell_starts,
    key_mask,
    weights_master,
    first_moment,
    second_moment,
    small_master,
    small_first,
    small_second,
    step_count,
):
    model_width = rows_in.shape[3]
    local_rows = rows_in.shape[2]
    length = key_mask.shape[2]
    shard_len = weights_master.shape[2]
    groups = lax.axis_size("seq")
    dp_count = lax.axis_size("dp")
    head_share = model_width // groups
    heads_here = HEADS // groups
    triple = 3 * head_share
    first_end = model_width * triple
    second_end = first_end + head_share * model_width
    third_end = second_end + model_width * model_width
    seq_here = lax.axis_index("seq")
    dp_here = lax.axis_index("dp")
    chip = seq_here // 2
    core = seq_here % 2
    z_here = dp_here // 2
    y_here = dp_here % 2
    planar = dp_count == 8 and shard_len * 2 == first_end
    shares = (core + 2 * chip, core + 2 * (1 - chip))

    chip_index = chip.reshape(1).astype(jnp.int32)

    def exchange_micro(own, sent):
        received = swap(sent, "seq", 2)
        first = jnp.where(chip == 0, own, received)
        second = jnp.where(chip == 0, received, own)
        return jnp.concatenate([first, second], axis=0)

    def widen(rows):
        return jnp.pad(rows, ((0, 0), (0, lanes(model_width) - model_width)))

    mark = small_master[:8, :128]

    ends = jnp.array([first_end, second_end, third_end, dp_count * shard_len], jnp.int32)
    begin = dp_here * shard_len
    lower_matrix = jnp.sum((begin >= ends).astype(jnp.int32))
    upper_matrix = jnp.sum((begin + shard_len - 1 >= ends).astype(jnp.int32))
    bound = jnp.minimum(pick(ends, lower_matrix) - begin, shard_len).reshape(1)
    matrices = jnp.arange(4, dtype=jnp.int32)

    def matrix_sums(pair):
        return jnp.where(matrices == lower_matrix, pair[0], 0.0) + jnp.where(
            matrices == upper_matrix, pair[1], 0.0
        )

    weight = weights_master
    low_weight = round_weights(weight)
    if planar:
        tall = low_weight.reshape(shard_len // triple, triple)
    own_first, sent_rows = take_rows(chip_index, rows_in)
    own_in = exchange_micro(own_first, sent_rows)[:, :model_width]
    own_cotangent, sent_cotangent = take_rows(chip_index, out_cotangent)
    inputs = own_in.astype(F32)
    hat_one, _ = norm_stats(inputs)
    low_one = widen((hat_one * small_master[0] + small_master[1]).astype(BF16))
    other_one = swap(low_one, "seq", 1)
    weight_squares = square_sums(bound, weight)
    y_index = y_here.reshape(1).astype(jnp.int32)
    if planar:
        wide = low_weight.reshape(shard_len // model_width, model_width)
        cut, tall_rows = wide.shape[0], tall.shape[0]
        lead = spread_lead(tall, z_here)
        across = [move_rest(wide, (1, 0), 0)]
        over = [move_rest(wide, (0, 2), 0)]
        lead, wide, across[0], over[0], other_one, sent_cotangent = tie(
            lead, wide, across[0], over[0], other_one, sent_cotangent
        )
        lead_across = swap(lead, "dp", 1)
        halves = (lead, lead_across, swap(lead, "seq", 2), swap(lead_across, "seq", 2))
        dp_index = dp_here.reshape(1).astype(jnp.int32)
        far = move_rest(wide, (4, 0), 0)
        near = move_rest(wide, (2, 0), 0)
    else:
        copies = lax.all_gather(low_weight.reshape(1, shard_len), ("dp", "seq"), axis=0, tiled=True)
        copies = copies.reshape(dp_count, groups, shard_len)
        per_share = [pick(copies, share, 1).reshape(dp_count * shard_len) for share in shares]
        halves = []
        for flat in per_share:
            matrix = flat[:first_end].reshape(model_width, triple)
            first = jnp.where(y_here == 0, matrix[: model_width // 2], matrix[model_width // 2 :])
            second = jnp.where(y_here == 0, matrix[model_width // 2 :], matrix[: model_width // 2])
            halves += [first, second]
        w_out = [flat[first_end:second_end].reshape(head_share, model_width) for flat in per_share]
        w_in = [flat[second_end:third_end].reshape(model_width, model_width) for flat in per_share]
        w_back = [flat[third_end:].reshape(model_width, model_width) for flat in per_share]

    def share_columns(vector, share):
        return lax.dynamic_slice_in_dim(vector, share * head_share, head_share)

    attn_biases = [
        jnp.concatenate(
            [
                share_columns(small_master[4], share),
                jnp.zeros((head_share,), F32),
                share_columns(small_master[5], share),
            ]
        )
        for share in shares
    ]
    ff_biases = jnp.stack([pick(small_master, 8 + share) for share in shares])

    starts = pick(cell_starts[:, 0], chip)
    lengths = pick(cell_lengths[:, 0], chip)
    places = jnp.arange(length, dtype=jnp.int32)
    inside = (places[:, None] >= starts[None, :]) & (places[:, None] < (starts + lengths)[None, :])
    first_key = jnp.max(jnp.where(inside, starts[None, :], -1), axis=1)
    first_key = jnp.where(first_key < 0, places, first_key)
    low_blocks = first_key.reshape(-1, local_rows)[:, 0] // local_rows
    block_starts = first_key.reshape(-1, 1, local_rows)
    core_index = core.reshape(1).astype(jnp.int32)

    if planar:
        both = [move_rest(over[0], (1, 0), 0)]
        halves, near, far, both[0], weight_squares = tie(
            halves, near, far, both[0], weight_squares
        )
        last = move_rest(far, (2, 0), 2)
        across += [move_rest(near, (1, 0), 1), move_rest(far, (1, 0), 2)]
        over += [move_rest(near, (0, 2), 1), move_rest(far, (0, 2), 2)]
    *qkv, rows_one, w_attn_mine, w_attn_theirs = project(
        y_index, low_one, other_one, halves, jnp.stack(attn_biases)
    )

    def attend(part):
        return attention_forward(low_blocks, core_index, block_starts, qkv[part], heads_here)

    attended = [attend(0)]
    if planar:
        qkv[1], last, across[1:3], over[1:3], sent_cotangent, _ = tie(
            qkv[1], last, across[1:3], over[1:3], sent_cotangent, attended[0][2]
        )
        across.append(move_rest(last, (1, 0), 3))
        over.append(move_rest(last, (0, 2), 3))
        both += [move_rest(over[1], (1, 0), 1), move_rest(across[2], (0, 2), 2)]
    own_e = exchange_micro(own_cotangent, sent_cotangent)
    attended.append(attend(1))
    if planar:
        dp_index, across, over, both, _ = tie(dp_index, across, over, both, attended[1][2])
        both.append(move_rest(over[3], (1, 0), 3))
        rest_mine = [block for pair in zip((wide, near, far, last), across) for block in pair]
        rest_theirs = [block for pair in zip(over, both) for block in pair]
        matrices_mine = unpack_share(dp_index, rest_mine, head_share, model_width)
        matrices_theirs = unpack_share(dp_index, rest_theirs, head_share, model_width)
        w_out, w_in, w_back = (list(pair) for pair in zip(matrices_mine, matrices_theirs))
        own_e, w_out[0] = tie(own_e, w_out[0])
    other_e = swap(own_e, "seq", 1)
    sent, kept = split_product([attended[0][0], attended[1][0]], w_out, False, model_width, F32)
    middle, low_two = middle_norm(own_in, kept, swap(sent, "seq", 1), small_master)
    other_two = swap(low_two, "seq", 1)

    weights = (w_in[0], w_in[1], w_back[0], w_back[1])
    *filled, out_sent, up_sent, sums_sent = feed_forward(
        other_two, other_e, 1, weights, ff_biases, None
    )
    out_received = swap(out_sent, "seq", 1)
    up_received = swap(up_sent, "seq", 1)
    *filled, out_kept, up_kept, sums_kept = feed_forward(
        low_two, own_e, 0, weights, ff_biases, filled
    )
    activated, inner, (rows_two, rows_e) = filled[:2], filled[2:4], filled[4:]
    inner_sums = sums_sent + sums_kept

    link = BF16 if planar else F32
    grad_mid, low_mid, sums_two = norm_back(
        middle, up_kept, up_received, own_e, small_master[2:3], True
    )
    low_mid, rows_e = tie(low_mid, rows_e)
    back_sent = dot_columns(activated[1], rows_e).astype(link)
    back_sent, low_mid = tie(back_sent, low_mid)
    other_mid = swap(low_mid, "seq", 1)
    rows_two, other_mid = tie(rows_two, other_mid)
    in_sent = dot_columns(rows_two, inner[1]).astype(link)
    in_sent, low_mid = tie(in_sent, low_mid)
    back_received = swap(back_sent, "seq", 2)
    in_received = swap(in_sent, "seq", 2)

    grad_att_mine, grad_att_theirs, rows_mid = out_grads(low_mid, other_mid, w_out)
    out_sent_theirs = dot_columns(attended[1][0], rows_mid).astype(link)
    out_sent_theirs, rows_two, rows_e, rows_mid = tie(out_sent_theirs, rows_two, rows_e, rows_mid)
    outer_received = swap(out_sent_theirs, "seq", 2)
    share_back = dot_columns(activated[0], rows_e)
    share_in = dot_columns(rows_two, inner[0])
    share_out = dot_columns(attended[0][0], rows_mid)
    share_back, share_in, share_out, grad_att_theirs = tie(
        share_back, share_in, share_out, grad_att_theirs
    )

    def return_rows(lower, upper):
        return swap(jnp.where(chip == 0, upper, lower), "seq", 2)

    def attend_back(part, grad_att):
        return attention_backward(
            low_blocks,
            core_index,
            block_starts,
            qkv[part],
            grad_att,
            attended[part][1],
            attended[part][2],
            heads_here,
        )

    packed_theirs = attend_back(1, grad_att_theirs)
    attn_sent = dot_columns(rows_one, packed_theirs).astype(link)
    attn_sent, packed_theirs = tie(attn_sent, packed_theirs)
    theirs_part = partial_product(packed_theirs, w_attn_theirs)
    attn_sent, theirs_part, y_index, out_received = tie(
        attn_sent, theirs_part, y_index, out_received
    )
    attn_received = swap(attn_sent, "seq", 2)
    if planar:
        kept_rest, sent_rest = pack_rest(
            y_index,
            (share_out, share_in, share_back),
            (outer_received, in_received, back_received),
            cut,
        )
        result_rows = widen(
            (middle + ((out_kept + out_received)[:, :model_width] + small_master[7])).astype(BF16)
        )
        sent_rest, grad_att_mine, result_rows = tie(sent_rest, grad_att_mine, result_rows)
        result_halves = (result_rows[:local_rows], result_rows[local_rows:])
        result_received = return_rows(*result_halves)
        got_rest = swap(sent_rest, "dp", 1)
    else:
        result_rows = widen(
            (middle + ((out_kept + out_received)[:, :model_width] + small_master[7])).astype(BF16)
        )
        result_halves = (result_rows[:local_rows], result_rows[local_rows:])
        result_received = return_rows(*result_halves)
        share_back, share_in, share_out = (
            share_back + back_received,
            share_in + in_received,
            share_out + outer_received,
        )

    packed_mine = attend_back(0, grad_att_mine)
    packed_mine, result_received = tie(packed_mine, result_received)
    sent, kept = split_product(
        [packed_mine], [w_attn_mine], True, model_width, BF16, [theirs_part]
    )
    packed_mine, sent = tie(packed_mine, sent)
    share_attn = dot_columns(rows_one, packed_mine) + attn_received.astype(F32)
    if planar:
        z_odd = z_here % 2 == 1
        kept_lead, sent_lead = halve_plane(share_attn[:tall_rows], share_attn[tall_rows:], y_here)
        kept_lead, sent_lead, kept_rest = tie(kept_lead, sent_lead, kept_rest)
        got_lead = swap(sent_lead, "dp", 1)
        held = [kept_rest[i] + got_rest[i].astype(F32) for i in range(3)]
        sent_near = jnp.where(z_odd, held[1], held[0]).astype(BF16)
        sent_last = held[2].astype(BF16)
        kept_near = jnp.where(z_odd, held[0], held[1])
        kept_last = held[2]
        sent_near, sent_last, kept_lead = tie(sent_near, sent_last, kept_lead)
        got_near = swap(sent_near, "dp", 2)
        got_last = permute(sent_last, "dp", lower_pairs([(0, 1), (2, 3)], 2))
    packed = [packed_mine, packed_theirs]
    if planar:
        held_lead = kept_lead + got_lead.astype(F32)
        sent_lead = held_lead.astype(BF16)
        sent_lead, held_lead, kept_near, kept_last = tie(
            sent_lead, held_lead, kept_near, kept_last
        )
        near_lead = permute(sent_lead, "dp", lower_pairs([(1, 0), (3, 2)], 2))
        held_near = kept_near + got_near.astype(F32)
        held_last = kept_last + got_last.astype(F32)
        sent_far = jnp.where(z_here == 1, held_last, held_near).astype(BF16)
        own_rest = jnp.where(z_here == 3, held_last, held_near)
        sent_far, own_rest, kept = tie(sent_far, own_rest, kept)
        got_far = permute(sent_far, "dp", lower_pairs([(3, 1), (0, 2), (1, 3)], 2))
    grad_x, sums_one = norm_back(
        own_in, kept, swap(sent, "seq", 1), grad_mid, small_master[0:1], False
    )
    if planar:
        sums_one, held_lead = tie(sums_one, held_lead)
        held_lead = held_lead + near_lead.astype(F32)
        sent_lead = held_lead.astype(BF16)
        sent_lead, held_lead, own_rest, grad_x = tie(sent_lead, held_lead, own_rest, grad_x)
        sent_lead, own_rest, mark = started(sent_lead, own_rest, mark)
        far_lead = permute(sent_lead, "dp", lower_pairs([(2, 0)], 2))

    result_all = place_rows(chip_index, result_rows, result_received, model_width)
    grad_halves = (grad_x[:local_rows], grad_x[local_rows:])
    grad_all = place_rows(chip_index, grad_x, return_rows(*grad_halves), model_width)

    def at_shares(columns):
        row = jnp.zeros((model_width,), F32)
        for share, column in zip(shares, columns):
            row = lax.dynamic_update_slice(row, column, (share * head_share,))
        return row

    bias_sums = [jnp.sum(packed[part].astype(F32), axis=0) for part in range(2)]
    inner_rows = jnp.zeros((4, model_width), F32)
    for part in range(2):
        inner_rows = lax.dynamic_update_slice(
            inner_rows, inner_sums[part : part + 1], (shares[part], 0)
        )
    small_now = jnp.concatenate(
        [
            sums_one[:2],
            sums_two[:2],
            at_shares([sums[:head_share] for sums in bias_sums])[None],
            at_shares([sums[2 * head_share : triple] for sums in bias_sums])[None],
            sums_two[2:4],
            inner_rows,
        ]
    )

    if planar:
        rest_grad = (own_rest + got_far.astype(F32)).reshape(1, 1, shard_len)
        held_lead, rest_grad, result_all, grad_all, small_now = tie(
            held_lead, rest_grad, result_all, grad_all, small_now
        )
        lead_grad = (held_lead + far_lead.astype(F32))[:, :triple].reshape(1, 1, shard_len)
        leads = z_here == 0
    else:
        flat_here = jnp.concatenate(
            [matrix.reshape(-1) for matrix in (share_attn[:, :triple], share_out, share_in, share_back)]
        )
        lead_grad = lax.psum_scatter(
            flat_here.reshape(dp_count, shard_len), "dp", scatter_dimension=0, tiled=True
        ).reshape(1, 1, shard_len)
        rest_grad = lead_grad
        leads = z_here >= 0

    steps_done = step_count[0].astype(F32)
    fix_one = 1.0 - jnp.exp(steps_done * math.log(BETA_ONE))
    fix_two = 1.0 - jnp.exp(steps_done * math.log(BETA_TWO))
    ints = jnp.concatenate([bound, leads.astype(jnp.int32).reshape(1)])
    reduced, moments, update, update_squares = new_moments(
        ints,
        jnp.stack([fix_one, fix_two]),
        lead_grad,
        rest_grad,
        first_moment,
        second_moment,
        weight,
    )
    matrix_rows = jnp.stack([matrix_sums(weight_squares), matrix_sums(update_squares)])
    small_sum = sum_everywhere(
        jnp.concatenate([small_now, jnp.pad(matrix_rows, ((0, 2), (0, model_width - 4)))])
    )
    small_grad = small_sum[:12]
    weight_norms = jnp.sqrt(small_sum[12, :4])
    update_norms = jnp.sqrt(small_sum[13, :4])
    ratios = weight_norms / update_norms
    new_weight, weight_copy = new_weights(
        ints, jnp.stack([pick(ratios, lower_matrix), pick(ratios, upper_matrix)]), weight, update
    )
    small_one = BETA_ONE * small_first + (1.0 - BETA_ONE) * small_grad
    small_two = BETA_TWO * small_second + (1.0 - BETA_TWO) * small_grad * small_grad
    small_late = lax.dynamic_update_slice(small_master, mark, (0, 0))
    small_updated = small_late - SMALL_RATE * (small_one / fix_one) / (
        jnp.sqrt(small_two / fix_two) + ADAM_EPS
    )
    return (
        result_all,
        grad_all,
        reduced,
        moments,
        new_weight,
        weight_copy,
        jnp.stack([weight_norms, update_norms, ratios]),
        small_grad,
        jnp.stack([small_one, small_two]),
        small_updated,
    )


def solution(mesh):
    in_specs = (
        P(None, "dp", "seq", None),
        P(None, "dp", "seq", None),
        P(None, "dp", None),
        P(None, "dp", None),
        P(None, "dp", None),
        P("dp", "seq", None),
        P("dp", "seq", None),
        P("dp", "seq", None),
        P(),
        P(),
        P(),
        P(),
    )
    out_specs = (
        P(None, "dp", "seq", None),
        P(None, "dp", "seq", None),
        P("dp", "seq", None),
        P(None, "dp", "seq", None),
        P("dp", "seq", None),
        P("dp", "seq", None),
        P(),
        P(),
        P(),
        P(),
    )
    return jax.shard_map(
        per_device, mesh=mesh, in_specs=in_specs, out_specs=out_specs, check_vma=False
    )
```

```python
import functools
import math

import jax
import jax.numpy as jnp
from jax import lax
from jax.experimental import pallas as pl
from jax.experimental.pallas import tpu as pltpu
from jax.sharding import PartitionSpec as P

HEADS = 20


NORM_EPS = 1e-05
BETA_ONE = 0.9
BETA_TWO = 0.999
ADAM_EPS = 1e-06
DECAY = 0.01
MATRIX_RATE = 0.3
SMALL_RATE = 0.25
MASKED = -1e30
LOG2_E = 1.4426950408889634
FF_ROWS = 256
SCALE = 1e9

F32 = jnp.float32
BF16 = jnp.bfloat16


def dot_rows(left, right):
    return lax.dot_general(left, right, (((1,), (0,)), ((), ())), preferred_element_type=F32)


def dot_transposed(left, right):
    return lax.dot_general(left, right, (((1,), (1,)), ((), ())), preferred_element_type=F32)


def dot_columns(left, right):
    return lax.dot_general(left, right, (((0,), (0,)), ((), ())), preferred_element_type=F32)


def norm_stats(rows):
    center = jnp.mean(rows, axis=-1, keepdims=True)
    centered = rows - center
    spread = jnp.mean(centered * centered, axis=-1, keepdims=True)
    scale = lax.rsqrt(spread + NORM_EPS)
    return centered * scale, scale


def norm_backward(upstream, hat, scale, gain):
    weighted = upstream * gain
    return (
        weighted
        - jnp.mean(weighted, axis=-1, keepdims=True)
        - hat * jnp.mean(weighted * hat, axis=-1, keepdims=True)
    ) * scale


def gelu_parts(values):
    inner = math.sqrt(2.0 / math.pi)
    squares = values * values
    bent = jnp.tanh(inner * (values + 0.044715 * values * squares))
    half = 0.5 * (1.0 + bent)
    slope = half + 0.5 * values * (1.0 - bent * bent) * inner * (1.0 + 3.0 * 0.044715 * squares)
    return values * half, slope


def block_place(core, block):
    return jnp.where(block % 2 == core, 0, 2) + block // 2


def block_rows(core, block, rows):
    return pl.ds(pl.multiple_of(block_place(core, block) * rows, rows), rows)


def attention_forward_body(
    heads, width, bq, low_ref, core_ref, start_ref, qkv_ref, out_ref, outt_ref, lse_ref, qs, ks, vt, acc
):
    length = qkv_ref.shape[0]
    flat = heads * width
    factor = width**-0.5 * LOG2_E
    core = core_ref[0]

    def unpack(block, carry):
        here = block_rows(core, block, bq)
        there = pl.ds(pl.multiple_of(block * bq, bq), bq)
        for h in range(heads):
            qs[h, there] = qkv_ref[here, h * width : (h + 1) * width]
            ks[h, there] = qkv_ref[here, flat + h * width : flat + (h + 1) * width]
        turned = qkv_ref[here, 2 * flat : 3 * flat].astype(F32).T
        for h in range(heads):
            vt[h, block] = turned[h * width : (h + 1) * width].astype(BF16)
        return carry

    lax.fori_loop(0, length // bq, unpack, 0)

    def query_step(qb, carry):
        q0 = pl.multiple_of(qb * bq, bq)
        start = start_ref[qb]
        query_place = q0 + lax.broadcasted_iota(jnp.int32, (1, bq), 1)
        acc[...] = jnp.zeros_like(acc)

        def key_step(kb, tops_totals):
            tops, totals = tops_totals
            k0 = pl.multiple_of(kb * bq, bq)
            key_place = k0 + lax.broadcasted_iota(jnp.int32, (bq, bq), 0)
            allowed = (key_place <= query_place) & (key_place >= start)
            new_tops, new_totals = [], []
            for h in range(heads):
                scores = dot_transposed(ks[h, pl.ds(k0, bq)], qs[h, pl.ds(q0, bq)]) * factor
                scores = jnp.where(allowed, scores, MASKED)
                top = jnp.maximum(tops[h], jnp.max(scores, axis=0, keepdims=True))
                fade = jnp.exp2(tops[h] - top)
                weights = jnp.exp2(scores - top)
                own = slice(h * width, (h + 1) * width)
                acc[own] = acc[own] * fade + dot_rows(vt[h, kb], weights.astype(BF16))
                new_tops.append(top)
                new_totals.append(totals[h] * fade + jnp.sum(weights, axis=0, keepdims=True))
            return tuple(new_tops), tuple(new_totals)

        first = (
            tuple(jnp.full((1, bq), -1e29, F32) for _ in range(heads)),
            tuple(jnp.zeros((1, bq), F32) for _ in range(heads)),
        )
        tops, totals = lax.fori_loop(low_ref[qb], qb + 1, key_step, first)
        for h in range(heads):
            own = slice(h * width, (h + 1) * width)
            acc[own] = acc[own] * (1.0 / totals[h])
            lse_ref[qb, h : h + 1, :] = tops[h] + jnp.log2(totals[h])
        mixed = acc[...]
        outt_ref[qb] = mixed
        out_ref[block_rows(core, qb, bq), :] = mixed.T.astype(BF16)
        return carry

    lax.fori_loop(0, length // bq, query_step, 0)


def attention_backward_body(
    heads,
    width,
    bq,
    low_ref,
    core_ref,
    start_ref,
    qkv_ref,
    dout_ref,
    outt_ref,
    lse_ref,
    grad_ref,
    qs,
    ks,
    vs,
    ds,
    kt,
    dk,
    dv,
    dqt,
):
    length = qkv_ref.shape[0]
    flat = heads * width
    score_scale = width**-0.5
    factor = score_scale * LOG2_E
    core = core_ref[0]

    def unpack(block, carry):
        here = block_rows(core, block, bq)
        there = pl.ds(pl.multiple_of(block * bq, bq), bq)
        for h in range(heads):
            qs[h, there] = qkv_ref[here, h * width : (h + 1) * width]
            ks[h, there] = qkv_ref[here, flat + h * width : flat + (h + 1) * width]
            vs[h, there] = qkv_ref[here, 2 * flat + h * width : 2 * flat + (h + 1) * width]
            ds[h, there] = dout_ref[here, h * width : (h + 1) * width]
        turned = qkv_ref[here, flat : 2 * flat].astype(F32).T
        for h in range(heads):
            kt[h, block] = turned[h * width : (h + 1) * width].astype(BF16)
        return carry

    lax.fori_loop(0, length // bq, unpack, 0)
    dk[...] = jnp.zeros_like(dk)
    dv[...] = jnp.zeros_like(dv)

    def query_step(qb, carry):
        q0 = pl.multiple_of(qb * bq, bq)
        queries = pl.ds(q0, bq)
        here = block_rows(core, qb, bq)
        start = start_ref[qb]
        query_place = q0 + lax.broadcasted_iota(jnp.int32, (1, bq), 1)
        products = dout_ref[here, :].astype(F32).T * outt_ref[qb]
        inners = [
            jnp.sum(products[h * width : (h + 1) * width], axis=0, keepdims=True)
            for h in range(heads)
        ]
        dqt[...] = jnp.zeros_like(dqt)

        def attend(key_block, key_part, query_part):
            key_count = key_part.stop - key_part.start
            count = query_part.stop - query_part.start
            k0 = pl.multiple_of(key_block * bq + key_part.start, key_count)
            keys = pl.ds(k0, key_count)
            rows = pl.ds(pl.multiple_of(q0 + query_part.start, count), count)
            key_place = k0 + lax.broadcasted_iota(jnp.int32, (key_count, count), 0)
            allowed = (key_place <= query_place[:, query_part]) & (
                key_place >= start[:, query_part]
            )
            for h in range(heads):
                scores = dot_transposed(ks[h, keys], qs[h, rows]) * factor
                weights = jnp.exp2(
                    jnp.where(allowed, scores - lse_ref[qb, h : h + 1, query_part], MASKED)
                )
                dweights = dot_transposed(vs[h, keys], ds[h, rows])
                dscores = (weights * (dweights - inners[h][:, query_part])).astype(BF16)
                dv[h, keys] += dot_rows(weights.astype(BF16), ds[h, rows])
                dk[h, keys] += dot_rows(dscores, qs[h, rows])
                dqt[h * width : (h + 1) * width, query_part] += dot_rows(
                    kt[h, key_block, :, key_part], dscores
                )

        every = slice(0, bq)

        def key_step(kb, inner_carry):
            attend(kb, every, every)
            return inner_carry

        lax.fori_loop(low_ref[qb], qb, key_step, 0)
        attend(qb, slice(0, bq // 2), every)
        attend(qb, slice(bq // 2, bq), slice(bq // 2, bq))
        grad_ref[here, 0:flat] = (dqt[...] * score_scale).T.astype(BF16)
        return carry

    lax.fori_loop(0, length // bq, query_step, 0)

    def write_keys(kb, carry):
        here = block_rows(core, kb, bq)
        rows = pl.ds(pl.multiple_of(kb * bq, bq), bq)
        grad_ref[here, flat : 2 * flat] = jnp.concatenate(
            [dk[h, rows] * score_scale for h in range(heads)], axis=1
        ).astype(BF16)
        grad_ref[here, 2 * flat : 3 * flat] = jnp.concatenate(
            [dv[h, rows] for h in range(heads)], axis=1
        ).astype(BF16)
        rest = grad_ref.shape[1] - 3 * flat
        if rest:
            grad_ref[here, 3 * flat :] = jnp.zeros((bq, rest), BF16)
        return carry

    lax.fori_loop(0, length // bq, write_keys, 0)


def whole_block(shape):
    return pl.BlockSpec(shape, lambda step, *refs: (0,) * len(shape))


def attention_forward(low_blocks, core, starts, qkv, heads):
    length, triple = qkv.shape
    flat = triple // 3
    width = flat // heads
    blocks, _, bq = starts.shape
    grid_spec = pltpu.PrefetchScalarGridSpec(
        num_scalar_prefetch=2,
        grid=(1,),
        in_specs=[whole_block((blocks, 1, bq)), whole_block((length, triple))],
        out_specs=[
            whole_block((length, flat)),
            whole_block((blocks, flat, bq)),
            whole_block((blocks, 8, bq)),
        ],
        scratch_shapes=[
            pltpu.VMEM((heads, length, width), BF16),
            pltpu.VMEM((heads, length, width), BF16),
            pltpu.VMEM((heads, blocks, width, bq), BF16),
            pltpu.VMEM((flat, bq), F32),
        ],
    )
    return pl.pallas_call(
        functools.partial(attention_forward_body, heads, width, bq),
        out_shape=[
            jax.ShapeDtypeStruct((length, flat), BF16),
            jax.ShapeDtypeStruct((blocks, flat, bq), F32),
            jax.ShapeDtypeStruct((blocks, 8, bq), F32),
        ],
        grid_spec=grid_spec,
        compiler_params=pltpu.CompilerParams(vmem_limit_bytes=48 << 20),
        cost_estimate=lasting(35),
        name="attention_forward",
    )(low_blocks, core, starts, qkv)


def attention_backward(low_blocks, core, starts, qkv, grad_out, out_turned, log_total, heads):
    length, triple = qkv.shape
    flat = triple // 3
    width = flat // heads
    blocks, _, bq = starts.shape
    per_head = pltpu.VMEM((heads, length, width), BF16)
    sums = pltpu.VMEM((heads, length, width), F32)
    grid_spec = pltpu.PrefetchScalarGridSpec(
        num_scalar_prefetch=2,
        grid=(1,),
        in_specs=[
            whole_block((blocks, 1, bq)),
            whole_block((length, triple)),
            whole_block((length, flat)),
            whole_block((blocks, flat, bq)),
            whole_block((blocks, 8, bq)),
        ],
        out_specs=whole_block((length, lanes(triple))),
        scratch_shapes=[
            per_head,
            per_head,
            per_head,
            per_head,
            pltpu.VMEM((heads, blocks, width, bq), BF16),
            sums,
            sums,
            pltpu.VMEM((flat, bq), F32),
        ],
    )
    return pl.pallas_call(
        functools.partial(attention_backward_body, heads, width, bq),
        out_shape=jax.ShapeDtypeStruct((length, lanes(triple)), BF16),
        grid_spec=grid_spec,
        compiler_params=pltpu.CompilerParams(vmem_limit_bytes=60 << 20),
        cost_estimate=lasting(56),
        name="attention_backward",
    )(low_blocks, core, starts, qkv, grad_out, out_turned, log_total)


def lasting(micros):
    return pl.CostEstimate(flops=int(micros * SCALE), bytes_accessed=1 << 12, transcendentals=0)


def lanes(width):
    return -(-width // 128) * 128


def put(ref, value):
    width = value.shape[1]
    ref[:, :width] = value.astype(ref.dtype)
    if width < ref.shape[1]:
        ref[:, width:] = jnp.zeros((value.shape[0], ref.shape[1] - width), ref.dtype)


def vmem(count):
    return pltpu.CompilerParams(vmem_limit_bytes=count << 20)


def fixed(shape):
    return pl.BlockSpec(shape, lambda *step: (0,) * len(shape), pipeline_mode=pl.Buffered(1))


def hbm():
    return pl.BlockSpec(memory_space=pl.ANY)


def round_weights_body(weight_ref, low_ref):
    low_ref[...] = weight_ref[0, 0, :].astype(BF16)


def round_weights(weight):
    whole = pl.BlockSpec(memory_space=pltpu.VMEM)
    return pl.pallas_call(
        round_weights_body,
        in_specs=[whole],
        out_specs=whole,
        out_shape=jax.ShapeDtypeStruct(weight.shape[2:], BF16),
        compiler_params=vmem(32),
        cost_estimate=lasting(6),
        name="round_weights",
    )(weight)


def add_squares(sums_ref, values, in_lower):
    squares = values * values
    lower = jnp.sum(jnp.where(in_lower, squares, 0.0))
    sums_ref[0] += lower
    sums_ref[1] += jnp.sum(squares) - lower


def square_sums_body(bound_ref, weight_ref, sums_ref):
    sums_ref[0] = 0.0
    sums_ref[1] = 0.0
    place = lax.broadcasted_iota(jnp.int32, weight_ref.shape, 2)
    add_squares(sums_ref, weight_ref[...], place < bound_ref[0])


def square_sums(bound, weight):
    smem = pl.BlockSpec(memory_space=pltpu.SMEM)
    return pl.pallas_call(
        square_sums_body,
        in_specs=[smem, pl.BlockSpec(memory_space=pltpu.VMEM)],
        out_specs=smem,
        out_shape=jax.ShapeDtypeStruct((2,), F32),
        compiler_params=vmem(32),
        cost_estimate=lasting(6),
        name="square_sums",
    )(bound, weight)


def moments_body(
    ints_ref, floats_ref, lead_ref, rest_ref, first_ref, second_ref, weight_ref,
    grad_ref, moments_ref, update_ref, sums_ref,
):
    step = pl.program_id(0)
    grad = jnp.where(ints_ref[1] == 1, lead_ref[...], rest_ref[...])
    grad_ref[...] = grad
    first = BETA_ONE * first_ref[...] + (1.0 - BETA_ONE) * grad
    second = BETA_TWO * second_ref[...] + (1.0 - BETA_TWO) * grad * grad
    moments_ref[0] = first
    moments_ref[1] = second
    update = (first / floats_ref[0]) / (jnp.sqrt(second / floats_ref[1]) + ADAM_EPS)
    update = update + DECAY * weight_ref[...]
    update_ref[...] = update
    count = grad.shape[2]
    place = step * count + lax.broadcasted_iota(jnp.int32, grad.shape, 2)

    @pl.when(step == 0)
    def clear():
        sums_ref[0] = 0.0
        sums_ref[1] = 0.0

    add_squares(sums_ref, update, place < ints_ref[0])


def flat_steps(count):
    return 7 if count % (7 * 128) == 0 else 1


def new_moments(ints, floats, lead, rest, first, second, weight):
    count = weight.shape[2]
    steps = flat_steps(count)
    smem = pl.BlockSpec(memory_space=pltpu.SMEM)
    flat = pl.BlockSpec((1, 1, count // steps), lambda i: (0, 0, i))
    pair = pl.BlockSpec((2, 1, 1, count // steps), lambda i: (0, 0, 0, i))
    return pl.pallas_call(
        moments_body,
        grid=(steps,),
        in_specs=[smem, smem] + [flat] * 5,
        out_specs=[flat, pair, flat, smem],
        out_shape=[
            jax.ShapeDtypeStruct(weight.shape, F32),
            jax.ShapeDtypeStruct((2,) + weight.shape, F32),
            jax.ShapeDtypeStruct(weight.shape, F32),
            jax.ShapeDtypeStruct((2,), F32),
        ],
        compiler_params=vmem(48),
        cost_estimate=lasting(10),
        name="new_moments",
    )(ints, floats, lead, rest, first, second, weight)


def new_weights_body(ints_ref, ratio_ref, weight_ref, update_ref, new_ref, copy_ref):
    count = weight_ref.shape[2]
    place = pl.program_id(0) * count + lax.broadcasted_iota(jnp.int32, weight_ref.shape, 2)
    rate = jnp.where(place < ints_ref[0], ratio_ref[0], ratio_ref[1])
    new = weight_ref[...] - MATRIX_RATE * rate * update_ref[...]
    new_ref[...] = new
    copy_ref[...] = new.astype(BF16)


def new_weights(ints, ratios, weight, update):
    count = weight.shape[2]
    steps = flat_steps(count)
    smem = pl.BlockSpec(memory_space=pltpu.SMEM)
    flat = pl.BlockSpec((1, 1, count // steps), lambda i: (0, 0, i))
    return pl.pallas_call(
        new_weights_body,
        grid=(steps,),
        in_specs=[smem, smem, flat, flat],
        out_specs=[flat, flat],
        out_shape=[
            jax.ShapeDtypeStruct(weight.shape, F32),
            jax.ShapeDtypeStruct(weight.shape, BF16),
        ],
        compiler_params=vmem(32),
        cost_estimate=lasting(6),
        name="new_weights",
    )(ints, ratios, weight, update)


def unpack_body(cut, out_rows, in_rows, place_ref, *refs):
    blocks, (w_out, w_in, w_back, held, sems) = refs[:8], refs[8:]
    here = place_ref[0]
    copies = [
        pltpu.make_async_copy(block, held.at[index ^ here], sems.at[index])
        for index, block in enumerate(blocks)
    ]
    for copy in copies:
        copy.start()
    for copy in copies:
        copy.wait()
    begin = 2 * cut
    for target, rows in ((w_out, out_rows), (w_in, in_rows), (w_back, in_rows)):
        done = 0
        while done < rows:
            block, offset = divmod(begin + done, cut)
            count = min(cut - offset, rows - done)
            target[done : done + count] = held[block, offset : offset + count]
            done += count
        begin += rows


def unpack_share(place, blocks, out_rows, in_rows):
    cut, columns = blocks[0].shape
    shapes = [(out_rows, columns), (in_rows, columns), (in_rows, columns)]
    return pl.pallas_call(
        functools.partial(unpack_body, cut, out_rows, in_rows),
        grid_spec=pltpu.PrefetchScalarGridSpec(
            num_scalar_prefetch=1,
            grid=(1,),
            in_specs=[hbm()] * 8,
            out_specs=[whole_block(shape) for shape in shapes],
            scratch_shapes=[
                pltpu.VMEM((8, cut, columns), BF16),
                pltpu.SemaphoreType.DMA((8,)),
            ],
        ),
        out_shape=[jax.ShapeDtypeStruct(shape, BF16) for shape in shapes],
        compiler_params=vmem(48),
        cost_estimate=lasting(6),
        name="unpack_share",
    )(place, *blocks)


def pack_rest_body(
    cut, place_ref, out_ref, in_ref, back_ref, out_got, in_got, back_got, kept_ref, sent_ref
):
    here = place_ref[0]
    place = 0
    for matrix, got in ((out_ref, out_got), (in_ref, in_got), (back_ref, back_got)):
        done, rows = 0, matrix.shape[0]
        while done < rows:
            block, offset = divmod(place, cut)
            count = min(cut - offset, rows - done)
            source = slice(done, done + count)
            target = slice(offset, offset + count)
            plane, side = divmod(block, 2)

            @pl.when(here == side)
            def keep(matrix=matrix, got=got, source=source, target=target, plane=plane):
                kept_ref[plane, target] = matrix[source] + got[source].astype(F32)

            @pl.when(here != side)
            def send(matrix=matrix, got=got, source=source, target=target, plane=plane):
                sent_ref[plane, target] = (matrix[source] + got[source].astype(F32)).astype(BF16)

            done += count
            place += count


def pack_rest(place, matrices, received, cut):
    columns = matrices[0].shape[1]
    whole = pl.BlockSpec(memory_space=pltpu.VMEM)
    return pl.pallas_call(
        functools.partial(pack_rest_body, cut),
        in_specs=[pl.BlockSpec(memory_space=pltpu.SMEM)] + [whole] * 6,
        out_specs=[whole] * 2,
        out_shape=[
            jax.ShapeDtypeStruct((3, cut, columns), F32),
            jax.ShapeDtypeStruct((3, cut, columns), BF16),
        ],
        compiler_params=vmem(40),
        cost_estimate=lasting(10),
        name="pack_rest",
    )(place, *matrices, *received)


def rows_of(step, steps, own_ref, other_ref, width):
    return jnp.where(step < steps, own_ref[:, :width], other_ref[:, :width])


def both_specs(block, width, steps):
    own = pl.BlockSpec((block, width), lambda i, *refs: (jnp.minimum(i, steps - 1), 0))
    other = pl.BlockSpec((block, width), lambda i, *refs: (jnp.maximum(i - steps, 0), 0))
    return own, other


def project_body(
    steps, place_ref, own_ref, other_ref, a0, a1, b0, b1, bias_ref,
    out_a, out_b, rows_ref, w_a, w_b, sems,
):
    step = pl.program_id(0)

    @pl.when(step == 0)
    def load():
        cut = a0.shape[0]
        here = place_ref[0]
        first = pl.ds(pl.multiple_of(here * cut, cut), cut)
        second = pl.ds(pl.multiple_of((1 - here) * cut, cut), cut)
        copies = [
            pltpu.make_async_copy(a0, w_a.at[first], sems.at[0]),
            pltpu.make_async_copy(a1, w_a.at[second], sems.at[1]),
            pltpu.make_async_copy(b0, w_b.at[first], sems.at[2]),
            pltpu.make_async_copy(b1, w_b.at[second], sems.at[3]),
        ]
        for copy in copies:
            copy.start()
        for copy in copies:
            copy.wait()

    rows = rows_of(step, steps, own_ref, other_ref, rows_ref.shape[1])
    rows_ref[...] = rows
    out_a[...] = (dot_rows(rows, w_a[...]) + bias_ref[0:1]).astype(BF16)
    out_b[...] = (dot_rows(rows, w_b[...]) + bias_ref[1:2]).astype(BF16)


def project(place, own, other, halves, biases):
    count, sent_width = own.shape
    cut, triple = halves[0].shape
    model_width = 2 * cut
    block = min(512, count)
    steps = count // block
    row_out = lambda width: pl.BlockSpec((block, width), lambda i, *refs: (i, 0))
    matrix = jax.ShapeDtypeStruct((2 * cut, triple), BF16)
    return pl.pallas_call(
        functools.partial(project_body, steps),
        grid_spec=pltpu.PrefetchScalarGridSpec(
            num_scalar_prefetch=1,
            grid=(2 * steps,),
            in_specs=[*both_specs(block, sent_width, steps)]
            + [hbm()] * 4
            + [fixed((2, triple))],
            out_specs=[row_out(triple), row_out(triple), row_out(model_width)]
            + [pl.BlockSpec(matrix.shape, lambda i, *refs: (0, 0))] * 2,
            scratch_shapes=[pltpu.SemaphoreType.DMA((4,))],
        ),
        out_shape=[jax.ShapeDtypeStruct((2 * count, triple), BF16)] * 2
        + [jax.ShapeDtypeStruct((2 * count, model_width), BF16), matrix, matrix],
        compiler_params=vmem(48),
        cost_estimate=lasting(16),
        name="project",
    )(place, own, other, *halves, biases)


def out_grads_body(steps, own_ref, other_ref, w_a, w_b, out_a, out_b, rows_ref):
    rows = rows_of(pl.program_id(0), steps, own_ref, other_ref, rows_ref.shape[1])
    rows_ref[...] = rows
    out_a[...] = dot_transposed(rows, w_a[...]).astype(BF16)
    out_b[...] = dot_transposed(rows, w_b[...]).astype(BF16)


def out_grads(own, other, w_out):
    count, sent_width = own.shape
    width, model_width = w_out[0].shape
    block = min(512, count)
    steps = count // block
    row_out = lambda columns: pl.BlockSpec((block, columns), lambda i: (i, 0))
    return pl.pallas_call(
        functools.partial(out_grads_body, steps),
        grid=(2 * steps,),
        in_specs=[*both_specs(block, sent_width, steps)] + [fixed(w_out[0].shape)] * 2,
        out_specs=[row_out(width), row_out(width), row_out(model_width)],
        out_shape=[jax.ShapeDtypeStruct((2 * count, width), BF16)] * 2
        + [jax.ShapeDtypeStruct((2 * count, model_width), BF16)],
        compiler_params=vmem(48),
        cost_estimate=lasting(8),
        name="out_grads",
    )(own, other, *w_out)


def row_products(turned, left_refs, weight_refs):
    product = None
    for left, weight in zip(left_refs, weight_refs):
        if turned:
            term = dot_transposed(left[:, : weight.shape[1]], weight[...])
        else:
            term = dot_rows(left[:, : weight.shape[0]], weight[...])
        product = term if product is None else product + term
    return product


def partial_product_body(left, weight, out_ref):
    out_ref[...] = row_products(True, [left], [weight])


def split_product_body(steps, turned, count, *refs):
    lefts, weights, rest = refs[:count], refs[count : 2 * count], refs[2 * count :]
    *partial, sent_ref, kept_ref = rest
    product = row_products(turned, lefts, weights)
    if partial:
        product = product + partial[0][...]
    step = pl.program_id(0)

    @pl.when(step < steps)
    def other_rows():
        put(sent_ref, product)

    @pl.when(step >= steps)
    def own_rows():
        put(kept_ref, product)


def other_first(block, width, steps):
    return pl.BlockSpec((block, width), lambda i: ((i + steps) % (2 * steps), 0))


def partial_product(left, weight):
    count, width = left.shape
    model_width = weight.shape[0]
    block = min(512, count // 2)
    steps = count // 2 // block
    return pl.pallas_call(
        partial_product_body,
        grid=(2 * steps,),
        in_specs=[other_first(block, width, steps), fixed(weight.shape)],
        out_specs=pl.BlockSpec((block, model_width), lambda i: (i, 0)),
        out_shape=jax.ShapeDtypeStruct((count, model_width), F32),
        compiler_params=vmem(48),
        cost_estimate=lasting(9),
        name="partial_product",
    )(left, weight)


def split_product(lefts, weights, turned, model_width, sent_type, partial=()):
    count, width = lefts[0].shape
    block = min(512, count // 2)
    steps = count // 2 // block
    parts = [
        jax.ShapeDtypeStruct((count // 2, lanes(model_width)), sent_type),
        jax.ShapeDtypeStruct((count // 2, model_width), F32),
    ]
    return pl.pallas_call(
        functools.partial(split_product_body, steps, turned, len(lefts)),
        grid=(2 * steps,),
        in_specs=[other_first(block, width, steps)] * len(lefts)
        + [fixed(weight.shape) for weight in weights]
        + [pl.BlockSpec((block, model_width), lambda i: (i, 0))] * len(partial),
        out_specs=[
            pl.BlockSpec((block, lanes(model_width)), lambda i: (jnp.minimum(i, steps - 1), 0)),
            pl.BlockSpec((block, model_width), lambda i: (jnp.maximum(i - steps, 0), 0)),
        ],
        out_shape=parts,
        compiler_params=vmem(48),
        cost_estimate=lasting(9),
        name="split_product",
    )(*lefts, *weights, *partial)


def middle_body(rows_ref, kept_ref, got_ref, small_ref, middle_ref, low_ref):
    middle = rows_ref[...].astype(F32) + (
        kept_ref[...] + got_ref[:, : kept_ref.shape[1]].astype(F32) + small_ref[6:7]
    )
    middle_ref[...] = middle
    hat, _ = norm_stats(middle)
    put(low_ref, (hat * small_ref[2:3] + small_ref[3:4]).astype(BF16))


def middle_norm(rows, kept, got, small):
    count, width = rows.shape
    block = min(256, count)
    part = pl.BlockSpec((block, width), lambda i: (i, 0))
    sent = pl.BlockSpec((block, lanes(width)), lambda i: (i, 0))
    return pl.pallas_call(
        middle_body,
        grid=(count // block,),
        in_specs=[part, part, sent, fixed(small.shape)],
        out_specs=[part, sent],
        out_shape=[
            jax.ShapeDtypeStruct((count, width), F32),
            jax.ShapeDtypeStruct((count, lanes(width)), BF16),
        ],
        compiler_params=vmem(32),
        cost_estimate=lasting(4),
        name="middle_norm",
    )(rows, kept, got, small)


def turn(block):
    return block.astype(F32).T.astype(BF16)


def take_rows_body(chip_ref, array_ref, own_ref, sent_ref):
    rows = turn(array_ref[0, 0])

    @pl.when(pl.program_id(0) == 0)
    def other_micro():
        put(sent_ref, rows)

    @pl.when(pl.program_id(0) == 1)
    def own_micro():
        put(own_ref, rows)


def take_rows(chip, array):
    turned = jnp.swapaxes(array, 2, 3)
    _, _, width, count = turned.shape
    out = pl.BlockSpec((count, lanes(width)), lambda i, chip_ref: (0, 0))
    return pl.pallas_call(
        take_rows_body,
        grid_spec=pltpu.PrefetchScalarGridSpec(
            num_scalar_prefetch=1,
            grid=(2,),
            in_specs=[
                pl.BlockSpec(
                    (1, 1, width, count),
                    lambda i, chip_ref: (jnp.where(i == 0, 1 - chip_ref[0], chip_ref[0]), 0, 0, 0),
                )
            ],
            out_specs=[out, out],
        ),
        out_shape=[jax.ShapeDtypeStruct((count, lanes(width)), BF16)] * 2,
        compiler_params=vmem(32),
        cost_estimate=lasting(4),
        name="take_rows",
    )(chip, turned)


def place_rows_body(chip_ref, rows_ref, received_ref, out_ref):
    width = out_ref.shape[2]
    rows = jnp.where(
        pl.program_id(0) == chip_ref[0], rows_ref[:, :width], received_ref[:, :width]
    )
    out_ref[0, 0] = turn(rows)


def place_rows(chip, rows, received, width):
    count, sent_width = received.shape
    turned = pl.pallas_call(
        place_rows_body,
        grid_spec=pltpu.PrefetchScalarGridSpec(
            num_scalar_prefetch=1,
            grid=(2,),
            in_specs=[
                pl.BlockSpec((count, sent_width), lambda i, chip_ref: (chip_ref[0], 0)),
                pl.BlockSpec((count, sent_width), lambda i, chip_ref: (0, 0)),
            ],
            out_specs=pl.BlockSpec((1, 1, width, count), lambda i, chip_ref: (i, 0, 0, 0)),
        ),
        out_shape=jax.ShapeDtypeStruct((2, 1, width, count), BF16),
        compiler_params=vmem(32),
        cost_estimate=lasting(4),
        name="place_rows",
    )(chip, rows, received)
    return jnp.swapaxes(turned, 2, 3)


def norm_back_body(wide_out, rows_ref, kept_ref, got_ref, base_ref, gain_ref, *outs):
    (full_ref, low_ref, sums_ref) = outs if wide_out else (None, *outs)
    rows = rows_ref[...].astype(F32)
    hat, scale = norm_stats(rows)
    width = rows.shape[1]
    upstream = kept_ref[:, :width] + got_ref[:, :width].astype(F32)
    base = base_ref[:, :width].astype(F32)
    grad = base + norm_backward(upstream, hat, scale, gain_ref[...])
    low = grad.astype(BF16)
    if wide_out:
        full_ref[...] = grad
    put(low_ref, low)

    @pl.when(pl.program_id(0) == 0)
    def clear():
        sums_ref[...] = jnp.zeros_like(sums_ref)

    for index, term in enumerate((upstream * hat, upstream, low.astype(F32), base)):
        sums_ref[index : index + 1] += jnp.sum(term, axis=0, keepdims=True)


def norm_back(rows, kept, got, base, gain, wide_out):
    count, width = rows.shape
    block = min(256, count)
    part = pl.BlockSpec((block, width), lambda i: (i, 0))
    sent = pl.BlockSpec((block, lanes(width)), lambda i: (i, 0))
    full = [jax.ShapeDtypeStruct((count, width), F32)] if wide_out else []
    return pl.pallas_call(
        functools.partial(norm_back_body, wide_out),
        grid=(count // block,),
        in_specs=[part, pl.BlockSpec((block, kept.shape[1]), lambda i: (i, 0)), sent]
        + [pl.BlockSpec((block, base.shape[1]), lambda i: (i, 0)), fixed((1, width))],
        out_specs=[part] * len(full) + [sent, pl.BlockSpec((8, width), lambda i: (0, 0))],
        out_shape=full
        + [
            jax.ShapeDtypeStruct((count, lanes(width)), BF16),
            jax.ShapeDtypeStruct((8, width), F32),
        ],
        compiler_params=vmem(40),
        cost_estimate=lasting(7),
        name="norm_back",
    )(rows, kept, got, base, gain)


def feed_forward_body(
    skipped,
    rows_ref,
    cot_ref,
    w_in_mine,
    w_in_theirs,
    w_back_mine,
    w_back_theirs,
    bias_ref,
    *refs,
):
    (
        act_mine, act_theirs, inner_mine, inner_theirs, rows_out, cot_out, out_ref, up_ref, sums_ref
    ) = refs[skipped:]
    model_width = rows_out.shape[1]
    rows, cot = rows_ref[:, :model_width], cot_ref[:, :model_width]
    rows_out[...] = rows
    cot_out[...] = cot

    @pl.when(pl.program_id(0) == 0)
    def clear():
        sums_ref[...] = jnp.zeros_like(sums_ref)

    out, up = None, None
    shares = (
        (w_in_mine, w_back_mine, act_mine, inner_mine),
        (w_in_theirs, w_back_theirs, act_theirs, inner_theirs),
    )
    for part, (w_in, w_back, act_ref, inner_ref) in enumerate(shares):
        hidden = dot_rows(rows, w_in[...]) + bias_ref[part : part + 1]
        value, slope = gelu_parts(hidden)
        act = value.astype(BF16)
        act_ref[...] = act
        inner = (dot_transposed(cot, w_back[...]) * slope).astype(BF16)
        inner_ref[...] = inner
        sums_ref[part : part + 1] += jnp.sum(inner.astype(F32), axis=0, keepdims=True)
        one_out = dot_rows(act, w_back[...])
        one_up = dot_transposed(inner, w_in[...])
        out = one_out if out is None else out + one_out
        up = one_up if up is None else up + one_up
    put(out_ref, out)
    put(up_ref, up)


def feed_forward(rows, cot, half, weights, biases, filled):
    count, sent_width = rows.shape
    model_width, ff_share = weights[0].shape
    block = min(FF_ROWS, count)
    steps = count // block
    row_spec = pl.BlockSpec((block, sent_width), lambda i: (i, 0))
    joined = lambda width: pl.BlockSpec((block, width), lambda i: (half * steps + i, 0))
    act_shape = jax.ShapeDtypeStruct((2 * count, ff_share), BF16)
    row_shape = jax.ShapeDtypeStruct((2 * count, model_width), BF16)
    part_shape = jax.ShapeDtypeStruct((count, sent_width), F32)
    filled = () if filled is None else tuple(filled)
    return pl.pallas_call(
        functools.partial(feed_forward_body, len(filled)),
        out_shape=[act_shape] * 4
        + [row_shape] * 2
        + [part_shape] * 2
        + [jax.ShapeDtypeStruct((8, ff_share), F32)],
        grid=(steps,),
        in_specs=[row_spec, row_spec]
        + [fixed(matrix.shape) for matrix in weights]
        + [fixed((2, ff_share))]
        + [hbm()] * len(filled),
        out_specs=[joined(ff_share)] * 4
        + [joined(model_width)] * 2
        + [row_spec] * 2
        + [pl.BlockSpec((8, ff_share), lambda i: (0, 0))],
        input_output_aliases={7 + i: i for i in range(len(filled))},
        compiler_params=vmem(58),
        cost_estimate=lasting(34),
        name="feed_forward",
    )(rows, cot, *weights, biases, *filled)


def permute(value, axis_name, pairs):
    return lax.ppermute(value, axis_name, pairs)


def swap(value, axis_name, distance):
    count = lax.axis_size(axis_name)
    return permute(value, axis_name, [(i, i ^ distance) for i in range(count)])


def tie(*values):
    return lax.optimization_barrier(values)


def started(sent, value, mark):
    sent, mark = tie(sent, mark)
    value, mark = tie(value, swap(mark, "seq", 1))
    return sent, value, mark


def lower_pairs(pairs, y_count):
    return [
        (source * y_count + y, target * y_count + y)
        for source, target in pairs
        for y in range(y_count)
    ]


def spread_lead(block, z_here):
    far = permute(block, "dp", lower_pairs([(0, 2)], 2))
    held = jnp.where(z_here == 0, block, far)
    near = permute(held, "dp", lower_pairs([(0, 1), (2, 3)], 2))
    return jnp.where(z_here % 2 == 0, held, near)


def move_rest(block, distance, plane_distance):
    over_dp, over_seq = distance
    pairs = []
    for d in range(8):
        if (d // 2) ^ plane_distance != 0:
            pairs += [(d * 4 + q, (d ^ over_dp) * 4 + (q ^ over_seq)) for q in range(4)]
    return permute(block, ("dp", "seq"), pairs)


def pick(stacked, index, axis=0):
    return lax.dynamic_index_in_dim(stacked, index, axis, keepdims=False)


def halve_plane(lower, upper, y_here):
    return (
        jnp.where(y_here == 0, lower, upper),
        jnp.where(y_here == 0, upper, lower).astype(BF16),
    )


def sum_everywhere(value):
    for axis_name in ("seq", "dp"):
        distance = 1
        while distance < lax.axis_size(axis_name):
            value = value + swap(value, axis_name, distance)
            distance *= 2
    return value


def per_device(
    rows_in,
    out_cotangent,
    cell_lengths,
    cell_starts,
    key_mask,
    weights_master,
    first_moment,
    second_moment,
    small_master,
    small_first,
    small_second,
    step_count,
):
    model_width = rows_in.shape[3]
    local_rows = rows_in.shape[2]
    length = key_mask.shape[2]
    shard_len = weights_master.shape[2]
    groups = lax.axis_size("seq")
    dp_count = lax.axis_size("dp")
    head_share = model_width // groups
    heads_here = HEADS // groups
    triple = 3 * head_share
    first_end = model_width * triple
    second_end = first_end + head_share * model_width
    third_end = second_end + model_width * model_width
    seq_here = lax.axis_index("seq")
    dp_here = lax.axis_index("dp")
    chip = seq_here // 2
    core = seq_here % 2
    z_here = dp_here // 2
    y_here = dp_here % 2
    planar = dp_count == 8 and shard_len * 2 == first_end
    shares = (core + 2 * chip, core + 2 * (1 - chip))

    chip_index = chip.reshape(1).astype(jnp.int32)

    def exchange_micro(own, sent):
        received = swap(sent, "seq", 2)
        first = jnp.where(chip == 0, own, received)
        second = jnp.where(chip == 0, received, own)
        return jnp.concatenate([first, second], axis=0)

    def widen(rows):
        return jnp.pad(rows, ((0, 0), (0, lanes(model_width) - model_width)))

    mark = small_master[:8, :128]

    ends = jnp.array([first_end, second_end, third_end, dp_count * shard_len], jnp.int32)
    begin = dp_here * shard_len
    lower_matrix = jnp.sum((begin >= ends).astype(jnp.int32))
    upper_matrix = jnp.sum((begin + shard_len - 1 >= ends).astype(jnp.int32))
    bound = jnp.minimum(pick(ends, lower_matrix) - begin, shard_len).reshape(1)
    matrices = jnp.arange(4, dtype=jnp.int32)

    def matrix_sums(pair):
        return jnp.where(matrices == lower_matrix, pair[0], 0.0) + jnp.where(
            matrices == upper_matrix, pair[1], 0.0
        )

    weight = weights_master
    low_weight = round_weights(weight)
    if planar:
        tall = low_weight.reshape(shard_len // triple, triple)
    own_first, sent_rows = take_rows(chip_index, rows_in)
    own_in = exchange_micro(own_first, sent_rows)[:, :model_width]
    own_cotangent, sent_cotangent = take_rows(chip_index, out_cotangent)
    inputs = own_in.astype(F32)
    hat_one, _ = norm_stats(inputs)
    low_one = widen((hat_one * small_master[0] + small_master[1]).astype(BF16))
    other_one = swap(low_one, "seq", 1)
    weight_squares = square_sums(bound, weight)
    y_index = y_here.reshape(1).astype(jnp.int32)
    if planar:
        wide = low_weight.reshape(shard_len // model_width, model_width)
        cut, tall_rows = wide.shape[0], tall.shape[0]
        lead = spread_lead(tall, z_here)
        across = [move_rest(wide, (1, 0), 0)]
        over = [move_rest(wide, (0, 2), 0)]
        lead, wide, across[0], over[0], other_one, sent_cotangent = tie(
            lead, wide, across[0], over[0], other_one, sent_cotangent
        )
        lead_across = swap(lead, "dp", 1)
        halves = (lead, lead_across, swap(lead, "seq", 2), swap(lead_across, "seq", 2))
        dp_index = dp_here.reshape(1).astype(jnp.int32)
        far = move_rest(wide, (4, 0), 0)
        near = move_rest(wide, (2, 0), 0)
    else:
        copies = lax.all_gather(low_weight.reshape(1, shard_len), ("dp", "seq"), axis=0, tiled=True)
        copies = copies.reshape(dp_count, groups, shard_len)
        per_share = [pick(copies, share, 1).reshape(dp_count * shard_len) for share in shares]
        halves = []
        for flat in per_share:
            matrix = flat[:first_end].reshape(model_width, triple)
            first = jnp.where(y_here == 0, matrix[: model_width // 2], matrix[model_width // 2 :])
            second = jnp.where(y_here == 0, matrix[model_width // 2 :], matrix[: model_width // 2])
            halves += [first, second]
        w_out = [flat[first_end:second_end].reshape(head_share, model_width) for flat in per_share]
        w_in = [flat[second_end:third_end].reshape(model_width, model_width) for flat in per_share]
        w_back = [flat[third_end:].reshape(model_width, model_width) for flat in per_share]

    def share_columns(vector, share):
        return lax.dynamic_slice_in_dim(vector, share * head_share, head_share)

    attn_biases = [
        jnp.concatenate(
            [
                share_columns(small_master[4], share),
                jnp.zeros((head_share,), F32),
                share_columns(small_master[5], share),
            ]
        )
        for share in shares
    ]
    ff_biases = jnp.stack([pick(small_master, 8 + share) for share in shares])

    starts = pick(cell_starts[:, 0], chip)
    lengths = pick(cell_lengths[:, 0], chip)
    places = jnp.arange(length, dtype=jnp.int32)
    inside = (places[:, None] >= starts[None, :]) & (places[:, None] < (starts + lengths)[None, :])
    first_key = jnp.max(jnp.where(inside, starts[None, :], -1), axis=1)
    first_key = jnp.where(first_key < 0, places, first_key)
    low_blocks = first_key.reshape(-1, local_rows)[:, 0] // local_rows
    block_starts = first_key.reshape(-1, 1, local_rows)
    core_index = core.reshape(1).astype(jnp.int32)

    if planar:
        both = [move_rest(over[0], (1, 0), 0)]
        halves, near, far, both[0], weight_squares = tie(
            halves, near, far, both[0], weight_squares
        )
        last = move_rest(far, (2, 0), 2)
        across += [move_rest(near, (1, 0), 1), move_rest(far, (1, 0), 2)]
        over += [move_rest(near, (0, 2), 1), move_rest(far, (0, 2), 2)]
    *qkv, rows_one, w_attn_mine, w_attn_theirs = project(
        y_index, low_one, other_one, halves, jnp.stack(attn_biases)
    )

    def attend(part):
        return attention_forward(low_blocks, core_index, block_starts, qkv[part], heads_here)

    attended = [attend(0)]
    if planar:
        qkv[1], last, across[1:3], over[1:3], sent_cotangent, _ = tie(
            qkv[1], last, across[1:3], over[1:3], sent_cotangent, attended[0][2]
        )
        across.append(move_rest(last, (1, 0), 3))
        over.append(move_rest(last, (0, 2), 3))
        both += [move_rest(over[1], (1, 0), 1), move_rest(across[2], (0, 2), 2)]
    own_e = exchange_micro(own_cotangent, sent_cotangent)
    attended.append(attend(1))
    if planar:
        dp_index, across, over, both, _ = tie(dp_index, across, over, both, attended[1][2])
        both.append(move_rest(over[3], (1, 0), 3))
        rest_mine = [block for pair in zip((wide, near, far, last), across) for block in pair]
        rest_theirs = [block for pair in zip(over, both) for block in pair]
        matrices_mine = unpack_share(dp_index, rest_mine, head_share, model_width)
        matrices_theirs = unpack_share(dp_index, rest_theirs, head_share, model_width)
        w_out, w_in, w_back = (list(pair) for pair in zip(matrices_mine, matrices_theirs))
        own_e, w_out[0] = tie(own_e, w_out[0])
    other_e = swap(own_e, "seq", 1)
    sent, kept = split_product([attended[0][0], attended[1][0]], w_out, False, model_width, BF16)
    middle, low_two = middle_norm(own_in, kept, swap(sent, "seq", 1), small_master)
    other_two = swap(low_two, "seq", 1)

    weights = (w_in[0], w_in[1], w_back[0], w_back[1])
    *filled, out_sent, up_sent, sums_sent = feed_forward(
        other_two, other_e, 1, weights, ff_biases, None
    )
    out_received = swap(out_sent, "seq", 1)
    up_received = swap(up_sent, "seq", 1)
    *filled, out_kept, up_kept, sums_kept = feed_forward(
        low_two, own_e, 0, weights, ff_biases, filled
    )
    activated, inner, (rows_two, rows_e) = filled[:2], filled[2:4], filled[4:]
    inner_sums = sums_sent + sums_kept

    link = BF16 if planar else F32
    grad_mid, low_mid, sums_two = norm_back(
        middle, up_kept, up_received, own_e, small_master[2:3], True
    )
    low_mid, rows_e = tie(low_mid, rows_e)
    back_sent = dot_columns(activated[1], rows_e).astype(link)
    back_sent, low_mid = tie(back_sent, low_mid)
    other_mid = swap(low_mid, "seq", 1)
    rows_two, other_mid = tie(rows_two, other_mid)
    in_sent = dot_columns(rows_two, inner[1]).astype(link)
    in_sent, low_mid = tie(in_sent, low_mid)
    back_received = swap(back_sent, "seq", 2)
    in_received = swap(in_sent, "seq", 2)

    grad_att_mine, grad_att_theirs, rows_mid = out_grads(low_mid, other_mid, w_out)
    out_sent_theirs = dot_columns(attended[1][0], rows_mid).astype(link)
    out_sent_theirs, rows_two, rows_e, rows_mid = tie(out_sent_theirs, rows_two, rows_e, rows_mid)
    outer_received = swap(out_sent_theirs, "seq", 2)
    share_back = dot_columns(activated[0], rows_e)
    share_in = dot_columns(rows_two, inner[0])
    share_out = dot_columns(attended[0][0], rows_mid)
    share_back, share_in, share_out, grad_att_theirs = tie(
        share_back, share_in, share_out, grad_att_theirs
    )

    def return_rows(lower, upper):
        return swap(jnp.where(chip == 0, upper, lower), "seq", 2)

    def attend_back(part, grad_att):
        return attention_backward(
            low_blocks,
            core_index,
            block_starts,
            qkv[part],
            grad_att,
            attended[part][1],
            attended[part][2],
            heads_here,
        )

    packed_theirs = attend_back(1, grad_att_theirs)
    attn_sent = dot_columns(rows_one, packed_theirs).astype(link)
    attn_sent, packed_theirs, outer_received = tie(attn_sent, packed_theirs, outer_received)
    theirs_part = partial_product(packed_theirs, w_attn_theirs)
    attn_sent, theirs_part, y_index, out_received = tie(
        attn_sent, theirs_part, y_index, out_received
    )
    attn_received = swap(attn_sent, "seq", 2)
    if planar:
        kept_rest, sent_rest = pack_rest(
            y_index,
            (share_out, share_in, share_back),
            (outer_received, in_received, back_received),
            cut,
        )
        result_rows = widen(
            (middle + ((out_kept + out_received)[:, :model_width] + small_master[7])).astype(BF16)
        )
        sent_rest, grad_att_mine, result_rows = tie(sent_rest, grad_att_mine, result_rows)
        result_halves = (result_rows[:local_rows], result_rows[local_rows:])
        result_received = return_rows(*result_halves)
        got_rest = swap(sent_rest, "dp", 1)
    else:
        result_rows = widen(
            (middle + ((out_kept + out_received)[:, :model_width] + small_master[7])).astype(BF16)
        )
        result_halves = (result_rows[:local_rows], result_rows[local_rows:])
        result_received = return_rows(*result_halves)
        share_back, share_in, share_out = (
            share_back + back_received,
            share_in + in_received,
            share_out + outer_received,
        )

    packed_mine = attend_back(0, grad_att_mine)
    packed_mine, result_received = tie(packed_mine, result_received)
    sent, kept = split_product(
        [packed_mine], [w_attn_mine], True, model_width, BF16, [theirs_part]
    )
    packed_mine, sent = tie(packed_mine, sent)
    share_attn = dot_columns(rows_one, packed_mine) + attn_received.astype(F32)
    if planar:
        z_odd = z_here % 2 == 1
        kept_lead, sent_lead = halve_plane(share_attn[:tall_rows], share_attn[tall_rows:], y_here)
        kept_lead, sent_lead, kept_rest = tie(kept_lead, sent_lead, kept_rest)
        got_lead = swap(sent_lead, "dp", 1)
        held = [kept_rest[i] + got_rest[i].astype(F32) for i in range(3)]
        sent_near = jnp.where(z_odd, held[1], held[0]).astype(BF16)
        sent_last = held[2].astype(BF16)
        kept_near = jnp.where(z_odd, held[0], held[1])
        kept_last = held[2]
        sent_near, sent_last, kept_lead = tie(sent_near, sent_last, kept_lead)
        got_near = swap(sent_near, "dp", 2)
        got_last = permute(sent_last, "dp", lower_pairs([(0, 1), (2, 3)], 2))
    packed = [packed_mine, packed_theirs]
    if planar:
        held_lead = kept_lead + got_lead.astype(F32)
        sent_lead = held_lead.astype(BF16)
        sent_lead, held_lead, kept_near, kept_last = tie(
            sent_lead, held_lead, kept_near, kept_last
        )
        near_lead = permute(sent_lead, "dp", lower_pairs([(1, 0), (3, 2)], 2))
        held_near = kept_near + got_near.astype(F32)
        held_last = kept_last + got_last.astype(F32)
        sent_far = jnp.where(z_here == 1, held_last, held_near).astype(BF16)
        own_rest = jnp.where(z_here == 3, held_last, held_near)
        sent_far, own_rest, held_lead = tie(sent_far, own_rest, held_lead)
        held_lead = held_lead + near_lead.astype(F32)
        sent_lead = held_lead.astype(BF16)
        sent_lead, held_lead, sent_far, kept = tie(sent_lead, held_lead, sent_far, kept)
        sent_lead, (kept, sent_far), mark = started(sent_lead, (kept, sent_far), mark)
        far_lead = permute(sent_lead, "dp", lower_pairs([(2, 0)], 2))
        got_far = permute(sent_far, "dp", lower_pairs([(3, 1), (0, 2), (1, 3)], 2))
    grad_x, sums_one = norm_back(
        own_in, kept, swap(sent, "seq", 1), grad_mid, small_master[0:1], False
    )

    result_all = place_rows(chip_index, result_rows, result_received, model_width)
    grad_halves = (grad_x[:local_rows], grad_x[local_rows:])
    grad_all = place_rows(chip_index, grad_x, return_rows(*grad_halves), model_width)

    def at_shares(columns):
        row = jnp.zeros((model_width,), F32)
        for share, column in zip(shares, columns):
            row = lax.dynamic_update_slice(row, column, (share * head_share,))
        return row

    bias_sums = [jnp.sum(packed[part].astype(F32), axis=0) for part in range(2)]
    inner_rows = jnp.zeros((4, model_width), F32)
    for part in range(2):
        inner_rows = lax.dynamic_update_slice(
            inner_rows, inner_sums[part : part + 1], (shares[part], 0)
        )
    small_now = jnp.concatenate(
        [
            sums_one[:2],
            sums_two[:2],
            at_shares([sums[:head_share] for sums in bias_sums])[None],
            at_shares([sums[2 * head_share : triple] for sums in bias_sums])[None],
            sums_two[2:4],
            inner_rows,
        ]
    )

    if planar:
        lead_grad = (held_lead + far_lead.astype(F32))[:, :triple].reshape(1, 1, shard_len)
        own_rest, lead_grad, result_all, grad_all, small_now = tie(
            own_rest, lead_grad, result_all, grad_all, small_now
        )
        rest_grad = (own_rest + got_far.astype(F32)).reshape(1, 1, shard_len)
        leads = z_here == 0
    else:
        flat_here = jnp.concatenate(
            [matrix.reshape(-1) for matrix in (share_attn[:, :triple], share_out, share_in, share_back)]
        )
        lead_grad = lax.psum_scatter(
            flat_here.reshape(dp_count, shard_len), "dp", scatter_dimension=0, tiled=True
        ).reshape(1, 1, shard_len)
        rest_grad = lead_grad
        leads = z_here >= 0

    steps_done = step_count[0].astype(F32)
    fix_one = 1.0 - jnp.exp(steps_done * math.log(BETA_ONE))
    fix_two = 1.0 - jnp.exp(steps_done * math.log(BETA_TWO))
    ints = jnp.concatenate([bound, leads.astype(jnp.int32).reshape(1)])
    reduced, moments, update, update_squares = new_moments(
        ints,
        jnp.stack([fix_one, fix_two]),
        lead_grad,
        rest_grad,
        first_moment,
        second_moment,
        weight,
    )
    matrix_rows = jnp.stack([matrix_sums(weight_squares), matrix_sums(update_squares)])
    small_sum = sum_everywhere(
        jnp.concatenate([small_now, jnp.pad(matrix_rows, ((0, 2), (0, model_width - 4)))])
    )
    small_grad = small_sum[:12]
    weight_norms = jnp.sqrt(small_sum[12, :4])
    update_norms = jnp.sqrt(small_sum[13, :4])
    ratios = weight_norms / update_norms
    new_weight, weight_copy = new_weights(
        ints, jnp.stack([pick(ratios, lower_matrix), pick(ratios, upper_matrix)]), weight, update
    )
    small_one = BETA_ONE * small_first + (1.0 - BETA_ONE) * small_grad
    small_two = BETA_TWO * small_second + (1.0 - BETA_TWO) * small_grad * small_grad
    small_late = lax.dynamic_update_slice(small_master, mark, (0, 0))
    small_updated = small_late - SMALL_RATE * (small_one / fix_one) / (
        jnp.sqrt(small_two / fix_two) + ADAM_EPS
    )
    return (
        result_all,
        grad_all,
        reduced,
        moments,
        new_weight,
        weight_copy,
        jnp.stack([weight_norms, update_norms, ratios]),
        small_grad,
        jnp.stack([small_one, small_two]),
        small_updated,
    )


def solution(mesh):
    in_specs = (
        P(None, "dp", "seq", None),
        P(None, "dp", "seq", None),
        P(None, "dp", None),
        P(None, "dp", None),
        P(None, "dp", None),
        P("dp", "seq", None),
        P("dp", "seq", None),
        P("dp", "seq", None),
        P(),
        P(),
        P(),
        P(),
    )
    out_specs = (
        P(None, "dp", "seq", None),
        P(None, "dp", "seq", None),
        P("dp", "seq", None),
        P(None, "dp", "seq", None),
        P("dp", "seq", None),
        P("dp", "seq", None),
        P(),
        P(),
        P(),
        P(),
    )
    return jax.shard_map(
        per_device, mesh=mesh, in_specs=in_specs, out_specs=out_specs, check_vma=False
    )
```

```python
import functools
import math

import jax
import jax.numpy as jnp
from jax import lax
from jax.experimental import pallas as pl
from jax.experimental.pallas import tpu as pltpu
from jax.sharding import PartitionSpec as P

HEADS = 20


NORM_EPS = 1e-05
BETA_ONE = 0.9
BETA_TWO = 0.999
ADAM_EPS = 1e-06
DECAY = 0.01
MATRIX_RATE = 0.3
SMALL_RATE = 0.25
MASKED = -1e30
LOG2_E = 1.4426950408889634
FF_ROWS = 256
SCALE = 1e9

F32 = jnp.float32
BF16 = jnp.bfloat16


def dot_rows(left, right):
    return lax.dot_general(left, right, (((1,), (0,)), ((), ())), preferred_element_type=F32)


def dot_transposed(left, right):
    return lax.dot_general(left, right, (((1,), (1,)), ((), ())), preferred_element_type=F32)


def dot_columns(left, right):
    return lax.dot_general(left, right, (((0,), (0,)), ((), ())), preferred_element_type=F32)


def norm_stats(rows):
    center = jnp.mean(rows, axis=-1, keepdims=True)
    centered = rows - center
    spread = jnp.mean(centered * centered, axis=-1, keepdims=True)
    scale = lax.rsqrt(spread + NORM_EPS)
    return centered * scale, scale


def norm_backward(upstream, hat, scale, gain):
    weighted = upstream * gain
    return (
        weighted
        - jnp.mean(weighted, axis=-1, keepdims=True)
        - hat * jnp.mean(weighted * hat, axis=-1, keepdims=True)
    ) * scale


def gelu_parts(values):
    inner = math.sqrt(2.0 / math.pi)
    squares = values * values
    bent = jnp.tanh(inner * (values + 0.044715 * values * squares))
    half = 0.5 * (1.0 + bent)
    slope = half + 0.5 * values * (1.0 - bent * bent) * inner * (1.0 + 3.0 * 0.044715 * squares)
    return values * half, slope


def block_place(core, block):
    return jnp.where(block % 2 == core, 0, 2) + block // 2


def block_rows(core, block, rows):
    return pl.ds(pl.multiple_of(block_place(core, block) * rows, rows), rows)


def attention_forward_body(
    heads, width, bq, low_ref, core_ref, start_ref, qkv_ref, out_ref, outt_ref, lse_ref, qs, ks, vt, acc
):
    length = qkv_ref.shape[0]
    flat = heads * width
    factor = width**-0.5 * LOG2_E
    core = core_ref[0]

    def unpack(block, carry):
        here = block_rows(core, block, bq)
        there = pl.ds(pl.multiple_of(block * bq, bq), bq)
        for h in range(heads):
            qs[h, there] = qkv_ref[here, h * width : (h + 1) * width]
            ks[h, there] = qkv_ref[here, flat + h * width : flat + (h + 1) * width]
        turned = qkv_ref[here, 2 * flat : 3 * flat].astype(F32).T
        for h in range(heads):
            vt[h, block] = turned[h * width : (h + 1) * width].astype(BF16)
        return carry

    lax.fori_loop(0, length // bq, unpack, 0)

    def query_step(qb, carry):
        q0 = pl.multiple_of(qb * bq, bq)
        start = start_ref[qb]
        query_place = q0 + lax.broadcasted_iota(jnp.int32, (1, bq), 1)
        acc[...] = jnp.zeros_like(acc)

        def key_step(kb, tops_totals):
            tops, totals = tops_totals
            k0 = pl.multiple_of(kb * bq, bq)
            key_place = k0 + lax.broadcasted_iota(jnp.int32, (bq, bq), 0)
            allowed = (key_place <= query_place) & (key_place >= start)
            new_tops, new_totals = [], []
            for h in range(heads):
                scores = dot_transposed(ks[h, pl.ds(k0, bq)], qs[h, pl.ds(q0, bq)]) * factor
                scores = jnp.where(allowed, scores, MASKED)
                top = jnp.maximum(tops[h], jnp.max(scores, axis=0, keepdims=True))
                fade = jnp.exp2(tops[h] - top)
                weights = jnp.exp2(scores - top)
                own = slice(h * width, (h + 1) * width)
                acc[own] = acc[own] * fade + dot_rows(vt[h, kb], weights.astype(BF16))
                new_tops.append(top)
                new_totals.append(totals[h] * fade + jnp.sum(weights, axis=0, keepdims=True))
            return tuple(new_tops), tuple(new_totals)

        first = (
            tuple(jnp.full((1, bq), -1e29, F32) for _ in range(heads)),
            tuple(jnp.zeros((1, bq), F32) for _ in range(heads)),
        )
        tops, totals = lax.fori_loop(low_ref[qb], qb + 1, key_step, first)
        for h in range(heads):
            own = slice(h * width, (h + 1) * width)
            acc[own] = acc[own] * (1.0 / totals[h])
            lse_ref[qb, h : h + 1, :] = tops[h] + jnp.log2(totals[h])
        mixed = acc[...]
        outt_ref[qb] = mixed
        out_ref[block_rows(core, qb, bq), :] = mixed.T.astype(BF16)
        return carry

    lax.fori_loop(0, length // bq, query_step, 0)


def attention_backward_body(
    heads,
    width,
    bq,
    low_ref,
    core_ref,
    start_ref,
    qkv_ref,
    dout_ref,
    outt_ref,
    lse_ref,
    grad_ref,
    qs,
    ks,
    vs,
    ds,
    kt,
    dk,
    dv,
    dqt,
):
    length = qkv_ref.shape[0]
    flat = heads * width
    score_scale = width**-0.5
    factor = score_scale * LOG2_E
    core = core_ref[0]

    def unpack(block, carry):
        here = block_rows(core, block, bq)
        there = pl.ds(pl.multiple_of(block * bq, bq), bq)
        for h in range(heads):
            qs[h, there] = qkv_ref[here, h * width : (h + 1) * width]
            ks[h, there] = qkv_ref[here, flat + h * width : flat + (h + 1) * width]
            vs[h, there] = qkv_ref[here, 2 * flat + h * width : 2 * flat + (h + 1) * width]
            ds[h, there] = dout_ref[here, h * width : (h + 1) * width]
        turned = qkv_ref[here, flat : 2 * flat].astype(F32).T
        for h in range(heads):
            kt[h, block] = turned[h * width : (h + 1) * width].astype(BF16)
        return carry

    lax.fori_loop(0, length // bq, unpack, 0)
    dk[...] = jnp.zeros_like(dk)
    dv[...] = jnp.zeros_like(dv)

    def query_step(qb, carry):
        q0 = pl.multiple_of(qb * bq, bq)
        queries = pl.ds(q0, bq)
        here = block_rows(core, qb, bq)
        start = start_ref[qb]
        query_place = q0 + lax.broadcasted_iota(jnp.int32, (1, bq), 1)
        products = dout_ref[here, :].astype(F32).T * outt_ref[qb]
        inners = [
            jnp.sum(products[h * width : (h + 1) * width], axis=0, keepdims=True)
            for h in range(heads)
        ]
        dqt[...] = jnp.zeros_like(dqt)

        def attend(key_block, key_part, query_part):
            key_count = key_part.stop - key_part.start
            count = query_part.stop - query_part.start
            k0 = pl.multiple_of(key_block * bq + key_part.start, key_count)
            keys = pl.ds(k0, key_count)
            rows = pl.ds(pl.multiple_of(q0 + query_part.start, count), count)
            key_place = k0 + lax.broadcasted_iota(jnp.int32, (key_count, count), 0)
            allowed = (key_place <= query_place[:, query_part]) & (
                key_place >= start[:, query_part]
            )
            for h in range(heads):
                scores = dot_transposed(ks[h, keys], qs[h, rows]) * factor
                weights = jnp.exp2(
                    jnp.where(allowed, scores - lse_ref[qb, h : h + 1, query_part], MASKED)
                )
                dweights = dot_transposed(vs[h, keys], ds[h, rows])
                dscores = (weights * (dweights - inners[h][:, query_part])).astype(BF16)
                dv[h, keys] += dot_rows(weights.astype(BF16), ds[h, rows])
                dk[h, keys] += dot_rows(dscores, qs[h, rows])
                dqt[h * width : (h + 1) * width, query_part] += dot_rows(
                    kt[h, key_block, :, key_part], dscores
                )

        every = slice(0, bq)

        def key_step(kb, inner_carry):
            attend(kb, every, every)
            return inner_carry

        lax.fori_loop(low_ref[qb], qb, key_step, 0)
        attend(qb, slice(0, bq // 2), every)
        attend(qb, slice(bq // 2, bq), slice(bq // 2, bq))
        grad_ref[here, 0:flat] = (dqt[...] * score_scale).T.astype(BF16)
        return carry

    lax.fori_loop(0, length // bq, query_step, 0)

    def write_keys(kb, carry):
        here = block_rows(core, kb, bq)
        rows = pl.ds(pl.multiple_of(kb * bq, bq), bq)
        grad_ref[here, flat : 2 * flat] = jnp.concatenate(
            [dk[h, rows] * score_scale for h in range(heads)], axis=1
        ).astype(BF16)
        grad_ref[here, 2 * flat : 3 * flat] = jnp.concatenate(
            [dv[h, rows] for h in range(heads)], axis=1
        ).astype(BF16)
        rest = grad_ref.shape[1] - 3 * flat
        if rest:
            grad_ref[here, 3 * flat :] = jnp.zeros((bq, rest), BF16)
        return carry

    lax.fori_loop(0, length // bq, write_keys, 0)


def whole_block(shape):
    return pl.BlockSpec(shape, lambda step, *refs: (0,) * len(shape))


def attention_forward(low_blocks, core, starts, qkv, heads):
    length, triple = qkv.shape
    flat = triple // 3
    width = flat // heads
    blocks, _, bq = starts.shape
    grid_spec = pltpu.PrefetchScalarGridSpec(
        num_scalar_prefetch=2,
        grid=(1,),
        in_specs=[whole_block((blocks, 1, bq)), whole_block((length, triple))],
        out_specs=[
            whole_block((length, flat)),
            whole_block((blocks, flat, bq)),
            whole_block((blocks, 8, bq)),
        ],
        scratch_shapes=[
            pltpu.VMEM((heads, length, width), BF16),
            pltpu.VMEM((heads, length, width), BF16),
            pltpu.VMEM((heads, blocks, width, bq), BF16),
            pltpu.VMEM((flat, bq), F32),
        ],
    )
    return pl.pallas_call(
        functools.partial(attention_forward_body, heads, width, bq),
        out_shape=[
            jax.ShapeDtypeStruct((length, flat), BF16),
            jax.ShapeDtypeStruct((blocks, flat, bq), F32),
            jax.ShapeDtypeStruct((blocks, 8, bq), F32),
        ],
        grid_spec=grid_spec,
        compiler_params=pltpu.CompilerParams(vmem_limit_bytes=48 << 20),
        cost_estimate=lasting(35),
        name="attention_forward",
    )(low_blocks, core, starts, qkv)


def attention_backward(low_blocks, core, starts, qkv, grad_out, out_turned, log_total, heads):
    length, triple = qkv.shape
    flat = triple // 3
    width = flat // heads
    blocks, _, bq = starts.shape
    per_head = pltpu.VMEM((heads, length, width), BF16)
    sums = pltpu.VMEM((heads, length, width), F32)
    grid_spec = pltpu.PrefetchScalarGridSpec(
        num_scalar_prefetch=2,
        grid=(1,),
        in_specs=[
            whole_block((blocks, 1, bq)),
            whole_block((length, triple)),
            whole_block((length, flat)),
            whole_block((blocks, flat, bq)),
            whole_block((blocks, 8, bq)),
        ],
        out_specs=whole_block((length, lanes(triple))),
        scratch_shapes=[
            per_head,
            per_head,
            per_head,
            per_head,
            pltpu.VMEM((heads, blocks, width, bq), BF16),
            sums,
            sums,
            pltpu.VMEM((flat, bq), F32),
        ],
    )
    return pl.pallas_call(
        functools.partial(attention_backward_body, heads, width, bq),
        out_shape=jax.ShapeDtypeStruct((length, lanes(triple)), BF16),
        grid_spec=grid_spec,
        compiler_params=pltpu.CompilerParams(vmem_limit_bytes=60 << 20),
        cost_estimate=lasting(56),
        name="attention_backward",
    )(low_blocks, core, starts, qkv, grad_out, out_turned, log_total)


def lasting(micros):
    return pl.CostEstimate(flops=int(micros * SCALE), bytes_accessed=1 << 12, transcendentals=0)


def lanes(width):
    return -(-width // 128) * 128


def put(ref, value):
    width = value.shape[1]
    ref[:, :width] = value.astype(ref.dtype)
    if width < ref.shape[1]:
        ref[:, width:] = jnp.zeros((value.shape[0], ref.shape[1] - width), ref.dtype)


def vmem(count):
    return pltpu.CompilerParams(vmem_limit_bytes=count << 20)


def fixed(shape):
    return pl.BlockSpec(shape, lambda *step: (0,) * len(shape), pipeline_mode=pl.Buffered(1))


def hbm():
    return pl.BlockSpec(memory_space=pl.ANY)


def round_weights_body(weight_ref, low_ref):
    low_ref[...] = weight_ref[0, 0, :].astype(BF16)


def round_weights(weight):
    whole = pl.BlockSpec(memory_space=pltpu.VMEM)
    return pl.pallas_call(
        round_weights_body,
        in_specs=[whole],
        out_specs=whole,
        out_shape=jax.ShapeDtypeStruct(weight.shape[2:], BF16),
        compiler_params=vmem(32),
        cost_estimate=lasting(6),
        name="round_weights",
    )(weight)


def add_squares(sums_ref, values, in_lower):
    squares = values * values
    lower = jnp.sum(jnp.where(in_lower, squares, 0.0))
    sums_ref[0] += lower
    sums_ref[1] += jnp.sum(squares) - lower


def square_sums_body(bound_ref, weight_ref, sums_ref):
    sums_ref[0] = 0.0
    sums_ref[1] = 0.0
    place = lax.broadcasted_iota(jnp.int32, weight_ref.shape, 2)
    add_squares(sums_ref, weight_ref[...], place < bound_ref[0])


def square_sums(bound, weight):
    smem = pl.BlockSpec(memory_space=pltpu.SMEM)
    return pl.pallas_call(
        square_sums_body,
        in_specs=[smem, pl.BlockSpec(memory_space=pltpu.VMEM)],
        out_specs=smem,
        out_shape=jax.ShapeDtypeStruct((2,), F32),
        compiler_params=vmem(32),
        cost_estimate=lasting(6),
        name="square_sums",
    )(bound, weight)


def moments_body(
    ints_ref, floats_ref, lead_ref, rest_ref, first_ref, second_ref, weight_ref,
    grad_ref, moments_ref, update_ref, sums_ref,
):
    step = pl.program_id(0)
    grad = jnp.where(ints_ref[1] == 1, lead_ref[...], rest_ref[...])
    grad_ref[...] = grad
    first = BETA_ONE * first_ref[...] + (1.0 - BETA_ONE) * grad
    second = BETA_TWO * second_ref[...] + (1.0 - BETA_TWO) * grad * grad
    moments_ref[0] = first
    moments_ref[1] = second
    update = (first / floats_ref[0]) / (jnp.sqrt(second / floats_ref[1]) + ADAM_EPS)
    update = update + DECAY * weight_ref[...]
    update_ref[...] = update
    count = grad.shape[2]
    place = step * count + lax.broadcasted_iota(jnp.int32, grad.shape, 2)

    @pl.when(step == 0)
    def clear():
        sums_ref[0] = 0.0
        sums_ref[1] = 0.0

    add_squares(sums_ref, update, place < ints_ref[0])


def flat_steps(count):
    return 7 if count % (7 * 128) == 0 else 1


def new_moments(ints, floats, lead, rest, first, second, weight):
    count = weight.shape[2]
    steps = flat_steps(count)
    smem = pl.BlockSpec(memory_space=pltpu.SMEM)
    flat = pl.BlockSpec((1, 1, count // steps), lambda i: (0, 0, i))
    pair = pl.BlockSpec((2, 1, 1, count // steps), lambda i: (0, 0, 0, i))
    return pl.pallas_call(
        moments_body,
        grid=(steps,),
        in_specs=[smem, smem] + [flat] * 5,
        out_specs=[flat, pair, flat, smem],
        out_shape=[
            jax.ShapeDtypeStruct(weight.shape, F32),
            jax.ShapeDtypeStruct((2,) + weight.shape, F32),
            jax.ShapeDtypeStruct(weight.shape, F32),
            jax.ShapeDtypeStruct((2,), F32),
        ],
        compiler_params=vmem(48),
        cost_estimate=lasting(10),
        name="new_moments",
    )(ints, floats, lead, rest, first, second, weight)


def new_weights_body(ints_ref, ratio_ref, weight_ref, update_ref, new_ref, copy_ref):
    count = weight_ref.shape[2]
    place = pl.program_id(0) * count + lax.broadcasted_iota(jnp.int32, weight_ref.shape, 2)
    rate = jnp.where(place < ints_ref[0], ratio_ref[0], ratio_ref[1])
    new = weight_ref[...] - MATRIX_RATE * rate * update_ref[...]
    new_ref[...] = new
    copy_ref[...] = new.astype(BF16)


def new_weights(ints, ratios, weight, update):
    count = weight.shape[2]
    steps = flat_steps(count)
    smem = pl.BlockSpec(memory_space=pltpu.SMEM)
    flat = pl.BlockSpec((1, 1, count // steps), lambda i: (0, 0, i))
    return pl.pallas_call(
        new_weights_body,
        grid=(steps,),
        in_specs=[smem, smem, flat, flat],
        out_specs=[flat, flat],
        out_shape=[
            jax.ShapeDtypeStruct(weight.shape, F32),
            jax.ShapeDtypeStruct(weight.shape, BF16),
        ],
        compiler_params=vmem(32),
        cost_estimate=lasting(6),
        name="new_weights",
    )(ints, ratios, weight, update)


def unpack_body(cut, rows, skipped, place_ref, *refs):
    blocks, (w_out, w_in, w_back, held, sems) = refs[:8], refs[8 + skipped :]
    here = place_ref[0]
    copies = [
        pltpu.make_async_copy(block, held.at[index ^ here], sems.at[index])
        for index, block in enumerate(blocks)
    ]
    for copy in copies:
        copy.start()
    for copy in copies:
        copy.wait()
    begin, columns = 2 * cut, held.shape[2]
    for target, count_rows in zip((w_out, w_in, w_back), rows):
        done = 0
        while done < count_rows:
            block, offset = divmod(begin + done, cut)
            count = min(cut - offset, count_rows - done)
            target[done : done + count, :columns] = held[block, offset : offset + count]
            done += count
        begin += count_rows
        if target.shape[1] > columns:
            target[:, columns:] = jnp.zeros((count_rows, target.shape[1] - columns), BF16)
    rest = w_back.shape[0] - rows[2]
    if rest:
        w_back[rows[2] :] = jnp.zeros((rest, w_back.shape[1]), BF16)


def unpack_share(place, blocks, out_rows, in_rows, part, joined):
    cut, columns = blocks[0].shape
    wide = lanes(columns)
    joined = () if joined is None else tuple(joined)
    return pl.pallas_call(
        functools.partial(unpack_body, cut, (out_rows, in_rows, columns), len(joined)),
        grid_spec=pltpu.PrefetchScalarGridSpec(
            num_scalar_prefetch=1,
            grid=(1,),
            in_specs=[hbm()] * (8 + len(joined)),
            out_specs=[
                whole_block((out_rows, columns)),
                pl.BlockSpec((in_rows, wide), lambda i, place_ref: (0, part)),
                pl.BlockSpec((wide, columns), lambda i, place_ref: (part, 0)),
            ],
            scratch_shapes=[
                pltpu.VMEM((8, cut, columns), BF16),
                pltpu.SemaphoreType.DMA((8,)),
            ],
        ),
        out_shape=[
            jax.ShapeDtypeStruct((out_rows, columns), BF16),
            jax.ShapeDtypeStruct((in_rows, 2 * wide), BF16),
            jax.ShapeDtypeStruct((2 * wide, columns), BF16),
        ],
        input_output_aliases={9 + i: 1 + i for i in range(len(joined))},
        compiler_params=vmem(48),
        cost_estimate=lasting(6),
        name="unpack_share",
    )(place, *blocks, *joined)


def pack_rest_body(
    cut, place_ref, out_ref, in_ref, back_ref, out_got, in_got, back_got, kept_ref, sent_ref
):
    here = place_ref[0]
    place = 0
    for matrix, got in ((out_ref, out_got), (in_ref, in_got), (back_ref, back_got)):
        done, rows = 0, matrix.shape[0]
        while done < rows:
            block, offset = divmod(place, cut)
            count = min(cut - offset, rows - done)
            source = slice(done, done + count)
            target = slice(offset, offset + count)
            plane, side = divmod(block, 2)

            @pl.when(here == side)
            def keep(matrix=matrix, got=got, source=source, target=target, plane=plane):
                kept_ref[plane, target] = matrix[source] + got[source].astype(F32)

            @pl.when(here != side)
            def send(matrix=matrix, got=got, source=source, target=target, plane=plane):
                sent_ref[plane, target] = (matrix[source] + got[source].astype(F32)).astype(BF16)

            done += count
            place += count


def pack_rest(place, matrices, received, cut):
    columns = matrices[0].shape[1]
    whole = pl.BlockSpec(memory_space=pltpu.VMEM)
    return pl.pallas_call(
        functools.partial(pack_rest_body, cut),
        in_specs=[pl.BlockSpec(memory_space=pltpu.SMEM)] + [whole] * 6,
        out_specs=[whole] * 2,
        out_shape=[
            jax.ShapeDtypeStruct((3, cut, columns), F32),
            jax.ShapeDtypeStruct((3, cut, columns), BF16),
        ],
        compiler_params=vmem(40),
        cost_estimate=lasting(10),
        name="pack_rest",
    )(place, *matrices, *received)


def rows_of(step, steps, own_ref, other_ref, width):
    return jnp.where(step < steps, own_ref[:, :width], other_ref[:, :width])


def both_specs(block, width, steps):
    own = pl.BlockSpec((block, width), lambda i, *refs: (jnp.minimum(i, steps - 1), 0))
    other = pl.BlockSpec((block, width), lambda i, *refs: (jnp.maximum(i - steps, 0), 0))
    return own, other


def project_body(
    steps, place_ref, own_ref, other_ref, a0, a1, b0, b1, bias_ref,
    out_a, out_b, rows_ref, w_a, w_b, sems,
):
    step = pl.program_id(0)

    @pl.when(step == 0)
    def load():
        cut = a0.shape[0]
        here = place_ref[0]
        first = pl.ds(pl.multiple_of(here * cut, cut), cut)
        second = pl.ds(pl.multiple_of((1 - here) * cut, cut), cut)
        copies = [
            pltpu.make_async_copy(a0, w_a.at[first], sems.at[0]),
            pltpu.make_async_copy(a1, w_a.at[second], sems.at[1]),
            pltpu.make_async_copy(b0, w_b.at[first], sems.at[2]),
            pltpu.make_async_copy(b1, w_b.at[second], sems.at[3]),
        ]
        for copy in copies:
            copy.start()
        for copy in copies:
            copy.wait()

    rows = rows_of(step, steps, own_ref, other_ref, rows_ref.shape[1])
    rows_ref[...] = rows
    out_a[...] = (dot_rows(rows, w_a[...]) + bias_ref[0:1]).astype(BF16)
    out_b[...] = (dot_rows(rows, w_b[...]) + bias_ref[1:2]).astype(BF16)


def project(place, own, other, halves, biases):
    count, sent_width = own.shape
    cut, triple = halves[0].shape
    model_width = 2 * cut
    block = min(512, count)
    steps = count // block
    row_out = lambda width: pl.BlockSpec((block, width), lambda i, *refs: (i, 0))
    matrix = jax.ShapeDtypeStruct((2 * cut, triple), BF16)
    return pl.pallas_call(
        functools.partial(project_body, steps),
        grid_spec=pltpu.PrefetchScalarGridSpec(
            num_scalar_prefetch=1,
            grid=(2 * steps,),
            in_specs=[*both_specs(block, sent_width, steps)]
            + [hbm()] * 4
            + [fixed((2, triple))],
            out_specs=[row_out(triple), row_out(triple), row_out(model_width)]
            + [pl.BlockSpec(matrix.shape, lambda i, *refs: (0, 0))] * 2,
            scratch_shapes=[pltpu.SemaphoreType.DMA((4,))],
        ),
        out_shape=[jax.ShapeDtypeStruct((2 * count, triple), BF16)] * 2
        + [jax.ShapeDtypeStruct((2 * count, model_width), BF16), matrix, matrix],
        compiler_params=vmem(48),
        cost_estimate=lasting(16),
        name="project",
    )(place, own, other, *halves, biases)


def out_grads_body(steps, own_ref, other_ref, w_a, w_b, out_a, out_b, rows_ref):
    rows = rows_of(pl.program_id(0), steps, own_ref, other_ref, rows_ref.shape[1])
    rows_ref[...] = rows
    out_a[...] = dot_transposed(rows, w_a[...]).astype(BF16)
    out_b[...] = dot_transposed(rows, w_b[...]).astype(BF16)


def out_grads(own, other, w_out):
    count, sent_width = own.shape
    width, model_width = w_out[0].shape
    block = min(512, count)
    steps = count // block
    row_out = lambda columns: pl.BlockSpec((block, columns), lambda i: (i, 0))
    return pl.pallas_call(
        functools.partial(out_grads_body, steps),
        grid=(2 * steps,),
        in_specs=[*both_specs(block, sent_width, steps)] + [fixed(w_out[0].shape)] * 2,
        out_specs=[row_out(width), row_out(width), row_out(model_width)],
        out_shape=[jax.ShapeDtypeStruct((2 * count, width), BF16)] * 2
        + [jax.ShapeDtypeStruct((2 * count, model_width), BF16)],
        compiler_params=vmem(48),
        cost_estimate=lasting(8),
        name="out_grads",
    )(own, other, *w_out)


def row_products(turned, left_refs, weight_refs):
    product = None
    for left, weight in zip(left_refs, weight_refs):
        if turned:
            term = dot_transposed(left[:, : weight.shape[1]], weight[...])
        else:
            term = dot_rows(left[:, : weight.shape[0]], weight[...])
        product = term if product is None else product + term
    return product


def partial_product_body(left, weight, out_ref):
    out_ref[...] = row_products(True, [left], [weight])


def split_product_body(steps, turned, count, *refs):
    lefts, weights, rest = refs[:count], refs[count : 2 * count], refs[2 * count :]
    *partial, sent_ref, kept_ref = rest
    product = row_products(turned, lefts, weights)
    if partial:
        product = product + partial[0][...]
    step = pl.program_id(0)

    @pl.when(step < steps)
    def other_rows():
        put(sent_ref, product)

    @pl.when(step >= steps)
    def own_rows():
        put(kept_ref, product)


def other_first(block, width, steps):
    return pl.BlockSpec((block, width), lambda i: ((i + steps) % (2 * steps), 0))


def partial_product(left, weight):
    count, width = left.shape
    model_width = weight.shape[0]
    block = min(512, count // 2)
    steps = count // 2 // block
    return pl.pallas_call(
        partial_product_body,
        grid=(2 * steps,),
        in_specs=[other_first(block, width, steps), fixed(weight.shape)],
        out_specs=pl.BlockSpec((block, model_width), lambda i: (i, 0)),
        out_shape=jax.ShapeDtypeStruct((count, model_width), F32),
        compiler_params=vmem(48),
        cost_estimate=lasting(9),
        name="partial_product",
    )(left, weight)


def split_product(lefts, weights, turned, model_width, sent_type, partial=()):
    count, width = lefts[0].shape
    block = min(512, count // 2)
    steps = count // 2 // block
    parts = [
        jax.ShapeDtypeStruct((count // 2, lanes(model_width)), sent_type),
        jax.ShapeDtypeStruct((count // 2, model_width), F32),
    ]
    return pl.pallas_call(
        functools.partial(split_product_body, steps, turned, len(lefts)),
        grid=(2 * steps,),
        in_specs=[other_first(block, width, steps)] * len(lefts)
        + [fixed(weight.shape) for weight in weights]
        + [pl.BlockSpec((block, model_width), lambda i: (i, 0))] * len(partial),
        out_specs=[
            pl.BlockSpec((block, lanes(model_width)), lambda i: (jnp.minimum(i, steps - 1), 0)),
            pl.BlockSpec((block, model_width), lambda i: (jnp.maximum(i - steps, 0), 0)),
        ],
        out_shape=parts,
        compiler_params=vmem(48),
        cost_estimate=lasting(9),
        name="split_product",
    )(*lefts, *weights, *partial)


def middle_body(rows_ref, kept_ref, got_ref, small_ref, middle_ref, low_ref):
    middle = rows_ref[...].astype(F32) + (
        kept_ref[...] + got_ref[:, : kept_ref.shape[1]].astype(F32) + small_ref[6:7]
    )
    middle_ref[...] = middle
    hat, _ = norm_stats(middle)
    put(low_ref, (hat * small_ref[2:3] + small_ref[3:4]).astype(BF16))


def middle_norm(rows, kept, got, small):
    count, width = rows.shape
    block = min(256, count)
    part = pl.BlockSpec((block, width), lambda i: (i, 0))
    sent = pl.BlockSpec((block, lanes(width)), lambda i: (i, 0))
    return pl.pallas_call(
        middle_body,
        grid=(count // block,),
        in_specs=[part, part, sent, fixed(small.shape)],
        out_specs=[part, sent],
        out_shape=[
            jax.ShapeDtypeStruct((count, width), F32),
            jax.ShapeDtypeStruct((count, lanes(width)), BF16),
        ],
        compiler_params=vmem(32),
        cost_estimate=lasting(4),
        name="middle_norm",
    )(rows, kept, got, small)


def turn(block):
    return block.astype(F32).T.astype(BF16)


def take_rows_body(chip_ref, array_ref, own_ref, sent_ref):
    rows = turn(array_ref[0, 0])

    @pl.when(pl.program_id(0) == 0)
    def other_micro():
        put(sent_ref, rows)

    @pl.when(pl.program_id(0) == 1)
    def own_micro():
        put(own_ref, rows)


def take_rows(chip, array):
    turned = jnp.swapaxes(array, 2, 3)
    _, _, width, count = turned.shape
    out = pl.BlockSpec((count, lanes(width)), lambda i, chip_ref: (0, 0))
    return pl.pallas_call(
        take_rows_body,
        grid_spec=pltpu.PrefetchScalarGridSpec(
            num_scalar_prefetch=1,
            grid=(2,),
            in_specs=[
                pl.BlockSpec(
                    (1, 1, width, count),
                    lambda i, chip_ref: (jnp.where(i == 0, 1 - chip_ref[0], chip_ref[0]), 0, 0, 0),
                )
            ],
            out_specs=[out, out],
        ),
        out_shape=[jax.ShapeDtypeStruct((count, lanes(width)), BF16)] * 2,
        compiler_params=vmem(32),
        cost_estimate=lasting(4),
        name="take_rows",
    )(chip, turned)


def place_rows_body(chip_ref, rows_ref, received_ref, out_ref):
    width = out_ref.shape[2]
    rows = jnp.where(
        pl.program_id(0) == chip_ref[0], rows_ref[:, :width], received_ref[:, :width]
    )
    out_ref[0, 0] = turn(rows)


def place_rows(chip, rows, received, width):
    count, sent_width = received.shape
    turned = pl.pallas_call(
        place_rows_body,
        grid_spec=pltpu.PrefetchScalarGridSpec(
            num_scalar_prefetch=1,
            grid=(2,),
            in_specs=[
                pl.BlockSpec((count, sent_width), lambda i, chip_ref: (chip_ref[0], 0)),
                pl.BlockSpec((count, sent_width), lambda i, chip_ref: (0, 0)),
            ],
            out_specs=pl.BlockSpec((1, 1, width, count), lambda i, chip_ref: (i, 0, 0, 0)),
        ),
        out_shape=jax.ShapeDtypeStruct((2, 1, width, count), BF16),
        compiler_params=vmem(32),
        cost_estimate=lasting(4),
        name="place_rows",
    )(chip, rows, received)
    return jnp.swapaxes(turned, 2, 3)


def norm_back_body(wide_out, rows_ref, kept_ref, got_ref, base_ref, gain_ref, *outs):
    (full_ref, low_ref, sums_ref) = outs if wide_out else (None, *outs)
    rows = rows_ref[...].astype(F32)
    hat, scale = norm_stats(rows)
    width = rows.shape[1]
    upstream = kept_ref[:, :width] + got_ref[:, :width].astype(F32)
    base = base_ref[:, :width].astype(F32)
    grad = base + norm_backward(upstream, hat, scale, gain_ref[...])
    low = grad.astype(BF16)
    if wide_out:
        full_ref[...] = grad
    put(low_ref, low)

    @pl.when(pl.program_id(0) == 0)
    def clear():
        sums_ref[...] = jnp.zeros_like(sums_ref)

    for index, term in enumerate((upstream * hat, upstream, low.astype(F32), base)):
        sums_ref[index : index + 1] += jnp.sum(term, axis=0, keepdims=True)


def norm_back(rows, kept, got, base, gain, wide_out):
    count, width = rows.shape
    block = min(256, count)
    part = pl.BlockSpec((block, width), lambda i: (i, 0))
    sent = pl.BlockSpec((block, lanes(width)), lambda i: (i, 0))
    full = [jax.ShapeDtypeStruct((count, width), F32)] if wide_out else []
    return pl.pallas_call(
        functools.partial(norm_back_body, wide_out),
        grid=(count // block,),
        in_specs=[part, pl.BlockSpec((block, kept.shape[1]), lambda i: (i, 0)), sent]
        + [pl.BlockSpec((block, base.shape[1]), lambda i: (i, 0)), fixed((1, width))],
        out_specs=[part] * len(full) + [sent, pl.BlockSpec((8, width), lambda i: (0, 0))],
        out_shape=full
        + [
            jax.ShapeDtypeStruct((count, lanes(width)), BF16),
            jax.ShapeDtypeStruct((8, width), F32),
        ],
        compiler_params=vmem(40),
        cost_estimate=lasting(7),
        name="norm_back",
    )(rows, kept, got, base, gain)


def feed_forward_body(skipped, rows_ref, cot_ref, w_in, w_back, bias_ref, *refs):
    (
        act_mine, act_theirs, inner_mine, inner_theirs, rows_out, cot_out, out_ref, up_ref, sums_ref
    ) = refs[skipped:]
    model_width = rows_out.shape[1]
    rows, cot = rows_ref[:, :model_width], cot_ref[:, :model_width]
    rows_out[...] = rows
    cot_out[...] = cot

    @pl.when(pl.program_id(0) == 0)
    def clear():
        sums_ref[...] = jnp.zeros_like(sums_ref)

    width = act_mine.shape[1]
    wide = w_in.shape[1] // 2
    value, slope = gelu_parts(dot_rows(rows, w_in[...]) + bias_ref[0:1])
    act = value.astype(BF16)
    inner = (dot_transposed(cot, w_back[...]) * slope).astype(BF16)
    sums_ref[0:1] += jnp.sum(inner.astype(F32), axis=0, keepdims=True)
    for part, (act_ref, inner_ref) in enumerate(
        ((act_mine, inner_mine), (act_theirs, inner_theirs))
    ):
        act_ref[...] = act[:, part * wide : part * wide + width]
        inner_ref[...] = inner[:, part * wide : part * wide + width]
    put(out_ref, dot_rows(act, w_back[...]))
    put(up_ref, dot_transposed(inner, w_in[...]))


def feed_forward(rows, cot, half, weights, biases, filled):
    count, sent_width = rows.shape
    model_width, both_wide = weights[0].shape
    ff_share = biases.shape[1]
    pad = both_wide // 2 - ff_share
    biases = jnp.pad(biases, ((0, 0), (0, pad))).reshape(1, both_wide)
    block = min(FF_ROWS, count)
    steps = count // block
    row_spec = pl.BlockSpec((block, sent_width), lambda i: (i, 0))
    joined = lambda width: pl.BlockSpec((block, width), lambda i: (half * steps + i, 0))
    act_shape = jax.ShapeDtypeStruct((2 * count, ff_share), BF16)
    row_shape = jax.ShapeDtypeStruct((2 * count, model_width), BF16)
    part_shape = jax.ShapeDtypeStruct((count, sent_width), F32)
    filled = () if filled is None else tuple(filled)
    return pl.pallas_call(
        functools.partial(feed_forward_body, len(filled)),
        out_shape=[act_shape] * 4
        + [row_shape] * 2
        + [part_shape] * 2
        + [jax.ShapeDtypeStruct((8, both_wide), F32)],
        grid=(steps,),
        in_specs=[row_spec, row_spec]
        + [fixed(matrix.shape) for matrix in weights]
        + [fixed((1, both_wide))]
        + [hbm()] * len(filled),
        out_specs=[joined(ff_share)] * 4
        + [joined(model_width)] * 2
        + [row_spec] * 2
        + [pl.BlockSpec((8, both_wide), lambda i: (0, 0))],
        input_output_aliases={5 + i: i for i in range(len(filled))},
        compiler_params=vmem(58),
        cost_estimate=lasting(34),
        name="feed_forward",
    )(rows, cot, *weights, biases, *filled)


def permute(value, axis_name, pairs):
    return lax.ppermute(value, axis_name, pairs)


def swap(value, axis_name, distance):
    count = lax.axis_size(axis_name)
    return permute(value, axis_name, [(i, i ^ distance) for i in range(count)])


def tie(*values):
    return lax.optimization_barrier(values)


def started(sent, value, mark):
    sent, mark = tie(sent, mark)
    value, mark = tie(value, swap(mark, "seq", 1))
    return sent, value, mark


def lower_pairs(pairs, y_count):
    return [
        (source * y_count + y, target * y_count + y)
        for source, target in pairs
        for y in range(y_count)
    ]


def spread_lead(block, z_here):
    far = permute(block, "dp", lower_pairs([(0, 2)], 2))
    held = jnp.where(z_here == 0, block, far)
    near = permute(held, "dp", lower_pairs([(0, 1), (2, 3)], 2))
    return jnp.where(z_here % 2 == 0, held, near)


def move_rest(block, distance, plane_distance):
    over_dp, over_seq = distance
    pairs = []
    for d in range(8):
        if (d // 2) ^ plane_distance != 0:
            pairs += [(d * 4 + q, (d ^ over_dp) * 4 + (q ^ over_seq)) for q in range(4)]
    return permute(block, ("dp", "seq"), pairs)


def pick(stacked, index, axis=0):
    return lax.dynamic_index_in_dim(stacked, index, axis, keepdims=False)


def halve_plane(lower, upper, y_here):
    return (
        jnp.where(y_here == 0, lower, upper),
        jnp.where(y_here == 0, upper, lower).astype(BF16),
    )


def sum_everywhere(value):
    for axis_name in ("seq", "dp"):
        distance = 1
        while distance < lax.axis_size(axis_name):
            value = value + swap(value, axis_name, distance)
            distance *= 2
    return value


def per_device(
    rows_in,
    out_cotangent,
    cell_lengths,
    cell_starts,
    key_mask,
    weights_master,
    first_moment,
    second_moment,
    small_master,
    small_first,
    small_second,
    step_count,
):
    model_width = rows_in.shape[3]
    local_rows = rows_in.shape[2]
    length = key_mask.shape[2]
    shard_len = weights_master.shape[2]
    groups = lax.axis_size("seq")
    dp_count = lax.axis_size("dp")
    head_share = model_width // groups
    heads_here = HEADS // groups
    triple = 3 * head_share
    first_end = model_width * triple
    second_end = first_end + head_share * model_width
    third_end = second_end + model_width * model_width
    seq_here = lax.axis_index("seq")
    dp_here = lax.axis_index("dp")
    chip = seq_here // 2
    core = seq_here % 2
    z_here = dp_here // 2
    y_here = dp_here % 2
    planar = dp_count == 8 and shard_len * 2 == first_end
    shares = (core + 2 * chip, core + 2 * (1 - chip))

    chip_index = chip.reshape(1).astype(jnp.int32)

    def exchange_micro(own, sent):
        received = swap(sent, "seq", 2)
        first = jnp.where(chip == 0, own, received)
        second = jnp.where(chip == 0, received, own)
        return jnp.concatenate([first, second], axis=0)

    def widen(rows):
        return jnp.pad(rows, ((0, 0), (0, lanes(model_width) - model_width)))

    mark = small_master[:8, :128]

    ends = jnp.array([first_end, second_end, third_end, dp_count * shard_len], jnp.int32)
    begin = dp_here * shard_len
    lower_matrix = jnp.sum((begin >= ends).astype(jnp.int32))
    upper_matrix = jnp.sum((begin + shard_len - 1 >= ends).astype(jnp.int32))
    bound = jnp.minimum(pick(ends, lower_matrix) - begin, shard_len).reshape(1)
    matrices = jnp.arange(4, dtype=jnp.int32)

    def matrix_sums(pair):
        return jnp.where(matrices == lower_matrix, pair[0], 0.0) + jnp.where(
            matrices == upper_matrix, pair[1], 0.0
        )

    weight = weights_master
    low_weight = round_weights(weight)
    if planar:
        tall = low_weight.reshape(shard_len // triple, triple)
    own_first, sent_rows = take_rows(chip_index, rows_in)
    own_in = exchange_micro(own_first, sent_rows)[:, :model_width]
    own_cotangent, sent_cotangent = take_rows(chip_index, out_cotangent)
    inputs = own_in.astype(F32)
    hat_one, _ = norm_stats(inputs)
    low_one = widen((hat_one * small_master[0] + small_master[1]).astype(BF16))
    other_one = swap(low_one, "seq", 1)
    weight_squares = square_sums(bound, weight)
    y_index = y_here.reshape(1).astype(jnp.int32)
    if planar:
        wide = low_weight.reshape(shard_len // model_width, model_width)
        cut, tall_rows = wide.shape[0], tall.shape[0]
        lead = spread_lead(tall, z_here)
        across = [move_rest(wide, (1, 0), 0)]
        over = [move_rest(wide, (0, 2), 0)]
        lead, wide, across[0], over[0], other_one, sent_cotangent = tie(
            lead, wide, across[0], over[0], other_one, sent_cotangent
        )
        lead_across = swap(lead, "dp", 1)
        halves = (lead, lead_across, swap(lead, "seq", 2), swap(lead_across, "seq", 2))
        dp_index = dp_here.reshape(1).astype(jnp.int32)
        far = move_rest(wide, (4, 0), 0)
        near = move_rest(wide, (2, 0), 0)
    else:
        copies = lax.all_gather(low_weight.reshape(1, shard_len), ("dp", "seq"), axis=0, tiled=True)
        copies = copies.reshape(dp_count, groups, shard_len)
        per_share = [pick(copies, share, 1).reshape(dp_count * shard_len) for share in shares]
        halves = []
        for flat in per_share:
            matrix = flat[:first_end].reshape(model_width, triple)
            first = jnp.where(y_here == 0, matrix[: model_width // 2], matrix[model_width // 2 :])
            second = jnp.where(y_here == 0, matrix[model_width // 2 :], matrix[: model_width // 2])
            halves += [first, second]
        w_out = [flat[first_end:second_end].reshape(head_share, model_width) for flat in per_share]
        beyond = lanes(model_width) - model_width
        w_in = jnp.concatenate(
            [
                jnp.pad(
                    flat[second_end:third_end].reshape(model_width, model_width),
                    ((0, 0), (0, beyond)),
                )
                for flat in per_share
            ],
            axis=1,
        )
        w_back = jnp.concatenate(
            [
                jnp.pad(flat[third_end:].reshape(model_width, model_width), ((0, beyond), (0, 0)))
                for flat in per_share
            ]
        )

    def share_columns(vector, share):
        return lax.dynamic_slice_in_dim(vector, share * head_share, head_share)

    attn_biases = [
        jnp.concatenate(
            [
                share_columns(small_master[4], share),
                jnp.zeros((head_share,), F32),
                share_columns(small_master[5], share),
            ]
        )
        for share in shares
    ]
    ff_biases = jnp.stack([pick(small_master, 8 + share) for share in shares])

    starts = pick(cell_starts[:, 0], chip)
    lengths = pick(cell_lengths[:, 0], chip)
    places = jnp.arange(length, dtype=jnp.int32)
    inside = (places[:, None] >= starts[None, :]) & (places[:, None] < (starts + lengths)[None, :])
    first_key = jnp.max(jnp.where(inside, starts[None, :], -1), axis=1)
    first_key = jnp.where(first_key < 0, places, first_key)
    low_blocks = first_key.reshape(-1, local_rows)[:, 0] // local_rows
    block_starts = first_key.reshape(-1, 1, local_rows)
    core_index = core.reshape(1).astype(jnp.int32)

    if planar:
        both = [move_rest(over[0], (1, 0), 0)]
        halves, near, far, both[0], weight_squares = tie(
            halves, near, far, both[0], weight_squares
        )
        last = move_rest(far, (2, 0), 2)
        across += [move_rest(near, (1, 0), 1), move_rest(far, (1, 0), 2)]
        over += [move_rest(near, (0, 2), 1), move_rest(far, (0, 2), 2)]
    *qkv, rows_one, w_attn_mine, w_attn_theirs = project(
        y_index, low_one, other_one, halves, jnp.stack(attn_biases)
    )

    def attend(part):
        return attention_forward(low_blocks, core_index, block_starts, qkv[part], heads_here)

    attended = [attend(0)]
    if planar:
        qkv[1], last, across[1:3], over[1:3], sent_cotangent, _ = tie(
            qkv[1], last, across[1:3], over[1:3], sent_cotangent, attended[0][2]
        )
        across.append(move_rest(last, (1, 0), 3))
        over.append(move_rest(last, (0, 2), 3))
        both += [move_rest(over[1], (1, 0), 1), move_rest(across[2], (0, 2), 2)]
    own_e = exchange_micro(own_cotangent, sent_cotangent)
    attended.append(attend(1))
    if planar:
        dp_index, across, over, both, _ = tie(dp_index, across, over, both, attended[1][2])
        both.append(move_rest(over[3], (1, 0), 3))
        rest_mine = [block for pair in zip((wide, near, far, last), across) for block in pair]
        rest_theirs = [block for pair in zip(over, both) for block in pair]
        out_mine, *joined = unpack_share(dp_index, rest_mine, head_share, model_width, 0, None)
        out_theirs, w_in, w_back = unpack_share(
            dp_index, rest_theirs, head_share, model_width, 1, joined
        )
        w_out = [out_mine, out_theirs]
        own_e, w_out[0] = tie(own_e, w_out[0])
    other_e = swap(own_e, "seq", 1)
    sent, kept = split_product([attended[0][0], attended[1][0]], w_out, False, model_width, BF16)
    middle, low_two = middle_norm(own_in, kept, swap(sent, "seq", 1), small_master)
    other_two = swap(low_two, "seq", 1)

    weights = (w_in, w_back)
    *filled, out_sent, up_sent, sums_sent = feed_forward(
        other_two, other_e, 1, weights, ff_biases, None
    )
    out_received = swap(out_sent, "seq", 1)
    up_received = swap(up_sent, "seq", 1)
    *filled, out_kept, up_kept, sums_kept = feed_forward(
        low_two, own_e, 0, weights, ff_biases, filled
    )
    activated, inner, (rows_two, rows_e) = filled[:2], filled[2:4], filled[4:]
    inner_sums = sums_sent + sums_kept

    link = BF16 if planar else F32
    grad_mid, low_mid, sums_two = norm_back(
        middle, up_kept, up_received, own_e, small_master[2:3], True
    )
    low_mid, rows_e = tie(low_mid, rows_e)
    back_sent = dot_columns(activated[1], rows_e).astype(link)
    back_sent, low_mid = tie(back_sent, low_mid)
    other_mid = swap(low_mid, "seq", 1)
    rows_two, other_mid = tie(rows_two, other_mid)
    in_sent = dot_columns(rows_two, inner[1]).astype(link)
    in_sent, low_mid = tie(in_sent, low_mid)
    back_received = swap(back_sent, "seq", 2)
    in_received = swap(in_sent, "seq", 2)

    grad_att_mine, grad_att_theirs, rows_mid = out_grads(low_mid, other_mid, w_out)
    out_sent_theirs = dot_columns(attended[1][0], rows_mid).astype(link)
    out_sent_theirs, rows_two, rows_e, rows_mid = tie(out_sent_theirs, rows_two, rows_e, rows_mid)
    outer_received = swap(out_sent_theirs, "seq", 2)
    share_back = dot_columns(activated[0], rows_e)
    share_in = dot_columns(rows_two, inner[0])
    share_out = dot_columns(attended[0][0], rows_mid)
    share_back, share_in, share_out, grad_att_theirs = tie(
        share_back, share_in, share_out, grad_att_theirs
    )

    def return_rows(lower, upper):
        return swap(jnp.where(chip == 0, upper, lower), "seq", 2)

    def attend_back(part, grad_att):
        return attention_backward(
            low_blocks,
            core_index,
            block_starts,
            qkv[part],
            grad_att,
            attended[part][1],
            attended[part][2],
            heads_here,
        )

    packed_theirs = attend_back(1, grad_att_theirs)
    attn_sent = dot_columns(rows_one, packed_theirs).astype(link)
    attn_sent, packed_theirs, outer_received = tie(attn_sent, packed_theirs, outer_received)
    theirs_part = partial_product(packed_theirs, w_attn_theirs)
    attn_sent, theirs_part, y_index, out_received = tie(
        attn_sent, theirs_part, y_index, out_received
    )
    attn_received = swap(attn_sent, "seq", 2)
    if planar:
        kept_rest, sent_rest = pack_rest(
            y_index,
            (share_out, share_in, share_back),
            (outer_received, in_received, back_received),
            cut,
        )
        result_rows = widen(
            (middle + ((out_kept + out_received)[:, :model_width] + small_master[7])).astype(BF16)
        )
        sent_rest, grad_att_mine, result_rows = tie(sent_rest, grad_att_mine, result_rows)
        result_halves = (result_rows[:local_rows], result_rows[local_rows:])
        result_received = return_rows(*result_halves)
        got_rest = swap(sent_rest, "dp", 1)
    else:
        result_rows = widen(
            (middle + ((out_kept + out_received)[:, :model_width] + small_master[7])).astype(BF16)
        )
        result_halves = (result_rows[:local_rows], result_rows[local_rows:])
        result_received = return_rows(*result_halves)
        share_back, share_in, share_out = (
            share_back + back_received,
            share_in + in_received,
            share_out + outer_received,
        )

    packed_mine = attend_back(0, grad_att_mine)
    packed_mine, result_received = tie(packed_mine, result_received)
    sent, kept = split_product(
        [packed_mine], [w_attn_mine], True, model_width, BF16, [theirs_part]
    )
    packed_mine, sent = tie(packed_mine, sent)
    share_attn = dot_columns(rows_one, packed_mine) + attn_received.astype(F32)
    if planar:
        z_odd = z_here % 2 == 1
        kept_lead, sent_lead = halve_plane(share_attn[:tall_rows], share_attn[tall_rows:], y_here)
        kept_lead, sent_lead, kept_rest = tie(kept_lead, sent_lead, kept_rest)
        got_lead = swap(sent_lead, "dp", 1)
        held = [kept_rest[i] + got_rest[i].astype(F32) for i in range(3)]
        sent_near = jnp.where(z_odd, held[1], held[0]).astype(BF16)
        sent_last = held[2].astype(BF16)
        kept_near = jnp.where(z_odd, held[0], held[1])
        kept_last = held[2]
        sent_near, sent_last, kept_lead = tie(sent_near, sent_last, kept_lead)
        got_near = swap(sent_near, "dp", 2)
        got_last = permute(sent_last, "dp", lower_pairs([(0, 1), (2, 3)], 2))
    packed = [packed_mine, packed_theirs]
    if planar:
        held_lead = kept_lead + got_lead.astype(F32)
        sent_lead = held_lead.astype(BF16)
        sent_lead, held_lead, kept_near, kept_last = tie(
            sent_lead, held_lead, kept_near, kept_last
        )
        near_lead = permute(sent_lead, "dp", lower_pairs([(1, 0), (3, 2)], 2))
        held_near = kept_near + got_near.astype(F32)
        held_last = kept_last + got_last.astype(F32)
        sent_far = jnp.where(z_here == 1, held_last, held_near).astype(BF16)
        own_rest = jnp.where(z_here == 3, held_last, held_near)
        sent_far, own_rest, held_lead = tie(sent_far, own_rest, held_lead)
        held_lead = held_lead + near_lead.astype(F32)
        sent_lead = held_lead.astype(BF16)
        sent_lead, held_lead, sent_far, kept = tie(sent_lead, held_lead, sent_far, kept)
        sent_lead, (kept, sent_far), mark = started(sent_lead, (kept, sent_far), mark)
        far_lead = permute(sent_lead, "dp", lower_pairs([(2, 0)], 2))
        got_far = permute(sent_far, "dp", lower_pairs([(3, 1), (0, 2), (1, 3)], 2))
    grad_x, sums_one = norm_back(
        own_in, kept, swap(sent, "seq", 1), grad_mid, small_master[0:1], False
    )

    result_all = place_rows(chip_index, result_rows, result_received, model_width)
    grad_halves = (grad_x[:local_rows], grad_x[local_rows:])
    grad_all = place_rows(chip_index, grad_x, return_rows(*grad_halves), model_width)

    def at_shares(columns):
        row = jnp.zeros((model_width,), F32)
        for share, column in zip(shares, columns):
            row = lax.dynamic_update_slice(row, column, (share * head_share,))
        return row

    bias_sums = [jnp.sum(packed[part].astype(F32), axis=0) for part in range(2)]
    inner_rows = jnp.zeros((4, model_width), F32)
    for part in range(2):
        first = part * lanes(model_width)
        inner_rows = lax.dynamic_update_slice(
            inner_rows, inner_sums[0:1, first : first + model_width], (shares[part], 0)
        )
    small_now = jnp.concatenate(
        [
            sums_one[:2],
            sums_two[:2],
            at_shares([sums[:head_share] for sums in bias_sums])[None],
            at_shares([sums[2 * head_share : triple] for sums in bias_sums])[None],
            sums_two[2:4],
            inner_rows,
        ]
    )

    if planar:
        lead_grad = (held_lead + far_lead.astype(F32))[:, :triple].reshape(1, 1, shard_len)
        own_rest, lead_grad, result_all, grad_all, small_now = tie(
            own_rest, lead_grad, result_all, grad_all, small_now
        )
        rest_grad = (own_rest + got_far.astype(F32)).reshape(1, 1, shard_len)
        leads = z_here == 0
    else:
        flat_here = jnp.concatenate(
            [matrix.reshape(-1) for matrix in (share_attn[:, :triple], share_out, share_in, share_back)]
        )
        lead_grad = lax.psum_scatter(
            flat_here.reshape(dp_count, shard_len), "dp", scatter_dimension=0, tiled=True
        ).reshape(1, 1, shard_len)
        rest_grad = lead_grad
        leads = z_here >= 0

    steps_done = step_count[0].astype(F32)
    fix_one = 1.0 - jnp.exp(steps_done * math.log(BETA_ONE))
    fix_two = 1.0 - jnp.exp(steps_done * math.log(BETA_TWO))
    ints = jnp.concatenate([bound, leads.astype(jnp.int32).reshape(1)])
    reduced, moments, update, update_squares = new_moments(
        ints,
        jnp.stack([fix_one, fix_two]),
        lead_grad,
        rest_grad,
        first_moment,
        second_moment,
        weight,
    )
    matrix_rows = jnp.stack([matrix_sums(weight_squares), matrix_sums(update_squares)])
    small_sum = sum_everywhere(
        jnp.concatenate([small_now, jnp.pad(matrix_rows, ((0, 2), (0, model_width - 4)))])
    )
    small_grad = small_sum[:12]
    weight_norms = jnp.sqrt(small_sum[12, :4])
    update_norms = jnp.sqrt(small_sum[13, :4])
    ratios = weight_norms / update_norms
    new_weight, weight_copy = new_weights(
        ints, jnp.stack([pick(ratios, lower_matrix), pick(ratios, upper_matrix)]), weight, update
    )
    small_one = BETA_ONE * small_first + (1.0 - BETA_ONE) * small_grad
    small_two = BETA_TWO * small_second + (1.0 - BETA_TWO) * small_grad * small_grad
    small_late = lax.dynamic_update_slice(small_master, mark, (0, 0))
    small_updated = small_late - SMALL_RATE * (small_one / fix_one) / (
        jnp.sqrt(small_two / fix_two) + ADAM_EPS
    )
    return (
        result_all,
        grad_all,
        reduced,
        moments,
        new_weight,
        weight_copy,
        jnp.stack([weight_norms, update_norms, ratios]),
        small_grad,
        jnp.stack([small_one, small_two]),
        small_updated,
    )


def solution(mesh):
    in_specs = (
        P(None, "dp", "seq", None),
        P(None, "dp", "seq", None),
        P(None, "dp", None),
        P(None, "dp", None),
        P(None, "dp", None),
        P("dp", "seq", None),
        P("dp", "seq", None),
        P("dp", "seq", None),
        P(),
        P(),
        P(),
        P(),
    )
    out_specs = (
        P(None, "dp", "seq", None),
        P(None, "dp", "seq", None),
        P("dp", "seq", None),
        P(None, "dp", "seq", None),
        P("dp", "seq", None),
        P("dp", "seq", None),
        P(),
        P(),
        P(),
        P(),
    )
    return jax.shard_map(
        per_device, mesh=mesh, in_specs=in_specs, out_specs=out_specs, check_vma=False
    )
```

```python
import functools
import math

import jax
import jax.numpy as jnp
from jax import lax
from jax.experimental import pallas as pl
from jax.experimental.pallas import tpu as pltpu
from jax.sharding import PartitionSpec as P

HEADS = 20


NORM_EPS = 1e-05
BETA_ONE = 0.9
BETA_TWO = 0.999
ADAM_EPS = 1e-06
DECAY = 0.01
MATRIX_RATE = 0.3
SMALL_RATE = 0.25
MASKED = -1e30
LOG2_E = 1.4426950408889634
FF_ROWS = 256
SCALE = 1e9

F32 = jnp.float32
BF16 = jnp.bfloat16


def dot_rows(left, right):
    return lax.dot_general(left, right, (((1,), (0,)), ((), ())), preferred_element_type=F32)


def dot_transposed(left, right):
    return lax.dot_general(left, right, (((1,), (1,)), ((), ())), preferred_element_type=F32)


def dot_columns(left, right):
    return lax.dot_general(left, right, (((0,), (0,)), ((), ())), preferred_element_type=F32)


def norm_stats(rows):
    center = jnp.mean(rows, axis=-1, keepdims=True)
    centered = rows - center
    spread = jnp.mean(centered * centered, axis=-1, keepdims=True)
    scale = lax.rsqrt(spread + NORM_EPS)
    return centered * scale, scale


def norm_backward(upstream, hat, scale, gain):
    weighted = upstream * gain
    return (
        weighted
        - jnp.mean(weighted, axis=-1, keepdims=True)
        - hat * jnp.mean(weighted * hat, axis=-1, keepdims=True)
    ) * scale


def gelu_parts(values):
    inner = math.sqrt(2.0 / math.pi)
    squares = values * values
    bent = jnp.tanh(inner * (values + 0.044715 * values * squares))
    half = 0.5 * (1.0 + bent)
    slope = half + 0.5 * values * (1.0 - bent * bent) * inner * (1.0 + 3.0 * 0.044715 * squares)
    return values * half, slope


def block_place(core, block):
    return jnp.where(block % 2 == core, 0, 2) + block // 2


def block_rows(core, block, rows):
    return pl.ds(pl.multiple_of(block_place(core, block) * rows, rows), rows)


def attention_forward_body(
    heads, width, bq, low_ref, core_ref, start_ref, qkv_ref, out_ref, outt_ref, lse_ref, qs, ks, vt, acc
):
    length = qkv_ref.shape[0]
    flat = heads * width
    factor = width**-0.5 * LOG2_E
    core = core_ref[0]

    def unpack(block, carry):
        here = block_rows(core, block, bq)
        there = pl.ds(pl.multiple_of(block * bq, bq), bq)
        for h in range(heads):
            qs[h, there] = qkv_ref[here, h * width : (h + 1) * width]
            ks[h, there] = qkv_ref[here, flat + h * width : flat + (h + 1) * width]
        turned = qkv_ref[here, 2 * flat : 3 * flat].astype(F32).T
        for h in range(heads):
            vt[h, block] = turned[h * width : (h + 1) * width].astype(BF16)
        return carry

    lax.fori_loop(0, length // bq, unpack, 0)

    def query_step(qb, carry):
        q0 = pl.multiple_of(qb * bq, bq)
        start = start_ref[qb]
        query_place = q0 + lax.broadcasted_iota(jnp.int32, (1, bq), 1)
        acc[...] = jnp.zeros_like(acc)

        def key_step(kb, tops_totals):
            tops, totals = tops_totals
            k0 = pl.multiple_of(kb * bq, bq)
            key_place = k0 + lax.broadcasted_iota(jnp.int32, (bq, bq), 0)
            allowed = (key_place <= query_place) & (key_place >= start)
            new_tops, new_totals = [], []
            for h in range(heads):
                scores = dot_transposed(ks[h, pl.ds(k0, bq)], qs[h, pl.ds(q0, bq)]) * factor
                scores = jnp.where(allowed, scores, MASKED)
                top = jnp.maximum(tops[h], jnp.max(scores, axis=0, keepdims=True))
                fade = jnp.exp2(tops[h] - top)
                weights = jnp.exp2(scores - top)
                own = slice(h * width, (h + 1) * width)
                acc[own] = acc[own] * fade + dot_rows(vt[h, kb], weights.astype(BF16))
                new_tops.append(top)
                new_totals.append(totals[h] * fade + jnp.sum(weights, axis=0, keepdims=True))
            return tuple(new_tops), tuple(new_totals)

        first = (
            tuple(jnp.full((1, bq), -1e29, F32) for _ in range(heads)),
            tuple(jnp.zeros((1, bq), F32) for _ in range(heads)),
        )
        tops, totals = lax.fori_loop(low_ref[qb], qb + 1, key_step, first)
        for h in range(heads):
            own = slice(h * width, (h + 1) * width)
            acc[own] = acc[own] * (1.0 / totals[h])
            lse_ref[qb, h : h + 1, :] = tops[h] + jnp.log2(totals[h])
        mixed = acc[...]
        outt_ref[qb] = mixed
        out_ref[block_rows(core, qb, bq), :] = mixed.T.astype(BF16)
        return carry

    lax.fori_loop(0, length // bq, query_step, 0)


def attention_backward_body(
    heads,
    width,
    bq,
    low_ref,
    core_ref,
    start_ref,
    qkv_ref,
    dout_ref,
    outt_ref,
    lse_ref,
    grad_ref,
    qs,
    ks,
    vs,
    ds,
    kt,
    dk,
    dv,
    dqt,
):
    length = qkv_ref.shape[0]
    flat = heads * width
    score_scale = width**-0.5
    factor = score_scale * LOG2_E
    core = core_ref[0]

    def unpack(block, carry):
        here = block_rows(core, block, bq)
        there = pl.ds(pl.multiple_of(block * bq, bq), bq)
        for h in range(heads):
            qs[h, there] = qkv_ref[here, h * width : (h + 1) * width]
            ks[h, there] = qkv_ref[here, flat + h * width : flat + (h + 1) * width]
            vs[h, there] = qkv_ref[here, 2 * flat + h * width : 2 * flat + (h + 1) * width]
            ds[h, there] = dout_ref[here, h * width : (h + 1) * width]
        turned = qkv_ref[here, flat : 2 * flat].astype(F32).T
        for h in range(heads):
            kt[h, block] = turned[h * width : (h + 1) * width].astype(BF16)
        return carry

    lax.fori_loop(0, length // bq, unpack, 0)
    dk[...] = jnp.zeros_like(dk)
    dv[...] = jnp.zeros_like(dv)

    def query_step(qb, carry):
        q0 = pl.multiple_of(qb * bq, bq)
        queries = pl.ds(q0, bq)
        here = block_rows(core, qb, bq)
        start = start_ref[qb]
        query_place = q0 + lax.broadcasted_iota(jnp.int32, (1, bq), 1)
        products = dout_ref[here, :].astype(F32).T * outt_ref[qb]
        inners = [
            jnp.sum(products[h * width : (h + 1) * width], axis=0, keepdims=True)
            for h in range(heads)
        ]
        dqt[...] = jnp.zeros_like(dqt)

        def attend(key_block, key_part, query_part):
            key_count = key_part.stop - key_part.start
            count = query_part.stop - query_part.start
            k0 = pl.multiple_of(key_block * bq + key_part.start, key_count)
            keys = pl.ds(k0, key_count)
            rows = pl.ds(pl.multiple_of(q0 + query_part.start, count), count)
            key_place = k0 + lax.broadcasted_iota(jnp.int32, (key_count, count), 0)
            allowed = (key_place <= query_place[:, query_part]) & (
                key_place >= start[:, query_part]
            )
            for h in range(heads):
                scores = dot_transposed(ks[h, keys], qs[h, rows]) * factor
                weights = jnp.exp2(
                    jnp.where(allowed, scores - lse_ref[qb, h : h + 1, query_part], MASKED)
                )
                dweights = dot_transposed(vs[h, keys], ds[h, rows])
                dscores = (weights * (dweights - inners[h][:, query_part])).astype(BF16)
                dv[h, keys] += dot_rows(weights.astype(BF16), ds[h, rows])
                dk[h, keys] += dot_rows(dscores, qs[h, rows])
                dqt[h * width : (h + 1) * width, query_part] += dot_rows(
                    kt[h, key_block, :, key_part], dscores
                )

        every = slice(0, bq)

        def key_step(kb, inner_carry):
            attend(kb, every, every)
            return inner_carry

        lax.fori_loop(low_ref[qb], qb, key_step, 0)
        attend(qb, slice(0, bq // 2), every)
        attend(qb, slice(bq // 2, bq), slice(bq // 2, bq))
        grad_ref[here, 0:flat] = (dqt[...] * score_scale).T.astype(BF16)
        return carry

    lax.fori_loop(0, length // bq, query_step, 0)

    def write_keys(kb, carry):
        here = block_rows(core, kb, bq)
        rows = pl.ds(pl.multiple_of(kb * bq, bq), bq)
        grad_ref[here, flat : 2 * flat] = jnp.concatenate(
            [dk[h, rows] * score_scale for h in range(heads)], axis=1
        ).astype(BF16)
        grad_ref[here, 2 * flat : 3 * flat] = jnp.concatenate(
            [dv[h, rows] for h in range(heads)], axis=1
        ).astype(BF16)
        rest = grad_ref.shape[1] - 3 * flat
        if rest:
            grad_ref[here, 3 * flat :] = jnp.zeros((bq, rest), BF16)
        return carry

    lax.fori_loop(0, length // bq, write_keys, 0)


def whole_block(shape):
    return pl.BlockSpec(shape, lambda step, *refs: (0,) * len(shape))


def attention_forward(low_blocks, core, starts, qkv, heads):
    length, triple = qkv.shape
    flat = triple // 3
    width = flat // heads
    blocks, _, bq = starts.shape
    grid_spec = pltpu.PrefetchScalarGridSpec(
        num_scalar_prefetch=2,
        grid=(1,),
        in_specs=[whole_block((blocks, 1, bq)), whole_block((length, triple))],
        out_specs=[
            whole_block((length, flat)),
            whole_block((blocks, flat, bq)),
            whole_block((blocks, 8, bq)),
        ],
        scratch_shapes=[
            pltpu.VMEM((heads, length, width), BF16),
            pltpu.VMEM((heads, length, width), BF16),
            pltpu.VMEM((heads, blocks, width, bq), BF16),
            pltpu.VMEM((flat, bq), F32),
        ],
    )
    return pl.pallas_call(
        functools.partial(attention_forward_body, heads, width, bq),
        out_shape=[
            jax.ShapeDtypeStruct((length, flat), BF16),
            jax.ShapeDtypeStruct((blocks, flat, bq), F32),
            jax.ShapeDtypeStruct((blocks, 8, bq), F32),
        ],
        grid_spec=grid_spec,
        compiler_params=pltpu.CompilerParams(vmem_limit_bytes=48 << 20),
        cost_estimate=lasting(35),
        name="attention_forward",
    )(low_blocks, core, starts, qkv)


def attention_backward(low_blocks, core, starts, qkv, grad_out, out_turned, log_total, heads):
    length, triple = qkv.shape
    flat = triple // 3
    width = flat // heads
    blocks, _, bq = starts.shape
    per_head = pltpu.VMEM((heads, length, width), BF16)
    sums = pltpu.VMEM((heads, length, width), F32)
    grid_spec = pltpu.PrefetchScalarGridSpec(
        num_scalar_prefetch=2,
        grid=(1,),
        in_specs=[
            whole_block((blocks, 1, bq)),
            whole_block((length, triple)),
            whole_block((length, flat)),
            whole_block((blocks, flat, bq)),
            whole_block((blocks, 8, bq)),
        ],
        out_specs=whole_block((length, lanes(triple))),
        scratch_shapes=[
            per_head,
            per_head,
            per_head,
            per_head,
            pltpu.VMEM((heads, blocks, width, bq), BF16),
            sums,
            sums,
            pltpu.VMEM((flat, bq), F32),
        ],
    )
    return pl.pallas_call(
        functools.partial(attention_backward_body, heads, width, bq),
        out_shape=jax.ShapeDtypeStruct((length, lanes(triple)), BF16),
        grid_spec=grid_spec,
        compiler_params=pltpu.CompilerParams(vmem_limit_bytes=60 << 20),
        cost_estimate=lasting(56),
        name="attention_backward",
    )(low_blocks, core, starts, qkv, grad_out, out_turned, log_total)


def lasting(micros):
    return pl.CostEstimate(flops=int(micros * SCALE), bytes_accessed=1 << 12, transcendentals=0)


def lanes(width):
    return -(-width // 128) * 128


def put(ref, value):
    width = value.shape[1]
    ref[:, :width] = value.astype(ref.dtype)
    if width < ref.shape[1]:
        ref[:, width:] = jnp.zeros((value.shape[0], ref.shape[1] - width), ref.dtype)


def vmem(count):
    return pltpu.CompilerParams(vmem_limit_bytes=count << 20)


def fixed(shape):
    return pl.BlockSpec(shape, lambda *step: (0,) * len(shape), pipeline_mode=pl.Buffered(1))


def hbm():
    return pl.BlockSpec(memory_space=pl.ANY)


def round_weights_body(weight_ref, low_ref):
    low_ref[...] = weight_ref[0, 0, :].astype(BF16)


def round_weights(weight):
    whole = pl.BlockSpec(memory_space=pltpu.VMEM)
    return pl.pallas_call(
        round_weights_body,
        in_specs=[whole],
        out_specs=whole,
        out_shape=jax.ShapeDtypeStruct(weight.shape[2:], BF16),
        compiler_params=vmem(32),
        cost_estimate=lasting(6),
        name="round_weights",
    )(weight)


def add_squares(sums_ref, values, in_lower):
    squares = values * values
    lower = jnp.sum(jnp.where(in_lower, squares, 0.0))
    sums_ref[0] += lower
    sums_ref[1] += jnp.sum(squares) - lower


def square_sums_body(bound_ref, weight_ref, sums_ref):
    sums_ref[0] = 0.0
    sums_ref[1] = 0.0
    place = lax.broadcasted_iota(jnp.int32, weight_ref.shape, 2)
    add_squares(sums_ref, weight_ref[...], place < bound_ref[0])


def square_sums(bound, weight):
    smem = pl.BlockSpec(memory_space=pltpu.SMEM)
    return pl.pallas_call(
        square_sums_body,
        in_specs=[smem, pl.BlockSpec(memory_space=pltpu.VMEM)],
        out_specs=smem,
        out_shape=jax.ShapeDtypeStruct((2,), F32),
        compiler_params=vmem(32),
        cost_estimate=lasting(6),
        name="square_sums",
    )(bound, weight)


def moments_body(
    ints_ref, floats_ref, lead_ref, rest_ref, first_ref, second_ref, weight_ref,
    grad_ref, moments_ref, update_ref, sums_ref,
):
    step = pl.program_id(0)
    grad = jnp.where(ints_ref[1] == 1, lead_ref[...], rest_ref[...])
    grad_ref[...] = grad
    first = BETA_ONE * first_ref[...] + (1.0 - BETA_ONE) * grad
    second = BETA_TWO * second_ref[...] + (1.0 - BETA_TWO) * grad * grad
    moments_ref[0] = first
    moments_ref[1] = second
    update = (first / floats_ref[0]) / (jnp.sqrt(second / floats_ref[1]) + ADAM_EPS)
    update = update + DECAY * weight_ref[...]
    update_ref[...] = update
    count = grad.shape[2]
    place = step * count + lax.broadcasted_iota(jnp.int32, grad.shape, 2)

    @pl.when(step == 0)
    def clear():
        sums_ref[0] = 0.0
        sums_ref[1] = 0.0

    add_squares(sums_ref, update, place < ints_ref[0])


def flat_steps(count):
    return 7 if count % (7 * 128) == 0 else 1


def new_moments(ints, floats, lead, rest, first, second, weight):
    count = weight.shape[2]
    steps = flat_steps(count)
    smem = pl.BlockSpec(memory_space=pltpu.SMEM)
    flat = pl.BlockSpec((1, 1, count // steps), lambda i: (0, 0, i))
    pair = pl.BlockSpec((2, 1, 1, count // steps), lambda i: (0, 0, 0, i))
    return pl.pallas_call(
        moments_body,
        grid=(steps,),
        in_specs=[smem, smem] + [flat] * 5,
        out_specs=[flat, pair, flat, smem],
        out_shape=[
            jax.ShapeDtypeStruct(weight.shape, F32),
            jax.ShapeDtypeStruct((2,) + weight.shape, F32),
            jax.ShapeDtypeStruct(weight.shape, F32),
            jax.ShapeDtypeStruct((2,), F32),
        ],
        compiler_params=vmem(48),
        cost_estimate=lasting(10),
        name="new_moments",
    )(ints, floats, lead, rest, first, second, weight)


def new_weights_body(ints_ref, ratio_ref, weight_ref, update_ref, new_ref, copy_ref):
    count = weight_ref.shape[2]
    place = pl.program_id(0) * count + lax.broadcasted_iota(jnp.int32, weight_ref.shape, 2)
    rate = jnp.where(place < ints_ref[0], ratio_ref[0], ratio_ref[1])
    new = weight_ref[...] - MATRIX_RATE * rate * update_ref[...]
    new_ref[...] = new
    copy_ref[...] = new.astype(BF16)


def new_weights(ints, ratios, weight, update):
    count = weight.shape[2]
    steps = flat_steps(count)
    smem = pl.BlockSpec(memory_space=pltpu.SMEM)
    flat = pl.BlockSpec((1, 1, count // steps), lambda i: (0, 0, i))
    return pl.pallas_call(
        new_weights_body,
        grid=(steps,),
        in_specs=[smem, smem, flat, flat],
        out_specs=[flat, flat],
        out_shape=[
            jax.ShapeDtypeStruct(weight.shape, F32),
            jax.ShapeDtypeStruct(weight.shape, BF16),
        ],
        compiler_params=vmem(32),
        cost_estimate=lasting(6),
        name="new_weights",
    )(ints, ratios, weight, update)


def unpack_body(cut, rows, skipped, place_ref, *refs):
    blocks, (w_out, w_in, w_back, held, sems) = refs[:8], refs[8 + skipped :]
    here = place_ref[0]
    copies = [
        pltpu.make_async_copy(block, held.at[index ^ here], sems.at[index])
        for index, block in enumerate(blocks)
    ]
    for copy in copies:
        copy.start()
    for copy in copies:
        copy.wait()
    begin, columns = 2 * cut, held.shape[2]
    for target, count_rows in zip((w_out, w_in, w_back), rows):
        done = 0
        while done < count_rows:
            block, offset = divmod(begin + done, cut)
            count = min(cut - offset, count_rows - done)
            target[done : done + count, :columns] = held[block, offset : offset + count]
            done += count
        begin += count_rows
        if target.shape[1] > columns:
            target[:, columns:] = jnp.zeros((count_rows, target.shape[1] - columns), BF16)
    rest = w_back.shape[0] - rows[2]
    if rest:
        w_back[rows[2] :] = jnp.zeros((rest, w_back.shape[1]), BF16)


def unpack_share(place, blocks, out_rows, in_rows, part, joined):
    cut, columns = blocks[0].shape
    wide = lanes(columns)
    joined = () if joined is None else tuple(joined)
    return pl.pallas_call(
        functools.partial(unpack_body, cut, (out_rows, in_rows, columns), len(joined)),
        grid_spec=pltpu.PrefetchScalarGridSpec(
            num_scalar_prefetch=1,
            grid=(1,),
            in_specs=[hbm()] * (8 + len(joined)),
            out_specs=[
                whole_block((out_rows, columns)),
                pl.BlockSpec((in_rows, wide), lambda i, place_ref: (0, part)),
                pl.BlockSpec((wide, columns), lambda i, place_ref: (part, 0)),
            ],
            scratch_shapes=[
                pltpu.VMEM((8, cut, columns), BF16),
                pltpu.SemaphoreType.DMA((8,)),
            ],
        ),
        out_shape=[
            jax.ShapeDtypeStruct((out_rows, columns), BF16),
            jax.ShapeDtypeStruct((in_rows, 2 * wide), BF16),
            jax.ShapeDtypeStruct((2 * wide, columns), BF16),
        ],
        input_output_aliases={9 + i: 1 + i for i in range(len(joined))},
        compiler_params=vmem(48),
        cost_estimate=lasting(6),
        name="unpack_share",
    )(place, *blocks, *joined)


def pack_rest_body(
    cut, place_ref, out_ref, in_ref, back_ref, out_got, in_got, back_got, kept_ref, sent_ref
):
    here = place_ref[0]
    place = 0
    for matrix, got in ((out_ref, out_got), (in_ref, in_got), (back_ref, back_got)):
        done, rows = 0, matrix.shape[0]
        while done < rows:
            block, offset = divmod(place, cut)
            count = min(cut - offset, rows - done)
            source = slice(done, done + count)
            target = slice(offset, offset + count)
            plane, side = divmod(block, 2)

            @pl.when(here == side)
            def keep(matrix=matrix, got=got, source=source, target=target, plane=plane):
                kept_ref[plane, target] = matrix[source] + got[source].astype(F32)

            @pl.when(here != side)
            def send(matrix=matrix, got=got, source=source, target=target, plane=plane):
                sent_ref[plane, target] = (matrix[source] + got[source].astype(F32)).astype(BF16)

            done += count
            place += count


def pack_rest(place, matrices, received, cut):
    columns = matrices[0].shape[1]
    whole = pl.BlockSpec(memory_space=pltpu.VMEM)
    return pl.pallas_call(
        functools.partial(pack_rest_body, cut),
        in_specs=[pl.BlockSpec(memory_space=pltpu.SMEM)] + [whole] * 6,
        out_specs=[whole] * 2,
        out_shape=[
            jax.ShapeDtypeStruct((3, cut, columns), F32),
            jax.ShapeDtypeStruct((3, cut, columns), BF16),
        ],
        compiler_params=vmem(40),
        cost_estimate=lasting(10),
        name="pack_rest",
    )(place, *matrices, *received)


def rows_of(step, steps, own_ref, other_ref, width):
    return jnp.where(step < steps, own_ref[:, :width], other_ref[:, :width])


def both_specs(block, width, steps):
    own = pl.BlockSpec((block, width), lambda i, *refs: (jnp.minimum(i, steps - 1), 0))
    other = pl.BlockSpec((block, width), lambda i, *refs: (jnp.maximum(i - steps, 0), 0))
    return own, other


def project_body(
    steps, place_ref, own_ref, other_ref, a0, a1, b0, b1, bias_ref,
    out_a, out_b, rows_ref, w_a, w_b, sems,
):
    step = pl.program_id(0)

    @pl.when(step == 0)
    def load():
        cut = a0.shape[0]
        here = place_ref[0]
        first = pl.ds(pl.multiple_of(here * cut, cut), cut)
        second = pl.ds(pl.multiple_of((1 - here) * cut, cut), cut)
        copies = [
            pltpu.make_async_copy(a0, w_a.at[first], sems.at[0]),
            pltpu.make_async_copy(a1, w_a.at[second], sems.at[1]),
            pltpu.make_async_copy(b0, w_b.at[first], sems.at[2]),
            pltpu.make_async_copy(b1, w_b.at[second], sems.at[3]),
        ]
        for copy in copies:
            copy.start()
        for copy in copies:
            copy.wait()

    rows = rows_of(step, steps, own_ref, other_ref, rows_ref.shape[1])
    rows_ref[...] = rows
    out_a[...] = (dot_rows(rows, w_a[...]) + bias_ref[0:1]).astype(BF16)
    out_b[...] = (dot_rows(rows, w_b[...]) + bias_ref[1:2]).astype(BF16)


def project(place, own, other, halves, biases):
    count, sent_width = own.shape
    cut, triple = halves[0].shape
    model_width = 2 * cut
    block = min(512, count)
    steps = count // block
    row_out = lambda width: pl.BlockSpec((block, width), lambda i, *refs: (i, 0))
    matrix = jax.ShapeDtypeStruct((2 * cut, triple), BF16)
    return pl.pallas_call(
        functools.partial(project_body, steps),
        grid_spec=pltpu.PrefetchScalarGridSpec(
            num_scalar_prefetch=1,
            grid=(2 * steps,),
            in_specs=[*both_specs(block, sent_width, steps)]
            + [hbm()] * 4
            + [fixed((2, triple))],
            out_specs=[row_out(triple), row_out(triple), row_out(model_width)]
            + [pl.BlockSpec(matrix.shape, lambda i, *refs: (0, 0))] * 2,
            scratch_shapes=[pltpu.SemaphoreType.DMA((4,))],
        ),
        out_shape=[jax.ShapeDtypeStruct((2 * count, triple), BF16)] * 2
        + [jax.ShapeDtypeStruct((2 * count, model_width), BF16), matrix, matrix],
        compiler_params=vmem(48),
        cost_estimate=lasting(16),
        name="project",
    )(place, own, other, *halves, biases)


def out_grads_body(steps, own_ref, other_ref, w_a, w_b, out_a, out_b, rows_ref):
    rows = rows_of(pl.program_id(0), steps, own_ref, other_ref, rows_ref.shape[1])
    rows_ref[...] = rows
    out_a[...] = dot_transposed(rows, w_a[...]).astype(BF16)
    out_b[...] = dot_transposed(rows, w_b[...]).astype(BF16)


def out_grads(own, other, w_out):
    count, sent_width = own.shape
    width, model_width = w_out[0].shape
    block = min(512, count)
    steps = count // block
    row_out = lambda columns: pl.BlockSpec((block, columns), lambda i: (i, 0))
    return pl.pallas_call(
        functools.partial(out_grads_body, steps),
        grid=(2 * steps,),
        in_specs=[*both_specs(block, sent_width, steps)] + [fixed(w_out[0].shape)] * 2,
        out_specs=[row_out(width), row_out(width), row_out(model_width)],
        out_shape=[jax.ShapeDtypeStruct((2 * count, width), BF16)] * 2
        + [jax.ShapeDtypeStruct((2 * count, model_width), BF16)],
        compiler_params=vmem(48),
        cost_estimate=lasting(8),
        name="out_grads",
    )(own, other, *w_out)


def row_products(turned, left_refs, weight_refs):
    product = None
    for left, weight in zip(left_refs, weight_refs):
        if turned:
            term = dot_transposed(left[:, : weight.shape[1]], weight[...])
        else:
            term = dot_rows(left[:, : weight.shape[0]], weight[...])
        product = term if product is None else product + term
    return product


def partial_product_body(left, weight, out_ref):
    out_ref[...] = row_products(True, [left], [weight])


def split_product_body(steps, turned, count, *refs):
    lefts, weights, rest = refs[:count], refs[count : 2 * count], refs[2 * count :]
    *partial, sent_ref, kept_ref = rest
    product = row_products(turned, lefts, weights)
    if partial:
        product = product + partial[0][...]
    step = pl.program_id(0)

    @pl.when(step < steps)
    def other_rows():
        put(sent_ref, product)

    @pl.when(step >= steps)
    def own_rows():
        put(kept_ref, product)


def other_first(block, width, steps):
    return pl.BlockSpec((block, width), lambda i: ((i + steps) % (2 * steps), 0))


def partial_product(left, weight):
    count, width = left.shape
    model_width = weight.shape[0]
    block = min(512, count // 2)
    steps = count // 2 // block
    return pl.pallas_call(
        partial_product_body,
        grid=(2 * steps,),
        in_specs=[other_first(block, width, steps), fixed(weight.shape)],
        out_specs=pl.BlockSpec((block, model_width), lambda i: (i, 0)),
        out_shape=jax.ShapeDtypeStruct((count, model_width), F32),
        compiler_params=vmem(48),
        cost_estimate=lasting(9),
        name="partial_product",
    )(left, weight)


def split_product(lefts, weights, turned, model_width, sent_type, partial=()):
    count, width = lefts[0].shape
    block = min(512, count // 2)
    steps = count // 2 // block
    parts = [
        jax.ShapeDtypeStruct((count // 2, lanes(model_width)), sent_type),
        jax.ShapeDtypeStruct((count // 2, model_width), F32),
    ]
    return pl.pallas_call(
        functools.partial(split_product_body, steps, turned, len(lefts)),
        grid=(2 * steps,),
        in_specs=[other_first(block, width, steps)] * len(lefts)
        + [fixed(weight.shape) for weight in weights]
        + [pl.BlockSpec((block, model_width), lambda i: (i, 0))] * len(partial),
        out_specs=[
            pl.BlockSpec((block, lanes(model_width)), lambda i: (jnp.minimum(i, steps - 1), 0)),
            pl.BlockSpec((block, model_width), lambda i: (jnp.maximum(i - steps, 0), 0)),
        ],
        out_shape=parts,
        compiler_params=vmem(48),
        cost_estimate=lasting(9),
        name="split_product",
    )(*lefts, *weights, *partial)


def middle_body(rows_ref, kept_ref, got_ref, small_ref, middle_ref, low_ref):
    middle = rows_ref[...].astype(F32) + (
        kept_ref[...] + got_ref[:, : kept_ref.shape[1]].astype(F32) + small_ref[6:7]
    )
    middle_ref[...] = middle
    hat, _ = norm_stats(middle)
    put(low_ref, (hat * small_ref[2:3] + small_ref[3:4]).astype(BF16))


def middle_norm(rows, kept, got, small):
    count, width = rows.shape
    block = min(256, count)
    part = pl.BlockSpec((block, width), lambda i: (i, 0))
    sent = pl.BlockSpec((block, lanes(width)), lambda i: (i, 0))
    return pl.pallas_call(
        middle_body,
        grid=(count // block,),
        in_specs=[part, part, sent, fixed(small.shape)],
        out_specs=[part, sent],
        out_shape=[
            jax.ShapeDtypeStruct((count, width), F32),
            jax.ShapeDtypeStruct((count, lanes(width)), BF16),
        ],
        compiler_params=vmem(32),
        cost_estimate=lasting(4),
        name="middle_norm",
    )(rows, kept, got, small)


def turn(block):
    return block.astype(F32).T.astype(BF16)


def take_rows_body(chip_ref, array_ref, own_ref, sent_ref):
    rows = turn(array_ref[0, 0])

    @pl.when(pl.program_id(0) == 0)
    def other_micro():
        put(sent_ref, rows)

    @pl.when(pl.program_id(0) == 1)
    def own_micro():
        put(own_ref, rows)


def take_rows(chip, array):
    turned = jnp.swapaxes(array, 2, 3)
    _, _, width, count = turned.shape
    out = pl.BlockSpec((count, lanes(width)), lambda i, chip_ref: (0, 0))
    return pl.pallas_call(
        take_rows_body,
        grid_spec=pltpu.PrefetchScalarGridSpec(
            num_scalar_prefetch=1,
            grid=(2,),
            in_specs=[
                pl.BlockSpec(
                    (1, 1, width, count),
                    lambda i, chip_ref: (jnp.where(i == 0, 1 - chip_ref[0], chip_ref[0]), 0, 0, 0),
                )
            ],
            out_specs=[out, out],
        ),
        out_shape=[jax.ShapeDtypeStruct((count, lanes(width)), BF16)] * 2,
        compiler_params=vmem(32),
        cost_estimate=lasting(4),
        name="take_rows",
    )(chip, turned)


def place_rows_body(chip_ref, rows_ref, received_ref, out_ref):
    width = out_ref.shape[2]
    rows = jnp.where(
        pl.program_id(0) == chip_ref[0], rows_ref[:, :width], received_ref[:, :width]
    )
    out_ref[0, 0] = turn(rows)


def place_rows(chip, rows, received, width):
    count, sent_width = received.shape
    turned = pl.pallas_call(
        place_rows_body,
        grid_spec=pltpu.PrefetchScalarGridSpec(
            num_scalar_prefetch=1,
            grid=(2,),
            in_specs=[
                pl.BlockSpec((count, sent_width), lambda i, chip_ref: (chip_ref[0], 0)),
                pl.BlockSpec((count, sent_width), lambda i, chip_ref: (0, 0)),
            ],
            out_specs=pl.BlockSpec((1, 1, width, count), lambda i, chip_ref: (i, 0, 0, 0)),
        ),
        out_shape=jax.ShapeDtypeStruct((2, 1, width, count), BF16),
        compiler_params=vmem(32),
        cost_estimate=lasting(4),
        name="place_rows",
    )(chip, rows, received)
    return jnp.swapaxes(turned, 2, 3)


def norm_back_body(wide_out, rows_ref, kept_ref, got_ref, base_ref, gain_ref, *outs):
    (full_ref, low_ref, sums_ref) = outs if wide_out else (None, *outs)
    rows = rows_ref[...].astype(F32)
    hat, scale = norm_stats(rows)
    width = rows.shape[1]
    upstream = kept_ref[:, :width] + got_ref[:, :width].astype(F32)
    base = base_ref[:, :width].astype(F32)
    grad = base + norm_backward(upstream, hat, scale, gain_ref[...])
    low = grad.astype(BF16)
    if wide_out:
        full_ref[...] = grad
    put(low_ref, low)

    @pl.when(pl.program_id(0) == 0)
    def clear():
        sums_ref[...] = jnp.zeros_like(sums_ref)

    for index, term in enumerate((upstream * hat, upstream, low.astype(F32), base)):
        sums_ref[index : index + 1] += jnp.sum(term, axis=0, keepdims=True)


def norm_back(rows, kept, got, base, gain, wide_out):
    count, width = rows.shape
    block = min(256, count)
    part = pl.BlockSpec((block, width), lambda i: (i, 0))
    sent = pl.BlockSpec((block, lanes(width)), lambda i: (i, 0))
    full = [jax.ShapeDtypeStruct((count, width), F32)] if wide_out else []
    return pl.pallas_call(
        functools.partial(norm_back_body, wide_out),
        grid=(count // block,),
        in_specs=[part, pl.BlockSpec((block, kept.shape[1]), lambda i: (i, 0)), sent]
        + [pl.BlockSpec((block, base.shape[1]), lambda i: (i, 0)), fixed((1, width))],
        out_specs=[part] * len(full) + [sent, pl.BlockSpec((8, width), lambda i: (0, 0))],
        out_shape=full
        + [
            jax.ShapeDtypeStruct((count, lanes(width)), BF16),
            jax.ShapeDtypeStruct((8, width), F32),
        ],
        compiler_params=vmem(40),
        cost_estimate=lasting(7),
        name="norm_back",
    )(rows, kept, got, base, gain)


def feed_forward_body(skipped, rows_ref, cot_ref, w_in, w_back, bias_ref, *refs):
    (
        act_mine, act_theirs, inner_mine, inner_theirs, rows_out, cot_out, out_ref, up_ref, sums_ref
    ) = refs[skipped:]
    model_width = rows_out.shape[1]
    rows, cot = rows_ref[:, :model_width], cot_ref[:, :model_width]
    rows_out[...] = rows
    cot_out[...] = cot

    @pl.when(pl.program_id(0) == 0)
    def clear():
        sums_ref[...] = jnp.zeros_like(sums_ref)

    width = act_mine.shape[1]
    wide = w_in.shape[1] // 2
    value, slope = gelu_parts(dot_rows(rows, w_in[...]) + bias_ref[0:1])
    act = value.astype(BF16)
    inner = (dot_transposed(cot, w_back[...]) * slope).astype(BF16)
    sums_ref[0:1] += jnp.sum(inner.astype(F32), axis=0, keepdims=True)
    for part, (act_ref, inner_ref) in enumerate(
        ((act_mine, inner_mine), (act_theirs, inner_theirs))
    ):
        act_ref[...] = act[:, part * wide : part * wide + width]
        inner_ref[...] = inner[:, part * wide : part * wide + width]
    put(out_ref, dot_rows(act, w_back[...]))
    put(up_ref, dot_transposed(inner, w_in[...]))


def feed_forward(rows, cot, half, weights, biases, filled):
    count, sent_width = rows.shape
    model_width, both_wide = weights[0].shape
    ff_share = biases.shape[1]
    pad = both_wide // 2 - ff_share
    biases = jnp.pad(biases, ((0, 0), (0, pad))).reshape(1, both_wide)
    block = min(FF_ROWS, count)
    steps = count // block
    row_spec = pl.BlockSpec((block, sent_width), lambda i: (i, 0))
    joined = lambda width: pl.BlockSpec((block, width), lambda i: (half * steps + i, 0))
    act_shape = jax.ShapeDtypeStruct((2 * count, ff_share), BF16)
    row_shape = jax.ShapeDtypeStruct((2 * count, model_width), BF16)
    part_shape = jax.ShapeDtypeStruct((count, sent_width), F32)
    filled = () if filled is None else tuple(filled)
    return pl.pallas_call(
        functools.partial(feed_forward_body, len(filled)),
        out_shape=[act_shape] * 4
        + [row_shape] * 2
        + [part_shape] * 2
        + [jax.ShapeDtypeStruct((8, both_wide), F32)],
        grid=(steps,),
        in_specs=[row_spec, row_spec]
        + [fixed(matrix.shape) for matrix in weights]
        + [fixed((1, both_wide))]
        + [hbm()] * len(filled),
        out_specs=[joined(ff_share)] * 4
        + [joined(model_width)] * 2
        + [row_spec] * 2
        + [pl.BlockSpec((8, both_wide), lambda i: (0, 0))],
        input_output_aliases={5 + i: i for i in range(len(filled))},
        compiler_params=vmem(58),
        cost_estimate=lasting(34),
        name="feed_forward",
    )(rows, cot, *weights, biases, *filled)


def permute(value, axis_name, pairs):
    return lax.ppermute(value, axis_name, pairs)


def swap(value, axis_name, distance):
    count = lax.axis_size(axis_name)
    return permute(value, axis_name, [(i, i ^ distance) for i in range(count)])


def tie(*values):
    return lax.optimization_barrier(values)


def started(sent, value, mark):
    sent, mark = tie(sent, mark)
    value, mark = tie(value, swap(mark, "seq", 1))
    return sent, value, mark


def lower_pairs(pairs, y_count):
    return [
        (source * y_count + y, target * y_count + y)
        for source, target in pairs
        for y in range(y_count)
    ]


def spread_lead(block, z_here):
    far = permute(block, "dp", lower_pairs([(0, 2)], 2))
    held = jnp.where(z_here == 0, block, far)
    near = permute(held, "dp", lower_pairs([(0, 1), (2, 3)], 2))
    return jnp.where(z_here % 2 == 0, held, near)


def move_rest(block, distance, plane_distance):
    over_dp, over_seq = distance
    pairs = []
    for d in range(8):
        if (d // 2) ^ plane_distance != 0:
            pairs += [(d * 4 + q, (d ^ over_dp) * 4 + (q ^ over_seq)) for q in range(4)]
    return permute(block, ("dp", "seq"), pairs)


def pick(stacked, index, axis=0):
    return lax.dynamic_index_in_dim(stacked, index, axis, keepdims=False)


def halve_plane(lower, upper, y_here):
    return (
        jnp.where(y_here == 0, lower, upper),
        jnp.where(y_here == 0, upper, lower).astype(BF16),
    )


def sum_everywhere(value):
    for axis_name in ("seq", "dp"):
        distance = 1
        while distance < lax.axis_size(axis_name):
            value = value + swap(value, axis_name, distance)
            distance *= 2
    return value


def per_device(
    rows_in,
    out_cotangent,
    cell_lengths,
    cell_starts,
    key_mask,
    weights_master,
    first_moment,
    second_moment,
    small_master,
    small_first,
    small_second,
    step_count,
):
    model_width = rows_in.shape[3]
    local_rows = rows_in.shape[2]
    length = key_mask.shape[2]
    shard_len = weights_master.shape[2]
    groups = lax.axis_size("seq")
    dp_count = lax.axis_size("dp")
    head_share = model_width // groups
    heads_here = HEADS // groups
    triple = 3 * head_share
    first_end = model_width * triple
    second_end = first_end + head_share * model_width
    third_end = second_end + model_width * model_width
    seq_here = lax.axis_index("seq")
    dp_here = lax.axis_index("dp")
    chip = seq_here // 2
    core = seq_here % 2
    z_here = dp_here // 2
    y_here = dp_here % 2
    planar = dp_count == 8 and shard_len * 2 == first_end
    shares = (core + 2 * chip, core + 2 * (1 - chip))

    chip_index = chip.reshape(1).astype(jnp.int32)

    def exchange_micro(own, sent):
        received = swap(sent, "seq", 2)
        first = jnp.where(chip == 0, own, received)
        second = jnp.where(chip == 0, received, own)
        return jnp.concatenate([first, second], axis=0)

    def widen(rows):
        return jnp.pad(rows, ((0, 0), (0, lanes(model_width) - model_width)))

    mark = small_master[:8, :128]

    ends = jnp.array([first_end, second_end, third_end, dp_count * shard_len], jnp.int32)
    begin = dp_here * shard_len
    lower_matrix = jnp.sum((begin >= ends).astype(jnp.int32))
    upper_matrix = jnp.sum((begin + shard_len - 1 >= ends).astype(jnp.int32))
    bound = jnp.minimum(pick(ends, lower_matrix) - begin, shard_len).reshape(1)
    matrices = jnp.arange(4, dtype=jnp.int32)

    def matrix_sums(pair):
        return jnp.where(matrices == lower_matrix, pair[0], 0.0) + jnp.where(
            matrices == upper_matrix, pair[1], 0.0
        )

    weight = weights_master
    low_weight = round_weights(weight)
    if planar:
        tall = low_weight.reshape(shard_len // triple, triple)
    own_first, sent_rows = take_rows(chip_index, rows_in)
    own_in = exchange_micro(own_first, sent_rows)[:, :model_width]
    own_cotangent, sent_cotangent = take_rows(chip_index, out_cotangent)
    inputs = own_in.astype(F32)
    hat_one, _ = norm_stats(inputs)
    low_one = widen((hat_one * small_master[0] + small_master[1]).astype(BF16))
    other_one = swap(low_one, "seq", 1)
    weight_squares = square_sums(bound, weight)
    y_index = y_here.reshape(1).astype(jnp.int32)
    if planar:
        wide = low_weight.reshape(shard_len // model_width, model_width)
        cut, tall_rows = wide.shape[0], tall.shape[0]
        lead = spread_lead(tall, z_here)
        across = [move_rest(wide, (1, 0), 0)]
        over = [move_rest(wide, (0, 2), 0)]
        lead, wide, across[0], over[0], other_one, sent_cotangent = tie(
            lead, wide, across[0], over[0], other_one, sent_cotangent
        )
        lead_across = swap(lead, "dp", 1)
        halves = (lead, lead_across, swap(lead, "seq", 2), swap(lead_across, "seq", 2))
        dp_index = dp_here.reshape(1).astype(jnp.int32)
        far = move_rest(wide, (4, 0), 0)
        near = move_rest(wide, (2, 0), 0)
    else:
        copies = lax.all_gather(low_weight.reshape(1, shard_len), ("dp", "seq"), axis=0, tiled=True)
        copies = copies.reshape(dp_count, groups, shard_len)
        per_share = [pick(copies, share, 1).reshape(dp_count * shard_len) for share in shares]
        halves = []
        for flat in per_share:
            matrix = flat[:first_end].reshape(model_width, triple)
            first = jnp.where(y_here == 0, matrix[: model_width // 2], matrix[model_width // 2 :])
            second = jnp.where(y_here == 0, matrix[model_width // 2 :], matrix[: model_width // 2])
            halves += [first, second]
        w_out = [flat[first_end:second_end].reshape(head_share, model_width) for flat in per_share]
        beyond = lanes(model_width) - model_width
        w_in = jnp.concatenate(
            [
                jnp.pad(
                    flat[second_end:third_end].reshape(model_width, model_width),
                    ((0, 0), (0, beyond)),
                )
                for flat in per_share
            ],
            axis=1,
        )
        w_back = jnp.concatenate(
            [
                jnp.pad(flat[third_end:].reshape(model_width, model_width), ((0, beyond), (0, 0)))
                for flat in per_share
            ]
        )

    def share_columns(vector, share):
        return lax.dynamic_slice_in_dim(vector, share * head_share, head_share)

    attn_biases = [
        jnp.concatenate(
            [
                share_columns(small_master[4], share),
                jnp.zeros((head_share,), F32),
                share_columns(small_master[5], share),
            ]
        )
        for share in shares
    ]
    ff_biases = jnp.stack([pick(small_master, 8 + share) for share in shares])

    starts = pick(cell_starts[:, 0], chip)
    lengths = pick(cell_lengths[:, 0], chip)
    places = jnp.arange(length, dtype=jnp.int32)
    inside = (places[:, None] >= starts[None, :]) & (places[:, None] < (starts + lengths)[None, :])
    first_key = jnp.max(jnp.where(inside, starts[None, :], -1), axis=1)
    first_key = jnp.where(first_key < 0, places, first_key)
    low_blocks = first_key.reshape(-1, local_rows)[:, 0] // local_rows
    block_starts = first_key.reshape(-1, 1, local_rows)
    core_index = core.reshape(1).astype(jnp.int32)

    if planar:
        both = [move_rest(over[0], (1, 0), 0)]
        halves, near, far, both[0], weight_squares = tie(
            halves, near, far, both[0], weight_squares
        )
        last = move_rest(far, (2, 0), 2)
        across += [move_rest(near, (1, 0), 1), move_rest(far, (1, 0), 2)]
        over += [move_rest(near, (0, 2), 1), move_rest(far, (0, 2), 2)]
    *qkv, rows_one, w_attn_mine, w_attn_theirs = project(
        y_index, low_one, other_one, halves, jnp.stack(attn_biases)
    )

    def attend(part):
        return attention_forward(low_blocks, core_index, block_starts, qkv[part], heads_here)

    attended = [attend(0)]
    if planar:
        qkv[1], last, across[1:3], over[1:3], sent_cotangent, _ = tie(
            qkv[1], last, across[1:3], over[1:3], sent_cotangent, attended[0][2]
        )
        across.append(move_rest(last, (1, 0), 3))
        over.append(move_rest(last, (0, 2), 3))
        both += [move_rest(over[1], (1, 0), 1), move_rest(across[2], (0, 2), 2)]
    own_e = exchange_micro(own_cotangent, sent_cotangent)
    attended.append(attend(1))
    if planar:
        dp_index, across, over, both, _ = tie(dp_index, across, over, both, attended[1][2])
        both.append(move_rest(over[3], (1, 0), 3))
        rest_mine = [block for pair in zip((wide, near, far, last), across) for block in pair]
        rest_theirs = [block for pair in zip(over, both) for block in pair]
        out_mine, *joined = unpack_share(dp_index, rest_mine, head_share, model_width, 0, None)
        out_theirs, w_in, w_back = unpack_share(
            dp_index, rest_theirs, head_share, model_width, 1, joined
        )
        w_out = [out_mine, out_theirs]
        own_e, w_out[0] = tie(own_e, w_out[0])
    other_e = swap(own_e, "seq", 1)
    sent, kept = split_product([attended[0][0], attended[1][0]], w_out, False, model_width, BF16)
    middle, low_two = middle_norm(own_in, kept, swap(sent, "seq", 1), small_master)
    other_two = swap(low_two, "seq", 1)

    weights = (w_in, w_back)
    *filled, out_sent, up_sent, sums_sent = feed_forward(
        other_two, other_e, 1, weights, ff_biases, None
    )
    out_received = swap(out_sent, "seq", 1)
    up_received = swap(up_sent, "seq", 1)
    *filled, out_kept, up_kept, sums_kept = feed_forward(
        low_two, own_e, 0, weights, ff_biases, filled
    )
    activated, inner, (rows_two, rows_e) = filled[:2], filled[2:4], filled[4:]
    inner_sums = sums_sent + sums_kept

    link = BF16 if planar else F32
    grad_mid, low_mid, sums_two = norm_back(
        middle, up_kept, up_received, own_e, small_master[2:3], True
    )
    low_mid, rows_e = tie(low_mid, rows_e)
    back_sent = dot_columns(activated[1], rows_e).astype(link)
    back_sent, low_mid = tie(back_sent, low_mid)
    other_mid = swap(low_mid, "seq", 1)
    rows_two, other_mid = tie(rows_two, other_mid)
    in_sent = dot_columns(rows_two, inner[1]).astype(link)
    in_sent, low_mid = tie(in_sent, low_mid)
    back_received = swap(back_sent, "seq", 2)
    in_received = swap(in_sent, "seq", 2)

    grad_att_mine, grad_att_theirs, rows_mid = out_grads(low_mid, other_mid, w_out)
    out_sent_theirs = dot_columns(attended[1][0], rows_mid).astype(link)
    out_sent_theirs, rows_two, rows_e, rows_mid = tie(out_sent_theirs, rows_two, rows_e, rows_mid)
    outer_received = swap(out_sent_theirs, "seq", 2)
    share_back = dot_columns(activated[0], rows_e)
    share_in = dot_columns(rows_two, inner[0])
    share_out = dot_columns(attended[0][0], rows_mid)
    share_back, share_in, share_out, grad_att_theirs = tie(
        share_back, share_in, share_out, grad_att_theirs
    )

    def return_rows(lower, upper):
        return swap(jnp.where(chip == 0, upper, lower), "seq", 2)

    def attend_back(part, grad_att):
        return attention_backward(
            low_blocks,
            core_index,
            block_starts,
            qkv[part],
            grad_att,
            attended[part][1],
            attended[part][2],
            heads_here,
        )

    packed_theirs = attend_back(1, grad_att_theirs)
    attn_sent = dot_columns(rows_one, packed_theirs).astype(link)
    attn_sent, packed_theirs, outer_received = tie(attn_sent, packed_theirs, outer_received)
    theirs_part = partial_product(packed_theirs, w_attn_theirs)
    attn_sent, theirs_part, y_index, out_received = tie(
        attn_sent, theirs_part, y_index, out_received
    )
    attn_received = swap(attn_sent, "seq", 2)
    if planar:
        kept_rest, sent_rest = pack_rest(
            y_index,
            (share_out, share_in, share_back),
            (outer_received, in_received, back_received),
            cut,
        )
        result_rows = widen(
            (middle + ((out_kept + out_received)[:, :model_width] + small_master[7])).astype(BF16)
        )
        sent_rest, grad_att_mine, result_rows = tie(sent_rest, grad_att_mine, result_rows)
        result_halves = (result_rows[:local_rows], result_rows[local_rows:])
        result_received = return_rows(*result_halves)
        got_rest = swap(sent_rest, "dp", 1)
    else:
        result_rows = widen(
            (middle + ((out_kept + out_received)[:, :model_width] + small_master[7])).astype(BF16)
        )
        result_halves = (result_rows[:local_rows], result_rows[local_rows:])
        result_received = return_rows(*result_halves)
        share_back, share_in, share_out = (
            share_back + back_received,
            share_in + in_received,
            share_out + outer_received,
        )

    packed_mine = attend_back(0, grad_att_mine)
    packed_mine, result_received = tie(packed_mine, result_received)
    sent, kept = split_product(
        [packed_mine], [w_attn_mine], True, model_width, BF16, [theirs_part]
    )
    packed_mine, sent = tie(packed_mine, sent)
    share_attn = dot_columns(rows_one, packed_mine) + attn_received.astype(F32)
    if planar:
        z_odd = z_here % 2 == 1
        kept_lead, sent_lead = halve_plane(share_attn[:tall_rows], share_attn[tall_rows:], y_here)
        kept_lead, sent_lead, kept_rest = tie(kept_lead, sent_lead, kept_rest)
        got_lead = swap(sent_lead, "dp", 1)
        held = [kept_rest[i] + got_rest[i].astype(F32) for i in range(3)]
        sent_near = jnp.where(z_odd, held[1], held[0]).astype(BF16)
        sent_last = held[2].astype(BF16)
        kept_near = jnp.where(z_odd, held[0], held[1])
        kept_last = held[2]
        sent_near, sent_last, kept_lead = tie(sent_near, sent_last, kept_lead)
        got_near = swap(sent_near, "dp", 2)
        got_last = permute(sent_last, "dp", lower_pairs([(0, 1), (2, 3)], 2))
    packed = [packed_mine, packed_theirs]
    if planar:
        held_lead = kept_lead + got_lead.astype(F32)
        sent_lead = held_lead.astype(BF16)
        sent_lead, held_lead, kept_near, kept_last = tie(
            sent_lead, held_lead, kept_near, kept_last
        )
        near_lead = permute(sent_lead, "dp", lower_pairs([(1, 0), (3, 2)], 2))
        held_near = kept_near + got_near.astype(F32)
        held_last = kept_last + got_last.astype(F32)
        sent_far = jnp.where(z_here == 1, held_last, held_near).astype(BF16)
        own_rest = jnp.where(z_here == 3, held_last, held_near)
        sent_far, own_rest, held_lead = tie(sent_far, own_rest, held_lead)
        held_lead = held_lead + near_lead.astype(F32)
        sent_lead = held_lead.astype(BF16)
        sent_lead, held_lead, sent_far, kept = tie(sent_lead, held_lead, sent_far, kept)
        sent_lead, (kept, sent_far), mark = started(sent_lead, (kept, sent_far), mark)
        far_lead = permute(sent_lead, "dp", lower_pairs([(2, 0)], 2))
        got_far = permute(sent_far, "dp", lower_pairs([(3, 1), (0, 2), (1, 3)], 2))
    grad_x, sums_one = norm_back(
        own_in, kept, swap(sent, "seq", 1), grad_mid, small_master[0:1], False
    )

    result_all = place_rows(chip_index, result_rows, result_received, model_width)
    grad_halves = (grad_x[:local_rows], grad_x[local_rows:])
    grad_all = place_rows(chip_index, grad_x, return_rows(*grad_halves), model_width)

    def at_shares(columns):
        row = jnp.zeros((model_width,), F32)
        for share, column in zip(shares, columns):
            row = lax.dynamic_update_slice(row, column, (share * head_share,))
        return row

    bias_sums = [jnp.sum(packed[part].astype(F32), axis=0) for part in range(2)]
    inner_rows = jnp.zeros((4, model_width), F32)
    for part in range(2):
        first = part * lanes(model_width)
        inner_rows = lax.dynamic_update_slice(
            inner_rows, inner_sums[0:1, first : first + model_width], (shares[part], 0)
        )
    small_now = jnp.concatenate(
        [
            sums_one[:2],
            sums_two[:2],
            at_shares([sums[:head_share] for sums in bias_sums])[None],
            at_shares([sums[2 * head_share : triple] for sums in bias_sums])[None],
            sums_two[2:4],
            inner_rows,
        ]
    )

    if planar:
        lead_grad = (held_lead + far_lead.astype(F32))[:, :triple].reshape(1, 1, shard_len)
        own_rest, lead_grad, result_all, small_now = tie(
            own_rest, lead_grad, result_all, small_now
        )
        rest_grad = (own_rest + got_far.astype(F32)).reshape(1, 1, shard_len)
        leads = z_here == 0
    else:
        flat_here = jnp.concatenate(
            [matrix.reshape(-1) for matrix in (share_attn[:, :triple], share_out, share_in, share_back)]
        )
        lead_grad = lax.psum_scatter(
            flat_here.reshape(dp_count, shard_len), "dp", scatter_dimension=0, tiled=True
        ).reshape(1, 1, shard_len)
        rest_grad = lead_grad
        leads = z_here >= 0

    steps_done = step_count[0].astype(F32)
    fix_one = 1.0 - jnp.exp(steps_done * math.log(BETA_ONE))
    fix_two = 1.0 - jnp.exp(steps_done * math.log(BETA_TWO))
    ints = jnp.concatenate([bound, leads.astype(jnp.int32).reshape(1)])
    reduced, moments, update, update_squares = new_moments(
        ints,
        jnp.stack([fix_one, fix_two]),
        lead_grad,
        rest_grad,
        first_moment,
        second_moment,
        weight,
    )
    matrix_rows = jnp.stack([matrix_sums(weight_squares), matrix_sums(update_squares)])
    small_sum = sum_everywhere(
        jnp.concatenate([small_now, jnp.pad(matrix_rows, ((0, 2), (0, model_width - 4)))])
    )
    small_grad = small_sum[:12]
    weight_norms = jnp.sqrt(small_sum[12, :4])
    update_norms = jnp.sqrt(small_sum[13, :4])
    ratios = weight_norms / update_norms
    new_weight, weight_copy = new_weights(
        ints, jnp.stack([pick(ratios, lower_matrix), pick(ratios, upper_matrix)]), weight, update
    )
    small_one = BETA_ONE * small_first + (1.0 - BETA_ONE) * small_grad
    small_two = BETA_TWO * small_second + (1.0 - BETA_TWO) * small_grad * small_grad
    small_late = lax.dynamic_update_slice(small_master, mark, (0, 0))
    small_updated = small_late - SMALL_RATE * (small_one / fix_one) / (
        jnp.sqrt(small_two / fix_two) + ADAM_EPS
    )
    return (
        result_all,
        grad_all,
        reduced,
        moments,
        new_weight,
        weight_copy,
        jnp.stack([weight_norms, update_norms, ratios]),
        small_grad,
        jnp.stack([small_one, small_two]),
        small_updated,
    )


def solution(mesh):
    in_specs = (
        P(None, "dp", "seq", None),
        P(None, "dp", "seq", None),
        P(None, "dp", None),
        P(None, "dp", None),
        P(None, "dp", None),
        P("dp", "seq", None),
        P("dp", "seq", None),
        P("dp", "seq", None),
        P(),
        P(),
        P(),
        P(),
    )
    out_specs = (
        P(None, "dp", "seq", None),
        P(None, "dp", "seq", None),
        P("dp", "seq", None),
        P(None, "dp", "seq", None),
        P("dp", "seq", None),
        P("dp", "seq", None),
        P(),
        P(),
        P(),
        P(),
    )
    return jax.shard_map(
        per_device, mesh=mesh, in_specs=in_specs, out_specs=out_specs, check_vma=False
    )
```
